32 devices in a mesh: dp: 4 (over y, x), seq: 8 (over z, core).
Axes of the slice: x: 2, y: 2, z: 4, core: 2. Of those that a mesh axis runs over, the one named last changes fastest.
Arguments:
- hidden_in: bfloat16 [4, 1024, 768], P('dp', 'seq'), may hold values from -6 to 6
- query_weight: bfloat16 [768, 768], P('seq'), may hold values from -0.4375 to 0.4375
- query_bias: bfloat16 [768], P('seq'), may hold values from -2 to 2
- key_weight: bfloat16 [768, 768], P('seq'), may hold values from -0.21875 to 0.21875
- value_weight: bfloat16 [768, 768], P('seq'), may hold values from -0.21875 to 0.21875
- value_bias: bfloat16 [768], P('seq'), may hold values from -2 to 2
- output_weight: bfloat16 [768, 768], P('seq'), may hold values from -0.875 to 0.875
- output_bias: bfloat16 [768], P('seq'), may hold values from -2 to 2
- first_gain: bfloat16 [768], P('seq'), may hold values from 0.25 to 1.75
- first_shift: bfloat16 [768], P('seq'), may hold values from -2 to 2
- inner_weight: bfloat16 [768, 3072], P('seq'), may hold values from -0.21875 to 0.21875
- inner_bias: bfloat16 [3072], P('seq'), may hold values from -2 to 2
- outer_weight: bfloat16 [3072, 768], P('seq'), may hold values from -0.109375 to 0.109375
- outer_bias: bfloat16 [768], P('seq'), may hold values from -2 to 2
- second_gain: bfloat16 [768], P('seq'), may hold values from 0.25 to 1.75
- second_shift: bfloat16 [768], P('seq'), may hold values from -2 to 2
- segments: int32 [4, 1024], P('dp'), may hold values from 0 to 3, never falling along the last dimension, each value on 1 to 512 neighbouring positions
- random_blocks: int32 [4, 16, 12, 3], P('dp'), may hold values from 0 to 15, as said below
- cotangent: bfloat16 [4, 1024, 768], P('dp', 'seq'), may hold values from -6 to 6
Outputs:
- layer_out: bfloat16 [4, 1024, 768], P('dp', 'seq')
- input_grad: float32 [4, 1024, 768], P('dp', 'seq')
- query_weight_grad: float32 [768, 768], P('seq')
- query_bias_grad: float32 [768], P('seq')
- key_weight_grad: float32 [768, 768], P('seq')
- value_weight_grad: float32 [768, 768], P('seq')
- value_bias_grad: float32 [768], P('seq')
- output_weight_grad: float32 [768, 768], P('seq')
- output_bias_grad: float32 [768], P('seq')
- first_gain_grad: float32 [768], P('seq')
- first_shift_grad: float32 [768], P('seq')
- inner_weight_grad: float32 [768, 3072], P('seq')
- inner_bias_grad: float32 [3072], P('seq')
- outer_weight_grad: float32 [3072, 768], P('seq')
- outer_bias_grad: float32 [768], P('seq')
- second_gain_grad: float32 [768], P('seq')
- second_shift_grad: float32 [768], P('seq')
The draws below stay inside these ranges and needn't reach their ends.
Inputs may be any that keep to these rules, and one draw needn't show every extreme that they name: `random_blocks`: entry [s, b, h, i] names a block of sequence s. Take one index o of seq: its query blocks o * 2 to o * 2 + 1 of the one sequence of one index of dp, over all heads and slots, make 72 entries; at most 14 of them name blocks of any one piece (blocks p * 2 to p * 2 + 1), and some piece is named exactly 14 times. An entry may repeat a sliding or global block.
All inputs are finite; a program needn't handle non-finite values.
Results may differ from the reference program's by a relative error of at most 0.017.
Values may be sent and summed in bfloat16 or wider, within the bound.
No kernel may reach another device: no remote copies, remote signals or barrier semaphores. Data moves between devices by JAX's collectives and lax.ppermute only.
A program may use at most 128 MiB of HBM per device.

```python
import math
import jax
import jax.numpy as jnp
import numpy as np
from jax import lax

D = 768
HEADS = 12
HD = 64
FF = 3072
BLOCK = 64
RAND = 3
BLK_DEV = 2
SEQ_DP = 1
SPLITS = 8
SEQ_LEN = 1024
NB = 16
SEQS = 4
REQS = 72
CAP = 14
DOC_MAX = 512
DOCS = 4


def draw_random_blocks(key, part):
    group_count = SEQS // SEQ_DP
    device_count = group_count * SPLITS
    slot_count = SPLITS * CAP
    key_full, key_order, key_shuffle, key_local = jax.random.split(key, 4)
    slot_owner = jnp.arange(slot_count, dtype=jnp.int32) // CAP
    favored = jax.random.randint(key_full, (device_count, 1), 0, SPLITS, dtype=jnp.int32)
    ranking = jax.random.randint(key_order, (device_count, slot_count), 0, 2 ** 20, dtype=jnp.int32) * slot_count + jnp.arange(slot_count, dtype=jnp.int32)[None, :]
    ranking = jnp.where(slot_owner[None, :] == favored, jnp.arange(slot_count, dtype=jnp.int32)[None, :] - slot_count, ranking)
    chosen = jnp.argsort(ranking, axis=1, stable=True)[:, :REQS]
    owners = slot_owner[chosen]
    mixing = jax.random.randint(key_shuffle, (device_count, REQS), 0, 2 ** 20, dtype=jnp.int32) * REQS + jnp.arange(REQS, dtype=jnp.int32)[None, :]
    owners = jnp.take_along_axis(owners, jnp.argsort(mixing, axis=1, stable=True), axis=1)
    local_ids = jax.random.randint(key_local, (device_count, REQS), 0, BLK_DEV, dtype=jnp.int32)
    picked = owners * BLK_DEV + local_ids
    picked = picked.reshape(group_count, SPLITS, SEQ_DP, BLK_DEV, HEADS, RAND).transpose(0, 2, 1, 3, 4, 5)
    return picked.reshape(SEQS, NB, HEADS, RAND)


def steps_of(key, shape, pieces, smallest, top_value):
    level, own = 1.0, jax.random.fold_in(key, 6)
    for axis_at, blocks in pieces:
        heights = jnp.exp(jax.random.uniform(jax.random.fold_in(own, axis_at), (blocks,), jnp.float32, smallest / len(pieces), top_value / len(pieces)))
        level = level * jnp.repeat(heights, shape[axis_at] // blocks).reshape([-1 if axis == axis_at else 1 for axis in range(len(shape))])
    return level


def length_profile(amount, total, limit, lean):
    weights = [(1 << 20) // math.isqrt(grade ** lean) + 1 for grade in range(2, amount + 1)]
    spare, given = total - limit - (amount - 1), [1] * (amount - 1)
    while spare > 0:
        movable = [i for i in range(amount - 1) if given[i] < limit]
        pool, remaining = sum([weights[i] for i in movable]), spare
        for i in movable:
            more = min(limit - given[i], max(1, remaining * weights[i] // pool), spare)
            given[i] = given[i] + more
            spare = spare - more
    return np.array([limit] + given)


def uneven(stream_key, count, total, limit, lean):
    if count == 2:
        one = jax.random.randint(stream_key, (), max(1, total - limit), min(limit, total - 1) + 1)
        return jnp.stack([one, total - one])
    lengths = jnp.asarray(length_profile(count, total, limit, lean), jnp.int32)
    twos = (count - 1) // 2
    donor, taker = lengths[1:1 + 2 * twos:2], lengths[2:2 + 2 * twos:2]
    room = jnp.minimum(donor - 1, limit - taker)
    moved = jax.random.randint(jax.random.fold_in(stream_key, 1), (twos,), 0, 1 << 20) % (room + 1)
    lengths = lengths.at[1:1 + 2 * twos:2].set(donor - moved).at[2:2 + 2 * twos:2].set(taker + moved)
    return lengths[jax.random.permutation(jax.random.fold_in(stream_key, 2), count)]


def gaussian(key, extent, width, bound, cuts=(), kind=jnp.bfloat16):
    entries = jax.random.normal(key, extent, jnp.float32) * width
    if len(cuts) > 0:
        entries = steps_of(key, extent, cuts, -0.22, 0.18) * entries
    return jnp.clip(entries, min=-bound, max=bound).astype(kind)


def setup_inputs(seed: int = 0) -> dict:
    splits = jax.random.split(jax.random.key(seed), 20)
    return {
        "hidden_in": gaussian(splits[0], (SEQS, SEQ_LEN, D), 1.0, 6.0, ((0, 4), (1, 8))),
        "query_weight": gaussian(splits[1], (D, D), (D // 4) ** -0.5, 0.4375, ((0, 8),)),
        "query_bias": gaussian(splits[2], (D,), 0.3, 2.0, ((0, 8),)),
        "key_weight": gaussian(splits[3], (D, D), D ** -0.5, 0.21875, ((0, 8),)),
        "value_weight": gaussian(splits[4], (D, D), D ** -0.5, 0.21875, ((0, 8),)),
        "value_bias": gaussian(splits[5], (D,), 0.3, 2.0, ((0, 8),)),
        "output_weight": gaussian(splits[6], (D, D), (D // 16) ** -0.5, 0.875, ((0, 8),)),
        "output_bias": gaussian(splits[7], (D,), 0.3, 2.0, ((0, 8),)),
        "first_gain": jnp.clip(1.0 + 0.15 * jax.random.normal(splits[8], (D,), jnp.float32), 0.25, 1.75).astype(jnp.bfloat16),
        "first_shift": gaussian(splits[9], (D,), 0.3, 2.0, ((0, 8),)),
        "inner_weight": gaussian(splits[10], (D, FF), D ** -0.5, 0.21875, ((0, 8),)),
        "inner_bias": gaussian(splits[11], (FF,), 0.3, 2.0, ((0, 8),)),
        "outer_weight": gaussian(splits[12], (FF, D), FF ** -0.5, 0.109375, ((0, 8),)),
        "outer_bias": gaussian(splits[13], (D,), 0.3, 2.0, ((0, 8),)),
        "second_gain": jnp.clip(1.0 + 0.15 * jax.random.normal(splits[14], (D,), jnp.float32), 0.25, 1.75).astype(jnp.bfloat16),
        "second_shift": gaussian(splits[15], (D,), 0.3, 2.0, ((0, 8),)),
        "segments": jax.vmap(lambda own: jnp.searchsorted(jnp.cumsum(uneven(own, DOCS, SEQ_LEN, DOC_MAX, 0)), jnp.arange(SEQ_LEN), side="right"))(jax.random.split(splits[16], SEQS)).reshape((SEQS, SEQ_LEN)).astype(jnp.int32),
        "random_blocks": draw_random_blocks(jax.random.fold_in(splits[19], 71), 0),
        "cotangent": gaussian(splits[18], (SEQS, SEQ_LEN, D), 1.0, 6.0, ((0, 4), (1, 8))),
    }


@jax.custom_vjp
def low(v):
    return lax.optimization_barrier(v.astype(jnp.bfloat16)).astype(jnp.float32)

@jax.custom_vjp
def low_back(v):
    return v

def low_keep(v):
    return (low(v), None)

def low_pass(kept, grad):
    return (grad,)

def back_keep(v):
    return (v, None)

def back_low(kept, grad):
    return (low(grad),)
low.defvjp(low_keep, low_pass)
low_back.defvjp(back_keep, back_low)
HIGH = lax.Precision.HIGHEST
EPSILON = 1e-12
MASKED = -1000000000.0

def matmul(left, right):
    return jnp.dot(left, right, precision=HIGH)

def layer_norm(values, gain, shift):
    center = values - lax.optimization_barrier(jnp.mean(values, -1, keepdims=True))
    spread = lax.optimization_barrier(jnp.mean(center * center, -1, keepdims=True))
    return center * lax.rsqrt(spread + EPSILON) * gain + shift

def attend_sequence(inputs):
    query, keys, values, segment_ids, random_ids = inputs
    block_count = query.shape[0] // BLOCK
    query_blocks = query.reshape(block_count, BLOCK, HEADS, HD)
    key_blocks = keys.reshape(block_count, BLOCK, HEADS, HD)
    value_blocks = values.reshape(block_count, BLOCK, HEADS, HD)
    zero_block = jnp.zeros((1, BLOCK, HEADS, HD), jnp.float32)
    key_padded = jnp.concatenate([zero_block, key_blocks, zero_block], 0)
    value_padded = jnp.concatenate([zero_block, value_blocks, zero_block], 0)
    seg_blocks = segment_ids.astype(jnp.int32).reshape(block_count, BLOCK)
    seg_edge = jnp.full((1, BLOCK), -1, jnp.int32)
    seg_padded = jnp.concatenate([seg_edge, seg_blocks, seg_edge], 0)
    positions = jnp.arange(block_count, dtype=jnp.int32)
    fixed_ids = jnp.stack([positions, positions + 1, positions + 2, jnp.ones_like(positions), jnp.full_like(positions, block_count)], 1).astype(jnp.int32)
    head_ids = jnp.arange(HEADS, dtype=jnp.int32)[None, :, None]
    random_ids = random_ids.astype(jnp.int32)

    def fixed_part(padded):
        picked = padded[fixed_ids]
        return picked.transpose(0, 3, 1, 2, 4).reshape(block_count, HEADS, 5 * BLOCK, HD)

    def random_part(blocks):
        by_head = blocks.transpose(2, 0, 1, 3)
        return by_head[head_ids, random_ids].reshape(block_count, HEADS, RAND * BLOCK, HD)
    key_all = jnp.concatenate([fixed_part(key_padded), random_part(key_blocks)], 2)
    value_all = jnp.concatenate([fixed_part(value_padded), random_part(value_blocks)], 2)
    sliding_seg = seg_padded[fixed_ids[:, :3]].reshape(block_count, 3 * BLOCK)
    global_seg = jnp.full((block_count, 2 * BLOCK), -2, jnp.int32)
    seg_fixed = jnp.concatenate([sliding_seg, global_seg], 1)
    seg_fixed = jnp.broadcast_to(seg_fixed.reshape(block_count, 1, 5 * BLOCK), (block_count, HEADS, 5 * BLOCK))
    seg_random = seg_blocks[random_ids].reshape(block_count, HEADS, RAND * BLOCK)
    seg_keys = jnp.concatenate([seg_fixed, seg_random], 2)
    scores = jnp.einsum('nqhe,nhke->nhqk', query_blocks, key_all, precision=HIGH) * HD ** (-0.5)
    allowed = (seg_blocks[:, None, :, None] == seg_keys[:, :, None, :]) | (seg_keys[:, :, None, :] == -2)
    scores = low_back(jnp.where(allowed, scores, MASKED))
    probs = low(jax.nn.softmax(scores, axis=-1))
    attended = jnp.einsum('nhqk,nhke->nqhe', probs, value_all, precision=HIGH)
    return attended.reshape(block_count * BLOCK, D)

def layer(hidden, query_weight, query_bias, key_weight, value_weight, value_bias, output_weight, output_bias, first_gain, first_shift, inner_weight, inner_bias, outer_weight, outer_bias, second_gain, second_shift, segments, random_blocks):
    flat = hidden.reshape(SEQS * SEQ_LEN, D)
    query = low_back(low(matmul(flat, query_weight) + query_bias))
    keys = low_back(low(matmul(flat, key_weight)))
    values = low_back(low(matmul(flat, value_weight) + value_bias))
    attended = lax.map(jax.checkpoint(attend_sequence), (query.reshape(SEQS, SEQ_LEN, D), keys.reshape(SEQS, SEQ_LEN, D), values.reshape(SEQS, SEQ_LEN, D), segments, random_blocks))
    attended = low_back(low(attended.reshape(SEQS * SEQ_LEN, D)))
    branch = low_back(matmul(attended, output_weight) + output_bias)
    first_norm = layer_norm(flat + branch, first_gain, first_shift)
    inner = low_back(matmul(low(first_norm), inner_weight) + inner_bias)
    activated = low(jax.nn.gelu(inner, approximate=True))
    mixed = low_back(matmul(activated, outer_weight) + outer_bias)
    return layer_norm(first_norm + mixed, second_gain, second_shift).reshape(SEQS, SEQ_LEN, D)

def reference(hidden_in, query_weight, query_bias, key_weight, value_weight, value_bias, output_weight, output_bias, first_gain, first_shift, inner_weight, inner_bias, outer_weight, outer_bias, second_gain, second_shift, segments, random_blocks, cotangent):
    floats = [item.astype(jnp.float32) for item in (hidden_in, query_weight, query_bias, key_weight, value_weight, value_bias, output_weight, output_bias, first_gain, first_shift, inner_weight, inner_bias, outer_weight, outer_bias, second_gain, second_shift)]

    def forward(*arrays):
        return layer(*arrays, segments, random_blocks)
    result, pullback = jax.vjp(forward, *floats)
    grads = pullback(cotangent.astype(jnp.float32))
    return (result.astype(jnp.bfloat16), grads[0], grads[1], grads[2], grads[3], grads[4], grads[5], grads[6], grads[7], grads[8], grads[9], grads[10], grads[11], grads[12], grads[13], grads[14], grads[15])
```

```python
import functools

import jax
import jax.numpy as jnp
from jax import lax
from jax.experimental import pallas as pl
from jax.experimental.pallas import tpu as pltpu
from jax.sharding import PartitionSpec as P

HEADS = 12
BLOCK = 64
EPSILON = 1e-12
MASKED = -1000000000.0
GELU_A = 0.7978845608028654
GELU_B = 0.044715
VMEM_BYTES = 48 << 20
bf16 = jnp.bfloat16
f32 = jnp.float32


def matmul(left, right):
    return jnp.dot(left, right, preferred_element_type=f32)


def left_product(left, right):
    return lax.dot_general(left, right, (((0,), (0,)), ((), ())), preferred_element_type=f32)


def right_product(left, right):
    return lax.dot_general(left, right, (((1,), (1,)), ((), ())), preferred_element_type=f32)


def run_kernel(kernel, name, outs, args, scratch=(), scalars=0, flops=0, powers=0):
    specs = [pl.BlockSpec(memory_space=pltpu.SMEM)] * scalars
    specs += [pl.BlockSpec(memory_space=pltpu.VMEM)] * (len(args) - scalars)
    out_shape = tuple(jax.ShapeDtypeStruct(shape, dtype) for shape, dtype in outs)
    moved = sum(a.size * a.dtype.itemsize for a in args)
    moved += sum(o.size * o.dtype.itemsize for o in out_shape)
    return pl.pallas_call(
        kernel,
        name=name,
        out_shape=out_shape,
        in_specs=specs,
        out_specs=tuple(pl.BlockSpec(memory_space=pltpu.VMEM) for _ in outs),
        scratch_shapes=list(scratch),
        compiler_params=pltpu.CompilerParams(vmem_limit_bytes=VMEM_BYTES),
        cost_estimate=pl.CostEstimate(flops=flops, bytes_accessed=moved, transcendentals=powers),
    )(*args)


def normalize(values):
    center = values - jnp.mean(values, -1, keepdims=True)
    spread = jnp.mean(center * center, -1, keepdims=True)
    inverse = lax.rsqrt(spread + EPSILON)
    return center * inverse, inverse


def norm_back(grad, normed, inverse, gain):
    scaled = grad * gain
    return inverse * (
        scaled
        - jnp.mean(scaled, -1, keepdims=True)
        - normed * jnp.mean(scaled * normed, -1, keepdims=True)
    )


def bias_rows(be_ref, bn, same, head, block, blocks, block_len):
    width = same.shape[1]
    rows = [
        jnp.broadcast_to(be_ref[head * blocks + block + i : head * blocks + block + i + 1, :], (block_len, width))
        for i in range(same.shape[0] // block_len)
    ]
    return jnp.where(same, jnp.concatenate(rows, 0), bn)


def attend_kernel(ids, hid, w, qb, vb, be, bn, sk, sq, att, qo, ko, vo, lse, qs):
    pieces, piece_len, width = qs.shape
    chips = pieces // 2
    core = ids[0]
    size = 64
    heads = width // size
    blocks = be.shape[0] // heads
    per_piece = blocks // chips
    block_len = piece_len // per_piece
    model = hid.shape[2]
    tokens = hid[:, :piece_len, :].reshape(pieces * piece_len, model)
    product = matmul(tokens, w[...])
    query = (product[:, :width] + qb[...]).astype(bf16) * bf16(size**-0.5)
    qs[...] = query.reshape(pieces, piece_len, width)
    ko[...] = product[:, width : 2 * width].astype(bf16)
    vo[...] = (product[:, 2 * width :] + vb[...]).astype(bf16)
    for chip in range(chips):
        qo[chip] = qs[2 * chip + core]
    lane = lax.broadcasted_iota(jnp.int32, (piece_len, 128), 1)
    for chip in range(chips):
        same = sq[chip * piece_len : (chip + 1) * piece_len, :] == sk[...]
        logs = jnp.zeros((piece_len, 128), f32)
        outs = []
        for head in range(heads):
            cols = slice(head * size, (head + 1) * size)
            scores = right_product(qo[chip, :, cols], ko[:, cols])
            scores = scores + bias_rows(be, bn[...], same, head, chip * per_piece, blocks, block_len)
            top = jnp.max(scores, -1, keepdims=True)
            powers = jnp.exp(scores - top)
            total = jnp.sum(powers, -1, keepdims=True)
            probs = (powers * (1.0 / total)).astype(bf16)
            outs.append(matmul(probs, vo[:, cols]).astype(bf16))
            logs = jnp.where(lane == head, top + jnp.log(total), logs)
        att[chip] = jnp.concatenate(outs, 1)
        lse[chip] = logs


def attend_back_kernel(
    ids, hid, q, k, v, ga, lse, be, bn, sk, sq, dq, mine, other, dwm, dwo, ds_all, p_all, dkv, dws
):
    chips, piece_len, width = q.shape
    pieces = 2 * chips
    core = ids[0]
    chip_at = ids[1]
    size = 64
    heads = width // size
    blocks = be.shape[0] // heads
    per_piece = blocks // chips
    block_len = piece_len // per_piece
    model = hid.shape[2]
    dks = []
    dvs = []
    dqs = [[None] * heads for _ in range(chips)]
    for head in range(heads):
        cols = slice(head * size, (head + 1) * size)
        key = k[:, cols]
        value = v[:, cols]
        for chip in range(chips):
            rows = slice(chip * piece_len, (chip + 1) * piece_len)
            same = sq[rows, :] == sk[...]
            scores = right_product(q[chip, :, cols], key)
            scores = scores + bias_rows(be, bn[...], same, head, chip * per_piece, blocks, block_len)
            probs = jnp.exp(scores - lse[chip, :, head : head + 1])
            grad = right_product(ga[chip, :, cols], value)
            weighted = jnp.sum(probs * grad, -1, keepdims=True)
            ds = (probs * (grad - weighted)).astype(bf16)
            ds_all[rows, :] = ds
            p_all[rows, :] = probs.astype(bf16)
            dqs[chip][head] = (matmul(ds, key) * (size**-0.5)).astype(bf16)
        queries = q[:, :, cols].reshape(chips * piece_len, size)
        grads = ga[:, :, cols].reshape(chips * piece_len, size)
        dks.append(left_product(ds_all[...], queries).astype(bf16))
        dvs.append(left_product(p_all[...], grads).astype(bf16))
    for chip in range(chips):
        dq[chip] = jnp.concatenate(dqs[chip], 1)
    joined = jnp.concatenate(dks + dvs, 1)
    dkv[...] = joined.reshape(pieces, piece_len, 2 * width)
    for chip in range(chips):
        mine[chip] = dkv[2 * chip + core]
        other[chip] = dkv[2 * chip + 1 - core]
    tokens = hid[:, :piece_len, :].reshape(pieces * piece_len, model)
    owned = jnp.concatenate([hid[2 * chip + core, :piece_len, :] for chip in range(chips)], 0)
    grad_q = dq[...].reshape(chips * piece_len, width)
    rows = model // pieces
    weights = jnp.concatenate([left_product(owned, grad_q), left_product(tokens, joined)], 1)
    dws[:, :rows, :] = weights.reshape(pieces, rows, 3 * width)
    sums = jnp.concatenate(
        [
            jnp.sum(grad_q.astype(f32), 0, keepdims=True),
            jnp.sum(joined.astype(f32), 0, keepdims=True),
        ],
        1,
    )
    for piece in range(pieces):
        keep = (chip_at == piece // 2).astype(f32)
        dws[piece, rows:, :] = jnp.broadcast_to(sums * keep, (8, 3 * width))
    for chip in range(chips):
        dwm[chip] = dws[2 * chip + core]
        dwo[chip] = dws[2 * chip + 1 - core].astype(bf16)


def input_grad_kernel(dq, mine, recv, w, out):
    chips, piece_len, width = dq.shape
    dkv = (mine[...].astype(f32) + recv[...].astype(f32)).astype(bf16)
    grads = jnp.concatenate([dq[...], dkv], 2).reshape(chips * piece_len, 3 * width)
    out[...] = right_product(grads, w[...]).astype(bf16).reshape(out.shape)


def project_kernel(att, wo, hid, vec, low, normed, inverse):
    chips, piece_len, width = att.shape
    weight = wo[...].reshape(chips * width, -1)
    branch = vec[2:3, :] + jnp.zeros((piece_len, weight.shape[1]), f32)
    for chip in range(chips):
        branch = branch + matmul(att[chip], weight[chip * width : (chip + 1) * width])
    n1, r1 = normalize(hid[...].astype(f32) + branch)
    low[...] = (n1 * vec[3:4, :] + vec[4:5, :]).astype(bf16)
    normed[...] = n1
    inverse[...] = jnp.broadcast_to(r1, inverse.shape)


def gelu_parts(v):
    inside = GELU_A * (v + GELU_B * (v * v * v))
    return jnp.tanh(inside)


def forward_kernel(ids, *refs):
    parts = (len(refs) - 5) // 2
    x = refs[:parts]
    w1, w2, vec = refs[parts : parts + 3]
    outs = refs[parts + 3 : 2 * parts + 3]
    inner_ref, act_ref = refs[2 * parts + 3 :]
    rows = x[0].shape[0]
    weight1 = w1[...].reshape(-1, w1.shape[-1])
    weight2 = w2[...].reshape(-1, w2.shape[-1])
    tokens = jnp.concatenate([r[...] for r in x], 0)
    inner = matmul(tokens, weight1) + vec[pl.ds(8 + ids[2], 1), :]
    act = (0.5 * inner * (1.0 + gelu_parts(inner))).astype(bf16)
    inner_ref[...] = inner
    act_ref[...] = act
    mixed = matmul(act, weight2)
    for i in range(parts):
        outs[i][...] = mixed[i * rows : (i + 1) * rows].astype(outs[i].dtype)


def middle_kernel(*refs):
    recv = refs[:-7]
    normed, cot, vec, out, low, mix, sums = refs[-7:]
    first = normed[...] * vec[3:4, :] + vec[4:5, :]
    mixed = vec[5:6, :]
    for r in recv:
        mixed = mixed + r[...].astype(f32)
    n2, r2 = normalize(first + mixed)
    gain = vec[6:7, :]
    out[...] = (n2 * gain + vec[7:8, :]).astype(bf16)
    g = cot[...].astype(f32)
    grad = norm_back(g, n2, r2, gain)
    rounded = grad.astype(bf16)
    mix[...] = grad
    low[...] = rounded
    sums[0:1, :] = jnp.sum(g * n2, 0, keepdims=True)
    sums[1:2, :] = jnp.sum(g, 0, keepdims=True)
    sums[2:3, :] = jnp.sum(rounded.astype(f32), 0, keepdims=True)
    sums[3:, :] = jnp.zeros((5, sums.shape[1]), f32)


def backward_kernel(*refs):
    parts = (len(refs) - 5) // 2
    grads = refs[:parts]
    w1, w2, inner_ref = refs[parts : parts + 3]
    outs = refs[parts + 3 : 2 * parts + 3]
    gi_ref, sum_ref = refs[2 * parts + 3 :]
    rows = grads[0].shape[0]
    weight1 = w1[...].reshape(-1, w1.shape[-1])
    weight2 = w2[...].reshape(-1, w2.shape[-1])
    gm = jnp.concatenate([r[...] for r in grads], 0)
    grad_act = right_product(gm, weight2)
    v = inner_ref[...]
    t = gelu_parts(v)
    slope = 0.5 * (1.0 + t) + 0.5 * v * (1.0 - t * t) * (GELU_A * (1.0 + 3.0 * GELU_B * (v * v)))
    gi = (grad_act * slope).astype(bf16)
    gi_ref[...] = gi
    sum_ref[...] = jnp.sum(gi.astype(f32), 0, keepdims=True)
    first = right_product(gi, weight1)
    for i in range(parts):
        outs[i][...] = first[i * rows : (i + 1) * rows].astype(outs[i].dtype)


def residual_kernel(*refs):
    recv = refs[:-9]
    mix, normed, inverse, vec, wo, res, low, back, sums = refs[-9:]
    first = mix[...]
    for r in recv:
        first = first + r[...].astype(f32)
    n1 = normed[...]
    grad = norm_back(first, n1, inverse[:, 0:1], vec[3:4, :])
    rounded = grad.astype(bf16)
    res[...] = grad
    low[...] = rounded
    sums[0:1, :] = jnp.sum(first * n1, 0, keepdims=True)
    sums[1:2, :] = jnp.sum(first, 0, keepdims=True)
    sums[2:3, :] = jnp.sum(rounded.astype(f32), 0, keepdims=True)
    sums[3:, :] = jnp.zeros((5, sums.shape[1]), f32)
    weight = wo[...].reshape(-1, wo.shape[-1])
    chips, _, width = back.shape
    for chip in range(chips):
        back[chip] = right_product(rounded, weight[chip * width : (chip + 1) * width]).astype(bf16)


def weight_grad_kernel(*refs):
    parts = (len(refs) - 7) // 2
    x = refs[:parts]
    gm = refs[parts : 2 * parts]
    gi, act, att, gb, d1, d2, do = refs[2 * parts :]
    rows = x[0].shape[0]
    tokens = jnp.concatenate([r[...] for r in x], 0)
    grads = jnp.concatenate([r[...] for r in gm], 0)
    d1[...] = left_product(tokens, gi[...]).astype(bf16).reshape(d1.shape)
    d2[...] = left_product(act[...], grads).astype(bf16).reshape(d2.shape)
    chips, _, width = att.shape
    for chip in range(chips):
        do[chip * width : (chip + 1) * width, :] = left_product(att[chip], gb[...]).astype(bf16)


def finish_kernel(t0, t1, t2, t3, gq, gk, gv, bias):
    chips, _, wide = t0.shape
    width = wide // 3
    rows = gq.shape[0]
    total = t0[...].astype(f32)
    for r in (t1, t2, t3):
        total = total + r[...].astype(f32)
    for i, out in enumerate((gq, gk, gv)):
        out[...] = jnp.concatenate(
            [total[chip, :rows, i * width : (i + 1) * width] for chip in range(chips)], 1
        )
    bias[...] = total[:, rows:, :]


def log_counts(count):
    return jnp.where(count > 0, jnp.log(jnp.maximum(count, 1).astype(f32)), MASKED)


class HeadAttention:
    def __init__(self, hidden, weights, biases, segments, random_blocks, vec_local):
        self.splits = splits = lax.axis_size("seq")
        self.chips = chips = splits // 2
        self.position = position = lax.axis_index("seq")
        core = position % 2
        chip = position // 2
        self.ids = jnp.stack([core, chip, lax.axis_index("dp")]).astype(jnp.int32)
        self.hidden = hidden
        piece_len, model = hidden.shape
        rows = model // splits
        width = model // chips
        heads = HEADS // chips
        self.lines = [[2 * i + c for i in range(chips)] for c in range(2)]
        self.swap = [(i, i ^ 1) for i in range(splits)]
        extra = 8 * model - vec_local.shape[0]
        tail = jnp.concatenate([vec_local, jnp.zeros((extra,), bf16)]).reshape(8, model)
        packed = lax.all_gather(jnp.concatenate([hidden, tail], 0), "seq")
        self.packed = packed
        self.vec_all = packed[:, piece_len : piece_len + 8].reshape(splits, 8 * model)[
            :, : vec_local.shape[0]
        ]
        split = jnp.concatenate([w.reshape(rows, chips, width) for w in weights], 2)
        lined = self.line(split.transpose(1, 0, 2))
        swapped = lax.ppermute(lined, "seq", self.swap)
        even = jnp.where(core == 0, lined, swapped)
        odd = jnp.where(core == 0, swapped, lined)
        self.weight = jnp.stack([even, odd], 1).reshape(model, 3 * width)
        pair = jnp.stack(biases, 0)
        pair_other = lax.ppermute(pair, "seq", self.swap)
        bias = jnp.where(
            core == 0,
            jnp.concatenate([pair, pair_other], 1),
            jnp.concatenate([pair_other, pair], 1),
        ).astype(f32)
        self.bias_q, self.bias_v = bias[0:1], bias[1:2]
        block_count = segments.shape[1] // BLOCK
        per_piece = piece_len // BLOCK
        own = random_blocks[0].reshape(chips, 2, per_piece, HEADS, -1)
        own = lax.dynamic_index_in_dim(own, core, 1, keepdims=False)
        own = lax.dynamic_slice_in_dim(own, chip * heads, heads, 2)
        own = own.reshape(chips * per_piece, heads, -1).transpose(1, 0, 2)
        block = jnp.arange(block_count, dtype=jnp.int32)
        mine = (
            (jnp.arange(chips, dtype=jnp.int32)[:, None] * 2 + core) * per_piece
            + jnp.arange(per_piece, dtype=jnp.int32)[None, :]
        ).reshape(-1)
        ends = ((block == 0) | (block == block_count - 1)).astype(jnp.int32)
        near = (jnp.abs(block[None, :] - mine[:, None]) <= 1).astype(jnp.int32)
        listed = jnp.sum((own[..., None] == block).astype(jnp.int32), 2)
        count = listed + near[None] + ends
        self.same_bias = jnp.repeat(log_counts(count).reshape(-1, block_count), BLOCK, axis=1)
        self.other_bias = jnp.repeat(
            jnp.where(ends > 0, 0.0, MASKED).astype(f32)[None], BLOCK, axis=1
        )
        self.key_seg = segments
        self.query_seg = lax.dynamic_index_in_dim(
            segments.reshape(chips, 2, piece_len), core, 1, keepdims=False
        ).reshape(chips * piece_len, 1)
        self.piece_len, self.width, self.model = piece_len, width, model

    def line(self, array):
        return lax.all_to_all(
            array, "seq", 0, 0, tiled=True, axis_index_groups=self.lines
        )

    def masks(self):
        return (self.same_bias, self.other_bias, self.key_seg, self.query_seg)

    def forward(self):
        chips, piece_len, width = self.chips, self.piece_len, self.width
        tokens = self.splits * piece_len
        one = (chips, piece_len, width)
        att, self.q, self.k, self.v, self.lse = run_kernel(
            attend_kernel,
            "attend",
            [
                (one, bf16),
                (one, bf16),
                ((tokens, width), bf16),
                ((tokens, width), bf16),
                ((chips, piece_len, 128), f32),
            ],
            (self.ids, self.packed, self.weight, self.bias_q, self.bias_v) + self.masks(),
            scratch=[pltpu.VMEM((self.splits, piece_len, width), bf16)],
            scalars=1,
            flops=6 * tokens * self.model * width + 2 * tokens * tokens * width,
            powers=tokens * tokens * 3 // 2,
        )
        return self.line(att)

    def backward(self, grad, grad_res):
        chips, piece_len, width = self.chips, self.piece_len, self.width
        splits, model = self.splits, self.model
        tokens = splits * piece_len
        rows = model // splits
        one = (chips, piece_len, width)
        two = (chips, piece_len, 2 * width)
        out = (chips, rows + 8, 3 * width)
        grad = self.line(grad)
        dq, mine, other, dw_mine, dw_other = run_kernel(
            attend_back_kernel,
            "attend_back",
            [(one, bf16), (two, bf16), (two, bf16), (out, f32), (out, bf16)],
            (self.ids, self.packed, self.q, self.k, self.v, grad, self.lse) + self.masks(),
            scratch=[
                pltpu.VMEM((chips * piece_len, tokens), bf16),
                pltpu.VMEM((chips * piece_len, tokens), bf16),
                pltpu.VMEM((splits, piece_len, 2 * width), bf16),
                pltpu.VMEM((splits, rows + 8, 3 * width), f32),
            ],
            scalars=1,
            flops=6 * tokens * model * width + 5 * tokens * tokens * width,
            powers=tokens * tokens * 3 // 2,
        )
        dw_recv = lax.ppermute(dw_other, "seq", self.swap)
        recv = lax.ppermute(other, "seq", self.swap)
        dw = self.line((dw_mine + dw_recv.astype(f32)).astype(bf16))
        (partial,) = run_kernel(
            input_grad_kernel,
            "input_grad",
            [((chips, piece_len, model), bf16)],
            (dq, mine, recv, self.weight),
            flops=3 * tokens * model * width,
        )
        dws = [dw] + [exchange(dw, k) for k in range(1, lax.axis_size("dp"))]
        partial = self.line(partial)
        input_grad = grad_res + jnp.sum(partial.astype(f32), 0)
        grad_w = [(rows, model), f32]
        gq, gk, gv, bias = run_kernel(
            finish_kernel,
            "finish",
            [((rows, model), f32)] * 3 + [((chips, 8, 3 * width), f32)],
            tuple(dws),
        )
        core, chip = self.position % 2, self.position // 2
        row = lax.dynamic_index_in_dim(bias, chip, 0, keepdims=False)[0]
        bias_q = lax.dynamic_slice_in_dim(row, core * rows, rows)
        bias_v = lax.dynamic_slice_in_dim(row, 2 * width + core * rows, rows)
        return input_grad, gq, bias_q, gk, gv, bias_v


def exchange(array, k):
    count = lax.axis_size("dp")
    return lax.ppermute(array, "dp", [(i, i ^ k) for i in range(count)])


def one_hot(index, count):
    return (index[..., None] == jnp.arange(count, dtype=jnp.int32)).astype(bf16)


def with_halo(block, axis, dim, width):
    count = lax.axis_size(axis)
    forward = [(i, i + 1) for i in range(count - 1)]
    backward = [(target, source) for source, target in forward]
    low = lax.ppermute(
        lax.slice_in_dim(block, block.shape[dim] - width, None, axis=dim), axis, forward
    )
    high = lax.ppermute(lax.slice_in_dim(block, 0, width, axis=dim), axis, backward)
    return jnp.concatenate([low, block, high], axis=dim)


def broadcast(block, axis, owner):
    block = jnp.where(lax.axis_index(axis) == owner, block, jnp.zeros_like(block))
    return lax.psum(block, axis)


class TokenAttention:
    def __init__(self, hidden, weights, biases, segments, random_blocks, vec_local):
        self.splits = splits = lax.axis_size("seq")
        self.position = position = lax.axis_index("seq")
        self.ids = jnp.stack([position % 2, position // 2, lax.axis_index("dp")]).astype(jnp.int32)
        self.hidden = hidden
        self.segments = segments
        self.random_blocks = random_blocks
        self.weights = [lax.all_gather(w, "seq", axis=0, tiled=True) for w in weights]
        self.vec_all = lax.all_gather(vec_local, "seq")

    def forward(self):
        hidden, segments = self.hidden, self.segments
        splits, position = self.splits, self.position
        seq_count = segments.shape[0]
        row_count, model = hidden.shape
        piece_len = row_count // seq_count
        size = model // HEADS
        per = piece_len // BLOCK
        slots = self.random_blocks.shape[3]
        reqs = seq_count * per * HEADS * slots
        cap = max(2, 3 * reqs // (2 * splits) + 1)
        rows = model // splits
        vec = self.vec_all.reshape(splits, -1, rows).transpose(1, 0, 2).reshape(-1, model)
        wq, wk, wv = self.weights
        query = (matmul(hidden, wq) + vec[0:1]).astype(bf16)
        keys = matmul(hidden, wk).astype(bf16)
        values = (matmul(hidden, wv) + vec[1:2]).astype(bf16)
        joined = jnp.concatenate([keys, values], 1).reshape(seq_count, piece_len, 2 * model)
        extended = with_halo(joined, "seq", 1, BLOCK)
        first = broadcast(joined[:, :BLOCK], "seq", 0)
        last = broadcast(joined[:, piece_len - BLOCK :], "seq", splits - 1)
        tiles = seq_count * per * HEADS
        tile_size = BLOCK * 2 * size
        kv_tiles = (
            joined.reshape(seq_count, per, BLOCK, 2, HEADS, size)
            .transpose(0, 1, 4, 2, 3, 5)
            .reshape(tiles, tile_size)
        )
        req = jnp.arange(reqs, dtype=jnp.int32)
        req_seq = req // (per * HEADS * slots)
        req_head = req // slots % HEADS
        earlier = (req[:, None] > req[None, :]).astype(jnp.int32)
        everyone = (
            self.random_blocks.reshape(seq_count, splits, per, HEADS, slots)
            .transpose(1, 0, 2, 3, 4)
            .reshape(splits, reqs)
        )
        is_mine = (everyone // per == position).astype(jnp.int32)
        place = jnp.sum(is_mine[:, None, :] * earlier, 2)
        slot = jnp.where(is_mine == 1, place, cap)
        tile_of = (req_seq * per + everyone % per) * HEADS + req_head
        chosen = slot[:, :, None] == jnp.arange(cap, dtype=jnp.int32)
        send = jnp.sum(jnp.where(chosen, tile_of[:, :, None], 0), 1).reshape(splits * cap)
        self.send = one_hot(send, tiles)
        outgoing = matmul(self.send, kv_tiles).astype(bf16).reshape(splits, cap, tile_size)
        incoming = lax.all_to_all(outgoing, "seq", 0, 0, tiled=True)
        asked = lax.dynamic_slice_in_dim(self.random_blocks, position * per, per, 1)
        owner = asked.reshape(reqs) // per
        before = jnp.sum((owner[:, None] == owner[None, :]).astype(jnp.int32) * earlier, 1)
        self.arrival = one_hot(owner * cap + before, splits * cap)
        fetched = matmul(self.arrival, incoming.reshape(splits * cap, tile_size)).astype(bf16)
        moved = fetched.reshape(seq_count, per, HEADS, slots * BLOCK, 2, size)
        spans = [slice(i * BLOCK, (i + 3) * BLOCK) for i in range(per)]
        fixed = jnp.stack(
            [jnp.concatenate([extended[:, span], first, last], 1) for span in spans], 1
        )
        fixed = fixed.reshape(seq_count, per, 5 * BLOCK, 2, HEADS, size)
        paired = jnp.concatenate(
            [fixed.transpose(3, 0, 1, 4, 2, 5), moved.transpose(4, 0, 1, 2, 3, 5)], 4
        )
        self.keys, self.values = paired[0], paired[1]
        edge = jnp.full((seq_count, BLOCK), -1, jnp.int32)
        padded = jnp.concatenate([edge, segments, edge], 1)
        query_seg = lax.dynamic_slice_in_dim(segments, position * piece_len, piece_len, 1)
        ext_seg = lax.dynamic_slice_in_dim(padded, position * piece_len, piece_len + 2 * BLOCK, 1)
        always = jnp.full((seq_count, 2 * BLOCK), -2, jnp.int32)
        seg_fixed = jnp.stack(
            [jnp.concatenate([ext_seg[:, span], always], 1) for span in spans], 1
        )
        seg_fixed = jnp.broadcast_to(
            seg_fixed[:, :, None], (seq_count, per, HEADS, 5 * BLOCK)
        )
        seg_blocks = segments.reshape(seq_count, -1, BLOCK)
        asked_hot = one_hot(asked, seg_blocks.shape[1])
        seg_moved = jnp.einsum(
            "gjhrb,gbt->gjhrt", asked_hot, seg_blocks.astype(bf16), preferred_element_type=f32
        ).astype(jnp.int32)
        key_seg = jnp.concatenate(
            [seg_fixed, seg_moved.reshape(seq_count, per, HEADS, slots * BLOCK)], 3
        )[:, :, :, None, :]
        self.allowed = (
            query_seg.reshape(seq_count, per, 1, BLOCK, 1) == key_seg
        ) | (key_seg == -2)
        self.query = query.reshape(seq_count, per, BLOCK, HEADS, size)
        scores = self.scores()
        top = jnp.max(scores, -1, keepdims=True)
        powers = jnp.exp(scores - top)
        total = jnp.sum(powers, -1, keepdims=True)
        self.log_total = top + jnp.log(total)
        attended = jnp.einsum(
            "gjhqk,gjhke->gjqhe",
            (powers / total).astype(bf16),
            self.values,
            preferred_element_type=f32,
        )
        return attended.astype(bf16).reshape(1, row_count, model)

    def scores(self):
        raw = jnp.einsum("gjqhe,gjhke->gjhqk", self.query, self.keys, preferred_element_type=f32)
        return jnp.where(self.allowed, raw * self.query.shape[-1] ** -0.5, MASKED)

    def backward(self, grad, grad_res):
        hidden = self.hidden
        splits, position = self.splits, self.position
        seq_count, per, _, _, size = self.query.shape
        row_count, model = hidden.shape
        piece_len = per * BLOCK
        slots = self.random_blocks.shape[3]
        scale = size**-0.5
        probs = jnp.exp(self.scores() - self.log_total)
        grad_split = grad.reshape(seq_count, per, BLOCK, HEADS, size)
        grad_probs = jnp.einsum(
            "gjqhe,gjhke->gjhqk", grad_split, self.values, preferred_element_type=f32
        )
        weighted = jnp.sum(probs * grad_probs, -1, keepdims=True)
        grad_scores = (probs * (grad_probs - weighted)).astype(bf16)
        grad_query = (
            jnp.einsum("gjhqk,gjhke->gjqhe", grad_scores, self.keys, preferred_element_type=f32)
            * scale
        )
        grad_key = (
            jnp.einsum("gjhqk,gjqhe->gjhke", grad_scores, self.query, preferred_element_type=f32)
            * scale
        )
        grad_value = jnp.einsum(
            "gjhqk,gjqhe->gjhke", probs.astype(bf16), grad_split, preferred_element_type=f32
        )
        paired = jnp.stack([grad_key, grad_value], 0)
        fixed_len = 5 * BLOCK
        fixed = (
            paired[:, :, :, :, :fixed_len]
            .transpose(1, 2, 4, 0, 3, 5)
            .reshape(seq_count, per, fixed_len, 2 * model)
        )
        moved = (
            paired[:, :, :, :, fixed_len:]
            .transpose(1, 2, 3, 4, 0, 5)
            .reshape(seq_count * per * HEADS * slots, BLOCK * 2 * size)
        )
        ext = jnp.zeros((seq_count, piece_len + 2 * BLOCK, 2 * model), f32)
        for i in range(per):
            ext = ext.at[:, i * BLOCK : (i + 3) * BLOCK].add(fixed[:, i, : 3 * BLOCK])
        first = jnp.sum(fixed[:, :, 3 * BLOCK : 4 * BLOCK], 1)
        last = jnp.sum(fixed[:, :, 4 * BLOCK :], 1)
        rims = jnp.concatenate([ext[:, :BLOCK], ext[:, piece_len + BLOCK :]], 1)
        beside = with_halo(rims.astype(bf16), "seq", 1, BLOCK).astype(f32)
        kv_grad = ext[:, BLOCK : BLOCK + piece_len]
        kv_grad = kv_grad.at[:, :BLOCK].add(beside[:, :BLOCK])
        kv_grad = kv_grad.at[:, piece_len - BLOCK :].add(beside[:, 3 * BLOCK :])
        first, last = lax.psum((first, last), "seq")
        kv_grad = kv_grad.at[:, :BLOCK].add(jnp.where(position == 0, first, 0.0))
        kv_grad = kv_grad.at[:, piece_len - BLOCK :].add(
            jnp.where(position == splits - 1, last, 0.0)
        )
        cap = self.send.shape[0] // splits
        outgoing = left_product(self.arrival, moved.astype(bf16)).astype(bf16)
        returned = lax.all_to_all(
            outgoing.reshape(splits, cap, -1), "seq", 0, 0, tiled=True
        ).reshape(splits * cap, -1)
        kv_grad = kv_grad + (
            left_product(self.send, returned)
            .reshape(seq_count, per, HEADS, BLOCK, 2, size)
            .transpose(0, 1, 3, 4, 2, 5)
            .reshape(seq_count, piece_len, 2 * model)
        )
        kv_grad = kv_grad.reshape(row_count, 2 * model).astype(bf16)
        grad_query = grad_query.reshape(row_count, model).astype(bf16)
        grads = (grad_query, kv_grad[:, :model], kv_grad[:, model:])
        input_grad = grad_res
        shares = []
        for part, weight in zip(grads, self.weights):
            input_grad = input_grad + right_product(part, weight)
            full = left_product(hidden, part)
            share = lax.psum_scatter(full, "seq", scatter_dimension=0, tiled=True)
            shares.append(lax.psum(share.astype(bf16), "dp").astype(f32))
        biases = jnp.stack([jnp.sum(grads[i].astype(f32), 0) for i in (0, 2)], 1)
        biases = lax.psum_scatter(biases, "seq", scatter_dimension=0, tiled=True)
        biases = lax.psum(biases.astype(bf16), "dp").astype(f32)
        return input_grad, shares[0], biases[:, 0], shares[1], shares[2], biases[:, 1]


def local(
    hidden_in,
    query_weight,
    query_bias,
    key_weight,
    value_weight,
    value_bias,
    output_weight,
    output_bias,
    first_gain,
    first_shift,
    inner_weight,
    inner_bias,
    outer_weight,
    outer_bias,
    second_gain,
    second_shift,
    segments,
    random_blocks,
    cotangent,
):
    seq_count, piece_len, model = hidden_in.shape
    splits = lax.axis_size("seq")
    groups = lax.axis_size("dp")
    group = lax.axis_index("dp")
    row_count = seq_count * piece_len
    rows = model // splits
    units = outer_weight.shape[0] // groups
    hidden = hidden_in.reshape(row_count, model)
    by_heads = seq_count == 1 and 2 < splits and splits % 2 == 0 and HEADS % (splits // 2) == 0
    vec_local = jnp.concatenate(
        [
            query_bias,
            value_bias,
            output_bias,
            first_gain,
            first_shift,
            outer_bias,
            second_gain,
            second_shift,
            inner_bias,
        ]
    )
    attention = (HeadAttention if by_heads else TokenAttention)(
        hidden,
        (query_weight, key_weight, value_weight),
        (query_bias, value_bias),
        segments,
        random_blocks,
        vec_local,
    )
    inner_part = lax.dynamic_index_in_dim(
        inner_weight.reshape(rows, splits, groups, units), group, 2, keepdims=False
    ).reshape(rows, splits * units)
    outer_part = lax.dynamic_index_in_dim(
        outer_weight.reshape(groups, units, model), group, 0, keepdims=False
    )
    w_out = lax.all_gather(output_weight, "seq", axis=0, tiled=True)
    w_both = lax.all_gather(jnp.concatenate([inner_part, outer_part], 0), "seq")
    w_in = w_both[:, :rows].reshape(model, splits * units)
    w_outer = w_both[:, rows:].reshape(splits * units, model)
    attended = attention.forward()
    vec = attention.vec_all.reshape(splits, 8 + groups, rows).transpose(1, 0, 2)
    vec = vec.reshape(8 + groups, model).astype(f32)
    ids = attention.ids
    full = (row_count, model)
    low, normed, inverse = run_kernel(
        project_kernel,
        "project",
        [(full, bf16), (full, f32), ((row_count, 128), f32)],
        (attended, w_out, hidden, vec),
        flops=2 * row_count * model * model,
    )
    lows = [low] + [exchange(low, k) for k in range(1, groups)]
    work = 2 * groups * row_count * model * splits * units
    parts = run_kernel(
        forward_kernel,
        "forward",
        [(full, f32)]
        + [(full, bf16)] * (groups - 1)
        + [((groups * row_count, splits * units), f32), ((groups * row_count, splits * units), bf16)],
        (ids, *lows, w_in, w_outer, vec),
        scalars=1,
        flops=2 * work,
        powers=groups * row_count * splits * units,
    )
    inner, act = parts[groups:]
    recv = [parts[0]] + [exchange(parts[k], k) for k in range(1, groups)]
    layer_out, grad_low, grad_mix, sums2 = run_kernel(
        middle_kernel,
        "middle",
        [(full, bf16), (full, bf16), (full, f32), ((8, model), f32)],
        (*recv, normed, cotangent.reshape(row_count, model), vec),
    )
    grads = [grad_low] + [exchange(grad_low, k) for k in range(1, groups)]
    parts = run_kernel(
        backward_kernel,
        "backward",
        [(full, f32)]
        + [(full, bf16)] * (groups - 1)
        + [((groups * row_count, splits * units), bf16), ((1, splits * units), f32)],
        (*grads, w_in, w_outer, inner),
        flops=2 * work,
        powers=groups * row_count * splits * units,
    )
    grad_inner, sum_inner = parts[groups:]
    recv = [parts[0]] + [exchange(parts[k], k) for k in range(1, groups)]
    grad_res, grad_branch, grad_att, sums1 = run_kernel(
        residual_kernel,
        "residual",
        [(full, f32), (full, bf16), (attended.shape, bf16), ((8, model), f32)],
        (*recv, grad_mix, normed, inverse, vec, w_out),
        flops=2 * row_count * model * model,
    )
    d_inner, d_outer, d_output = run_kernel(
        weight_grad_kernel,
        "weight_grad",
        [((model, splits * units), bf16), ((splits * units, model), bf16), ((model, model), bf16)],
        (*lows, *grads, grad_inner, act, attended, grad_branch),
        flops=2 * work + 2 * row_count * model * model,
    )
    sums = jnp.concatenate([sums2[:3], sums1[:3], sum_inner], 0)
    sums = sums.reshape(7, splits, rows).transpose(1, 0, 2).reshape(splits, 1, 7 * rows)
    sums = jnp.pad(sums, ((0, 0), (0, 7), (0, model - 7 * rows))).astype(bf16)
    stacked = jnp.concatenate(
        [
            d_inner.reshape(splits, rows, -1),
            d_outer.reshape(splits, units, model),
            d_output.reshape(splits, rows, model),
            sums,
        ],
        1,
    )
    share = lax.psum_scatter(stacked, "seq", scatter_dimension=0, tiled=False)
    every = lax.all_gather(share, "dp")
    d_inner = (
        every[:, :rows].reshape(groups, rows, splits, units).transpose(1, 2, 0, 3)
    ).reshape(rows, -1).astype(f32)
    d_outer = every[:, rows : rows + units].reshape(groups * units, model).astype(f32)
    d_output = jnp.sum(every[:, rows + units : 2 * rows + units].astype(f32), 0)
    small = every[:, 2 * rows + units, : 7 * rows].astype(f32).reshape(groups, 7, rows)
    vectors = jnp.sum(small[:, :6], 0)
    d_inner_bias = small[:, 6].reshape(-1)
    input_grad, gq, bias_q, gk, gv, bias_v = attention.backward(grad_att, grad_res)
    return (
        layer_out.reshape(seq_count, piece_len, model),
        input_grad.reshape(seq_count, piece_len, model),
        gq,
        bias_q,
        gk,
        gv,
        bias_v,
        d_output,
        vectors[5],
        vectors[3],
        vectors[4],
        d_inner,
        d_inner_bias,
        d_outer,
        vectors[2],
        vectors[0],
        vectors[1],
    )


def solution(mesh):
    in_specs = (
        P("dp", "seq", None),
        P("seq", None),
        P("seq"),
        P("seq", None),
        P("seq", None),
        P("seq"),
        P("seq", None),
        P("seq"),
        P("seq"),
        P("seq"),
        P("seq", None),
        P("seq"),
        P("seq", None),
        P("seq"),
        P("seq"),
        P("seq"),
        P("dp", None),
        P("dp", None, None, None),
        P("dp", "seq", None),
    )
    out_specs = (
        P("dp", "seq", None),
        P("dp", "seq", None),
        P("seq", None),
        P("seq"),
        P("seq", None),
        P("seq", None),
        P("seq"),
        P("seq", None),
        P("seq"),
        P("seq"),
        P("seq"),
        P("seq", None),
        P("seq"),
        P("seq", None),
        P("seq"),
        P("seq"),
        P("seq"),
    )
    return jax.shard_map(local, mesh=mesh, in_specs=in_specs, out_specs=out_specs, check_vma=False)
```

```python
import functools

import jax
import jax.numpy as jnp
from jax import lax
from jax.experimental import pallas as pl
from jax.experimental.pallas import tpu as pltpu
from jax.sharding import PartitionSpec as P

HEADS = 12
BLOCK = 64
EPSILON = 1e-12
MASKED = -1000000000.0
GELU_A = 0.7978845608028654
GELU_B = 0.044715
VMEM_BYTES = 6 << 20
bf16 = jnp.bfloat16
f32 = jnp.float32


def matmul(left, right):
    return jnp.dot(left, right, preferred_element_type=f32)


def left_product(left, right):
    return lax.dot_general(left, right, (((0,), (0,)), ((), ())), preferred_element_type=f32)


def right_product(left, right):
    return lax.dot_general(left, right, (((1,), (1,)), ((), ())), preferred_element_type=f32)


def run_kernel(kernel, name, outs, args, scratch=(), scalars=0, flops=0, powers=0, grant=VMEM_BYTES):
    specs = [pl.BlockSpec(memory_space=pltpu.SMEM)] * scalars
    specs += [pl.BlockSpec(memory_space=pltpu.VMEM)] * (len(args) - scalars)
    out_shape = tuple(jax.ShapeDtypeStruct(shape, dtype) for shape, dtype in outs)
    moved = sum(a.size * a.dtype.itemsize for a in args)
    moved += sum(o.size * o.dtype.itemsize for o in out_shape)
    return pl.pallas_call(
        kernel,
        name=name,
        out_shape=out_shape,
        in_specs=specs,
        out_specs=tuple(pl.BlockSpec(memory_space=pltpu.VMEM) for _ in outs),
        scratch_shapes=list(scratch),
        compiler_params=pltpu.CompilerParams(vmem_limit_bytes=grant),
        cost_estimate=pl.CostEstimate(flops=flops, bytes_accessed=moved, transcendentals=powers),
    )(*args)


def normalize(values):
    center = values - jnp.mean(values, -1, keepdims=True)
    spread = jnp.mean(center * center, -1, keepdims=True)
    inverse = lax.rsqrt(spread + EPSILON)
    return center * inverse, inverse


def norm_back(grad, normed, inverse, gain):
    scaled = grad * gain
    return inverse * (
        scaled
        - jnp.mean(scaled, -1, keepdims=True)
        - normed * jnp.mean(scaled * normed, -1, keepdims=True)
    )


def bias_rows(be_ref, bn, same, head, block, blocks, block_len):
    width = same.shape[1]
    rows = [
        jnp.broadcast_to(be_ref[head * blocks + block + i : head * blocks + block + i + 1, :], (block_len, width))
        for i in range(same.shape[0] // block_len)
    ]
    return jnp.where(same, jnp.concatenate(rows, 0), bn)


def bias_rows(lines, bn, same):
    count, width = lines.shape
    length = same.shape[0] // count
    rows = [jnp.broadcast_to(lines[i : i + 1, :], (length, width)) for i in range(count)]
    return jnp.where(same, jnp.concatenate(rows, 0), bn)


def assemble_kernel(ids, mine, mine_next, other, other_next, out, *, bit, relative):
    core = ids[0]
    half = lax.rem(ids[2] // bit, 2)
    for k in range(mine.shape[0]):
        chip = ids[1] ^ k if relative else k
        out[2 * chip + core, half] = mine[k]
        out[2 * chip + core, 1 - half] = mine_next[k]
        out[2 * chip + 1 - core, half] = other[k]
        out[2 * chip + 1 - core, 1 - half] = other_next[k]


def attend_kernel(ids, hid, w, qb, vb, be, bn, sk, sq, *refs):
    outs = refs[:-5]
    qo, ko, vo, lse, qs = refs[-5:]
    pieces, piece_len, width = qs.shape
    chips = pieces // 2
    core = ids[0]
    size = 64
    heads = width // size
    model = hid.shape[2]
    tokens = hid[...].reshape(pieces * piece_len, model)
    product = matmul(tokens, w[...])
    query = (product[:, :width] + qb[...]).astype(bf16) * bf16(size**-0.5)
    qs[...] = query.reshape(pieces, piece_len, width)
    ko[...] = product[:, width : 2 * width].astype(bf16)
    vo[...] = (product[:, 2 * width :] + vb[...]).astype(bf16)
    lane = lax.broadcasted_iota(jnp.int32, (piece_len, 128), 1)
    for k in range(chips):
        chip = ids[1] ^ k
        qo[k] = qs[2 * chip + core]
        same = sq[chip] == sk[...]
        logs = jnp.zeros((piece_len, 128), f32)
        parts = []
        for head in range(heads):
            cols = slice(head * size, (head + 1) * size)
            scores = right_product(qo[k, :, cols], ko[:, cols])
            scores = scores + bias_rows(be[head * chips + chip], bn[...], same)
            top = jnp.max(scores, -1, keepdims=True)
            powers = jnp.exp(scores - top)
            total = jnp.sum(powers, -1, keepdims=True)
            probs = (powers * (1.0 / total)).astype(bf16)
            parts.append(matmul(probs, vo[:, cols]))
            logs = jnp.where(lane == head, top + jnp.log(total), logs)
        outs[k][...] = jnp.concatenate(parts, 1).T.astype(bf16)
        lse[k] = logs


def attend_back_kernel(ids, q, k, v, lse, be, bn, sk, sq, *refs):
    chips, piece_len, width = q.shape
    ga = refs[:chips]
    dq, own, mine, other, ds_all, p_all, dkv = refs[chips:]
    pieces = 2 * chips
    core = ids[0]
    size = 64
    heads = width // size
    dks = []
    dvs = []
    dqs = [[None] * heads for _ in range(chips)]
    gas = [g[...].astype(f32).T.astype(bf16) for g in ga]
    for head in range(heads):
        cols = slice(head * size, (head + 1) * size)
        key = k[:, cols]
        value = v[:, cols]
        for i in range(chips):
            chip = ids[1] ^ i
            rows = slice(i * piece_len, (i + 1) * piece_len)
            same = sq[chip] == sk[...]
            scores = right_product(q[i, :, cols], key)
            scores = scores + bias_rows(be[head * chips + chip], bn[...], same)
            probs = jnp.exp(scores - lse[i, :, head : head + 1])
            grad = right_product(gas[i][:, cols], value)
            weighted = jnp.sum(probs * grad, -1, keepdims=True)
            ds = (probs * (grad - weighted)).astype(bf16)
            ds_all[rows, :] = ds
            p_all[rows, :] = probs.astype(bf16)
            dqs[i][head] = (matmul(ds, key) * (size**-0.5)).astype(bf16)
        queries = q[:, :, cols].reshape(chips * piece_len, size)
        grads = jnp.concatenate([g[:, cols] for g in gas], 0)
        dks.append(left_product(ds_all[...], queries).astype(bf16))
        dvs.append(left_product(p_all[...], grads).astype(bf16))
    for i in range(chips):
        dq[i] = jnp.concatenate(dqs[i], 1)
    joined = jnp.concatenate(dks + dvs, 1)
    own[...] = joined
    dkv[...] = joined.reshape(pieces, piece_len, 2 * width)
    for i in range(chips):
        chip = ids[1] ^ i
        mine[i] = dkv[2 * chip + core]
        other[i] = dkv[2 * chip + 1 - core]


def attend_weight_kernel(ids, hid, dq, dkv, mine, other, sums, dws):
    pieces, piece_len, model = hid.shape
    chips, _, width = dq.shape
    core = ids[0]
    tokens = hid[...].reshape(pieces * piece_len, model)
    owned = jnp.concatenate([hid[2 * (ids[1] ^ k) + core] for k in range(chips)], 0)
    grad_q = dq[...].reshape(chips * piece_len, width)
    grad_kv = dkv[...]
    weights = jnp.concatenate([left_product(owned, grad_q), left_product(tokens, grad_kv)], 1)
    quarters, _, rows, _ = mine.shape
    dws[...] = weights.reshape(dws.shape)
    for k in range(chips):
        chip = ids[1] ^ k
        for j in range(quarters):
            mine[j, k] = dws[2 * chip + core, ids[2] ^ j]
            other[j, k] = dws[2 * chip + 1 - core, ids[2] ^ j].astype(bf16)
    total = jnp.concatenate(
        [
            jnp.sum(grad_q.astype(f32), 0, keepdims=True),
            jnp.sum(grad_kv.astype(f32), 0, keepdims=True),
        ],
        1,
    )
    sums[...] = jnp.broadcast_to(total, sums.shape)


def input_grad_kernel(dq, mine, recv, w, *outs):
    chips, piece_len, width = dq.shape
    dkv = (mine[...].astype(f32) + recv[...].astype(f32)).astype(bf16)
    grads = jnp.concatenate([dq[...], dkv], 2).reshape(chips * piece_len, 3 * width)
    total = right_product(grads, w[...])
    for k, out in enumerate(outs):
        out[...] = total[k * piece_len : (k + 1) * piece_len].astype(out.dtype)


def add_split_kernel(left, right, *outs):
    for k, out in enumerate(outs):
        out[...] = (left[k].astype(f32) + right[k].astype(f32)).astype(out.dtype)


def sum_split_kernel(*refs, parts):
    total = refs[0][...].astype(f32)
    for r in refs[1:parts]:
        total = total + r[...].astype(f32)
    outs = refs[parts:]
    if len(outs) == 1:
        outs[0][...] = total.astype(outs[0].dtype)
    else:
        for k, out in enumerate(outs):
            out[...] = total[k].astype(out.dtype)


def stack_kernel(*refs):
    for k, r in enumerate(refs[:-1]):
        refs[-1][k] = r[...]


def project_kernel(ids, wo, hid, vec, *refs):
    att = refs[:-3]
    low, normed, inverse = refs[-3:]
    branch = vec[2:3, :] + jnp.zeros(hid.shape, f32)
    for k, r in enumerate(att):
        branch = branch + left_product(r[...], wo[ids[1] ^ k])
    n1, r1 = normalize(hid[...].astype(f32) + branch)
    low[...] = (n1 * vec[3:4, :] + vec[4:5, :]).astype(bf16)
    normed[...] = n1
    inverse[...] = jnp.broadcast_to(r1, inverse.shape)


def gelu_parts(v):
    return jnp.tanh(GELU_A * (v + GELU_B * (v * v * v)))


def two_weights(both):
    pieces, rows, model = both.shape
    half = rows // 2
    first = both[:, :half, :].reshape(pieces * half, model)
    return first, both[:, half:, :].reshape(pieces * half, model)


def forward_kernel(ids, *refs):
    parts = (len(refs) - 4) // 2
    x = refs[:parts]
    both, vec = refs[parts : parts + 2]
    outs = refs[parts + 2 : 2 * parts + 2]
    inner_ref, act_ref = refs[2 * parts + 2 :]
    rows = x[0].shape[0]
    weight1, weight2 = two_weights(both)
    tokens = jnp.concatenate([r[...] for r in x], 0)
    inner = matmul(tokens, weight1) + vec[pl.ds(8 + ids[2], 1), :]
    act = (0.5 * inner * (1.0 + gelu_parts(inner))).astype(bf16)
    inner_ref[...] = inner
    act_ref[...] = act
    mixed = matmul(act, weight2)
    for i in range(parts):
        outs[i][...] = mixed[i * rows : (i + 1) * rows].astype(outs[i].dtype)


def middle_kernel(*refs):
    recv = refs[:-7]
    normed, cot, vec, out, low, mix, sums = refs[-7:]
    first = normed[...] * vec[3:4, :] + vec[4:5, :]
    mixed = vec[5:6, :]
    for r in recv:
        mixed = mixed + r[...].astype(f32)
    n2, r2 = normalize(first + mixed)
    gain = vec[6:7, :]
    out[...] = (n2 * gain + vec[7:8, :]).astype(bf16)
    g = cot[...].astype(f32)
    grad = norm_back(g, n2, r2, gain)
    rounded = grad.astype(bf16)
    mix[...] = grad
    low[...] = rounded
    sums[0:1, :] = jnp.sum(g * n2, 0, keepdims=True)
    sums[1:2, :] = jnp.sum(g, 0, keepdims=True)
    sums[2:3, :] = jnp.sum(rounded.astype(f32), 0, keepdims=True)
    sums[3:, :] = jnp.zeros((5, sums.shape[1]), f32)


def backward_kernel(*refs):
    parts = (len(refs) - 4) // 2
    grads = refs[:parts]
    both, inner_ref = refs[parts : parts + 2]
    outs = refs[parts + 2 : 2 * parts + 2]
    gi_ref, sum_ref = refs[2 * parts + 2 :]
    rows = grads[0].shape[0]
    weight1, weight2 = two_weights(both)
    gm = jnp.concatenate([r[...] for r in grads], 0)
    grad_act = right_product(gm, weight2)
    v = inner_ref[...]
    t = gelu_parts(v)
    slope = 0.5 * (1.0 + t) + 0.5 * v * (1.0 - t * t) * (GELU_A * (1.0 + 3.0 * GELU_B * (v * v)))
    gi = (grad_act * slope).astype(bf16)
    gi_ref[...] = gi
    sum_ref[...] = jnp.sum(gi.astype(f32), 0, keepdims=True)
    first = right_product(gi, weight1)
    for i in range(parts):
        outs[i][...] = first[i * rows : (i + 1) * rows].astype(outs[i].dtype)


def residual_kernel(ids, mix, normed, inverse, vec, wo, *refs, parts):
    first = mix[...]
    for r in refs[:parts]:
        first = first + r[...].astype(f32)
    res, low, sums = refs[parts : parts + 3]
    n1 = normed[...]
    grad = norm_back(first, n1, inverse[:, 0:1], vec[3:4, :])
    rounded = grad.astype(bf16)
    for k, back in enumerate(refs[parts + 3 :]):
        back[...] = right_product(wo[ids[1] ^ k], rounded).astype(bf16)
    res[...] = grad
    low[...] = rounded
    sums[0:1, :] = jnp.sum(first * n1, 0, keepdims=True)
    sums[1:2, :] = jnp.sum(first, 0, keepdims=True)
    sums[2:3, :] = jnp.sum(rounded.astype(f32), 0, keepdims=True)
    sums[3:, :] = jnp.zeros((5, sums.shape[1]), f32)


def put_vectors(out, piece, row, vectors, rows):
    parts = [v[:, piece * rows : (piece + 1) * rows] for v in vectors]
    fill = out.shape[2] - rows * len(parts)
    line = jnp.concatenate(parts + [jnp.zeros((1, fill), f32)], 1)
    out[piece, row : row + 8, :] = jnp.broadcast_to(line, (8, out.shape[2])).astype(bf16)


def inner_outer_kernel(*refs):
    parts = (len(refs) - 5) // 2
    x = refs[:parts]
    gm = refs[parts : 2 * parts]
    gi, act, sums, sum_inner, out = refs[2 * parts :]
    pieces, tall, model = out.shape
    rows = (tall - 8) // 2
    tokens = jnp.concatenate([r[...] for r in x], 0)
    grads = jnp.concatenate([r[...] for r in gm], 0)
    out[:, :rows, :] = left_product(tokens, gi[...]).astype(bf16).reshape(pieces, rows, model)
    out[:, rows : 2 * rows, :] = (
        left_product(act[...], grads).astype(bf16).reshape(pieces, rows, model)
    )
    vectors = [sums[i : i + 1, :] for i in range(3)] + [sum_inner[...]]
    for piece in range(pieces):
        put_vectors(out, piece, 2 * rows, vectors, rows)


def output_grad_kernel(ids, gb, sums, *refs):
    mine, other, dws = refs[-3:]
    core = ids[0]
    chips, tall, model = mine.shape
    rows = tall - 8
    grad = gb[...]
    vectors = [sums[i : i + 1, :] for i in range(3)]
    for piece in range(2 * chips):
        put_vectors(dws, piece, rows, vectors, rows)
    for k in range(chips):
        chip = ids[1] ^ k
        part = matmul(refs[k][...], grad).astype(bf16)
        for i in range(2):
            dws[2 * chip + i, :rows, :] = part[i * rows : (i + 1) * rows]
        mine[k] = dws[2 * chip + core]
        other[k] = dws[2 * chip + 1 - core]


def ordered(ids, refs, scratch):
    for k, r in enumerate(refs):
        scratch[ids[2] ^ k] = r[...]


def finish_inner_kernel(ids, *refs):
    parts = len(refs) - 4
    inner, outer, vectors, scratch = refs[parts:]
    ordered(ids, refs[:parts], scratch)
    rows = inner.shape[0]
    units = outer.shape[0] // parts
    pieces = scratch.shape[2] // units
    for piece in range(pieces):
        inner[:, piece * parts * units : (piece + 1) * parts * units] = jnp.concatenate(
            [
                scratch[g, :rows, piece * units : (piece + 1) * units].astype(f32)
                for g in range(parts)
            ],
            1,
        )
    total = jnp.zeros((1, scratch.shape[2]), f32)
    for g in range(parts):
        outer[g * units : (g + 1) * units, :] = scratch[g, rows : rows + units, :].astype(f32)
        line = scratch[g, rows + units : rows + units + 8, :].astype(f32)[0:1]
        vectors[g : g + 1, :] = line
        total = total + line
    vectors[parts : parts + 1, :] = total


def finish_output_kernel(p0, p1, p2, p3, out, vectors):
    rows = out.shape[0]
    total = p0[...].astype(f32)
    for r in (p1, p2, p3):
        total = total + r[...].astype(f32)
    out[...] = total[:rows]
    vectors[...] = total[rows:]


def finish_kernel(ids, *refs):
    parts = len(refs) - 4
    gq, gk, gv, scratch = refs[parts:]
    quarters, chips, rows, wide = scratch.shape
    for j, r in enumerate(refs[:parts]):
        for k in range(chips):
            scratch[ids[2] ^ j, ids[1] ^ k] = r[k]
    width = wide // 3
    for part in range(quarters):
        block = [scratch[part, chip].astype(f32) for chip in range(chips)]
        for i, out in enumerate((gq, gk, gv)):
            out[part * rows : (part + 1) * rows, :] = jnp.concatenate(
                [b[:, i * width : (i + 1) * width] for b in block], 1
            )


def log_counts(count):
    return jnp.where(count > 0, jnp.log(jnp.maximum(count, 1).astype(f32)), MASKED)


def exchange(array, k):
    count = lax.axis_size("dp")
    return lax.ppermute(array, "dp", [(i, i ^ k) for i in range(count)])


def exchange_all(array):
    return [array] + [exchange(array, k) for k in range(1, lax.axis_size("dp"))]


def exchange_parts(parts):
    return [parts[0]] + [exchange(parts[k], k) for k in range(1, lax.axis_size("dp"))]


def swap_cores(array):
    count = lax.axis_size("seq")
    return lax.ppermute(array, "seq", [(i, i ^ 1) for i in range(count)])


def line_exchange(array, k):
    count = lax.axis_size("seq")
    return lax.ppermute(array, "seq", [(i, i ^ (2 * k)) for i in range(count)])


def line_parts(parts):
    return [parts[0]] + [line_exchange(parts[k], k) for k in range(1, len(parts))]


def tied(value, *others):
    return lax.optimization_barrier((value,) + others)[0]


def add_split(left, right, outs):
    return run_kernel(add_split_kernel, "add", outs, (left, right))


def sum_split(arrays, outs):
    return run_kernel(
        functools.partial(sum_split_kernel, parts=len(arrays)), "sum", outs, tuple(arrays)
    )


def along_line(array):
    count = lax.axis_size("seq")
    lines = [[2 * i + c for i in range(count // 2)] for c in range(2)]
    return lax.all_to_all(array, "seq", 0, 0, tiled=True, axis_index_groups=lines)


def device_ids():
    position = lax.axis_index("seq")
    return jnp.stack([position % 2, position // 2, lax.axis_index("dp")]).astype(jnp.int32)


def assemble(ids, mine, bit, relative):
    mine_next = exchange(mine, bit)
    other = swap_cores(mine)
    other_next = swap_cores(mine_next)
    chips, half, width = mine.shape
    (out,) = run_kernel(
        functools.partial(assemble_kernel, bit=bit, relative=relative),
        "assemble",
        [((2 * chips, 2, half, width), bf16)],
        (ids, mine, mine_next, other, other_next),
        scalars=1,
    )
    return out.reshape(4 * chips * half, width)


class HeadAttention:
    def __init__(self, hidden, weights, biases, segments, random_blocks, output_weight, vec_local):
        self.splits = splits = lax.axis_size("seq")
        self.chips = chips = splits // 2
        self.position = position = lax.axis_index("seq")
        core = position % 2
        chip = position // 2
        group = lax.axis_index("dp")
        self.ids = device_ids()
        piece_len, model = hidden.shape
        rows = model // splits
        width = model // chips
        heads = HEADS // chips
        self.packed = lax.all_gather(hidden, "seq")
        half = rows // 2
        start = group % 2 * half
        split = jnp.concatenate(
            [
                lax.dynamic_slice_in_dim(w, start, half, 0).reshape(half, chips, width)
                for w in weights
            ],
            2,
        )
        self.weight = assemble(self.ids, along_line(split.transpose(1, 0, 2)), 1, False)
        out_half = lax.dynamic_slice_in_dim(output_weight, group // 2 % 2 * half, half, 0)
        self.out_parts = [out_half] + [line_exchange(out_half, k) for k in range(1, chips)]
        tall = -(-vec_local.shape[0] // 16) * 16
        vec = jnp.pad(vec_local, ((0, tall - vec_local.shape[0]), (0, 128 - rows)))
        vec = lax.all_to_all(
            jnp.broadcast_to(vec[None], (splits,) + vec.shape), "seq", 0, 0, tiled=True
        )
        self.vec = (
            vec[:, : vec_local.shape[0], :rows].transpose(1, 0, 2).reshape(-1, model).astype(f32)
        )
        pair = jnp.stack(biases, 0)
        pair_other = swap_cores(pair)
        bias = jnp.where(
            core == 0,
            jnp.concatenate([pair, pair_other], 1),
            jnp.concatenate([pair_other, pair], 1),
        ).astype(f32)
        self.bias_q, self.bias_v = bias[0:1], bias[1:2]
        block_count = segments.shape[1] // BLOCK
        per_piece = piece_len // BLOCK
        own = random_blocks[0].reshape(chips, 2, per_piece, HEADS, -1)
        own = lax.dynamic_index_in_dim(own, core, 1, keepdims=False)
        own = lax.dynamic_slice_in_dim(own, chip * heads, heads, 2)
        own = own.reshape(chips * per_piece, heads, -1).transpose(1, 0, 2)
        block = jnp.arange(block_count, dtype=jnp.int32)
        mine = (
            (jnp.arange(chips, dtype=jnp.int32)[:, None] * 2 + core) * per_piece
            + jnp.arange(per_piece, dtype=jnp.int32)[None, :]
        ).reshape(-1)
        ends = ((block == 0) | (block == block_count - 1)).astype(jnp.int32)
        near = (jnp.abs(block[None, :] - mine[:, None]) <= 1).astype(jnp.int32)
        listed = jnp.sum((own[..., None] == block).astype(jnp.int32), 2)
        count = listed + near[None] + ends
        self.same_bias = jnp.repeat(log_counts(count), BLOCK, axis=2).reshape(
            heads * chips, per_piece, -1
        )
        self.other_bias = jnp.repeat(
            jnp.where(ends > 0, 0.0, MASKED).astype(f32)[None], BLOCK, axis=1
        )
        self.key_seg = segments
        self.query_seg = lax.dynamic_index_in_dim(
            segments.reshape(chips, 2, piece_len), core, 1, keepdims=False
        ).reshape(chips, piece_len, 1)
        self.piece_len, self.width, self.model = piece_len, width, model

    def masks(self):
        return (self.same_bias, self.other_bias, self.key_seg, self.query_seg)

    def forward(self):
        chips, piece_len, width, model = self.chips, self.piece_len, self.width, self.model
        tokens = self.splits * piece_len
        one = (chips, piece_len, width)
        *att, self.q, self.k, self.v, self.lse = run_kernel(
            attend_kernel,
            "attend",
            [((width, piece_len), bf16)] * chips
            + [
                (one, bf16),
                ((tokens, width), bf16),
                ((tokens, width), bf16),
                ((chips, piece_len, 128), f32),
            ],
            (self.ids, self.packed, self.weight, self.bias_q, self.bias_v) + self.masks(),
            scratch=[pltpu.VMEM((self.splits, piece_len, width), bf16)],
            scalars=1,
            flops=6 * tokens * model * width + 2 * tokens * tokens * width,
            powers=tokens * tokens * 3 // 2,
        )
        parts = lax.optimization_barrier((tuple(self.out_parts), att[0]))[0]
        rows = parts[0].shape
        (mine,) = run_kernel(stack_kernel, "stack", [((chips,) + rows, bf16)], parts)
        weight = assemble(self.ids, mine, 2, True)
        self.output_weight = weight.reshape(chips, width, model)
        return line_parts(att)

    def output_grad(self, attended, grad_branch, sums):
        chips, model = self.chips, self.model
        rows = model // self.splits
        one = (rows + 8, model)
        mine, other = run_kernel(
            output_grad_kernel,
            "output_grad",
            [((chips,) + one, bf16)] * 2,
            (self.ids, grad_branch, sums, *attended),
            scratch=[pltpu.VMEM((self.splits,) + one, bf16)],
            scalars=1,
            flops=2 * self.piece_len * model * model,
        )
        parts = add_split(mine, swap_cores(other), [(one, bf16)] * chips)
        (share,) = sum_split(line_parts(parts), [(one, bf16)])
        out, vectors = run_kernel(
            finish_output_kernel,
            "finish_output",
            [((rows, model), f32), ((8, model), f32)],
            tuple(exchange_all(share)),
        )
        return out, vectors[0]

    def backward(self, grads, grad_res, share):
        chips, piece_len, width = self.chips, self.piece_len, self.width
        splits, model = self.splits, self.model
        groups = lax.axis_size("dp")
        tokens = splits * piece_len
        rows = model // splits
        one = (chips, piece_len, width)
        two = (chips, piece_len, 2 * width)
        dq, dkv, mine, other = run_kernel(
            attend_back_kernel,
            "attend_back",
            [(one, bf16), ((tokens, 2 * width), bf16), (two, bf16), (two, bf16)],
            (self.ids, self.q, self.k, self.v, self.lse) + self.masks() + tuple(grads),
            scratch=[
                pltpu.VMEM((chips * piece_len, tokens), bf16),
                pltpu.VMEM((chips * piece_len, tokens), bf16),
                pltpu.VMEM((splits, piece_len, 2 * width), bf16),
            ],
            scalars=1,
            flops=5 * tokens * tokens * width,
            powers=tokens * tokens * 3 // 2,
            grant=10 << 20,
        )
        recv = swap_cores(other)
        quarter = (rows // groups, 3 * width)
        part = (groups, chips) + quarter
        dw_mine, dw_other, sums = run_kernel(
            attend_weight_kernel,
            "attend_weight",
            [(part, f32), (part, bf16), ((8, 3 * width), f32)],
            (self.ids, self.packed, dq, dkv),
            scratch=[pltpu.VMEM((splits, groups) + quarter, f32)],
            scalars=1,
            flops=6 * tokens * model * width,
        )
        dws = add_split(dw_mine, swap_cores(dw_other), [(part[1:], bf16)] * groups)
        dws = exchange_parts(dws)
        full = (piece_len, model)
        partial = run_kernel(
            input_grad_kernel,
            "input_grad",
            [(full, f32)] + [(full, bf16)] * (chips - 1),
            (dq, mine, recv, self.weight),
            flops=3 * tokens * model * width,
        )
        partial = line_parts(partial)
        dws = sum_split(dws, [(quarter, bf16)] * chips)
        share = tied(share, dws[0])
        dws = line_parts(dws)
        shares = exchange_all(share)
        (dw,) = run_kernel(stack_kernel, "stack", [(part[1:], bf16)], tuple(dws))
        gq, gk, gv = run_kernel(
            finish_kernel,
            "finish",
            [((rows, model), f32)] * 3,
            (self.ids, *exchange_all(dw)),
            scratch=[pltpu.VMEM(part, bf16)],
            scalars=1,
        )
        (input_grad,) = sum_split([grad_res] + partial, [(full, f32)])
        sums = sum(exchange_all(sums + swap_cores(sums)))
        core = self.position % 2
        bias_q = lax.dynamic_slice_in_dim(sums[0], core * rows, rows)
        bias_v = lax.dynamic_slice_in_dim(sums[0], 2 * width + core * rows, rows)
        return input_grad, gq, bias_q, gk, gv, bias_v, shares


def one_hot(index, count):
    return (index[..., None] == jnp.arange(count, dtype=jnp.int32)).astype(bf16)


def with_halo(block, axis, dim, width):
    count = lax.axis_size(axis)
    forward = [(i, i + 1) for i in range(count - 1)]
    backward = [(target, source) for source, target in forward]
    low = lax.ppermute(
        lax.slice_in_dim(block, block.shape[dim] - width, None, axis=dim), axis, forward
    )
    high = lax.ppermute(lax.slice_in_dim(block, 0, width, axis=dim), axis, backward)
    return jnp.concatenate([low, block, high], axis=dim)


def broadcast(block, axis, owner):
    block = jnp.where(lax.axis_index(axis) == owner, block, jnp.zeros_like(block))
    return lax.psum(block, axis)


class TokenAttention:
    def __init__(self, hidden, weights, biases, segments, random_blocks, output_weight, vec_local):
        self.splits = splits = lax.axis_size("seq")
        self.position = position = lax.axis_index("seq")
        self.ids = device_ids() * jnp.array([1, 0, 1], jnp.int32)
        self.hidden = hidden
        self.segments = segments
        self.random_blocks = random_blocks
        self.weights = [lax.all_gather(w, "seq", axis=0, tiled=True) for w in weights]
        self.output_weight = lax.all_gather(output_weight, "seq", axis=0, tiled=True)[None]
        vec = lax.all_gather(vec_local, "seq")
        self.vec = vec.transpose(1, 0, 2).reshape(vec_local.shape[0], -1).astype(f32)

    def forward(self):
        hidden, segments = self.hidden, self.segments
        splits, position = self.splits, self.position
        seq_count = segments.shape[0]
        row_count, model = hidden.shape
        piece_len = row_count // seq_count
        size = model // HEADS
        per = piece_len // BLOCK
        slots = self.random_blocks.shape[3]
        reqs = seq_count * per * HEADS * slots
        cap = max(2, 3 * reqs // (2 * splits) + 1)
        vec = self.vec
        wq, wk, wv = self.weights
        query = (matmul(hidden, wq) + vec[0:1]).astype(bf16)
        keys = matmul(hidden, wk).astype(bf16)
        values = (matmul(hidden, wv) + vec[1:2]).astype(bf16)
        joined = jnp.concatenate([keys, values], 1).reshape(seq_count, piece_len, 2 * model)
        extended = with_halo(joined, "seq", 1, BLOCK)
        first = broadcast(joined[:, :BLOCK], "seq", 0)
        last = broadcast(joined[:, piece_len - BLOCK :], "seq", splits - 1)
        tiles = seq_count * per * HEADS
        tile_size = BLOCK * 2 * size
        kv_tiles = (
            joined.reshape(seq_count, per, BLOCK, 2, HEADS, size)
            .transpose(0, 1, 4, 2, 3, 5)
            .reshape(tiles, tile_size)
        )
        req = jnp.arange(reqs, dtype=jnp.int32)
        req_seq = req // (per * HEADS * slots)
        req_head = req // slots % HEADS
        earlier = (req[:, None] > req[None, :]).astype(jnp.int32)
        everyone = (
            self.random_blocks.reshape(seq_count, splits, per, HEADS, slots)
            .transpose(1, 0, 2, 3, 4)
            .reshape(splits, reqs)
        )
        is_mine = (everyone // per == position).astype(jnp.int32)
        place = jnp.sum(is_mine[:, None, :] * earlier, 2)
        slot = jnp.where(is_mine == 1, place, cap)
        tile_of = (req_seq * per + everyone % per) * HEADS + req_head
        chosen = slot[:, :, None] == jnp.arange(cap, dtype=jnp.int32)
        send = jnp.sum(jnp.where(chosen, tile_of[:, :, None], 0), 1).reshape(splits * cap)
        self.send = one_hot(send, tiles)
        outgoing = matmul(self.send, kv_tiles).astype(bf16).reshape(splits, cap, tile_size)
        incoming = lax.all_to_all(outgoing, "seq", 0, 0, tiled=True)
        asked = lax.dynamic_slice_in_dim(self.random_blocks, position * per, per, 1)
        owner = asked.reshape(reqs) // per
        before = jnp.sum((owner[:, None] == owner[None, :]).astype(jnp.int32) * earlier, 1)
        self.arrival = one_hot(owner * cap + before, splits * cap)
        fetched = matmul(self.arrival, incoming.reshape(splits * cap, tile_size)).astype(bf16)
        moved = fetched.reshape(seq_count, per, HEADS, slots * BLOCK, 2, size)
        spans = [slice(i * BLOCK, (i + 3) * BLOCK) for i in range(per)]
        fixed = jnp.stack(
            [jnp.concatenate([extended[:, span], first, last], 1) for span in spans], 1
        )
        fixed = fixed.reshape(seq_count, per, 5 * BLOCK, 2, HEADS, size)
        paired = jnp.concatenate(
            [fixed.transpose(3, 0, 1, 4, 2, 5), moved.transpose(4, 0, 1, 2, 3, 5)], 4
        )
        self.keys, self.values = paired[0], paired[1]
        edge = jnp.full((seq_count, BLOCK), -1, jnp.int32)
        padded = jnp.concatenate([edge, segments, edge], 1)
        query_seg = lax.dynamic_slice_in_dim(segments, position * piece_len, piece_len, 1)
        ext_seg = lax.dynamic_slice_in_dim(padded, position * piece_len, piece_len + 2 * BLOCK, 1)
        always = jnp.full((seq_count, 2 * BLOCK), -2, jnp.int32)
        seg_fixed = jnp.stack(
            [jnp.concatenate([ext_seg[:, span], always], 1) for span in spans], 1
        )
        seg_fixed = jnp.broadcast_to(
            seg_fixed[:, :, None], (seq_count, per, HEADS, 5 * BLOCK)
        )
        seg_blocks = segments.reshape(seq_count, -1, BLOCK)
        asked_hot = one_hot(asked, seg_blocks.shape[1])
        seg_moved = jnp.einsum(
            "gjhrb,gbt->gjhrt", asked_hot, seg_blocks.astype(bf16), preferred_element_type=f32
        ).astype(jnp.int32)
        key_seg = jnp.concatenate(
            [seg_fixed, seg_moved.reshape(seq_count, per, HEADS, slots * BLOCK)], 3
        )[:, :, :, None, :]
        self.allowed = (
            query_seg.reshape(seq_count, per, 1, BLOCK, 1) == key_seg
        ) | (key_seg == -2)
        self.query = query.reshape(seq_count, per, BLOCK, HEADS, size)
        scores = self.scores()
        top = jnp.max(scores, -1, keepdims=True)
        powers = jnp.exp(scores - top)
        total = jnp.sum(powers, -1, keepdims=True)
        self.log_total = top + jnp.log(total)
        attended = jnp.einsum(
            "gjhqk,gjhke->gjqhe",
            (powers / total).astype(bf16),
            self.values,
            preferred_element_type=f32,
        )
        return [attended.astype(bf16).reshape(row_count, model).T]

    def scores(self):
        raw = jnp.einsum("gjqhe,gjhke->gjhqk", self.query, self.keys, preferred_element_type=f32)
        return jnp.where(self.allowed, raw * self.query.shape[-1] ** -0.5, MASKED)

    def output_grad(self, attended, grad_branch, sums):
        splits = self.splits
        full = matmul(attended[0], grad_branch)
        share = lax.psum_scatter(full, "seq", scatter_dimension=0, tiled=True)
        total = lax.psum(share.astype(bf16), "dp").astype(f32)
        lines = lax.psum(sums[:3], ("dp", "seq")).reshape(3, splits, -1)
        lines = lax.dynamic_index_in_dim(lines, self.position, 1, keepdims=False)
        return total, lines.reshape(-1)

    def backward(self, grads, grad_res, inner_share):
        hidden = self.hidden
        grad = grads[0].T
        splits, position = self.splits, self.position
        seq_count, per, _, _, size = self.query.shape
        row_count, model = hidden.shape
        piece_len = per * BLOCK
        slots = self.random_blocks.shape[3]
        scale = size**-0.5
        probs = jnp.exp(self.scores() - self.log_total)
        grad_split = grad.reshape(seq_count, per, BLOCK, HEADS, size)
        grad_probs = jnp.einsum(
            "gjqhe,gjhke->gjhqk", grad_split, self.values, preferred_element_type=f32
        )
        weighted = jnp.sum(probs * grad_probs, -1, keepdims=True)
        grad_scores = (probs * (grad_probs - weighted)).astype(bf16)
        grad_query = (
            jnp.einsum("gjhqk,gjhke->gjqhe", grad_scores, self.keys, preferred_element_type=f32)
            * scale
        )
        grad_key = (
            jnp.einsum("gjhqk,gjqhe->gjhke", grad_scores, self.query, preferred_element_type=f32)
            * scale
        )
        grad_value = jnp.einsum(
            "gjhqk,gjqhe->gjhke", probs.astype(bf16), grad_split, preferred_element_type=f32
        )
        paired = jnp.stack([grad_key, grad_value], 0)
        fixed_len = 5 * BLOCK
        fixed = (
            paired[:, :, :, :, :fixed_len]
            .transpose(1, 2, 4, 0, 3, 5)
            .reshape(seq_count, per, fixed_len, 2 * model)
        )
        moved = (
            paired[:, :, :, :, fixed_len:]
            .transpose(1, 2, 3, 4, 0, 5)
            .reshape(seq_count * per * HEADS * slots, BLOCK * 2 * size)
        )
        ext = jnp.zeros((seq_count, piece_len + 2 * BLOCK, 2 * model), f32)
        for i in range(per):
            ext = ext.at[:, i * BLOCK : (i + 3) * BLOCK].add(fixed[:, i, : 3 * BLOCK])
        first = jnp.sum(fixed[:, :, 3 * BLOCK : 4 * BLOCK], 1)
        last = jnp.sum(fixed[:, :, 4 * BLOCK :], 1)
        rims = jnp.concatenate([ext[:, :BLOCK], ext[:, piece_len + BLOCK :]], 1)
        beside = with_halo(rims.astype(bf16), "seq", 1, BLOCK).astype(f32)
        kv_grad = ext[:, BLOCK : BLOCK + piece_len]
        kv_grad = kv_grad.at[:, :BLOCK].add(beside[:, :BLOCK])
        kv_grad = kv_grad.at[:, piece_len - BLOCK :].add(beside[:, 3 * BLOCK :])
        first, last = lax.psum((first, last), "seq")
        kv_grad = kv_grad.at[:, :BLOCK].add(jnp.where(position == 0, first, 0.0))
        kv_grad = kv_grad.at[:, piece_len - BLOCK :].add(
            jnp.where(position == splits - 1, last, 0.0)
        )
        cap = self.send.shape[0] // splits
        outgoing = left_product(self.arrival, moved.astype(bf16)).astype(bf16)
        returned = lax.all_to_all(
            outgoing.reshape(splits, cap, -1), "seq", 0, 0, tiled=True
        ).reshape(splits * cap, -1)
        kv_grad = kv_grad + (
            left_product(self.send, returned)
            .reshape(seq_count, per, HEADS, BLOCK, 2, size)
            .transpose(0, 1, 3, 4, 2, 5)
            .reshape(seq_count, piece_len, 2 * model)
        )
        kv_grad = kv_grad.reshape(row_count, 2 * model).astype(bf16)
        grad_query = grad_query.reshape(row_count, model).astype(bf16)
        grads = (grad_query, kv_grad[:, :model], kv_grad[:, model:])
        input_grad = grad_res
        shares = []
        for part, weight in zip(grads, self.weights):
            input_grad = input_grad + right_product(part, weight)
            full = left_product(hidden, part)
            share = lax.psum_scatter(full, "seq", scatter_dimension=0, tiled=True)
            shares.append(lax.psum(share.astype(bf16), "dp").astype(f32))
        biases = jnp.stack([jnp.sum(grads[i].astype(f32), 0) for i in (0, 2)], 1)
        biases = lax.psum_scatter(biases, "seq", scatter_dimension=0, tiled=True)
        biases = lax.psum(biases.astype(bf16), "dp").astype(f32)
        parts = exchange_all(inner_share)
        return input_grad, shares[0], biases[:, 0], shares[1], shares[2], biases[:, 1], parts


def local(
    hidden_in,
    query_weight,
    query_bias,
    key_weight,
    value_weight,
    value_bias,
    output_weight,
    output_bias,
    first_gain,
    first_shift,
    inner_weight,
    inner_bias,
    outer_weight,
    outer_bias,
    second_gain,
    second_shift,
    segments,
    random_blocks,
    cotangent,
):
    seq_count, piece_len, model = hidden_in.shape
    splits = lax.axis_size("seq")
    groups = lax.axis_size("dp")
    group = lax.axis_index("dp")
    row_count = seq_count * piece_len
    rows = model // splits
    units = outer_weight.shape[0] // groups
    hidden = hidden_in.reshape(row_count, model)
    by_heads = (
        seq_count == 1 and groups == 4 and 2 < splits and HEADS % max(1, splits // 2) == 0
    )
    vec_local = jnp.concatenate(
        [
            v.reshape(-1, rows)
            for v in (
                query_bias,
                value_bias,
                output_bias,
                first_gain,
                first_shift,
                outer_bias,
                second_gain,
                second_shift,
                inner_bias,
            )
        ]
    )
    attention = (HeadAttention if by_heads else TokenAttention)(
        hidden,
        (query_weight, key_weight, value_weight),
        (query_bias, value_bias),
        segments,
        random_blocks,
        output_weight,
        vec_local,
    )
    inner_part = lax.dynamic_index_in_dim(
        inner_weight.reshape(rows, splits, groups, units), group, 2, keepdims=False
    ).reshape(rows, splits * units)
    outer_part = lax.dynamic_index_in_dim(
        outer_weight.reshape(groups, units, model), group, 0, keepdims=False
    )
    both = jnp.concatenate([inner_part, outer_part], 0)
    if by_heads:
        both = tied(both, attention.packed, attention.weight)
    both = lax.all_gather(both, "seq")
    if not by_heads:
        both = both.reshape(splits, 2, rows, model).transpose(1, 0, 2, 3)
        both = both.reshape(1, 2 * model, model)
    attended = attention.forward()
    vec = attention.vec
    ids = attention.ids
    w_out = attention.output_weight
    full = (row_count, model)
    wide = (groups * row_count, splits * units)
    low, normed, inverse = run_kernel(
        project_kernel,
        "project",
        [(full, bf16), (full, f32), ((row_count, 128), f32)],
        (ids, w_out, hidden, vec, *attended),
        scalars=1,
        flops=2 * row_count * model * model,
    )
    lows = exchange_all(low)
    work = 2 * wide[0] * wide[1] * model
    parts = run_kernel(
        forward_kernel,
        "forward",
        [(full, f32)] + [(full, bf16)] * (groups - 1) + [(wide, f32), (wide, bf16)],
        (ids, *lows, both, vec),
        scalars=1,
        flops=2 * work,
        powers=wide[0] * wide[1],
    )
    inner, act = parts[groups:]
    layer_out, grad_low, grad_mix, sums2 = run_kernel(
        middle_kernel,
        "middle",
        [(full, bf16), (full, bf16), (full, f32), ((8, model), f32)],
        (*exchange_parts(parts), normed, cotangent.reshape(row_count, model), vec),
    )
    grads = exchange_all(grad_low)
    parts = run_kernel(
        backward_kernel,
        "backward",
        [(full, f32)] + [(full, bf16)] * (groups - 1) + [(wide, bf16), ((1, wide[1]), f32)],
        (*grads, both, inner),
        flops=2 * work,
        powers=wide[0] * wide[1],
    )
    grad_inner, sum_inner = parts[groups:]
    recv = exchange_parts(parts)
    (stacked,) = run_kernel(
        inner_outer_kernel,
        "inner_outer",
        [((splits, 2 * rows + 8, model), bf16)],
        (*lows, *grads, tied(grad_inner, recv[1]), act, sums2, sum_inner),
        flops=2 * work,
    )
    grad_res, grad_branch, sums1, *grad_att = run_kernel(
        functools.partial(residual_kernel, parts=groups),
        "residual",
        [(full, f32), (full, bf16), ((8, model), f32)] + [(a.shape, bf16) for a in attended],
        (ids, grad_mix, normed, inverse, vec, w_out, *recv),
        scalars=1,
        flops=2 * row_count * model * model,
    )
    share = lax.psum_scatter(stacked, "seq", scatter_dimension=0, tiled=False)
    if by_heads:
        grad_att = line_parts(grad_att)
    input_grad, gq, bias_q, gk, gv, bias_v, shares = attention.backward(
        grad_att, grad_res, share
    )
    d_output, first_sums = attention.output_grad(attended, grad_branch, sums1)
    d_inner, d_outer, vectors = run_kernel(
        finish_inner_kernel,
        "finish_inner",
        [((rows, groups * splits * units), f32), ((groups * units, model), f32), ((8, model), f32)],
        (ids, *shares),
        scratch=[pltpu.VMEM((groups,) + share.shape, bf16)],
        scalars=1,
    )
    second_sums = vectors[groups]

    def cut(line, i):
        return line[i * rows : (i + 1) * rows]

    return (
        layer_out.reshape(seq_count, piece_len, model),
        input_grad.reshape(seq_count, piece_len, model),
        gq,
        bias_q,
        gk,
        gv,
        bias_v,
        d_output,
        cut(first_sums, 2),
        cut(first_sums, 0),
        cut(first_sums, 1),
        d_inner,
        vectors[:groups, 3 * rows : 3 * rows + units].reshape(-1),
        d_outer,
        cut(second_sums, 2),
        cut(second_sums, 0),
        cut(second_sums, 1),
    )


def solution(mesh):
    in_specs = (
        P("dp", "seq", None),
        P("seq", None),
        P("seq"),
        P("seq", None),
        P("seq", None),
        P("seq"),
        P("seq", None),
        P("seq"),
        P("seq"),
        P("seq"),
        P("seq", None),
        P("seq"),
        P("seq", None),
        P("seq"),
        P("seq"),
        P("seq"),
        P("dp", None),
        P("dp", None, None, None),
        P("dp", "seq", None),
    )
    out_specs = (
        P("dp", "seq", None),
        P("dp", "seq", None),
        P("seq", None),
        P("seq"),
        P("seq", None),
        P("seq", None),
        P("seq"),
        P("seq", None),
        P("seq"),
        P("seq"),
        P("seq"),
        P("seq", None),
        P("seq"),
        P("seq", None),
        P("seq"),
        P("seq"),
        P("seq"),
    )
    return jax.shard_map(local, mesh=mesh, in_specs=in_specs, out_specs=out_specs, check_vma=False)
```

```python
import functools

import jax
import jax.numpy as jnp
from jax import lax
from jax.experimental import pallas as pl
from jax.experimental.pallas import tpu as pltpu
from jax.sharding import PartitionSpec as P

HEADS = 12
BLOCK = 64
EPSILON = 1e-12
MASKED = -1000000000.0
GELU_A = 0.7978845608028654
GELU_B = 0.044715
VMEM_BYTES = 6 << 20
bf16 = jnp.bfloat16
f32 = jnp.float32


def matmul(left, right):
    return jnp.dot(left, right, preferred_element_type=f32)


def left_product(left, right):
    return lax.dot_general(left, right, (((0,), (0,)), ((), ())), preferred_element_type=f32)


def right_product(left, right):
    return lax.dot_general(left, right, (((1,), (1,)), ((), ())), preferred_element_type=f32)


def run_kernel(
    kernel, name, outs, args, scratch=(), scalars=0, raw=(), raw_outs=(), flops=0, powers=0, grant=VMEM_BYTES
):
    def spec(i, held):
        return pl.BlockSpec(memory_space=pltpu.MemorySpace.HBM if i in held else pltpu.VMEM)

    specs = [pl.BlockSpec(memory_space=pltpu.SMEM)] * scalars
    specs += [spec(i, raw) for i in range(scalars, len(args))]
    shapes = [jax.ShapeDtypeStruct(shape, dtype) for shape, dtype in outs]
    moved = sum(a.size * a.dtype.itemsize for a in (*args, *shapes))
    out_shape = tuple(pltpu.HBM(o.shape, o.dtype) if i in raw_outs else o for i, o in enumerate(shapes))
    args = [
        pltpu.with_memory_space_constraint(a, pltpu.HBM) if i in raw else a
        for i, a in enumerate(args)
    ]
    return pl.pallas_call(
        kernel,
        name=name,
        out_shape=out_shape,
        in_specs=specs,
        out_specs=tuple(spec(i, raw_outs) for i in range(len(outs))),
        scratch_shapes=list(scratch),
        compiler_params=pltpu.CompilerParams(vmem_limit_bytes=grant),
        cost_estimate=pl.CostEstimate(flops=flops, bytes_accessed=moved, transcendentals=powers),
    )(*args)


def normalize(values):
    center = values - jnp.mean(values, -1, keepdims=True)
    spread = jnp.mean(center * center, -1, keepdims=True)
    inverse = lax.rsqrt(spread + EPSILON)
    return center * inverse, inverse


def norm_back(grad, normed, inverse, gain):
    scaled = grad * gain
    return inverse * (
        scaled
        - jnp.mean(scaled, -1, keepdims=True)
        - normed * jnp.mean(scaled * normed, -1, keepdims=True)
    )


def bias_rows(be_ref, bn, same, head, block, blocks, block_len):
    width = same.shape[1]
    rows = [
        jnp.broadcast_to(be_ref[head * blocks + block + i : head * blocks + block + i + 1, :], (block_len, width))
        for i in range(same.shape[0] // block_len)
    ]
    return jnp.where(same, jnp.concatenate(rows, 0), bn)


def bias_rows(lines, bn, same):
    count, width = lines.shape
    length = same.shape[0] // count
    rows = [jnp.broadcast_to(lines[i : i + 1, :], (length, width)) for i in range(count)]
    return jnp.where(same, jnp.concatenate(rows, 0), bn)


def place(ids, mine, other, out):
    for k in range(out.shape[0] // 2):
        chip = ids[1] ^ k
        out[2 * chip + ids[0]] = mine[k]
        out[2 * chip + 1 - ids[0]] = other[k]


def concat_kernel(*refs):
    out = refs[-1]
    at = 0
    for r in refs[:-1]:
        rows = r.shape[0]
        out[at : at + rows] = r[...]
        at += rows


def stack_kernel(*refs):
    for k, r in enumerate(refs[:-1]):
        refs[-1][k] = r[...]


def cut_kernel(ids, wq, wk, wv, *refs):
    outs = refs[:-3]
    raw, scratch, sems = refs[-3:]
    _, half, _ = raw.shape
    start = pl.multiple_of(lax.rem(ids[2], 2) * half, half)
    copies = [
        pltpu.make_async_copy(w.at[pl.ds(start, half), :], raw.at[i], sems.at[i])
        for i, w in enumerate((wq, wk, wv))
    ]
    for copy in copies:
        copy.start()
    for copy in copies:
        copy.wait()
    chips, _, wide = scratch.shape
    width = wide // 3
    for chip in range(chips):
        scratch[chip] = jnp.concatenate(
            [raw[i, :, chip * width : (chip + 1) * width] for i in range(3)], 1
        )
    for k, out in enumerate(outs):
        out[...] = scratch[ids[1] ^ k]


def assemble_kernel(ids, mine, other, out):
    core = ids[0]
    own = lax.rem(ids[2], 2)
    _, chips, _, _ = mine.shape
    for h in range(2):
        for k in range(chips):
            chip = ids[1] ^ k
            out[2 * chip + core, own ^ h] = mine[h, k]
            out[2 * chip + 1 - core, own ^ h] = other[h, k]


def cut_output_kernel(ids, wo, vec, out):
    half = wo.shape[0] // 2
    count, rows = vec.shape
    start = pl.multiple_of(lax.rem(ids[2] // 2, 2) * half, half)
    tall, model = out.shape
    out[:half, :] = wo[pl.ds(start, half), :]
    line = jnp.concatenate([vec[...], jnp.zeros((count, model - rows), bf16)], 1)
    out[half:, :] = jnp.concatenate([line, jnp.zeros((tall - half - count, model), bf16)], 0)


def cut_inner_kernel(ids, w1, w2, out, scratch):
    groups, rows, model = scratch.shape
    units = w2.shape[0] // groups
    pieces = model // units
    for g in range(groups):
        scratch[g] = jnp.concatenate(
            [
                w1[:, (s * groups + g) * units : (s * groups + g + 1) * units]
                for s in range(pieces)
            ],
            1,
        )
    out[:rows, :] = scratch[ids[2]]
    out[rows:, :] = w2[pl.ds(pl.multiple_of(ids[2] * units, units), units), :]


def assemble_output_kernel(ids, mine, other, out, vec, scratch):
    core = ids[0]
    pieces, _, half, _ = out.shape
    chips = pieces // 2
    own = lax.rem(ids[2] // 2, 2)
    for k in range(chips):
        chip = ids[1] ^ k
        scratch[2 * chip + core] = mine[0, k, half:, :]
        scratch[2 * chip + 1 - core] = other[0, k, half:, :]
        for h in range(2):
            out[2 * chip + core, own ^ h] = mine[h, k, :half, :]
            out[2 * chip + 1 - core, own ^ h] = other[h, k, :half, :]
    rows = 2 * half
    vec[...] = jnp.concatenate(
        [scratch[piece].astype(f32)[:, :rows] for piece in range(pieces)], 1
    )


def attend_kernel(ids, w, be, bn, sk, sq, hid, ours, theirs, *refs):
    att = refs[0]
    kept = refs[1:5]
    qo, ko, vo, lse, qs, sems = refs[5:]
    copies = [
        pltpu.make_async_copy(here, there, sems.at[i])
        for i, (here, there) in enumerate(zip((qo, ko, vo, lse), kept))
    ]
    pieces, piece_len, width = qs.shape
    chips = pieces // 2
    core = ids[0]
    size = 64
    heads = width // size
    model = hid.shape[2]
    ours, theirs = ours[...].astype(f32), theirs[...].astype(f32)
    first = jnp.where(core == 0, ours, theirs)
    second = jnp.where(core == 0, theirs, ours)
    biases = jnp.concatenate([first, second], 1)
    qb, vb = biases[0:1, :], biases[1:2, :]
    tokens = hid[...].reshape(pieces * piece_len, model)
    product = matmul(tokens, w[...])
    query = (product[:, :width] + qb).astype(bf16) * bf16(size**-0.5)
    qs[...] = query.reshape(pieces, piece_len, width)
    ko[...] = product[:, width : 2 * width].astype(bf16)
    vo[...] = (product[:, 2 * width :] + vb).astype(bf16)
    lane = lax.broadcasted_iota(jnp.int32, (piece_len, 128), 1)
    for k in range(chips):
        qo[k] = qs[2 * (ids[1] ^ k) + core]
    for copy in copies[:3]:
        copy.start()
    for k in range(chips):
        chip = ids[1] ^ k
        same = sq[chip] == sk[...]
        logs = jnp.zeros((piece_len, 128), f32)
        parts = []
        for head in range(heads):
            cols = slice(head * size, (head + 1) * size)
            scores = right_product(qo[k, :, cols], ko[:, cols])
            scores = scores + bias_rows(be[head * chips + chip], bn[...], same)
            top = jnp.max(scores, -1, keepdims=True)
            powers = jnp.exp(scores - top)
            total = jnp.sum(powers, -1, keepdims=True)
            probs = (powers * (1.0 / total)).astype(bf16)
            parts.append(matmul(probs, vo[:, cols]))
            logs = jnp.where(lane == head, top + jnp.log(total), logs)
        att[chip] = jnp.concatenate(parts, 1).T.astype(bf16)
        lse[k] = logs
    copies[3].start()
    for copy in copies:
        copy.wait()


def attend_back_kernel(ids, hid_raw, q_raw, k_raw, v_raw, lse_raw, be, bn, sk, sq, *refs):
    chips, piece_len, width = q_raw.shape
    ga = refs[:chips]
    dq, mine, other, dw_mine, dw_other = refs[chips : chips + 5]
    hid, q, k, v, lse, ds_all, p_all, dkv, dws, sems = refs[chips + 5 :]
    copies = [
        pltpu.make_async_copy(there, here, sems.at[i])
        for i, (there, here) in enumerate(
            zip((q_raw, k_raw, v_raw, lse_raw, hid_raw), (q, k, v, lse, hid))
        )
    ]
    for copy in copies:
        copy.start()
    pieces = 2 * chips
    core = ids[0]
    size = 64
    heads = width // size
    dks = []
    dvs = []
    dqs = [[None] * heads for _ in range(chips)]
    for copy in copies[:4]:
        copy.wait()
    gas = [g[...].astype(f32).T.astype(bf16) for g in ga]
    for head in range(heads):
        cols = slice(head * size, (head + 1) * size)
        key = k[:, cols]
        value = v[:, cols]
        for i in range(chips):
            chip = ids[1] ^ i
            rows = slice(i * piece_len, (i + 1) * piece_len)
            same = sq[chip] == sk[...]
            scores = right_product(q[i, :, cols], key)
            scores = scores + bias_rows(be[head * chips + chip], bn[...], same)
            probs = jnp.exp(scores - lse[i, :, head : head + 1])
            grad = right_product(gas[i][:, cols], value)
            weighted = jnp.sum(probs * grad, -1, keepdims=True)
            ds = (probs * (grad - weighted)).astype(bf16)
            ds_all[rows, :] = ds
            p_all[rows, :] = probs.astype(bf16)
            dqs[i][head] = (matmul(ds, key) * (size**-0.5)).astype(bf16)
        queries = q[:, :, cols].reshape(chips * piece_len, size)
        grads = jnp.concatenate([g[:, cols] for g in gas], 0)
        dks.append(left_product(ds_all[...], queries).astype(bf16))
        dvs.append(left_product(p_all[...], grads).astype(bf16))
    for i in range(chips):
        dq[i] = jnp.concatenate(dqs[i], 1)
    joined = jnp.concatenate(dks + dvs, 1)
    dkv[...] = joined.reshape(pieces, piece_len, 2 * width)
    for i in range(chips):
        chip = ids[1] ^ i
        mine[i] = dkv[2 * chip + core]
        other[i] = dkv[2 * chip + 1 - core]
    copies[4].wait()
    _, _, model = hid.shape
    tokens = hid[...].reshape(pieces * piece_len, model)
    owned = jnp.concatenate([hid[2 * (ids[1] ^ i) + core] for i in range(chips)], 0)
    grad_q = dq[...].reshape(chips * piece_len, width)
    weights = jnp.concatenate([left_product(owned, grad_q), left_product(tokens, joined)], 1)
    groups = dw_mine.shape[0]
    rows = dws.shape[2]
    dws[...] = weights.reshape(dws.shape)
    for i in range(chips):
        chip = ids[1] ^ i
        for j in range(groups):
            span = slice(i * rows, (i + 1) * rows)
            dw_mine[j, span] = dws[2 * chip + core, ids[2] ^ j]
            dw_other[j, span] = dws[2 * chip + 1 - core, ids[2] ^ j].astype(bf16)
    total = jnp.concatenate(
        [
            jnp.sum(grad_q.astype(f32), 0, keepdims=True),
            jnp.sum(joined.astype(f32), 0, keepdims=True),
        ],
        1,
    )
    total = jnp.broadcast_to(total, (8, 3 * width))
    for j in range(groups):
        dw_mine[j, chips * rows :] = total
        dw_other[j, chips * rows :] = total.astype(bf16)


def input_grad_kernel(ids, dq, mine, recv, w, out, scratch):
    chips, piece_len, width = dq.shape
    dkv = (mine[...].astype(f32) + recv[...].astype(f32)).astype(bf16)
    grads = jnp.concatenate([dq[...], dkv], 2).reshape(chips * piece_len, 3 * width)
    total = right_product(grads, w[...])
    scratch[...] = total.astype(bf16).reshape(scratch.shape)
    for chip in range(chips):
        out[chip] = scratch[ids[1] ^ chip]


def add_kernel(left, right, out):
    out[...] = (left[...].astype(f32) + right[...].astype(f32)).astype(out.dtype)


def sum_rows_kernel(first, parts, out):
    total = first[...]
    for i in range(parts.shape[0]):
        total = total + parts[i].astype(f32)
    out[...] = total


def add_split_kernel(left, right, *outs):
    for k, out in enumerate(outs):
        out[...] = (left[k].astype(f32) + right[k].astype(f32)).astype(out.dtype)


def sum_split_kernel(*refs, parts, rows):
    total = refs[0][...].astype(f32)
    for r in refs[1:parts]:
        total = total + r[...].astype(f32)
    for k, out in enumerate(refs[parts:]):
        out[...] = total[k * rows : k * rows + out.shape[0]].astype(out.dtype)


def sum_lead_kernel(parts, *outs, rows):
    total = parts[0].astype(f32)
    for i in range(1, parts.shape[0]):
        total = total + parts[i].astype(f32)
    for k, out in enumerate(outs):
        out[...] = total[k * rows : k * rows + out.shape[0]].astype(out.dtype)


def project_kernel(wo, hid, vec, att, low, normed, inverse):
    branch = vec[2:3, :] + jnp.zeros(hid.shape, f32)
    for chip in range(att.shape[0]):
        branch = branch + left_product(att[chip], wo[chip])
    n1, r1 = normalize(hid[...].astype(f32) + branch)
    low[...] = (n1 * vec[3:4, :] + vec[4:5, :]).astype(bf16)
    normed[...] = n1
    inverse[...] = jnp.broadcast_to(r1, inverse.shape)


def gelu_parts(v):
    return jnp.tanh(GELU_A * (v + GELU_B * (v * v * v)))


def two_weights(both):
    pieces, rows, model = both.shape
    half = rows // 2
    first = both[:, :half, :].reshape(pieces * half, model)
    return first, both[:, half:, :].reshape(pieces * half, model)


def forward_kernel(ids, vec, both_raw, *refs, parts):
    raw = refs[:parts]
    outs = refs[parts : 2 * parts]
    inner_ref, act_ref, both, x, sems = refs[2 * parts :]
    copies = [pltpu.make_async_copy(r, x.at[i], sems.at[i]) for i, r in enumerate(raw)]
    copies.append(pltpu.make_async_copy(both_raw, both, sems.at[parts]))
    for copy in copies:
        copy.start()
    for copy in copies:
        copy.wait()
    _, rows, model = x.shape
    weight1, weight2 = two_weights(both)
    inner = matmul(x[...].reshape(parts * rows, model), weight1) + vec[pl.ds(8 + ids[2], 1), :]
    act = (0.5 * inner * (1.0 + gelu_parts(inner))).astype(bf16)
    inner_ref[...] = inner
    act_ref[...] = act
    mixed = matmul(act, weight2)
    for i in range(parts):
        outs[i][...] = mixed[i * rows : (i + 1) * rows].astype(outs[i].dtype)


def middle_kernel(*refs):
    recv = refs[:-7]
    normed, cot, vec, out, low, mix, sums = refs[-7:]
    first = normed[...] * vec[3:4, :] + vec[4:5, :]
    mixed = vec[5:6, :]
    for r in recv:
        mixed = mixed + r[...].astype(f32)
    n2, r2 = normalize(first + mixed)
    gain = vec[6:7, :]
    out[...] = (n2 * gain + vec[7:8, :]).astype(bf16)
    g = cot[...].astype(f32)
    grad = norm_back(g, n2, r2, gain)
    rounded = grad.astype(bf16)
    mix[...] = grad
    low[...] = rounded
    sums[0:1, :] = jnp.sum(g * n2, 0, keepdims=True)
    sums[1:2, :] = jnp.sum(g, 0, keepdims=True)
    sums[2:3, :] = jnp.sum(rounded.astype(f32), 0, keepdims=True)
    sums[3:, :] = jnp.zeros((5, sums.shape[1]), f32)


def backward_kernel(ids, both, inner_ref, act, sums, *refs, parts):
    x = refs[:parts]
    grads = refs[parts : 2 * parts]
    outs = refs[2 * parts : 3 * parts]
    rest = refs[3 * parts :]
    rows = grads[0].shape[0]
    weight1, weight2 = two_weights(both)
    gm = jnp.concatenate([r[...] for r in grads], 0)
    grad_act = right_product(gm, weight2)
    v = inner_ref[...]
    t = gelu_parts(v)
    slope = 0.5 * (1.0 + t) + 0.5 * v * (1.0 - t * t) * (GELU_A * (1.0 + 3.0 * GELU_B * (v * v)))
    gi = (grad_act * slope).astype(bf16)
    first = right_product(gi, weight1)
    for i in range(parts):
        outs[i][...] = first[i * rows : (i + 1) * rows].astype(outs[i].dtype)
    tokens = jnp.concatenate([r[...] for r in x], 0)
    inner = left_product(tokens, gi).astype(bf16)
    outer = left_product(act[...], gm).astype(bf16)
    total = jnp.sum(gi.astype(f32), 0, keepdims=True)
    vectors = [sums[i : i + 1, :] for i in range(3)] + [total]

    def write(place_of):
        for piece in range(inner.shape[0] // units):
            out, at = place_of(piece)
            span = slice(piece * units, (piece + 1) * units)
            out[at, :units, :] = inner[span]
            out[at, units : 2 * units, :] = outer[span]
            put_vectors(out, piece, at, 2 * units, vectors, units)

    units = (rest[0].shape[1] - 8) // 2
    write(lambda piece: (rest[0], piece))


def residual_kernel(ids, mix, normed, inverse, vec, wo, *refs, parts):
    first = mix[...]
    for r in refs[:parts]:
        first = first + r[...].astype(f32)
    res, low, sums = refs[parts : parts + 3]
    n1 = normed[...]
    grad = norm_back(first, n1, inverse[:, 0:1], vec[3:4, :])
    rounded = grad.astype(bf16)
    for k, back in enumerate(refs[parts + 3 :]):
        back[...] = right_product(wo[ids[1] ^ k], rounded).astype(bf16)
    res[...] = grad
    low[...] = rounded
    sums[0:1, :] = jnp.sum(first * n1, 0, keepdims=True)
    sums[1:2, :] = jnp.sum(first, 0, keepdims=True)
    sums[2:3, :] = jnp.sum(rounded.astype(f32), 0, keepdims=True)
    sums[3:, :] = jnp.zeros((5, sums.shape[1]), f32)


def put_vectors(out, piece, at, row, vectors, rows):
    parts = [v[:, piece * rows : (piece + 1) * rows] for v in vectors]
    fill = out.shape[2] - rows * len(parts)
    line = jnp.concatenate(parts + [jnp.zeros((1, fill), f32)], 1)
    out[at, row : row + 8, :] = jnp.broadcast_to(line, (8, out.shape[2])).astype(bf16)


def output_grad_kernel(gb, sums, att, out):
    rows = out.shape[1] - 8
    grad = gb[...]
    vectors = [sums[i : i + 1, :] for i in range(3)]
    for chip in range(att.shape[0]):
        part = matmul(att[chip], grad).astype(bf16)
        for i in range(2):
            piece = 2 * chip + i
            out[piece, :rows] = part[i * rows : (i + 1) * rows]
            put_vectors(out, piece, piece, rows, vectors, rows)


def ordered(ids, refs, scratch):
    for k, r in enumerate(refs):
        scratch[ids[2] ^ k] = r[...]


def finish_inner_kernel(ids, *refs, parts):
    inner, outer, vectors, scratch = refs[parts:]
    ordered(ids, refs[:parts], scratch)
    rows = inner.shape[0]
    units = outer.shape[0] // parts
    pieces = scratch.shape[2] // units
    for piece in range(pieces):
        inner[:, piece * parts * units : (piece + 1) * parts * units] = jnp.concatenate(
            [
                scratch[g, :rows, piece * units : (piece + 1) * units].astype(f32)
                for g in range(parts)
            ],
            1,
        )
    total = jnp.zeros((1, scratch.shape[2]), f32)
    at = rows + units
    for g in range(parts):
        outer[g * units : (g + 1) * units, :] = scratch[g, rows:at, :].astype(f32)
        line = scratch[g, at : at + 8, :].astype(f32)[0:1]
        vectors[g : g + 1, :] = line
        total = total + line
    vectors[parts : parts + 1, :] = total


def finish_output_kernel(p0, p1, p2, p3, out, vectors):
    rows = out.shape[0]
    total = p0[...].astype(f32)
    for r in (p1, p2, p3):
        total = total + r[...].astype(f32)
    out[...] = total[:rows]
    vectors[...] = total[rows:]


def finish_kernel(ids, *refs):
    parts = len(refs) - 4
    gq, gk, gv, scratch = refs[parts:]
    quarters, chips, rows, wide = scratch.shape
    for j, r in enumerate(refs[:parts]):
        for k in range(chips):
            scratch[ids[2] ^ j, ids[1] ^ k] = r[k]
    width = wide // 3
    for part in range(quarters):
        block = [scratch[part, chip].astype(f32) for chip in range(chips)]
        for i, out in enumerate((gq, gk, gv)):
            out[part * rows : (part + 1) * rows, :] = jnp.concatenate(
                [b[:, i * width : (i + 1) * width] for b in block], 1
            )


def log_counts(count):
    return jnp.where(count > 0, jnp.log(jnp.maximum(count, 1).astype(f32)), MASKED)


def exchange(array, k):
    count = lax.axis_size("dp")
    return lax.ppermute(array, "dp", [(i, i ^ k) for i in range(count)])


def exchange_all(array):
    return [array] + [exchange(array, k) for k in range(1, lax.axis_size("dp"))]


def exchange_parts(parts):
    return [parts[0]] + [exchange(parts[k], k) for k in range(1, lax.axis_size("dp"))]


def swap_cores(array):
    count = lax.axis_size("seq")
    return lax.ppermute(array, "seq", [(i, i ^ 1) for i in range(count)])


def line_exchange(array, k):
    count = lax.axis_size("seq")
    return lax.ppermute(array, "seq", [(i, i ^ (2 * k)) for i in range(count)])


def line_parts(parts):
    return [parts[0]] + [line_exchange(parts[k], k) for k in range(1, len(parts))]


def tied(value, *others):
    return lax.optimization_barrier((value,) + others)[0]


def add_split(left, right, outs):
    return run_kernel(add_split_kernel, "add", outs, (left, right))


def sum_split(arrays, outs):
    return run_kernel(
        functools.partial(sum_split_kernel, parts=len(arrays), rows=outs[0][0][0]),
        "sum",
        outs,
        tuple(arrays),
    )


def line_all(array):
    return [array] + [line_exchange(array, k) for k in range(1, lax.axis_size("seq") // 2)]


def along_line(array):
    count = lax.axis_size("seq")
    lines = [[2 * i + c for i in range(count // 2)] for c in range(2)]
    return lax.all_to_all(array, "seq", 0, 0, tiled=True, axis_index_groups=lines)


def stack(*arrays):
    shape = (len(arrays),) + arrays[0].shape
    return run_kernel(stack_kernel, "stack", [(shape, bf16)], arrays)[0]


def concat(*arrays):
    shape = (sum(a.shape[0] for a in arrays),) + arrays[0].shape[1:]
    return run_kernel(concat_kernel, "concat", [(shape, bf16)], arrays)[0]


def device_ids():
    position = lax.axis_index("seq")
    return jnp.stack([position % 2, position // 2, lax.axis_index("dp")]).astype(jnp.int32)


def finish_inner(ids, shares, rows):
    groups = len(shares)
    share = shares[0]
    model = share.shape[1]
    return run_kernel(
        functools.partial(finish_inner_kernel, parts=groups),
        "finish_inner",
        [((rows, groups * model), f32), ((groups * rows, model), f32), ((8, model), f32)],
        (ids, *shares),
        scratch=[pltpu.VMEM((groups,) + share.shape, bf16)],
        scalars=1,
    )


class HeadAttention:
    def __init__(self, hidden, weights, biases, segments, random_blocks, output_weight, vec_local):
        self.splits = splits = lax.axis_size("seq")
        self.chips = chips = splits // 2
        self.position = position = lax.axis_index("seq")
        core = position % 2
        chip = position // 2
        group = lax.axis_index("dp")
        self.ids = device_ids()
        self.packed = lax.all_gather(hidden, "seq")
        piece_len, model = hidden.shape
        rows = model // splits
        width = model // chips
        heads = HEADS // chips
        half = rows // 2
        cut = run_kernel(
            cut_kernel,
            "cut",
            [((half, 3 * width), bf16)] * chips,
            (self.ids, *weights),
            scratch=[
                pltpu.VMEM((3, half, model), bf16),
                pltpu.VMEM((chips, half, 3 * width), bf16),
                pltpu.SemaphoreType.DMA((3,)),
            ],
            scalars=1,
            raw=range(1, 4),
        )
        cut = stack(*line_parts(cut))
        cut_next = exchange(cut, 1)
        (out_half,) = run_kernel(
            cut_output_kernel,
            "cut_output",
            [((half + 16, model), bf16)],
            (self.ids, output_weight, vec_local),
            scalars=1,
        )
        cut = stack(cut, cut_next)
        (weight,) = run_kernel(
            assemble_kernel,
            "assemble",
            [((splits, 2, half, 3 * width), bf16)],
            (self.ids, cut, swap_cores(cut)),
            scalars=1,
        )
        self.out_half = stack(*line_all(tied(out_half, cut_next)))
        self.out_next = exchange(self.out_half, 2)
        self.weight = weight.reshape(model, 3 * width)
        self.biases = biases
        self.hidden = hidden
        block_count = segments.shape[1] // BLOCK
        per_piece = piece_len // BLOCK
        own = random_blocks[0].reshape(chips, 2, per_piece, HEADS, -1)
        own = lax.dynamic_index_in_dim(own, core, 1, keepdims=False)
        own = lax.dynamic_slice_in_dim(own, chip * heads, heads, 2)
        own = own.reshape(chips * per_piece, heads, -1).transpose(1, 0, 2)
        block = jnp.arange(block_count, dtype=jnp.int32)
        mine = (
            (jnp.arange(chips, dtype=jnp.int32)[:, None] * 2 + core) * per_piece
            + jnp.arange(per_piece, dtype=jnp.int32)[None, :]
        ).reshape(-1)
        ends = ((block == 0) | (block == block_count - 1)).astype(jnp.int32)
        near = (jnp.abs(block[None, :] - mine[:, None]) <= 1).astype(jnp.int32)
        listed = jnp.sum((own[..., None] == block).astype(jnp.int32), 2)
        count = listed + near[None] + ends
        self.same_bias = jnp.repeat(log_counts(count), BLOCK, axis=2).reshape(
            heads * chips, per_piece, -1
        )
        self.other_bias = jnp.repeat(
            jnp.where(ends > 0, 0.0, MASKED).astype(f32)[None], BLOCK, axis=1
        )
        self.key_seg = segments
        self.query_seg = lax.dynamic_index_in_dim(
            segments.reshape(chips, 2, piece_len), core, 1, keepdims=False
        ).reshape(chips, piece_len, 1)
        self.piece_len, self.width, self.model = piece_len, width, model

    def masks(self):
        return (self.same_bias, self.other_bias, self.key_seg, self.query_seg)

    def inner_weights(self, inner_weight, outer_weight):
        groups = lax.axis_size("dp")
        rows = inner_weight.shape[0]
        units = outer_weight.shape[0] // groups
        (both,) = run_kernel(
            cut_inner_kernel,
            "cut_inner",
            [((rows + units, self.model), bf16)],
            (self.ids, inner_weight, outer_weight),
            scratch=[pltpu.VMEM((groups, rows, self.model), bf16)],
            scalars=1,
        )
        self.pair = jnp.stack(self.biases, 0)
        self.pair_other = swap_cores(self.pair)
        self.both = lax.all_gather(tied(both, self.packed, self.weight, self.out_half), "seq")

    def forward(self):
        chips, piece_len, width, model = self.chips, self.piece_len, self.width, self.model
        tokens = self.splits * piece_len
        one = (chips, piece_len, width)
        kept = [
            (one, bf16),
            ((tokens, width), bf16),
            ((tokens, width), bf16),
            ((chips, piece_len, 128), f32),
        ]
        att, self.q, self.k, self.v, self.lse = run_kernel(
            attend_kernel,
            "attend",
            [((chips, width, piece_len), bf16)] + kept,
            (self.ids, self.weight, *self.masks(), self.packed, self.pair, self.pair_other),
            scratch=[pltpu.VMEM(*spec) for spec in kept]
            + [
                pltpu.VMEM((self.splits, piece_len, width), bf16),
                pltpu.SemaphoreType.DMA((len(kept),)),
            ],
            scalars=1,
            raw_outs=range(1, 1 + len(kept)),
            flops=6 * tokens * model * width + 2 * tokens * tokens * width,
            powers=tokens * tokens * 3 // 2,
            grant=12 << 20,
        )
        out_half = stack(tied(self.out_half, att), self.out_next)
        half = model // self.splits // 2
        weight, self.vec = run_kernel(
            assemble_output_kernel,
            "assemble_output",
            [((self.splits, 2, half, model), bf16), ((16, model), f32)],
            (self.ids, out_half, swap_cores(out_half)),
            scratch=[pltpu.VMEM((self.splits, 16, model), bf16)],
            scalars=1,
        )
        self.output_weight = weight.reshape(chips, width, model)
        att = along_line(att)
        return att

    def inner_shapes(self, tall):
        return [((self.splits, tall, self.model), bf16)]

    def inner_grads(self, stacked):
        self.share = lax.psum_scatter(stacked, "seq", scatter_dimension=0, tiled=False)

    def output_grad(self, attended, grad_branch, sums):
        chips, model = self.chips, self.model
        (stacked,) = run_kernel(
            output_grad_kernel,
            "output_grad",
            [((self.splits, model // self.splits + 8, model), bf16)],
            (grad_branch, sums, attended),
            flops=2 * self.piece_len * model * model,
        )
        stacked = tied(stacked, self.share)
        self.output_share = lax.psum_scatter(stacked, "seq", scatter_dimension=0, tiled=False)

    def finish_grads(self, after):
        model = self.model
        groups = lax.axis_size("dp")
        rows = model // self.splits
        d_inner, d_outer, vectors = finish_inner(self.ids, self.shares, rows)
        d_output, lines = run_kernel(
            finish_output_kernel,
            "finish_output",
            [((rows, model), f32), ((8, model), f32)],
            tuple(exchange_all(self.output_share)),
        )
        return d_inner, d_outer, d_output, lines[0], vectors

    def backward(self, grads, grad_res):
        chips, piece_len, width = self.chips, self.piece_len, self.width
        splits, model = self.splits, self.model
        groups = lax.axis_size("dp")
        tokens = splits * piece_len
        rows = model // splits
        one = (chips, piece_len, width)
        two = (chips, piece_len, 2 * width)
        quarter = (rows // groups, 3 * width)
        group = (chips * quarter[0] + 8, 3 * width)
        wide = ((groups,) + group, bf16)
        keep = (self.packed, self.q, self.k, self.v, self.lse)
        dq, mine, other, dw_mine, dw_other = run_kernel(
            attend_back_kernel,
            "attend_back",
            [(one, bf16), (two, bf16), (two, bf16), (wide[0], f32), wide],
            (self.ids,) + keep + self.masks() + tuple(grads),
            scratch=[pltpu.VMEM(a.shape, a.dtype) for a in keep]
            + [
                pltpu.VMEM((chips * piece_len, tokens), bf16),
                pltpu.VMEM((chips * piece_len, tokens), bf16),
                pltpu.VMEM((splits, piece_len, 2 * width), bf16),
                pltpu.VMEM((splits, groups) + quarter, f32),
                pltpu.SemaphoreType.DMA((len(keep),)),
            ],
            scalars=1,
            raw=range(1, 6),
            flops=5 * tokens * tokens * width + 6 * tokens * model * width,
            powers=tokens * tokens * 3 // 2,
            grant=18 << 20,
        )
        recv = swap_cores(other)
        dws = add_split(dw_mine, swap_cores(dw_other), [(group, bf16)] * groups)
        dq = tied(dq, dws[0])
        self.last = dws[0]
        dws = exchange_parts(dws)
        full = (piece_len, model)
        (partial,) = run_kernel(
            input_grad_kernel,
            "input_grad",
            [((chips,) + full, bf16)],
            (self.ids, dq, mine, recv, self.weight),
            scratch=[pltpu.VMEM((chips,) + full, bf16)],
            scalars=1,
            flops=3 * tokens * model * width,
        )
        *dws, sums = sum_split(dws, [(quarter, bf16)] * chips + [((8, 3 * width), f32)])
        dws = line_parts(dws)
        self.shares = exchange_all(tied(self.share, dws[0]))
        partial = along_line(tied(partial, *dws[1:], self.shares[1]))
        part = (chips,) + quarter
        dw = stack(*dws)
        gq, gk, gv = run_kernel(
            finish_kernel,
            "finish",
            [((rows, model), f32)] * 3,
            (self.ids, *exchange_all(dw)),
            scratch=[pltpu.VMEM((groups,) + part, bf16)],
            scalars=1,
        )
        (input_grad,) = run_kernel(
            sum_rows_kernel, "sum_rows", [(full, f32)], (grad_res, partial)
        )
        core = self.position % 2
        bias_q = lax.dynamic_slice_in_dim(sums[0], core * rows, rows)
        bias_v = lax.dynamic_slice_in_dim(sums[0], 2 * width + core * rows, rows)
        return input_grad, gq, bias_q, gk, gv, bias_v, dws[0]


def one_hot(index, count):
    return (index[..., None] == jnp.arange(count, dtype=jnp.int32)).astype(bf16)


def with_halo(block, axis, dim, width):
    count = lax.axis_size(axis)
    forward = [(i, i + 1) for i in range(count - 1)]
    backward = [(target, source) for source, target in forward]
    low = lax.ppermute(
        lax.slice_in_dim(block, block.shape[dim] - width, None, axis=dim), axis, forward
    )
    high = lax.ppermute(lax.slice_in_dim(block, 0, width, axis=dim), axis, backward)
    return jnp.concatenate([low, block, high], axis=dim)


def broadcast(block, axis, owner):
    block = jnp.where(lax.axis_index(axis) == owner, block, jnp.zeros_like(block))
    return lax.psum(block, axis)


class TokenAttention:
    def __init__(self, hidden, weights, biases, segments, random_blocks, output_weight, vec_local):
        self.splits = splits = lax.axis_size("seq")
        self.position = position = lax.axis_index("seq")
        self.ids = device_ids() * jnp.array([1, 0, 1], jnp.int32)
        self.hidden = hidden
        self.segments = segments
        self.random_blocks = random_blocks
        self.weights = [lax.all_gather(w, "seq", axis=0, tiled=True) for w in weights]
        self.output_weight = lax.all_gather(output_weight, "seq", axis=0, tiled=True)[None]
        vec = lax.all_gather(vec_local, "seq")
        self.vec = vec.transpose(1, 0, 2).reshape(vec_local.shape[0], -1).astype(f32)

    def forward(self):
        hidden, segments = self.hidden, self.segments
        splits, position = self.splits, self.position
        seq_count = segments.shape[0]
        row_count, model = hidden.shape
        piece_len = row_count // seq_count
        size = model // HEADS
        per = piece_len // BLOCK
        slots = self.random_blocks.shape[3]
        reqs = seq_count * per * HEADS * slots
        cap = max(2, 3 * reqs // (2 * splits) + 1)
        vec = self.vec
        wq, wk, wv = self.weights
        query = (matmul(hidden, wq) + vec[0:1]).astype(bf16)
        keys = matmul(hidden, wk).astype(bf16)
        values = (matmul(hidden, wv) + vec[1:2]).astype(bf16)
        joined = jnp.concatenate([keys, values], 1).reshape(seq_count, piece_len, 2 * model)
        extended = with_halo(joined, "seq", 1, BLOCK)
        first = broadcast(joined[:, :BLOCK], "seq", 0)
        last = broadcast(joined[:, piece_len - BLOCK :], "seq", splits - 1)
        tiles = seq_count * per * HEADS
        tile_size = BLOCK * 2 * size
        kv_tiles = (
            joined.reshape(seq_count, per, BLOCK, 2, HEADS, size)
            .transpose(0, 1, 4, 2, 3, 5)
            .reshape(tiles, tile_size)
        )
        req = jnp.arange(reqs, dtype=jnp.int32)
        req_seq = req // (per * HEADS * slots)
        req_head = req // slots % HEADS
        earlier = (req[:, None] > req[None, :]).astype(jnp.int32)
        everyone = (
            self.random_blocks.reshape(seq_count, splits, per, HEADS, slots)
            .transpose(1, 0, 2, 3, 4)
            .reshape(splits, reqs)
        )
        is_mine = (everyone // per == position).astype(jnp.int32)
        place = jnp.sum(is_mine[:, None, :] * earlier, 2)
        slot = jnp.where(is_mine == 1, place, cap)
        tile_of = (req_seq * per + everyone % per) * HEADS + req_head
        chosen = slot[:, :, None] == jnp.arange(cap, dtype=jnp.int32)
        send = jnp.sum(jnp.where(chosen, tile_of[:, :, None], 0), 1).reshape(splits * cap)
        self.send = one_hot(send, tiles)
        outgoing = matmul(self.send, kv_tiles).astype(bf16).reshape(splits, cap, tile_size)
        incoming = lax.all_to_all(outgoing, "seq", 0, 0, tiled=True)
        asked = lax.dynamic_slice_in_dim(self.random_blocks, position * per, per, 1)
        owner = asked.reshape(reqs) // per
        before = jnp.sum((owner[:, None] == owner[None, :]).astype(jnp.int32) * earlier, 1)
        self.arrival = one_hot(owner * cap + before, splits * cap)
        fetched = matmul(self.arrival, incoming.reshape(splits * cap, tile_size)).astype(bf16)
        moved = fetched.reshape(seq_count, per, HEADS, slots * BLOCK, 2, size)
        spans = [slice(i * BLOCK, (i + 3) * BLOCK) for i in range(per)]
        fixed = jnp.stack(
            [jnp.concatenate([extended[:, span], first, last], 1) for span in spans], 1
        )
        fixed = fixed.reshape(seq_count, per, 5 * BLOCK, 2, HEADS, size)
        paired = jnp.concatenate(
            [fixed.transpose(3, 0, 1, 4, 2, 5), moved.transpose(4, 0, 1, 2, 3, 5)], 4
        )
        self.keys, self.values = paired[0], paired[1]
        edge = jnp.full((seq_count, BLOCK), -1, jnp.int32)
        padded = jnp.concatenate([edge, segments, edge], 1)
        query_seg = lax.dynamic_slice_in_dim(segments, position * piece_len, piece_len, 1)
        ext_seg = lax.dynamic_slice_in_dim(padded, position * piece_len, piece_len + 2 * BLOCK, 1)
        always = jnp.full((seq_count, 2 * BLOCK), -2, jnp.int32)
        seg_fixed = jnp.stack(
            [jnp.concatenate([ext_seg[:, span], always], 1) for span in spans], 1
        )
        seg_fixed = jnp.broadcast_to(
            seg_fixed[:, :, None], (seq_count, per, HEADS, 5 * BLOCK)
        )
        seg_blocks = segments.reshape(seq_count, -1, BLOCK)
        asked_hot = one_hot(asked, seg_blocks.shape[1])
        seg_moved = jnp.einsum(
            "gjhrb,gbt->gjhrt", asked_hot, seg_blocks.astype(bf16), preferred_element_type=f32
        ).astype(jnp.int32)
        key_seg = jnp.concatenate(
            [seg_fixed, seg_moved.reshape(seq_count, per, HEADS, slots * BLOCK)], 3
        )[:, :, :, None, :]
        self.allowed = (
            query_seg.reshape(seq_count, per, 1, BLOCK, 1) == key_seg
        ) | (key_seg == -2)
        self.query = query.reshape(seq_count, per, BLOCK, HEADS, size)
        scores = self.scores()
        top = jnp.max(scores, -1, keepdims=True)
        powers = jnp.exp(scores - top)
        total = jnp.sum(powers, -1, keepdims=True)
        self.log_total = top + jnp.log(total)
        attended = jnp.einsum(
            "gjhqk,gjhke->gjqhe",
            (powers / total).astype(bf16),
            self.values,
            preferred_element_type=f32,
        )
        return attended.astype(bf16).reshape(row_count, model).T[None]

    def scores(self):
        raw = jnp.einsum("gjqhe,gjhke->gjhqk", self.query, self.keys, preferred_element_type=f32)
        return jnp.where(self.allowed, raw * self.query.shape[-1] ** -0.5, MASKED)

    def inner_weights(self, inner_weight, outer_weight):
        splits = self.splits
        groups, group = lax.axis_size("dp"), lax.axis_index("dp")
        rows = inner_weight.shape[0]
        units, model = outer_weight.shape[0] // groups, outer_weight.shape[1]
        inner = inner_weight.reshape(rows, splits, groups, units)
        outer = outer_weight.reshape(groups, units, model)
        inner = lax.dynamic_index_in_dim(inner, group, 2, keepdims=False).reshape(rows, model)
        outer = lax.dynamic_index_in_dim(outer, group, 0, keepdims=False)
        both = lax.all_gather(jnp.concatenate([inner, outer], 0), "seq")
        both = both.reshape(splits, 2, rows, model).transpose(1, 0, 2, 3)
        self.both = both.reshape(1, 2 * model, model)

    def inner_shapes(self, tall):
        return [((self.splits, tall, self.hidden.shape[1]), bf16)]

    def inner_grads(self, stacked):
        self.share = lax.psum_scatter(stacked, "seq", scatter_dimension=0, tiled=False)

    def output_grad(self, attended, grad_branch, sums):
        splits = self.splits
        full = matmul(attended[0], grad_branch)
        share = lax.psum_scatter(full, "seq", scatter_dimension=0, tiled=True)
        self.total = lax.psum(share.astype(bf16), "dp").astype(f32)
        lines = lax.psum(sums[:3], ("dp", "seq")).reshape(3, splits, -1)
        self.lines = lax.dynamic_index_in_dim(lines, self.position, 1, keepdims=False)

    def finish_grads(self, after):
        model = self.hidden.shape[1]
        groups = lax.axis_size("dp")
        rows = model // self.splits
        d_inner, d_outer, vectors = finish_inner(self.ids, exchange_all(self.share), rows)
        return d_inner, d_outer, self.total, self.lines.reshape(-1), vectors

    def backward(self, grads, grad_res):
        hidden = self.hidden
        grad = grads[0].T
        splits, position = self.splits, self.position
        seq_count, per, _, _, size = self.query.shape
        row_count, model = hidden.shape
        piece_len = per * BLOCK
        slots = self.random_blocks.shape[3]
        scale = size**-0.5
        probs = jnp.exp(self.scores() - self.log_total)
        grad_split = grad.reshape(seq_count, per, BLOCK, HEADS, size)
        grad_probs = jnp.einsum(
            "gjqhe,gjhke->gjhqk", grad_split, self.values, preferred_element_type=f32
        )
        weighted = jnp.sum(probs * grad_probs, -1, keepdims=True)
        grad_scores = (probs * (grad_probs - weighted)).astype(bf16)
        grad_query = (
            jnp.einsum("gjhqk,gjhke->gjqhe", grad_scores, self.keys, preferred_element_type=f32)
            * scale
        )
        grad_key = (
            jnp.einsum("gjhqk,gjqhe->gjhke", grad_scores, self.query, preferred_element_type=f32)
            * scale
        )
        grad_value = jnp.einsum(
            "gjhqk,gjqhe->gjhke", probs.astype(bf16), grad_split, preferred_element_type=f32
        )
        paired = jnp.stack([grad_key, grad_value], 0)
        fixed_len = 5 * BLOCK
        fixed = (
            paired[:, :, :, :, :fixed_len]
            .transpose(1, 2, 4, 0, 3, 5)
            .reshape(seq_count, per, fixed_len, 2 * model)
        )
        moved = (
            paired[:, :, :, :, fixed_len:]
            .transpose(1, 2, 3, 4, 0, 5)
            .reshape(seq_count * per * HEADS * slots, BLOCK * 2 * size)
        )
        ext = jnp.zeros((seq_count, piece_len + 2 * BLOCK, 2 * model), f32)
        for i in range(per):
            ext = ext.at[:, i * BLOCK : (i + 3) * BLOCK].add(fixed[:, i, : 3 * BLOCK])
        first = jnp.sum(fixed[:, :, 3 * BLOCK : 4 * BLOCK], 1)
        last = jnp.sum(fixed[:, :, 4 * BLOCK :], 1)
        rims = jnp.concatenate([ext[:, :BLOCK], ext[:, piece_len + BLOCK :]], 1)
        beside = with_halo(rims.astype(bf16), "seq", 1, BLOCK).astype(f32)
        kv_grad = ext[:, BLOCK : BLOCK + piece_len]
        kv_grad = kv_grad.at[:, :BLOCK].add(beside[:, :BLOCK])
        kv_grad = kv_grad.at[:, piece_len - BLOCK :].add(beside[:, 3 * BLOCK :])
        first, last = lax.psum((first, last), "seq")
        kv_grad = kv_grad.at[:, :BLOCK].add(jnp.where(position == 0, first, 0.0))
        kv_grad = kv_grad.at[:, piece_len - BLOCK :].add(
            jnp.where(position == splits - 1, last, 0.0)
        )
        cap = self.send.shape[0] // splits
        outgoing = left_product(self.arrival, moved.astype(bf16)).astype(bf16)
        returned = lax.all_to_all(
            outgoing.reshape(splits, cap, -1), "seq", 0, 0, tiled=True
        ).reshape(splits * cap, -1)
        kv_grad = kv_grad + (
            left_product(self.send, returned)
            .reshape(seq_count, per, HEADS, BLOCK, 2, size)
            .transpose(0, 1, 3, 4, 2, 5)
            .reshape(seq_count, piece_len, 2 * model)
        )
        kv_grad = kv_grad.reshape(row_count, 2 * model).astype(bf16)
        grad_query = grad_query.reshape(row_count, model).astype(bf16)
        grads = (grad_query, kv_grad[:, :model], kv_grad[:, model:])
        input_grad = grad_res
        shares = []
        for part, weight in zip(grads, self.weights):
            input_grad = input_grad + right_product(part, weight)
            full = left_product(hidden, part)
            share = lax.psum_scatter(full, "seq", scatter_dimension=0, tiled=True)
            shares.append(lax.psum(share.astype(bf16), "dp").astype(f32))
        biases = jnp.stack([jnp.sum(grads[i].astype(f32), 0) for i in (0, 2)], 1)
        biases = lax.psum_scatter(biases, "seq", scatter_dimension=0, tiled=True)
        biases = lax.psum(biases.astype(bf16), "dp").astype(f32)
        self.last = input_grad
        return input_grad, shares[0], biases[:, 0], shares[1], shares[2], biases[:, 1], biases


def local(
    hidden_in,
    query_weight,
    query_bias,
    key_weight,
    value_weight,
    value_bias,
    output_weight,
    output_bias,
    first_gain,
    first_shift,
    inner_weight,
    inner_bias,
    outer_weight,
    outer_bias,
    second_gain,
    second_shift,
    segments,
    random_blocks,
    cotangent,
):
    seq_count, piece_len, model = hidden_in.shape
    splits = lax.axis_size("seq")
    groups = lax.axis_size("dp")
    row_count = seq_count * piece_len
    rows = model // splits
    units = outer_weight.shape[0] // groups
    hidden = hidden_in.reshape(row_count, model)
    by_heads = (
        seq_count == 1 and groups == 4 and 2 < splits and HEADS % max(1, splits // 2) == 0
    )
    vec_local = jnp.concatenate(
        [
            v.reshape(-1, rows)
            for v in (
                query_bias,
                value_bias,
                output_bias,
                first_gain,
                first_shift,
                outer_bias,
                second_gain,
                second_shift,
                inner_bias,
            )
        ]
    )
    attention = (HeadAttention if by_heads else TokenAttention)(
        hidden,
        (query_weight, key_weight, value_weight),
        (query_bias, value_bias),
        segments,
        random_blocks,
        output_weight,
        vec_local,
    )
    attention.inner_weights(inner_weight, outer_weight)
    attended = attention.forward()
    vec = attention.vec
    ids = attention.ids
    w_out = attention.output_weight
    full = (row_count, model)
    wide = (groups * row_count, splits * units)
    low, normed, inverse = run_kernel(
        project_kernel,
        "project",
        [(full, bf16), (full, f32), ((row_count, 128), f32)],
        (w_out, hidden, vec, attended),
        flops=2 * row_count * model * model,
    )
    lows = exchange_all(low)
    work = 2 * wide[0] * wide[1] * model
    both = attention.both
    parts = run_kernel(
        functools.partial(forward_kernel, parts=groups),
        "forward",
        [(full, f32)] + [(full, bf16)] * (groups - 1) + [(wide, f32), (wide, bf16)],
        (ids, vec, both, *lows),
        scratch=[
            pltpu.VMEM(both.shape, bf16),
            pltpu.VMEM((groups,) + full, bf16),
            pltpu.SemaphoreType.DMA((groups + 1,)),
        ],
        scalars=1,
        raw=range(2, 3 + groups),
        flops=2 * work,
        powers=wide[0] * wide[1],
        grant=10 << 20,
    )
    inner, act = parts[groups:]
    layer_out, grad_low, grad_mix, sums2 = run_kernel(
        middle_kernel,
        "middle",
        [(full, bf16), (full, bf16), (full, f32), ((8, model), f32)],
        (*exchange_parts(parts), normed, cotangent.reshape(row_count, model), vec),
    )
    grads = exchange_all(grad_low)
    parts = run_kernel(
        functools.partial(backward_kernel, parts=groups),
        "backward",
        [(full, f32)] + [(full, bf16)] * (groups - 1) + attention.inner_shapes(2 * rows + 8),
        (ids, both, inner, act, sums2, *lows, *grads),
        scalars=1,
        flops=4 * work,
        powers=wide[0] * wide[1],
        grant=VMEM_BYTES if by_heads else 4 * VMEM_BYTES,
    )
    recv = exchange_parts(parts[:groups])
    attention.inner_grads(*parts[groups:])
    grad_res, grad_branch, sums1, *grad_att = run_kernel(
        functools.partial(residual_kernel, parts=groups),
        "residual",
        [(full, f32), (full, bf16), ((8, model), f32)]
        + [(attended.shape[1:], bf16)] * attended.shape[0],
        (ids, grad_mix, normed, inverse, vec, w_out, *recv),
        scalars=1,
        flops=2 * row_count * model * model,
    )
    if by_heads:
        grad_att = line_parts(grad_att)
    input_grad, gq, bias_q, gk, gv, bias_v, after = attention.backward(grad_att, grad_res)
    attention.output_grad(attended, tied(grad_branch, attention.last), sums1)
    d_inner, d_outer, d_output, first_sums, vectors = attention.finish_grads(after)
    second_sums = vectors[groups]

    def cut(line, i):
        return line[i * rows : (i + 1) * rows]

    return (
        layer_out.reshape(seq_count, piece_len, model),
        input_grad.reshape(seq_count, piece_len, model),
        gq,
        bias_q,
        gk,
        gv,
        bias_v,
        d_output,
        cut(first_sums, 2),
        cut(first_sums, 0),
        cut(first_sums, 1),
        d_inner,
        vectors[:groups, 3 * rows : 3 * rows + units].reshape(-1),
        d_outer,
        cut(second_sums, 2),
        cut(second_sums, 0),
        cut(second_sums, 1),
    )


def solution(mesh):
    in_specs = (
        P("dp", "seq", None),
        P("seq", None),
        P("seq"),
        P("seq", None),
        P("seq", None),
        P("seq"),
        P("seq", None),
        P("seq"),
        P("seq"),
        P("seq"),
        P("seq", None),
        P("seq"),
        P("seq", None),
        P("seq"),
        P("seq"),
        P("seq"),
        P("dp", None),
        P("dp", None, None, None),
        P("dp", "seq", None),
    )
    out_specs = (
        P("dp", "seq", None),
        P("dp", "seq", None),
        P("seq", None),
        P("seq"),
        P("seq", None),
        P("seq", None),
        P("seq"),
        P("seq", None),
        P("seq"),
        P("seq"),
        P("seq"),
        P("seq", None),
        P("seq"),
        P("seq", None),
        P("seq"),
        P("seq"),
        P("seq"),
    )
    return jax.shard_map(local, mesh=mesh, in_specs=in_specs, out_specs=out_specs, check_vma=False)
```

```python
import functools

import jax
import jax.numpy as jnp
from jax import lax
from jax.experimental import pallas as pl
from jax.experimental.pallas import tpu as pltpu
from jax.sharding import PartitionSpec as P

HEADS = 12
BLOCK = 64
EPSILON = 1e-12
MASKED = -1000000000.0
GELU_A = 0.7978845608028654
GELU_B = 0.044715
VMEM_BYTES = 6 << 20
bf16 = jnp.bfloat16
f32 = jnp.float32


def matmul(left, right):
    return jnp.dot(left, right, preferred_element_type=f32)


def left_product(left, right):
    return lax.dot_general(left, right, (((0,), (0,)), ((), ())), preferred_element_type=f32)


def right_product(left, right):
    return lax.dot_general(left, right, (((1,), (1,)), ((), ())), preferred_element_type=f32)


def run_kernel(
    kernel, name, outs, args, scratch=(), scalars=0, raw=(), raw_outs=(), flops=0, powers=0, grant=VMEM_BYTES
):
    def spec(i, held):
        return pl.BlockSpec(memory_space=pltpu.MemorySpace.HBM if i in held else pltpu.VMEM)

    specs = [pl.BlockSpec(memory_space=pltpu.SMEM)] * scalars
    specs += [spec(i, raw) for i in range(scalars, len(args))]
    shapes = [jax.ShapeDtypeStruct(shape, dtype) for shape, dtype in outs]
    moved = sum(a.size * a.dtype.itemsize for a in (*args, *shapes))
    out_shape = tuple(pltpu.HBM(o.shape, o.dtype) if i in raw_outs else o for i, o in enumerate(shapes))
    args = [
        pltpu.with_memory_space_constraint(a, pltpu.HBM) if i in raw else a
        for i, a in enumerate(args)
    ]
    return pl.pallas_call(
        kernel,
        name=name,
        out_shape=out_shape,
        in_specs=specs,
        out_specs=tuple(spec(i, raw_outs) for i in range(len(outs))),
        scratch_shapes=list(scratch),
        compiler_params=pltpu.CompilerParams(vmem_limit_bytes=grant),
        cost_estimate=pl.CostEstimate(flops=flops, bytes_accessed=moved, transcendentals=powers),
    )(*args)


def normalize(values):
    center = values - jnp.mean(values, -1, keepdims=True)
    spread = jnp.mean(center * center, -1, keepdims=True)
    inverse = lax.rsqrt(spread + EPSILON)
    return center * inverse, inverse


def norm_back(grad, normed, inverse, gain):
    scaled = grad * gain
    return inverse * (
        scaled
        - jnp.mean(scaled, -1, keepdims=True)
        - normed * jnp.mean(scaled * normed, -1, keepdims=True)
    )


def bias_rows(be_ref, bn, same, head, block, blocks, block_len):
    width = same.shape[1]
    rows = [
        jnp.broadcast_to(be_ref[head * blocks + block + i : head * blocks + block + i + 1, :], (block_len, width))
        for i in range(same.shape[0] // block_len)
    ]
    return jnp.where(same, jnp.concatenate(rows, 0), bn)


def bias_rows(lines, bn, same):
    count, width = lines.shape
    length = same.shape[0] // count
    rows = [jnp.broadcast_to(lines[i : i + 1, :], (length, width)) for i in range(count)]
    return jnp.where(same, jnp.concatenate(rows, 0), bn)


def place(ids, mine, other, out):
    for k in range(out.shape[0] // 2):
        chip = ids[1] ^ k
        out[2 * chip + ids[0]] = mine[k]
        out[2 * chip + 1 - ids[0]] = other[k]


def concat_kernel(*refs):
    out = refs[-1]
    at = 0
    for r in refs[:-1]:
        rows = r.shape[0]
        out[at : at + rows] = r[...]
        at += rows


def stack_kernel(*refs):
    for k, r in enumerate(refs[:-1]):
        refs[-1][k] = r[...]


def cut_kernel(ids, wq, wk, wv, *refs):
    outs = refs[:-3]
    raw, scratch, sems = refs[-3:]
    _, half, _ = raw.shape
    start = pl.multiple_of(lax.rem(ids[2], 2) * half, half)
    copies = [
        pltpu.make_async_copy(w.at[pl.ds(start, half), :], raw.at[i], sems.at[i])
        for i, w in enumerate((wq, wk, wv))
    ]
    for copy in copies:
        copy.start()
    for copy in copies:
        copy.wait()
    chips, _, wide = scratch.shape
    width = wide // 3
    for chip in range(chips):
        scratch[chip] = jnp.concatenate(
            [raw[i, :, chip * width : (chip + 1) * width] for i in range(3)], 1
        )
    for k, out in enumerate(outs):
        out[...] = scratch[ids[1] ^ k]


def assemble_kernel(ids, mine, other, out):
    core = ids[0]
    own = lax.rem(ids[2], 2)
    _, chips, _, _ = mine.shape
    for h in range(2):
        for k in range(chips):
            chip = ids[1] ^ k
            out[2 * chip + core, own ^ h] = mine[h, k]
            out[2 * chip + 1 - core, own ^ h] = other[h, k]


def cut_output_kernel(ids, wo, vec, out):
    half = wo.shape[0] // 2
    count, rows = vec.shape
    start = pl.multiple_of(lax.rem(ids[2] // 2, 2) * half, half)
    tall, model = out.shape
    out[:half, :] = wo[pl.ds(start, half), :]
    line = jnp.concatenate([vec[...], jnp.zeros((count, model - rows), bf16)], 1)
    out[half:, :] = jnp.concatenate([line, jnp.zeros((tall - half - count, model), bf16)], 0)


def cut_inner_kernel(ids, w1, w2, out, scratch):
    groups, rows, model = scratch.shape
    units = w2.shape[0] // groups
    pieces = model // units
    for g in range(groups):
        scratch[g] = jnp.concatenate(
            [
                w1[:, (s * groups + g) * units : (s * groups + g + 1) * units]
                for s in range(pieces)
            ],
            1,
        )
    out[:rows, :] = scratch[ids[2]]
    out[rows:, :] = w2[pl.ds(pl.multiple_of(ids[2] * units, units), units), :]


def assemble_output_kernel(ids, mine, other, out, vec, scratch):
    core = ids[0]
    pieces, _, half, _ = out.shape
    chips = pieces // 2
    own = lax.rem(ids[2] // 2, 2)
    for k in range(chips):
        chip = ids[1] ^ k
        scratch[2 * chip + core] = mine[0, k, half:, :]
        scratch[2 * chip + 1 - core] = other[0, k, half:, :]
        for h in range(2):
            out[2 * chip + core, own ^ h] = mine[h, k, :half, :]
            out[2 * chip + 1 - core, own ^ h] = other[h, k, :half, :]
    rows = 2 * half
    vec[...] = jnp.concatenate(
        [scratch[piece].astype(f32)[:, :rows] for piece in range(pieces)], 1
    )


def attend_kernel(ids, w, be, bn, sk, sq, hid, ours, theirs, *refs):
    att = refs[0]
    kept = refs[1:5]
    qo, ko, vo, lse, qs, s_all, p_all, sems = refs[5:]
    copies = [
        pltpu.make_async_copy(here, there, sems.at[i])
        for i, (here, there) in enumerate(zip((qo, ko, vo, lse), kept))
    ]
    pieces, piece_len, width = qs.shape
    chips = pieces // 2
    core = ids[0]
    size = 64
    heads = width // size
    model = hid.shape[2]
    ours, theirs = ours[...].astype(f32), theirs[...].astype(f32)
    first = jnp.where(core == 0, ours, theirs)
    second = jnp.where(core == 0, theirs, ours)
    biases = jnp.concatenate([first, second], 1)
    qb, vb = biases[0:1, :], biases[1:2, :]
    tokens = hid[...].reshape(pieces * piece_len, model)
    product = matmul(tokens, w[...])
    query = (product[:, :width] + qb).astype(bf16) * bf16(size**-0.5)
    qs[...] = query.reshape(pieces, piece_len, width)
    ko[...] = product[:, width : 2 * width].astype(bf16)
    vo[...] = (product[:, 2 * width :] + vb).astype(bf16)
    lane = lax.broadcasted_iota(jnp.int32, (piece_len, 128), 1)
    for k in range(chips):
        qo[k] = qs[2 * (ids[1] ^ k) + core]
    for copy in copies[:3]:
        copy.start()
    logs = [jnp.zeros((piece_len, 128), f32)] * chips
    parts = [[] for _ in range(chips)]
    for head in range(heads):
        cols = slice(head * size, (head + 1) * size)
        queries = qo[:, :, cols].reshape(chips * piece_len, size)
        s_all[...] = right_product(queries, ko[:, cols])
        shares = []
        for k in range(chips):
            chip = ids[1] ^ k
            rows = slice(k * piece_len, (k + 1) * piece_len)
            same = sq[chip] == sk[...]
            scores = s_all[rows, :] + bias_rows(be[head * chips + chip], bn[...], same)
            top = jnp.max(scores, -1, keepdims=True)
            powers = jnp.exp(scores - top)
            total = jnp.sum(powers, -1, keepdims=True)
            p_all[rows, :] = powers.astype(bf16)
            shares.append(1.0 / total)
            logs[k] = jnp.where(lane == head, top + jnp.log(total), logs[k])
        out = matmul(p_all[...], vo[:, cols])
        for k in range(chips):
            parts[k].append(out[k * piece_len : (k + 1) * piece_len] * shares[k])
    for k in range(chips):
        att[ids[1] ^ k] = jnp.concatenate(parts[k], 1).T.astype(bf16)
        lse[k] = logs[k]
    copies[3].start()
    for copy in copies:
        copy.wait()


def attend_back_kernel(ids, hid_raw, q_raw, k_raw, v_raw, lse_raw, be, bn, sk, sq, *refs):
    chips, piece_len, width = q_raw.shape
    ga_raw = refs[:chips]
    dq, mine, other, dw_mine, dw_other = refs[chips : chips + 5]
    hid, q, k, v, lse, ga, s_all, g_all, ds_all, p_all, dkv, dws, sems = refs[chips + 5 :]
    copies = [
        pltpu.make_async_copy(there, here, sems.at[i])
        for i, (there, here) in enumerate(
            zip((q_raw, k_raw, v_raw, lse_raw, hid_raw), (q, k, v, lse, hid))
        )
    ]
    copies[4:4] = [
        pltpu.make_async_copy(there, ga.at[i], sems.at[5 + i]) for i, there in enumerate(ga_raw)
    ]
    for copy in copies:
        copy.start()
    pieces = 2 * chips
    core = ids[0]
    size = 64
    heads = width // size
    dks = []
    dvs = []
    dqs = [[None] * heads for _ in range(chips)]
    for copy in copies[:-1]:
        copy.wait()
    gas = jnp.concatenate([ga[i].astype(f32).T.astype(bf16) for i in range(chips)], 0)
    for head in range(heads):
        cols = slice(head * size, (head + 1) * size)
        key = k[:, cols]
        value = v[:, cols]
        queries = q[:, :, cols].reshape(chips * piece_len, size)
        grads = gas[:, cols]
        s_all[...] = right_product(queries, key)
        g_all[...] = right_product(grads, value)
        for i in range(chips):
            chip = ids[1] ^ i
            rows = slice(i * piece_len, (i + 1) * piece_len)
            same = sq[chip] == sk[...]
            scores = s_all[rows, :] + bias_rows(be[head * chips + chip], bn[...], same)
            probs = jnp.exp(scores - lse[i, :, head : head + 1])
            grad = g_all[rows, :]
            weighted = jnp.sum(probs * grad, -1, keepdims=True)
            ds_all[rows, :] = (probs * (grad - weighted)).astype(bf16)
            p_all[rows, :] = probs.astype(bf16)
        grad_q = (matmul(ds_all[...], key) * (size**-0.5)).astype(bf16)
        for i in range(chips):
            dqs[i][head] = grad_q[i * piece_len : (i + 1) * piece_len]
        dks.append(left_product(ds_all[...], queries).astype(bf16))
        dvs.append(left_product(p_all[...], grads).astype(bf16))
    for i in range(chips):
        dq[i] = jnp.concatenate(dqs[i], 1)
    joined = jnp.concatenate(dks + dvs, 1)
    dkv[...] = joined.reshape(pieces, piece_len, 2 * width)
    for i in range(chips):
        chip = ids[1] ^ i
        mine[i] = dkv[2 * chip + core]
        other[i] = dkv[2 * chip + 1 - core]
    copies[-1].wait()
    _, _, model = hid.shape
    tokens = hid[...].reshape(pieces * piece_len, model)
    owned = jnp.concatenate([hid[2 * (ids[1] ^ i) + core] for i in range(chips)], 0)
    grad_q = dq[...].reshape(chips * piece_len, width)
    weights = jnp.concatenate([left_product(owned, grad_q), left_product(tokens, joined)], 1)
    groups = dw_mine.shape[0]
    rows = dws.shape[2]
    dws[...] = weights.reshape(dws.shape)
    for i in range(chips):
        chip = ids[1] ^ i
        for j in range(groups):
            span = slice(i * rows, (i + 1) * rows)
            dw_mine[j, span] = dws[2 * chip + core, ids[2] ^ j]
            dw_other[j, span] = dws[2 * chip + 1 - core, ids[2] ^ j].astype(bf16)
    total = jnp.concatenate(
        [
            jnp.sum(grad_q.astype(f32), 0, keepdims=True),
            jnp.sum(joined.astype(f32), 0, keepdims=True),
        ],
        1,
    )
    total = jnp.broadcast_to(total, (8, 3 * width))
    for j in range(groups):
        dw_mine[j, chips * rows :] = total
        dw_other[j, chips * rows :] = total.astype(bf16)


def input_grad_kernel(ids, dq, mine, recv, w, out, scratch):
    chips, piece_len, width = dq.shape
    dkv = (mine[...].astype(f32) + recv[...].astype(f32)).astype(bf16)
    grads = jnp.concatenate([dq[...], dkv], 2).reshape(chips * piece_len, 3 * width)
    total = right_product(grads, w[...])
    scratch[...] = total.astype(bf16).reshape(scratch.shape)
    for chip in range(chips):
        out[chip] = scratch[ids[1] ^ chip]


def add_kernel(left, right, out):
    out[...] = (left[...].astype(f32) + right[...].astype(f32)).astype(out.dtype)


def sum_rows_kernel(first, parts, out):
    total = first[...]
    for i in range(parts.shape[0]):
        total = total + parts[i].astype(f32)
    out[...] = total


def add_split_kernel(left, right, *outs):
    for k, out in enumerate(outs):
        out[...] = (left[k].astype(f32) + right[k].astype(f32)).astype(out.dtype)


def sum_split_kernel(*refs, parts, rows):
    total = refs[0][...].astype(f32)
    for r in refs[1:parts]:
        total = total + r[...].astype(f32)
    for k, out in enumerate(refs[parts:]):
        out[...] = total[k * rows : k * rows + out.shape[0]].astype(out.dtype)


def sum_lead_kernel(parts, *outs, rows):
    total = parts[0].astype(f32)
    for i in range(1, parts.shape[0]):
        total = total + parts[i].astype(f32)
    for k, out in enumerate(outs):
        out[...] = total[k * rows : k * rows + out.shape[0]].astype(out.dtype)


def project_kernel(wo, hid, vec, att, low, normed, inverse):
    branch = vec[2:3, :] + jnp.zeros(hid.shape, f32)
    for chip in range(att.shape[0]):
        branch = branch + left_product(att[chip], wo[chip])
    n1, r1 = normalize(hid[...].astype(f32) + branch)
    low[...] = (n1 * vec[3:4, :] + vec[4:5, :]).astype(bf16)
    normed[...] = n1
    inverse[...] = jnp.broadcast_to(r1, inverse.shape)


def gelu_parts(v):
    return jnp.tanh(GELU_A * (v + GELU_B * (v * v * v)))


def two_weights(both):
    pieces, rows, model = both.shape
    half = rows // 2
    first = both[:, :half, :].reshape(pieces * half, model)
    return first, both[:, half:, :].reshape(pieces * half, model)


def forward_kernel(ids, vec, both_raw, *refs, parts):
    raw = refs[:parts]
    outs = refs[parts : 2 * parts]
    inner_ref, act_ref, both, x, sems = refs[2 * parts :]
    copies = [pltpu.make_async_copy(r, x.at[i], sems.at[i]) for i, r in enumerate(raw)]
    copies.append(pltpu.make_async_copy(both_raw, both, sems.at[parts]))
    for copy in copies:
        copy.start()
    for copy in copies:
        copy.wait()
    _, rows, model = x.shape
    weight1, weight2 = two_weights(both)
    inner = matmul(x[...].reshape(parts * rows, model), weight1) + vec[pl.ds(8 + ids[2], 1), :]
    act = (0.5 * inner * (1.0 + gelu_parts(inner))).astype(bf16)
    inner_ref[...] = inner
    act_ref[...] = act
    mixed = matmul(act, weight2)
    for i in range(parts):
        outs[i][...] = mixed[i * rows : (i + 1) * rows].astype(outs[i].dtype)


def middle_kernel(*refs):
    recv = refs[:-7]
    normed, cot, vec, out, low, mix, sums = refs[-7:]
    first = normed[...] * vec[3:4, :] + vec[4:5, :]
    mixed = vec[5:6, :]
    for r in recv:
        mixed = mixed + r[...].astype(f32)
    n2, r2 = normalize(first + mixed)
    gain = vec[6:7, :]
    out[...] = (n2 * gain + vec[7:8, :]).astype(bf16)
    g = cot[...].astype(f32)
    grad = norm_back(g, n2, r2, gain)
    rounded = grad.astype(bf16)
    mix[...] = grad
    low[...] = rounded
    sums[0:1, :] = jnp.sum(g * n2, 0, keepdims=True)
    sums[1:2, :] = jnp.sum(g, 0, keepdims=True)
    sums[2:3, :] = jnp.sum(rounded.astype(f32), 0, keepdims=True)
    sums[3:, :] = jnp.zeros((5, sums.shape[1]), f32)


def backward_kernel(ids, both, inner_ref, act, sums, *refs, parts):
    x = refs[:parts]
    grads = refs[parts : 2 * parts]
    outs = refs[2 * parts : 3 * parts]
    out = refs[3 * parts]
    rows = grads[0].shape[0]
    pieces, tall, model = out.shape
    units = (tall - 8) // 2
    weight1, weight2 = two_weights(both)
    gm = jnp.concatenate([r[...] for r in grads], 0)
    grad_act = right_product(gm, weight2)
    v = inner_ref[...]
    t = gelu_parts(v)
    slope = 0.5 * (1.0 + t) + 0.5 * v * (1.0 - t * t) * (GELU_A * (1.0 + 3.0 * GELU_B * (v * v)))
    gi = (grad_act * slope).astype(bf16)
    first = right_product(gi, weight1)
    for i in range(parts):
        outs[i][...] = first[i * rows : (i + 1) * rows].astype(outs[i].dtype)
    tokens = jnp.concatenate([r[...] for r in x], 0)
    out[:, :units, :] = left_product(tokens, gi).astype(bf16).reshape(pieces, units, model)
    out[:, units : 2 * units, :] = (
        left_product(act[...], gm).astype(bf16).reshape(pieces, units, model)
    )
    total = jnp.sum(gi.astype(f32), 0, keepdims=True)
    vectors = [sums[i : i + 1, :] for i in range(3)] + [total]
    for piece in range(pieces):
        put_vectors(out, piece, piece, 2 * units, vectors, units)


def residual_kernel(ids, mix, normed, inverse, vec, wo, *refs, parts):
    recv = refs[:parts]
    low, sums, res_raw = refs[parts : parts + 3]
    back_raw = refs[parts + 3 : -3]
    res, back, sems = refs[-3:]
    first = mix[...]
    for r in recv:
        first = first + r[...].astype(f32)
    n1 = normed[...]
    grad = norm_back(first, n1, inverse[:, 0:1], vec[3:4, :])
    rounded = grad.astype(bf16)
    copies = []
    for k, out in enumerate(back_raw):
        back[k] = right_product(wo[ids[1] ^ k], rounded).astype(bf16)
        copies.append(pltpu.make_async_copy(back.at[k], out, sems.at[k]))
        copies[-1].start()
    res[...] = grad
    copies.append(pltpu.make_async_copy(res, res_raw, sems.at[len(back_raw)]))
    copies[-1].start()
    low[...] = rounded
    sums[0:1, :] = jnp.sum(first * n1, 0, keepdims=True)
    sums[1:2, :] = jnp.sum(first, 0, keepdims=True)
    sums[2:3, :] = jnp.sum(rounded.astype(f32), 0, keepdims=True)
    sums[3:, :] = jnp.zeros((5, sums.shape[1]), f32)
    for copy in copies:
        copy.wait()


def put_vectors(out, piece, at, row, vectors, rows):
    parts = [v[:, piece * rows : (piece + 1) * rows] for v in vectors]
    fill = out.shape[2] - rows * len(parts)
    line = jnp.concatenate(parts + [jnp.zeros((1, fill), f32)], 1)
    out[at, row : row + 8, :] = jnp.broadcast_to(line, (8, out.shape[2])).astype(bf16)


def output_grad_kernel(gb, sums, att, above, stacked, out, sems):
    tall = above.shape[1]
    first = pltpu.make_async_copy(above, stacked.at[:, pl.ds(0, tall), :], sems.at[0])
    first.start()
    rows = out.shape[1] - 8
    grad = gb[...]
    vectors = [sums[i : i + 1, :] for i in range(3)]
    for chip in range(att.shape[0]):
        part = matmul(att[chip], grad).astype(bf16)
        for i in range(2):
            piece = 2 * chip + i
            out[piece, :rows] = part[i * rows : (i + 1) * rows]
            put_vectors(out, piece, piece, rows, vectors, rows)
    second = pltpu.make_async_copy(out, stacked.at[:, pl.ds(tall, rows + 8), :], sems.at[1])
    second.start()
    first.wait()
    second.wait()


def ordered(ids, refs, scratch):
    for k, r in enumerate(refs):
        scratch[ids[2] ^ k] = r[...]


def finish_inner_kernel(ids, *refs, parts):
    inner, outer, output, vectors, scratch = refs[parts:]
    ordered(ids, refs[:parts], scratch)
    rows = inner.shape[0]
    units = outer.shape[0] // parts
    pieces = scratch.shape[2] // units
    for piece in range(pieces):
        inner[:, piece * parts * units : (piece + 1) * parts * units] = jnp.concatenate(
            [
                scratch[g, :rows, piece * units : (piece + 1) * units].astype(f32)
                for g in range(parts)
            ],
            1,
        )
    total = jnp.zeros((1, scratch.shape[2]), f32)
    at = rows + units
    for g in range(parts):
        outer[g * units : (g + 1) * units, :] = scratch[g, rows:at, :].astype(f32)
        line = scratch[g, at : at + 8, :].astype(f32)[0:1]
        vectors[g : g + 1, :] = line
        total = total + line
    vectors[parts : parts + 1, :] = total
    if scratch.shape[1] > at + 8:
        last = scratch[0, at + 8 :, :].astype(f32)
        for g in range(1, parts):
            last = last + scratch[g, at + 8 :, :].astype(f32)
        output[...] = last[:rows]
        vectors[parts + 1 : parts + 2, :] = last[rows : rows + 1]


def finish_kernel(ids, *refs):
    parts = len(refs) - 4
    gq, gk, gv, scratch = refs[parts:]
    quarters, chips, rows, wide = scratch.shape
    for j, r in enumerate(refs[:parts]):
        for k in range(chips):
            scratch[ids[2] ^ j, ids[1] ^ k] = r[k]
    width = wide // 3
    for part in range(quarters):
        block = [scratch[part, chip].astype(f32) for chip in range(chips)]
        for i, out in enumerate((gq, gk, gv)):
            out[part * rows : (part + 1) * rows, :] = jnp.concatenate(
                [b[:, i * width : (i + 1) * width] for b in block], 1
            )


def log_counts(count):
    return jnp.where(count > 0, jnp.log(jnp.maximum(count, 1).astype(f32)), MASKED)


def exchange(array, k):
    count = lax.axis_size("dp")
    return lax.ppermute(array, "dp", [(i, i ^ k) for i in range(count)])


def exchange_all(array):
    return [array] + [exchange(array, k) for k in range(1, lax.axis_size("dp"))]


def exchange_parts(parts):
    return [parts[0]] + [exchange(parts[k], k) for k in range(1, lax.axis_size("dp"))]


def swap_cores(array):
    count = lax.axis_size("seq")
    return lax.ppermute(array, "seq", [(i, i ^ 1) for i in range(count)])


def line_exchange(array, k):
    count = lax.axis_size("seq")
    return lax.ppermute(array, "seq", [(i, i ^ (2 * k)) for i in range(count)])


def line_parts(parts):
    return [parts[0]] + [line_exchange(parts[k], k) for k in range(1, len(parts))]


def tied(value, *others):
    return lax.optimization_barrier((value,) + others)[0]


def add_split(left, right, outs):
    return run_kernel(add_split_kernel, "add", outs, (left, right))


def sum_split(arrays, outs):
    return run_kernel(
        functools.partial(sum_split_kernel, parts=len(arrays), rows=outs[0][0][0]),
        "sum",
        outs,
        tuple(arrays),
    )


def line_all(array):
    return [array] + [line_exchange(array, k) for k in range(1, lax.axis_size("seq") // 2)]


def along_line(array):
    count = lax.axis_size("seq")
    lines = [[2 * i + c for i in range(count // 2)] for c in range(2)]
    return lax.all_to_all(array, "seq", 0, 0, tiled=True, axis_index_groups=lines)


def stack(*arrays):
    shape = (len(arrays),) + arrays[0].shape
    return run_kernel(stack_kernel, "stack", [(shape, bf16)], arrays)[0]


def concat(*arrays):
    shape = (sum(a.shape[0] for a in arrays),) + arrays[0].shape[1:]
    return run_kernel(concat_kernel, "concat", [(shape, bf16)], arrays)[0]


def device_ids():
    position = lax.axis_index("seq")
    return jnp.stack([position % 2, position // 2, lax.axis_index("dp")]).astype(jnp.int32)


def finish_inner(ids, shares, rows):
    groups = len(shares)
    share = shares[0]
    model = share.shape[1]
    return run_kernel(
        functools.partial(finish_inner_kernel, parts=groups),
        "finish_inner",
        [
            ((rows, groups * model), f32),
            ((groups * rows, model), f32),
            ((rows, model), f32),
            ((8, model), f32),
        ],
        (ids, *shares),
        scratch=[pltpu.VMEM((groups,) + share.shape, bf16)],
        scalars=1,
    )


class HeadAttention:
    def __init__(self, hidden, weights, biases, segments, random_blocks, output_weight, vec_local):
        self.splits = splits = lax.axis_size("seq")
        self.chips = chips = splits // 2
        self.position = position = lax.axis_index("seq")
        core = position % 2
        chip = position // 2
        group = lax.axis_index("dp")
        self.ids = device_ids()
        self.packed = lax.all_gather(hidden, "seq")
        piece_len, model = hidden.shape
        rows = model // splits
        width = model // chips
        heads = HEADS // chips
        half = rows // 2
        cut = run_kernel(
            cut_kernel,
            "cut",
            [((half, 3 * width), bf16)] * chips,
            (self.ids, *weights),
            scratch=[
                pltpu.VMEM((3, half, model), bf16),
                pltpu.VMEM((chips, half, 3 * width), bf16),
                pltpu.SemaphoreType.DMA((3,)),
            ],
            scalars=1,
            raw=range(1, 4),
        )
        cut = stack(*line_parts(cut))
        cut_next = exchange(cut, 1)
        (out_half,) = run_kernel(
            cut_output_kernel,
            "cut_output",
            [((half + 16, model), bf16)],
            (self.ids, output_weight, vec_local),
            scalars=1,
        )
        cut = stack(cut, cut_next)
        (weight,) = run_kernel(
            assemble_kernel,
            "assemble",
            [((splits, 2, half, 3 * width), bf16)],
            (self.ids, cut, swap_cores(cut)),
            scalars=1,
        )
        self.out_half = stack(*line_all(tied(out_half, cut_next)))
        self.out_next = exchange(self.out_half, 2)
        self.weight = weight.reshape(model, 3 * width)
        self.biases = biases
        self.hidden = hidden
        block_count = segments.shape[1] // BLOCK
        per_piece = piece_len // BLOCK
        own = random_blocks[0].reshape(chips, 2, per_piece, HEADS, -1)
        own = lax.dynamic_index_in_dim(own, core, 1, keepdims=False)
        own = lax.dynamic_slice_in_dim(own, chip * heads, heads, 2)
        own = own.reshape(chips * per_piece, heads, -1).transpose(1, 0, 2)
        block = jnp.arange(block_count, dtype=jnp.int32)
        mine = (
            (jnp.arange(chips, dtype=jnp.int32)[:, None] * 2 + core) * per_piece
            + jnp.arange(per_piece, dtype=jnp.int32)[None, :]
        ).reshape(-1)
        ends = ((block == 0) | (block == block_count - 1)).astype(jnp.int32)
        near = (jnp.abs(block[None, :] - mine[:, None]) <= 1).astype(jnp.int32)
        listed = jnp.sum((own[..., None] == block).astype(jnp.int32), 2)
        count = listed + near[None] + ends
        self.same_bias = jnp.repeat(log_counts(count), BLOCK, axis=2).reshape(
            heads * chips, per_piece, -1
        )
        self.other_bias = jnp.repeat(
            jnp.where(ends > 0, 0.0, MASKED).astype(f32)[None], BLOCK, axis=1
        )
        self.key_seg = segments
        self.query_seg = lax.dynamic_index_in_dim(
            segments.reshape(chips, 2, piece_len), core, 1, keepdims=False
        ).reshape(chips, piece_len, 1)
        self.piece_len, self.width, self.model = piece_len, width, model

    def masks(self):
        return (self.same_bias, self.other_bias, self.key_seg, self.query_seg)

    def inner_weights(self, inner_weight, outer_weight):
        groups = lax.axis_size("dp")
        rows = inner_weight.shape[0]
        units = outer_weight.shape[0] // groups
        (both,) = run_kernel(
            cut_inner_kernel,
            "cut_inner",
            [((rows + units, self.model), bf16)],
            (self.ids, inner_weight, outer_weight),
            scratch=[pltpu.VMEM((groups, rows, self.model), bf16)],
            scalars=1,
        )
        self.pair = jnp.stack(self.biases, 0)
        self.pair_other = swap_cores(self.pair)
        self.both = lax.all_gather(tied(both, self.packed, self.weight, self.out_half), "seq")

    def forward(self):
        chips, piece_len, width, model = self.chips, self.piece_len, self.width, self.model
        tokens = self.splits * piece_len
        one = (chips, piece_len, width)
        kept = [
            (one, bf16),
            ((tokens, width), bf16),
            ((tokens, width), bf16),
            ((chips, piece_len, 128), f32),
        ]
        att, self.q, self.k, self.v, self.lse = run_kernel(
            attend_kernel,
            "attend",
            [((chips, width, piece_len), bf16)] + kept,
            (self.ids, self.weight, *self.masks(), self.packed, self.pair, self.pair_other),
            scratch=[pltpu.VMEM(*spec) for spec in kept]
            + [
                pltpu.VMEM((self.splits, piece_len, width), bf16),
                pltpu.VMEM((chips * piece_len, tokens), f32),
                pltpu.VMEM((chips * piece_len, tokens), bf16),
                pltpu.SemaphoreType.DMA((len(kept),)),
            ],
            scalars=1,
            raw_outs=range(1, 1 + len(kept)),
            flops=6 * tokens * model * width + 2 * tokens * tokens * width,
            powers=tokens * tokens * 3 // 2,
            grant=16 << 20,
        )
        out_half = stack(tied(self.out_half, att), self.out_next)
        half = model // self.splits // 2
        weight, self.vec = run_kernel(
            assemble_output_kernel,
            "assemble_output",
            [((self.splits, 2, half, model), bf16), ((16, model), f32)],
            (self.ids, out_half, swap_cores(out_half)),
            scratch=[pltpu.VMEM((self.splits, 16, model), bf16)],
            scalars=1,
        )
        self.output_weight = weight.reshape(chips, width, model)
        att = along_line(att)
        return att

    def inner_grads(self, stacked):
        self.stacked = stacked

    def output_grad(self, attended, grad_branch, sums):
        chips, model = self.chips, self.model
        rows = model // self.splits + 8
        below = self.stacked.shape[1]
        (stacked,) = run_kernel(
            output_grad_kernel,
            "output_grad",
            [((self.splits, below + rows, model), bf16)],
            (grad_branch, sums, attended, self.stacked),
            scratch=[
                pltpu.VMEM((self.splits, rows, model), bf16),
                pltpu.SemaphoreType.DMA((2,)),
            ],
            raw_outs=(0,),
            flops=2 * self.piece_len * model * model,
        )
        self.share = lax.psum_scatter(stacked, "seq", scatter_dimension=0, tiled=False)

    def finish_grads(self, after):
        rows = self.model // self.splits
        d_inner, d_outer, d_output, vectors = finish_inner(self.ids, self.shares, rows)
        return d_inner, d_outer, d_output, vectors[len(self.shares) + 1], vectors

    def backward(self, grads, grad_res):
        chips, piece_len, width = self.chips, self.piece_len, self.width
        splits, model = self.splits, self.model
        groups = lax.axis_size("dp")
        tokens = splits * piece_len
        rows = model // splits
        one = (chips, piece_len, width)
        two = (chips, piece_len, 2 * width)
        quarter = (rows // groups, 3 * width)
        group = (chips * quarter[0] + 8, 3 * width)
        wide = ((groups,) + group, bf16)
        keep = (self.packed, self.q, self.k, self.v, self.lse)
        dq, mine, other, dw_mine, dw_other = run_kernel(
            attend_back_kernel,
            "attend_back",
            [(one, bf16), (two, bf16), (two, bf16), (wide[0], f32), wide],
            (self.ids,) + keep + self.masks() + tuple(grads),
            scratch=[pltpu.VMEM(a.shape, a.dtype) for a in keep]
            + [
                pltpu.VMEM((chips,) + grads[0].shape, bf16),
                pltpu.VMEM((chips * piece_len, tokens), f32),
                pltpu.VMEM((chips * piece_len, tokens), f32),
                pltpu.VMEM((chips * piece_len, tokens), bf16),
                pltpu.VMEM((chips * piece_len, tokens), bf16),
                pltpu.VMEM((splits, piece_len, 2 * width), bf16),
                pltpu.VMEM((splits, groups) + quarter, f32),
                pltpu.SemaphoreType.DMA((len(keep) + chips,)),
            ],
            scalars=1,
            raw=(*range(1, 6), *range(10, 10 + chips)),
            flops=5 * tokens * tokens * width + 6 * tokens * model * width,
            powers=tokens * tokens * 3 // 2,
            grant=24 << 20,
        )
        recv = swap_cores(other)
        dws = add_split(dw_mine, swap_cores(dw_other), [(group, bf16)] * groups)
        dq = tied(dq, dws[0])
        dws = exchange_parts(dws)
        full = (piece_len, model)
        (partial,) = run_kernel(
            input_grad_kernel,
            "input_grad",
            [((chips,) + full, bf16)],
            (self.ids, dq, mine, recv, self.weight),
            scratch=[pltpu.VMEM((chips,) + full, bf16)],
            scalars=1,
            flops=3 * tokens * model * width,
        )
        *dws, sums = sum_split(dws, [(quarter, bf16)] * chips + [((8, 3 * width), f32)])
        dws = line_parts(dws)
        part = (chips,) + quarter
        dw = stack(*dws)
        every = exchange_all(dw)
        self.shares = exchange_all(tied(self.share, *every[1:]))
        count = splits
        lines = [[2 * i + c for i in range(count // 2)] for c in range(2)]
        partial = lax.psum_scatter(
            partial, "seq", scatter_dimension=0, axis_index_groups=lines, tiled=False
        )[None]
        gq, gk, gv = run_kernel(
            finish_kernel,
            "finish",
            [((rows, model), f32)] * 3,
            (self.ids, *every),
            scratch=[pltpu.VMEM((groups,) + part, bf16)],
            scalars=1,
        )
        (input_grad,) = run_kernel(
            sum_rows_kernel, "sum_rows", [(full, f32)], (grad_res, partial)
        )
        core = self.position % 2
        bias_q = lax.dynamic_slice_in_dim(sums[0], core * rows, rows)
        bias_v = lax.dynamic_slice_in_dim(sums[0], 2 * width + core * rows, rows)
        return input_grad, gq, bias_q, gk, gv, bias_v, dws[0]


def one_hot(index, count):
    return (index[..., None] == jnp.arange(count, dtype=jnp.int32)).astype(bf16)


def with_halo(block, axis, dim, width):
    count = lax.axis_size(axis)
    forward = [(i, i + 1) for i in range(count - 1)]
    backward = [(target, source) for source, target in forward]
    low = lax.ppermute(
        lax.slice_in_dim(block, block.shape[dim] - width, None, axis=dim), axis, forward
    )
    high = lax.ppermute(lax.slice_in_dim(block, 0, width, axis=dim), axis, backward)
    return jnp.concatenate([low, block, high], axis=dim)


def broadcast(block, axis, owner):
    block = jnp.where(lax.axis_index(axis) == owner, block, jnp.zeros_like(block))
    return lax.psum(block, axis)


class TokenAttention:
    def __init__(self, hidden, weights, biases, segments, random_blocks, output_weight, vec_local):
        self.splits = splits = lax.axis_size("seq")
        self.position = position = lax.axis_index("seq")
        self.ids = device_ids() * jnp.array([1, 0, 1], jnp.int32)
        self.hidden = hidden
        self.segments = segments
        self.random_blocks = random_blocks
        self.weights = [lax.all_gather(w, "seq", axis=0, tiled=True) for w in weights]
        self.output_weight = lax.all_gather(output_weight, "seq", axis=0, tiled=True)[None]
        vec = lax.all_gather(vec_local, "seq")
        self.vec = vec.transpose(1, 0, 2).reshape(vec_local.shape[0], -1).astype(f32)

    def forward(self):
        hidden, segments = self.hidden, self.segments
        splits, position = self.splits, self.position
        seq_count = segments.shape[0]
        row_count, model = hidden.shape
        piece_len = row_count // seq_count
        size = model // HEADS
        per = piece_len // BLOCK
        slots = self.random_blocks.shape[3]
        reqs = seq_count * per * HEADS * slots
        cap = max(2, 3 * reqs // (2 * splits) + 1)
        vec = self.vec
        wq, wk, wv = self.weights
        query = (matmul(hidden, wq) + vec[0:1]).astype(bf16)
        keys = matmul(hidden, wk).astype(bf16)
        values = (matmul(hidden, wv) + vec[1:2]).astype(bf16)
        joined = jnp.concatenate([keys, values], 1).reshape(seq_count, piece_len, 2 * model)
        extended = with_halo(joined, "seq", 1, BLOCK)
        first = broadcast(joined[:, :BLOCK], "seq", 0)
        last = broadcast(joined[:, piece_len - BLOCK :], "seq", splits - 1)
        tiles = seq_count * per * HEADS
        tile_size = BLOCK * 2 * size
        kv_tiles = (
            joined.reshape(seq_count, per, BLOCK, 2, HEADS, size)
            .transpose(0, 1, 4, 2, 3, 5)
            .reshape(tiles, tile_size)
        )
        req = jnp.arange(reqs, dtype=jnp.int32)
        req_seq = req // (per * HEADS * slots)
        req_head = req // slots % HEADS
        earlier = (req[:, None] > req[None, :]).astype(jnp.int32)
        everyone = (
            self.random_blocks.reshape(seq_count, splits, per, HEADS, slots)
            .transpose(1, 0, 2, 3, 4)
            .reshape(splits, reqs)
        )
        is_mine = (everyone // per == position).astype(jnp.int32)
        place = jnp.sum(is_mine[:, None, :] * earlier, 2)
        slot = jnp.where(is_mine == 1, place, cap)
        tile_of = (req_seq * per + everyone % per) * HEADS + req_head
        chosen = slot[:, :, None] == jnp.arange(cap, dtype=jnp.int32)
        send = jnp.sum(jnp.where(chosen, tile_of[:, :, None], 0), 1).reshape(splits * cap)
        self.send = one_hot(send, tiles)
        outgoing = matmul(self.send, kv_tiles).astype(bf16).reshape(splits, cap, tile_size)
        incoming = lax.all_to_all(outgoing, "seq", 0, 0, tiled=True)
        asked = lax.dynamic_slice_in_dim(self.random_blocks, position * per, per, 1)
        owner = asked.reshape(reqs) // per
        before = jnp.sum((owner[:, None] == owner[None, :]).astype(jnp.int32) * earlier, 1)
        self.arrival = one_hot(owner * cap + before, splits * cap)
        fetched = matmul(self.arrival, incoming.reshape(splits * cap, tile_size)).astype(bf16)
        moved = fetched.reshape(seq_count, per, HEADS, slots * BLOCK, 2, size)
        spans = [slice(i * BLOCK, (i + 3) * BLOCK) for i in range(per)]
        fixed = jnp.stack(
            [jnp.concatenate([extended[:, span], first, last], 1) for span in spans], 1
        )
        fixed = fixed.reshape(seq_count, per, 5 * BLOCK, 2, HEADS, size)
        paired = jnp.concatenate(
            [fixed.transpose(3, 0, 1, 4, 2, 5), moved.transpose(4, 0, 1, 2, 3, 5)], 4
        )
        self.keys, self.values = paired[0], paired[1]
        edge = jnp.full((seq_count, BLOCK), -1, jnp.int32)
        padded = jnp.concatenate([edge, segments, edge], 1)
        query_seg = lax.dynamic_slice_in_dim(segments, position * piece_len, piece_len, 1)
        ext_seg = lax.dynamic_slice_in_dim(padded, position * piece_len, piece_len + 2 * BLOCK, 1)
        always = jnp.full((seq_count, 2 * BLOCK), -2, jnp.int32)
        seg_fixed = jnp.stack(
            [jnp.concatenate([ext_seg[:, span], always], 1) for span in spans], 1
        )
        seg_fixed = jnp.broadcast_to(
            seg_fixed[:, :, None], (seq_count, per, HEADS, 5 * BLOCK)
        )
        seg_blocks = segments.reshape(seq_count, -1, BLOCK)
        asked_hot = one_hot(asked, seg_blocks.shape[1])
        seg_moved = jnp.einsum(
            "gjhrb,gbt->gjhrt", asked_hot, seg_blocks.astype(bf16), preferred_element_type=f32
        ).astype(jnp.int32)
        key_seg = jnp.concatenate(
            [seg_fixed, seg_moved.reshape(seq_count, per, HEADS, slots * BLOCK)], 3
        )[:, :, :, None, :]
        self.allowed = (
            query_seg.reshape(seq_count, per, 1, BLOCK, 1) == key_seg
        ) | (key_seg == -2)
        self.query = query.reshape(seq_count, per, BLOCK, HEADS, size)
        scores = self.scores()
        top = jnp.max(scores, -1, keepdims=True)
        powers = jnp.exp(scores - top)
        total = jnp.sum(powers, -1, keepdims=True)
        self.log_total = top + jnp.log(total)
        attended = jnp.einsum(
            "gjhqk,gjhke->gjqhe",
            (powers / total).astype(bf16),
            self.values,
            preferred_element_type=f32,
        )
        return attended.astype(bf16).reshape(row_count, model).T[None]

    def scores(self):
        raw = jnp.einsum("gjqhe,gjhke->gjhqk", self.query, self.keys, preferred_element_type=f32)
        return jnp.where(self.allowed, raw * self.query.shape[-1] ** -0.5, MASKED)

    def inner_weights(self, inner_weight, outer_weight):
        splits = self.splits
        groups, group = lax.axis_size("dp"), lax.axis_index("dp")
        rows = inner_weight.shape[0]
        units, model = outer_weight.shape[0] // groups, outer_weight.shape[1]
        inner = inner_weight.reshape(rows, splits, groups, units)
        outer = outer_weight.reshape(groups, units, model)
        inner = lax.dynamic_index_in_dim(inner, group, 2, keepdims=False).reshape(rows, model)
        outer = lax.dynamic_index_in_dim(outer, group, 0, keepdims=False)
        both = lax.all_gather(jnp.concatenate([inner, outer], 0), "seq")
        both = both.reshape(splits, 2, rows, model).transpose(1, 0, 2, 3)
        self.both = both.reshape(1, 2 * model, model)

    def inner_grads(self, stacked):
        self.share = lax.psum_scatter(stacked, "seq", scatter_dimension=0, tiled=False)

    def output_grad(self, attended, grad_branch, sums):
        splits = self.splits
        full = matmul(attended[0], grad_branch)
        share = lax.psum_scatter(full, "seq", scatter_dimension=0, tiled=True)
        self.total = lax.psum(share.astype(bf16), "dp").astype(f32)
        lines = lax.psum(sums[:3], ("dp", "seq")).reshape(3, splits, -1)
        self.lines = lax.dynamic_index_in_dim(lines, self.position, 1, keepdims=False)

    def finish_grads(self, after):
        model = self.hidden.shape[1]
        groups = lax.axis_size("dp")
        rows = model // self.splits
        d_inner, d_outer, _, vectors = finish_inner(self.ids, exchange_all(self.share), rows)
        return d_inner, d_outer, self.total, self.lines.reshape(-1), vectors

    def backward(self, grads, grad_res):
        hidden = self.hidden
        grad = grads[0].T
        splits, position = self.splits, self.position
        seq_count, per, _, _, size = self.query.shape
        row_count, model = hidden.shape
        piece_len = per * BLOCK
        slots = self.random_blocks.shape[3]
        scale = size**-0.5
        probs = jnp.exp(self.scores() - self.log_total)
        grad_split = grad.reshape(seq_count, per, BLOCK, HEADS, size)
        grad_probs = jnp.einsum(
            "gjqhe,gjhke->gjhqk", grad_split, self.values, preferred_element_type=f32
        )
        weighted = jnp.sum(probs * grad_probs, -1, keepdims=True)
        grad_scores = (probs * (grad_probs - weighted)).astype(bf16)
        grad_query = (
            jnp.einsum("gjhqk,gjhke->gjqhe", grad_scores, self.keys, preferred_element_type=f32)
            * scale
        )
        grad_key = (
            jnp.einsum("gjhqk,gjqhe->gjhke", grad_scores, self.query, preferred_element_type=f32)
            * scale
        )
        grad_value = jnp.einsum(
            "gjhqk,gjqhe->gjhke", probs.astype(bf16), grad_split, preferred_element_type=f32
        )
        paired = jnp.stack([grad_key, grad_value], 0)
        fixed_len = 5 * BLOCK
        fixed = (
            paired[:, :, :, :, :fixed_len]
            .transpose(1, 2, 4, 0, 3, 5)
            .reshape(seq_count, per, fixed_len, 2 * model)
        )
        moved = (
            paired[:, :, :, :, fixed_len:]
            .transpose(1, 2, 3, 4, 0, 5)
            .reshape(seq_count * per * HEADS * slots, BLOCK * 2 * size)
        )
        ext = jnp.zeros((seq_count, piece_len + 2 * BLOCK, 2 * model), f32)
        for i in range(per):
            ext = ext.at[:, i * BLOCK : (i + 3) * BLOCK].add(fixed[:, i, : 3 * BLOCK])
        first = jnp.sum(fixed[:, :, 3 * BLOCK : 4 * BLOCK], 1)
        last = jnp.sum(fixed[:, :, 4 * BLOCK :], 1)
        rims = jnp.concatenate([ext[:, :BLOCK], ext[:, piece_len + BLOCK :]], 1)
        beside = with_halo(rims.astype(bf16), "seq", 1, BLOCK).astype(f32)
        kv_grad = ext[:, BLOCK : BLOCK + piece_len]
        kv_grad = kv_grad.at[:, :BLOCK].add(beside[:, :BLOCK])
        kv_grad = kv_grad.at[:, piece_len - BLOCK :].add(beside[:, 3 * BLOCK :])
        first, last = lax.psum((first, last), "seq")
        kv_grad = kv_grad.at[:, :BLOCK].add(jnp.where(position == 0, first, 0.0))
        kv_grad = kv_grad.at[:, piece_len - BLOCK :].add(
            jnp.where(position == splits - 1, last, 0.0)
        )
        cap = self.send.shape[0] // splits
        outgoing = left_product(self.arrival, moved.astype(bf16)).astype(bf16)
        returned = lax.all_to_all(
            outgoing.reshape(splits, cap, -1), "seq", 0, 0, tiled=True
        ).reshape(splits * cap, -1)
        kv_grad = kv_grad + (
            left_product(self.send, returned)
            .reshape(seq_count, per, HEADS, BLOCK, 2, size)
            .transpose(0, 1, 3, 4, 2, 5)
            .reshape(seq_count, piece_len, 2 * model)
        )
        kv_grad = kv_grad.reshape(row_count, 2 * model).astype(bf16)
        grad_query = grad_query.reshape(row_count, model).astype(bf16)
        grads = (grad_query, kv_grad[:, :model], kv_grad[:, model:])
        input_grad = grad_res
        shares = []
        for part, weight in zip(grads, self.weights):
            input_grad = input_grad + right_product(part, weight)
            full = left_product(hidden, part)
            share = lax.psum_scatter(full, "seq", scatter_dimension=0, tiled=True)
            shares.append(lax.psum(share.astype(bf16), "dp").astype(f32))
        biases = jnp.stack([jnp.sum(grads[i].astype(f32), 0) for i in (0, 2)], 1)
        biases = lax.psum_scatter(biases, "seq", scatter_dimension=0, tiled=True)
        biases = lax.psum(biases.astype(bf16), "dp").astype(f32)
        return input_grad, shares[0], biases[:, 0], shares[1], shares[2], biases[:, 1], biases


def local(
    hidden_in,
    query_weight,
    query_bias,
    key_weight,
    value_weight,
    value_bias,
    output_weight,
    output_bias,
    first_gain,
    first_shift,
    inner_weight,
    inner_bias,
    outer_weight,
    outer_bias,
    second_gain,
    second_shift,
    segments,
    random_blocks,
    cotangent,
):
    seq_count, piece_len, model = hidden_in.shape
    splits = lax.axis_size("seq")
    groups = lax.axis_size("dp")
    row_count = seq_count * piece_len
    rows = model // splits
    units = outer_weight.shape[0] // groups
    hidden = hidden_in.reshape(row_count, model)
    by_heads = (
        seq_count == 1 and groups == 4 and 2 < splits and HEADS % max(1, splits // 2) == 0
    )
    vec_local = jnp.concatenate(
        [
            v.reshape(-1, rows)
            for v in (
                query_bias,
                value_bias,
                output_bias,
                first_gain,
                first_shift,
                outer_bias,
                second_gain,
                second_shift,
                inner_bias,
            )
        ]
    )
    attention = (HeadAttention if by_heads else TokenAttention)(
        hidden,
        (query_weight, key_weight, value_weight),
        (query_bias, value_bias),
        segments,
        random_blocks,
        output_weight,
        vec_local,
    )
    attention.inner_weights(inner_weight, outer_weight)
    attended = attention.forward()
    vec = attention.vec
    ids = attention.ids
    w_out = attention.output_weight
    full = (row_count, model)
    wide = (groups * row_count, splits * units)
    low, normed, inverse = run_kernel(
        project_kernel,
        "project",
        [(full, bf16), (full, f32), ((row_count, 128), f32)],
        (w_out, hidden, vec, attended),
        flops=2 * row_count * model * model,
    )
    lows = exchange_all(low)
    work = 2 * wide[0] * wide[1] * model
    both = attention.both
    parts = run_kernel(
        functools.partial(forward_kernel, parts=groups),
        "forward",
        [(full, f32)] + [(full, bf16)] * (groups - 1) + [(wide, f32), (wide, bf16)],
        (ids, vec, both, *lows),
        scratch=[
            pltpu.VMEM(both.shape, bf16),
            pltpu.VMEM((groups,) + full, bf16),
            pltpu.SemaphoreType.DMA((groups + 1,)),
        ],
        scalars=1,
        raw=range(2, 3 + groups),
        flops=2 * work,
        powers=wide[0] * wide[1],
        grant=10 << 20,
    )
    inner, act = parts[groups:]
    layer_out, grad_low, grad_mix, sums2 = run_kernel(
        middle_kernel,
        "middle",
        [(full, bf16), (full, bf16), (full, f32), ((8, model), f32)],
        (*exchange_parts(parts), normed, cotangent.reshape(row_count, model), vec),
    )
    grads = exchange_all(grad_low)
    stacked = ((splits, 2 * rows + 8, model), bf16)
    parts = run_kernel(
        functools.partial(backward_kernel, parts=groups),
        "backward",
        [(full, f32)] + [(full, bf16)] * (groups - 1) + [stacked],
        (ids, both, inner, act, sums2, *lows, *grads),
        scalars=1,
        flops=4 * work,
        powers=wide[0] * wide[1],
        grant=(2 if by_heads else 5) * VMEM_BYTES,
    )
    recv = exchange_parts(parts[:groups])
    attention.inner_grads(*parts[groups:])
    slots = attended.shape[0]
    grad_branch, sums1, grad_res, *grad_att = run_kernel(
        functools.partial(residual_kernel, parts=groups),
        "residual",
        [(full, bf16), ((8, model), f32), (full, f32)] + [(attended.shape[1:], bf16)] * slots,
        (ids, grad_mix, normed, inverse, vec, w_out, *recv),
        scratch=[
            pltpu.VMEM(full, f32),
            pltpu.VMEM(attended.shape, bf16),
            pltpu.SemaphoreType.DMA((slots + 1,)),
        ],
        scalars=1,
        raw_outs=range(2, 3 + slots),
        flops=2 * row_count * model * model,
    )
    if by_heads:
        grad_att = line_parts(grad_att)
    attention.output_grad(attended, grad_branch, sums1)
    input_grad, gq, bias_q, gk, gv, bias_v, after = attention.backward(grad_att, grad_res)
    d_inner, d_outer, d_output, first_sums, vectors = attention.finish_grads(after)
    second_sums = vectors[groups]

    def cut(line, i):
        return line[i * rows : (i + 1) * rows]

    return (
        layer_out.reshape(seq_count, piece_len, model),
        input_grad.reshape(seq_count, piece_len, model),
        gq,
        bias_q,
        gk,
        gv,
        bias_v,
        d_output,
        cut(first_sums, 2),
        cut(first_sums, 0),
        cut(first_sums, 1),
        d_inner,
        vectors[:groups, 3 * rows : 3 * rows + units].reshape(-1),
        d_outer,
        cut(second_sums, 2),
        cut(second_sums, 0),
        cut(second_sums, 1),
    )


def solution(mesh):
    in_specs = (
        P("dp", "seq", None),
        P("seq", None),
        P("seq"),
        P("seq", None),
        P("seq", None),
        P("seq"),
        P("seq", None),
        P("seq"),
        P("seq"),
        P("seq"),
        P("seq", None),
        P("seq"),
        P("seq", None),
        P("seq"),
        P("seq"),
        P("seq"),
        P("dp", None),
        P("dp", None, None, None),
        P("dp", "seq", None),
    )
    out_specs = (
        P("dp", "seq", None),
        P("dp", "seq", None),
        P("seq", None),
        P("seq"),
        P("seq", None),
        P("seq", None),
        P("seq"),
        P("seq", None),
        P("seq"),
        P("seq"),
        P("seq"),
        P("seq", None),
        P("seq"),
        P("seq", None),
        P("seq"),
        P("seq"),
        P("seq"),
    )
    return jax.shard_map(local, mesh=mesh, in_specs=in_specs, out_specs=out_specs, check_vma=False)
```

```python
import functools

import jax
import jax.numpy as jnp
from jax import lax
from jax.experimental import pallas as pl
from jax.experimental.pallas import tpu as pltpu
from jax.sharding import PartitionSpec as P

HEADS = 12
BLOCK = 64
EPSILON = 1e-12
MASKED = -1000000000.0
GELU_A = 0.7978845608028654
GELU_B = 0.044715
VMEM_BYTES = 6 << 20
bf16 = jnp.bfloat16
f32 = jnp.float32


def matmul(left, right):
    return jnp.dot(left, right, preferred_element_type=f32)


def left_product(left, right):
    return lax.dot_general(left, right, (((0,), (0,)), ((), ())), preferred_element_type=f32)


def right_product(left, right):
    return lax.dot_general(left, right, (((1,), (1,)), ((), ())), preferred_element_type=f32)


def run_kernel(
    kernel, name, outs, args, scratch=(), scalars=0, raw=(), raw_outs=(), flops=0, powers=0, grant=VMEM_BYTES
):
    def spec(i, held):
        return pl.BlockSpec(memory_space=pltpu.MemorySpace.HBM if i in held else pltpu.VMEM)

    specs = [pl.BlockSpec(memory_space=pltpu.SMEM)] * scalars
    specs += [spec(i, raw) for i in range(scalars, len(args))]
    shapes = [jax.ShapeDtypeStruct(shape, dtype) for shape, dtype in outs]
    moved = sum(a.size * a.dtype.itemsize for a in (*args, *shapes))
    out_shape = tuple(pltpu.HBM(o.shape, o.dtype) if i in raw_outs else o for i, o in enumerate(shapes))
    args = [
        pltpu.with_memory_space_constraint(a, pltpu.HBM) if i in raw else a
        for i, a in enumerate(args)
    ]
    return pl.pallas_call(
        kernel,
        name=name,
        out_shape=out_shape,
        in_specs=specs,
        out_specs=tuple(spec(i, raw_outs) for i in range(len(outs))),
        scratch_shapes=list(scratch),
        compiler_params=pltpu.CompilerParams(vmem_limit_bytes=grant),
        cost_estimate=pl.CostEstimate(flops=flops, bytes_accessed=moved, transcendentals=powers),
    )(*args)


def normalize(values):
    center = values - jnp.mean(values, -1, keepdims=True)
    spread = jnp.mean(center * center, -1, keepdims=True)
    inverse = lax.rsqrt(spread + EPSILON)
    return center * inverse, inverse


def norm_back(grad, normed, inverse, gain):
    scaled = grad * gain
    return inverse * (
        scaled
        - jnp.mean(scaled, -1, keepdims=True)
        - normed * jnp.mean(scaled * normed, -1, keepdims=True)
    )


def bias_rows(be_ref, bn, same, head, block, blocks, block_len):
    width = same.shape[1]
    rows = [
        jnp.broadcast_to(be_ref[head * blocks + block + i : head * blocks + block + i + 1, :], (block_len, width))
        for i in range(same.shape[0] // block_len)
    ]
    return jnp.where(same, jnp.concatenate(rows, 0), bn)


def bias_rows(lines, bn, same):
    count, width = lines.shape
    length = same.shape[0] // count
    rows = [jnp.broadcast_to(lines[i : i + 1, :], (length, width)) for i in range(count)]
    return jnp.where(same, jnp.concatenate(rows, 0), bn)


def place(ids, mine, other, out):
    for k in range(out.shape[0] // 2):
        chip = ids[1] ^ k
        out[2 * chip + ids[0]] = mine[k]
        out[2 * chip + 1 - ids[0]] = other[k]


def concat_kernel(*refs):
    out = refs[-1]
    at = 0
    for r in refs[:-1]:
        rows = r.shape[0]
        out[at : at + rows] = r[...]
        at += rows


def stack_kernel(*refs):
    for k, r in enumerate(refs[:-1]):
        refs[-1][k] = r[...]


def cut_kernel(ids, wq, wk, wv, *refs):
    outs = refs[:-3]
    raw, scratch, sems = refs[-3:]
    _, half, _ = raw.shape
    start = pl.multiple_of(lax.rem(ids[2], 2) * half, half)
    copies = [
        pltpu.make_async_copy(w.at[pl.ds(start, half), :], raw.at[i], sems.at[i])
        for i, w in enumerate((wq, wk, wv))
    ]
    for copy in copies:
        copy.start()
    for copy in copies:
        copy.wait()
    chips, _, wide = scratch.shape
    width = wide // 3
    for chip in range(chips):
        scratch[chip] = jnp.concatenate(
            [raw[i, :, chip * width : (chip + 1) * width] for i in range(3)], 1
        )
    for k, out in enumerate(outs):
        out[...] = scratch[ids[1] ^ k]


def assemble_kernel(ids, mine, other, out):
    core = ids[0]
    own = lax.rem(ids[2], 2)
    _, chips, _, _ = mine.shape
    for h in range(2):
        for k in range(chips):
            chip = ids[1] ^ k
            out[2 * chip + core, own ^ h] = mine[h, k]
            out[2 * chip + 1 - core, own ^ h] = other[h, k]


def cut_output_kernel(ids, wo, vec, out):
    half = wo.shape[0] // 2
    count, rows = vec.shape
    start = pl.multiple_of(lax.rem(ids[2] // 2, 2) * half, half)
    tall, model = out.shape
    each = model // rows
    out[:half, :] = wo[pl.ds(start, half), :]
    lines = []
    for first in range(0, count, each):
        parts = [vec[i : i + 1, :] for i in range(first, min(count, first + each))]
        parts += [jnp.zeros((1, rows), bf16)] * (each - len(parts))
        lines.append(jnp.concatenate(parts, 1))
    fill = jnp.zeros((tall - half - len(lines), model), bf16)
    out[half:, :] = jnp.concatenate(lines + [fill], 0)


def cut_inner_kernel(ids, w1, w2, out, scratch):
    groups, rows, model = scratch.shape
    units = w2.shape[0] // groups
    pieces = model // units
    for g in range(groups):
        scratch[g] = jnp.concatenate(
            [
                w1[:, (s * groups + g) * units : (s * groups + g + 1) * units]
                for s in range(pieces)
            ],
            1,
        )
    out[:rows, :] = scratch[ids[2]]
    out[rows:, :] = w2[pl.ds(pl.multiple_of(ids[2] * units, units), units), :]


def assemble_output_kernel(ids, mine, other, out, vec, scratch):
    core = ids[0]
    pieces, _, half, _ = out.shape
    chips = pieces // 2
    own = lax.rem(ids[2] // 2, 2)
    for k in range(chips):
        chip = ids[1] ^ k
        scratch[2 * chip + core] = mine[0, k, half:, :]
        scratch[2 * chip + 1 - core] = other[0, k, half:, :]
        for h in range(2):
            out[2 * chip + core, own ^ h] = mine[h, k, :half, :]
            out[2 * chip + 1 - core, own ^ h] = other[h, k, :half, :]
    rows = 2 * half
    each = vec.shape[1] // rows
    lines = [scratch[piece].astype(f32) for piece in range(pieces)]
    for i in range(vec.shape[0]):
        at, first = i // each, i % each * rows
        vec[i : i + 1, :] = jnp.concatenate(
            [line[at : at + 1, first : first + rows] for line in lines], 1
        )


def attend_kernel(ids, w, be, bn, sk, sq, ours, theirs, hid_raw, *refs):
    att = refs[0]
    kept = refs[1:5]
    hid, qo, ko, vo, lse, qs, s_all, p_all, sems = refs[5:]
    count = 2
    step = hid_raw.shape[0] // count
    loads = [
        pltpu.make_async_copy(
            hid_raw.at[pl.ds(i * step, step)], hid.at[pl.ds(i * step, step)], sems.at[4 + i]
        )
        for i in range(count)
    ]
    for load in loads:
        load.start()
    copies = [
        pltpu.make_async_copy(here, there, sems.at[i])
        for i, (here, there) in enumerate(zip((qo, ko, vo, lse), kept))
    ]
    pieces, piece_len, width = qs.shape
    chips = pieces // 2
    core = ids[0]
    size = 64
    heads = width // size
    model = hid.shape[2]
    ours, theirs = ours[...].astype(f32), theirs[...].astype(f32)
    first = jnp.where(core == 0, ours, theirs)
    second = jnp.where(core == 0, theirs, ours)
    biases = jnp.concatenate([first, second], 1)
    qb, vb = biases[0:1, :], biases[1:2, :]
    for i, load in enumerate(loads):
        load.wait()
        some = slice(i * step, (i + 1) * step)
        span = slice(i * step * piece_len, (i + 1) * step * piece_len)
        product = matmul(hid[some].reshape(step * piece_len, model), w[...])
        query = (product[:, :width] + qb).astype(bf16) * bf16(size**-0.5)
        qs[some] = query.reshape(step, piece_len, width)
        ko[span] = product[:, width : 2 * width].astype(bf16)
        vo[span] = (product[:, 2 * width :] + vb).astype(bf16)
    lane = lax.broadcasted_iota(jnp.int32, (piece_len, 128), 1)
    for k in range(chips):
        qo[k] = qs[2 * (ids[1] ^ k) + core]
    for copy in copies[:3]:
        copy.start()
    logs = [jnp.zeros((piece_len, 128), f32)] * chips
    parts = [[] for _ in range(chips)]
    for head in range(heads):
        cols = slice(head * size, (head + 1) * size)
        queries = qo[:, :, cols].reshape(chips * piece_len, size)
        s_all[...] = right_product(queries, ko[:, cols])
        shares = []
        for k in range(chips):
            chip = ids[1] ^ k
            rows = slice(k * piece_len, (k + 1) * piece_len)
            same = sq[chip] == sk[...]
            scores = s_all[rows, :] + bias_rows(be[head * chips + chip], bn[...], same)
            top = jnp.max(scores, -1, keepdims=True)
            powers = jnp.exp(scores - top)
            total = jnp.sum(powers, -1, keepdims=True)
            p_all[rows, :] = powers.astype(bf16)
            shares.append(1.0 / total)
            logs[k] = jnp.where(lane == head, top + jnp.log(total), logs[k])
        out = matmul(p_all[...], vo[:, cols])
        for k in range(chips):
            parts[k].append(out[k * piece_len : (k + 1) * piece_len] * shares[k])
    for k in range(chips):
        att[ids[1] ^ k] = jnp.concatenate(parts[k], 1).T.astype(bf16)
        lse[k] = logs[k]
    copies[3].start()
    for copy in copies:
        copy.wait()


def attend_back_kernel(ids, hid_raw, q_raw, k_raw, v_raw, lse_raw, be, bn, sk, sq, *refs):
    chips, piece_len, width = q_raw.shape
    ga_raw = refs[:chips]
    dq, mine, other, dw_mine, dw_other = refs[chips : chips + 5]
    hid, q, k, v, lse, ga, s_all, g_all, ds_all, p_all, dkv, dws, sems = refs[chips + 5 :]
    copies = [
        pltpu.make_async_copy(there, here, sems.at[i])
        for i, (there, here) in enumerate(
            zip((q_raw, k_raw, v_raw, lse_raw, hid_raw), (q, k, v, lse, hid))
        )
    ]
    copies[4:4] = [
        pltpu.make_async_copy(there, ga.at[i], sems.at[5 + i]) for i, there in enumerate(ga_raw)
    ]
    for copy in copies:
        copy.start()
    pieces = 2 * chips
    core = ids[0]
    size = 64
    heads = width // size
    dks = []
    dvs = []
    dqs = [[None] * heads for _ in range(chips)]
    for copy in copies[:-1]:
        copy.wait()
    gas = jnp.concatenate([ga[i].astype(f32).T.astype(bf16) for i in range(chips)], 0)
    for head in range(heads):
        cols = slice(head * size, (head + 1) * size)
        key = k[:, cols]
        value = v[:, cols]
        queries = q[:, :, cols].reshape(chips * piece_len, size)
        grads = gas[:, cols]
        s_all[...] = right_product(queries, key)
        g_all[...] = right_product(grads, value)
        for i in range(chips):
            chip = ids[1] ^ i
            rows = slice(i * piece_len, (i + 1) * piece_len)
            same = sq[chip] == sk[...]
            scores = s_all[rows, :] + bias_rows(be[head * chips + chip], bn[...], same)
            probs = jnp.exp(scores - lse[i, :, head : head + 1])
            grad = g_all[rows, :]
            weighted = jnp.sum(probs * grad, -1, keepdims=True)
            ds_all[rows, :] = (probs * (grad - weighted)).astype(bf16)
            p_all[rows, :] = probs.astype(bf16)
        grad_q = (matmul(ds_all[...], key) * (size**-0.5)).astype(bf16)
        for i in range(chips):
            dqs[i][head] = grad_q[i * piece_len : (i + 1) * piece_len]
        dks.append(left_product(ds_all[...], queries).astype(bf16))
        dvs.append(left_product(p_all[...], grads).astype(bf16))
    for i in range(chips):
        dq[i] = jnp.concatenate(dqs[i], 1)
    joined = jnp.concatenate(dks + dvs, 1)
    dkv[...] = joined.reshape(pieces, piece_len, 2 * width)
    for i in range(chips):
        chip = ids[1] ^ i
        mine[i] = dkv[2 * chip + core]
        other[i] = dkv[2 * chip + 1 - core]
    copies[-1].wait()
    _, _, model = hid.shape
    tokens = hid[...].reshape(pieces * piece_len, model)
    owned = jnp.concatenate([hid[2 * (ids[1] ^ i) + core] for i in range(chips)], 0)
    grad_q = dq[...].reshape(chips * piece_len, width)
    weights = jnp.concatenate([left_product(owned, grad_q), left_product(tokens, joined)], 1)
    groups = dw_mine.shape[0]
    rows = dws.shape[2]
    dws[...] = weights.reshape(dws.shape)
    for i in range(chips):
        chip = ids[1] ^ i
        for j in range(groups):
            span = slice(i * rows, (i + 1) * rows)
            dw_mine[j, span] = dws[2 * chip + core, ids[2] ^ j]
            dw_other[j, span] = dws[2 * chip + 1 - core, ids[2] ^ j].astype(bf16)
    total = jnp.concatenate(
        [
            jnp.sum(grad_q.astype(f32), 0, keepdims=True),
            jnp.sum(joined.astype(f32), 0, keepdims=True),
        ],
        1,
    )
    total = jnp.broadcast_to(total, (8, 3 * width))
    for j in range(groups):
        dw_mine[j, chips * rows :] = total
        dw_other[j, chips * rows :] = total.astype(bf16)


def input_grad_kernel(ids, dq, mine, recv, w, out, scratch):
    chips, piece_len, width = dq.shape
    dkv = (mine[...].astype(f32) + recv[...].astype(f32)).astype(bf16)
    grads = jnp.concatenate([dq[...], dkv], 2).reshape(chips * piece_len, 3 * width)
    total = right_product(grads, w[...])
    scratch[...] = total.astype(bf16).reshape(scratch.shape)
    for chip in range(chips):
        out[chip] = scratch[ids[1] ^ chip]


def add_kernel(left, right, out):
    out[...] = (left[...].astype(f32) + right[...].astype(f32)).astype(out.dtype)


def sum_rows_kernel(first, parts, out):
    total = first[...]
    for i in range(parts.shape[0]):
        total = total + parts[i].astype(f32)
    out[...] = total


def add_split_kernel(left, right, *outs):
    for k, out in enumerate(outs):
        out[...] = (left[k].astype(f32) + right[k].astype(f32)).astype(out.dtype)


def sum_split_kernel(*refs, parts, rows):
    total = refs[0][...].astype(f32)
    for r in refs[1:parts]:
        total = total + r[...].astype(f32)
    for k, out in enumerate(refs[parts:]):
        out[...] = total[k * rows : k * rows + out.shape[0]].astype(out.dtype)


def sum_lead_kernel(parts, *outs, rows):
    total = parts[0].astype(f32)
    for i in range(1, parts.shape[0]):
        total = total + parts[i].astype(f32)
    for k, out in enumerate(outs):
        out[...] = total[k * rows : k * rows + out.shape[0]].astype(out.dtype)


def project_kernel(wo, hid, vec, att, low, normed, inverse):
    branch = vec[2:3, :] + jnp.zeros(hid.shape, f32)
    for chip in range(att.shape[0]):
        branch = branch + left_product(att[chip], wo[chip])
    n1, r1 = normalize(hid[...].astype(f32) + branch)
    low[...] = (n1 * vec[3:4, :] + vec[4:5, :]).astype(bf16)
    normed[...] = n1
    inverse[...] = jnp.broadcast_to(r1, inverse.shape)


def gelu_parts(v):
    return jnp.tanh(GELU_A * (v + GELU_B * (v * v * v)))


def two_weights(both):
    pieces, rows, model = both.shape
    half = rows // 2
    first = both[:, :half, :].reshape(pieces * half, model)
    return first, both[:, half:, :].reshape(pieces * half, model)


def forward_kernel(ids, vec, both_raw, *refs, parts):
    raw = refs[:parts]
    outs = refs[parts : 2 * parts]
    inner_ref, act_ref, both, x, sems = refs[2 * parts :]
    half = both.shape[1] // 2
    copies = [pltpu.make_async_copy(r, x.at[i], sems.at[i]) for i, r in enumerate(raw)]
    for i in range(2):
        span = (slice(None), pl.ds(i * half, half), slice(None))
        copies.append(pltpu.make_async_copy(both_raw.at[span], both.at[span], sems.at[parts + i]))
    for copy in copies:
        copy.start()
    for copy in copies[:-1]:
        copy.wait()
    _, rows, model = x.shape
    weight1 = both[:, :half, :].reshape(-1, model)
    inner = matmul(x[...].reshape(parts * rows, model), weight1) + vec[pl.ds(8 + ids[2], 1), :]
    act = (0.5 * inner * (1.0 + gelu_parts(inner))).astype(bf16)
    inner_ref[...] = inner
    act_ref[...] = act
    copies[-1].wait()
    mixed = matmul(act, both[:, half:, :].reshape(-1, model))
    for i in range(parts):
        outs[i][...] = mixed[i * rows : (i + 1) * rows].astype(outs[i].dtype)


def middle_kernel(*refs):
    recv = refs[:-7]
    normed, cot, vec, out, low, mix, sums = refs[-7:]
    first = normed[...] * vec[3:4, :] + vec[4:5, :]
    mixed = vec[5:6, :]
    for r in recv:
        mixed = mixed + r[...].astype(f32)
    n2, r2 = normalize(first + mixed)
    gain = vec[6:7, :]
    out[...] = (n2 * gain + vec[7:8, :]).astype(bf16)
    g = cot[...].astype(f32)
    grad = norm_back(g, n2, r2, gain)
    rounded = grad.astype(bf16)
    mix[...] = grad
    low[...] = rounded
    sums[0:1, :] = jnp.sum(g * n2, 0, keepdims=True)
    sums[1:2, :] = jnp.sum(g, 0, keepdims=True)
    sums[2:3, :] = jnp.sum(rounded.astype(f32), 0, keepdims=True)
    sums[3:, :] = jnp.zeros((5, sums.shape[1]), f32)


def backward_kernel(both, inner_ref, *refs, parts):
    grads = refs[:parts]
    outs = refs[parts : 2 * parts]
    gi_ref, total = refs[2 * parts :]
    rows = grads[0].shape[0]
    weight1, weight2 = two_weights(both)
    gm = jnp.concatenate([r[...] for r in grads], 0)
    grad_act = right_product(gm, weight2)
    v = inner_ref[...]
    t = gelu_parts(v)
    slope = 0.5 * (1.0 + t) + 0.5 * v * (1.0 - t * t) * (GELU_A * (1.0 + 3.0 * GELU_B * (v * v)))
    gi = (grad_act * slope).astype(bf16)
    gi_ref[...] = gi
    first = right_product(gi, weight1)
    for i in range(parts):
        outs[i][...] = first[i * rows : (i + 1) * rows].astype(outs[i].dtype)
    total[...] = jnp.sum(gi.astype(f32), 0, keepdims=True)


def inner_outer_kernel(gi, act, sums, total, *refs, parts):
    x = refs[:parts]
    grads = refs[parts : 2 * parts]
    out = refs[2 * parts]
    pieces, tall, model = out.shape
    units = (tall - 8) // 2
    gm = jnp.concatenate([r[...] for r in grads], 0)
    tokens = jnp.concatenate([r[...] for r in x], 0)
    out[:, :units, :] = left_product(tokens, gi[...]).astype(bf16).reshape(pieces, units, model)
    out[:, units : 2 * units, :] = (
        left_product(act[...], gm).astype(bf16).reshape(pieces, units, model)
    )
    vectors = [sums[i : i + 1, :] for i in range(3)] + [total[...]]
    for piece in range(pieces):
        put_vectors(out, piece, piece, 2 * units, vectors, units)


def residual_kernel(ids, mix, normed, inverse, vec, wo, att, above, *refs, parts):
    recv = refs[:parts]
    res_raw, stacked = refs[parts : parts + 2]
    back_raw = refs[parts + 2 : -4]
    res, back, out, sems = refs[-4:]
    copies = []

    def send(here, there):
        copies.append(pltpu.make_async_copy(here, there, sems.at[len(copies)]))
        copies[-1].start()

    tall = above.shape[1]
    send(above, stacked.at[:, pl.ds(0, tall), :])
    first = mix[...]
    for r in recv:
        first = first + r[...].astype(f32)
    n1 = normed[...]
    grad = norm_back(first, n1, inverse[:, 0:1], vec[3:4, :])
    rounded = grad.astype(bf16)
    for k, raw in enumerate(back_raw):
        back[k] = right_product(wo[ids[1] ^ k], rounded).astype(bf16)
        send(back.at[k], raw)
    res[...] = grad
    send(res, res_raw)
    vectors = [
        jnp.sum(first * n1, 0, keepdims=True),
        jnp.sum(first, 0, keepdims=True),
        jnp.sum(rounded.astype(f32), 0, keepdims=True),
    ]
    rows = out.shape[1] - 8
    each = out.shape[0] // att.shape[0]
    for chip in range(att.shape[0]):
        part = matmul(att[chip], rounded).astype(bf16)
        for i in range(each):
            piece = each * chip + i
            out[piece, :rows] = part[i * rows : (i + 1) * rows]
            put_vectors(out, piece, piece, rows, vectors, rows)
    send(out, stacked.at[:, pl.ds(tall, rows + 8), :])
    for copy in copies:
        copy.wait()


def put_vectors(out, piece, at, row, vectors, rows):
    parts = [v[:, piece * rows : (piece + 1) * rows] for v in vectors]
    fill = out.shape[2] - rows * len(parts)
    line = jnp.concatenate(parts + [jnp.zeros((1, fill), f32)], 1)
    out[at, row : row + 8, :] = jnp.broadcast_to(line, (8, out.shape[2])).astype(bf16)


def ordered(ids, refs, scratch):
    for k, r in enumerate(refs):
        scratch[ids[2] ^ k] = r[...]


def finish_inner_kernel(ids, *refs, parts):
    inner, outer, output, vectors, scratch = refs[parts:]
    ordered(ids, refs[:parts], scratch)
    rows = inner.shape[0]
    units = outer.shape[0] // parts
    pieces = scratch.shape[2] // units
    for piece in range(pieces):
        inner[:, piece * parts * units : (piece + 1) * parts * units] = jnp.concatenate(
            [
                scratch[g, :rows, piece * units : (piece + 1) * units].astype(f32)
                for g in range(parts)
            ],
            1,
        )
    total = jnp.zeros((1, scratch.shape[2]), f32)
    at = rows + units
    for g in range(parts):
        outer[g * units : (g + 1) * units, :] = scratch[g, rows:at, :].astype(f32)
        line = scratch[g, at : at + 8, :].astype(f32)[0:1]
        vectors[g : g + 1, :] = line
        total = total + line
    vectors[parts : parts + 1, :] = total
    if scratch.shape[1] > at + 8:
        last = scratch[0, at + 8 :, :].astype(f32)
        for g in range(1, parts):
            last = last + scratch[g, at + 8 :, :].astype(f32)
        output[...] = last[:rows]
        vectors[parts + 1 : parts + 2, :] = last[rows : rows + 1]


def finish_kernel(ids, *refs):
    parts = len(refs) - 4
    gq, gk, gv, scratch = refs[parts:]
    quarters, chips, rows, wide = scratch.shape
    for j, r in enumerate(refs[:parts]):
        for k in range(chips):
            scratch[ids[2] ^ j, ids[1] ^ k] = r[k]
    width = wide // 3
    for part in range(quarters):
        block = [scratch[part, chip].astype(f32) for chip in range(chips)]
        for i, out in enumerate((gq, gk, gv)):
            out[part * rows : (part + 1) * rows, :] = jnp.concatenate(
                [b[:, i * width : (i + 1) * width] for b in block], 1
            )


def log_counts(count):
    return jnp.where(count > 0, jnp.log(jnp.maximum(count, 1).astype(f32)), MASKED)


def exchange(array, k):
    count = lax.axis_size("dp")
    return lax.ppermute(array, "dp", [(i, i ^ k) for i in range(count)])


def exchange_all(array):
    return [array] + [exchange(array, k) for k in range(1, lax.axis_size("dp"))]


def exchange_parts(parts):
    return [parts[0]] + [exchange(parts[k], k) for k in range(1, lax.axis_size("dp"))]


def swap_cores(array):
    count = lax.axis_size("seq")
    return lax.ppermute(array, "seq", [(i, i ^ 1) for i in range(count)])


def line_exchange(array, k):
    count = lax.axis_size("seq")
    return lax.ppermute(array, "seq", [(i, i ^ (2 * k)) for i in range(count)])


def line_parts(parts):
    return [parts[0]] + [line_exchange(parts[k], k) for k in range(1, len(parts))]


def tied(value, *others):
    return lax.optimization_barrier((value,) + others)[0]


def add_split(left, right, outs):
    return run_kernel(add_split_kernel, "add", outs, (left, right))


def sum_split(arrays, outs):
    return run_kernel(
        functools.partial(sum_split_kernel, parts=len(arrays), rows=outs[0][0][0]),
        "sum",
        outs,
        tuple(arrays),
    )


def line_all(array):
    return [array] + [line_exchange(array, k) for k in range(1, lax.axis_size("seq") // 2)]


def along_line(array):
    count = lax.axis_size("seq")
    lines = [[2 * i + c for i in range(count // 2)] for c in range(2)]
    return lax.all_to_all(array, "seq", 0, 0, tiled=True, axis_index_groups=lines)


def stack(*arrays):
    shape = (len(arrays),) + arrays[0].shape
    return run_kernel(stack_kernel, "stack", [(shape, bf16)], arrays)[0]


def concat(*arrays):
    shape = (sum(a.shape[0] for a in arrays),) + arrays[0].shape[1:]
    return run_kernel(concat_kernel, "concat", [(shape, bf16)], arrays)[0]


def device_ids():
    position = lax.axis_index("seq")
    return jnp.stack([position % 2, position // 2, lax.axis_index("dp")]).astype(jnp.int32)


def finish_inner(ids, shares, rows):
    groups = len(shares)
    share = shares[0]
    model = share.shape[1]
    return run_kernel(
        functools.partial(finish_inner_kernel, parts=groups),
        "finish_inner",
        [
            ((rows, groups * model), f32),
            ((groups * rows, model), f32),
            ((rows, model), f32),
            ((8, model), f32),
        ],
        (ids, *shares),
        scratch=[pltpu.VMEM((groups,) + share.shape, bf16)],
        scalars=1,
    )


class HeadAttention:
    def __init__(self, hidden, weights, biases, segments, random_blocks, output_weight, vec_local):
        self.splits = splits = lax.axis_size("seq")
        self.chips = chips = splits // 2
        self.position = position = lax.axis_index("seq")
        core = position % 2
        chip = position // 2
        group = lax.axis_index("dp")
        self.ids = device_ids()
        self.packed = lax.all_gather(hidden, "seq")
        piece_len, model = hidden.shape
        rows = model // splits
        width = model // chips
        heads = HEADS // chips
        half = rows // 2
        cut = run_kernel(
            cut_kernel,
            "cut",
            [((half, 3 * width), bf16)] * chips,
            (self.ids, *weights),
            scratch=[
                pltpu.VMEM((3, half, model), bf16),
                pltpu.VMEM((chips, half, 3 * width), bf16),
                pltpu.SemaphoreType.DMA((3,)),
            ],
            scalars=1,
            raw=range(1, 4),
        )
        cut = stack(*line_parts(cut))
        cut_next = exchange(cut, 1)
        (out_half,) = run_kernel(
            cut_output_kernel,
            "cut_output",
            [((half + 8, model), bf16)],
            (self.ids, output_weight, vec_local),
            scalars=1,
        )
        cut = stack(cut, cut_next)
        (weight,) = run_kernel(
            assemble_kernel,
            "assemble",
            [((splits, 2, half, 3 * width), bf16)],
            (self.ids, cut, swap_cores(cut)),
            scalars=1,
        )
        self.out_half = stack(*line_all(tied(out_half, cut_next)))
        self.out_next = exchange(self.out_half, 2)
        self.weight = weight.reshape(model, 3 * width)
        self.biases = biases
        self.hidden = hidden
        block_count = segments.shape[1] // BLOCK
        per_piece = piece_len // BLOCK
        own = random_blocks[0].reshape(chips, 2, per_piece, HEADS, -1)
        own = lax.dynamic_index_in_dim(own, core, 1, keepdims=False)
        own = lax.dynamic_slice_in_dim(own, chip * heads, heads, 2)
        own = own.reshape(chips * per_piece, heads, -1).transpose(1, 0, 2)
        block = jnp.arange(block_count, dtype=jnp.int32)
        mine = (
            (jnp.arange(chips, dtype=jnp.int32)[:, None] * 2 + core) * per_piece
            + jnp.arange(per_piece, dtype=jnp.int32)[None, :]
        ).reshape(-1)
        ends = ((block == 0) | (block == block_count - 1)).astype(jnp.int32)
        near = (jnp.abs(block[None, :] - mine[:, None]) <= 1).astype(jnp.int32)
        listed = jnp.sum((own[..., None] == block).astype(jnp.int32), 2)
        count = listed + near[None] + ends
        self.same_bias = jnp.repeat(log_counts(count), BLOCK, axis=2).reshape(
            heads * chips, per_piece, -1
        )
        self.other_bias = jnp.repeat(
            jnp.where(ends > 0, 0.0, MASKED).astype(f32)[None], BLOCK, axis=1
        )
        self.key_seg = segments
        self.query_seg = lax.dynamic_index_in_dim(
            segments.reshape(chips, 2, piece_len), core, 1, keepdims=False
        ).reshape(chips, piece_len, 1)
        self.piece_len, self.width, self.model = piece_len, width, model

    def masks(self):
        return (self.same_bias, self.other_bias, self.key_seg, self.query_seg)

    def inner_weights(self, inner_weight, outer_weight):
        groups = lax.axis_size("dp")
        rows = inner_weight.shape[0]
        units = outer_weight.shape[0] // groups
        (both,) = run_kernel(
            cut_inner_kernel,
            "cut_inner",
            [((rows + units, self.model), bf16)],
            (self.ids, inner_weight, outer_weight),
            scratch=[pltpu.VMEM((groups, rows, self.model), bf16)],
            scalars=1,
        )
        self.pair = jnp.stack(self.biases, 0)
        self.pair_other = swap_cores(self.pair)
        self.both = lax.all_gather(tied(both, self.packed, self.weight, self.out_half), "seq")

    def forward(self):
        chips, piece_len, width, model = self.chips, self.piece_len, self.width, self.model
        tokens = self.splits * piece_len
        one = (chips, piece_len, width)
        kept = [
            (one, bf16),
            ((tokens, width), bf16),
            ((tokens, width), bf16),
            ((chips, piece_len, 128), f32),
        ]
        att, self.q, self.k, self.v, self.lse = run_kernel(
            attend_kernel,
            "attend",
            [((chips, width, piece_len), bf16)] + kept,
            (self.ids, self.weight, *self.masks(), self.pair, self.pair_other, self.packed),
            scratch=[pltpu.VMEM(self.packed.shape, bf16)]
            + [pltpu.VMEM(*spec) for spec in kept]
            + [
                pltpu.VMEM((self.splits, piece_len, width), bf16),
                pltpu.VMEM((chips * piece_len, tokens), f32),
                pltpu.VMEM((chips * piece_len, tokens), bf16),
                pltpu.SemaphoreType.DMA((len(kept) + 2,)),
            ],
            scalars=1,
            raw=(8,),
            raw_outs=range(1, 1 + len(kept)),
            flops=6 * tokens * model * width + 2 * tokens * tokens * width,
            powers=tokens * tokens * 3 // 2,
            grant=16 << 20,
        )
        out_half = stack(tied(self.out_half, att), self.out_next)
        half = model // self.splits // 2
        weight, self.vec = run_kernel(
            assemble_output_kernel,
            "assemble_output",
            [((self.splits, 2, half, model), bf16), ((16, model), f32)],
            (self.ids, out_half, swap_cores(out_half)),
            scratch=[pltpu.VMEM((self.splits, 8, model), bf16)],
            scalars=1,
        )
        self.output_weight = weight.reshape(chips, width, model)
        att = along_line(att)
        return att

    def backward(self, grads, grad_res, share):
        chips, piece_len, width = self.chips, self.piece_len, self.width
        splits, model = self.splits, self.model
        groups = lax.axis_size("dp")
        tokens = splits * piece_len
        rows = model // splits
        one = (chips, piece_len, width)
        two = (chips, piece_len, 2 * width)
        quarter = (rows // groups, 3 * width)
        group = (chips * quarter[0] + 8, 3 * width)
        wide = ((groups,) + group, bf16)
        keep = (self.packed, self.q, self.k, self.v, self.lse)
        dq, mine, other, dw_mine, dw_other = run_kernel(
            attend_back_kernel,
            "attend_back",
            [(one, bf16), (two, bf16), (two, bf16), (wide[0], f32), wide],
            (self.ids,) + keep + self.masks() + tuple(grads),
            scratch=[pltpu.VMEM(a.shape, a.dtype) for a in keep]
            + [
                pltpu.VMEM((chips,) + grads[0].shape, bf16),
                pltpu.VMEM((chips * piece_len, tokens), f32),
                pltpu.VMEM((chips * piece_len, tokens), f32),
                pltpu.VMEM((chips * piece_len, tokens), bf16),
                pltpu.VMEM((chips * piece_len, tokens), bf16),
                pltpu.VMEM((splits, piece_len, 2 * width), bf16),
                pltpu.VMEM((splits, groups) + quarter, f32),
                pltpu.SemaphoreType.DMA((len(keep) + chips,)),
            ],
            scalars=1,
            raw=(*range(1, 6), *range(10, 10 + chips)),
            flops=5 * tokens * tokens * width + 6 * tokens * model * width,
            powers=tokens * tokens * 3 // 2,
            grant=24 << 20,
        )
        recv = swap_cores(other)
        dws = add_split(dw_mine, swap_cores(dw_other), [(group, bf16)] * groups)
        dws = exchange_parts(dws)
        full = (piece_len, model)
        *dws, sums = sum_split(dws, [(quarter, bf16)] * chips + [((8, 3 * width), f32)])
        dq = tied(dq, dws[0])
        (partial,) = run_kernel(
            input_grad_kernel,
            "input_grad",
            [((chips,) + full, bf16)],
            (self.ids, dq, mine, recv, self.weight),
            scratch=[pltpu.VMEM((chips,) + full, bf16)],
            scalars=1,
            flops=3 * tokens * model * width,
        )
        dws = line_parts(dws)
        part = (chips,) + quarter
        dw = stack(*dws)
        every = exchange_all(dw)
        self.shares = exchange_all(tied(share, *every[1:]))
        count = splits
        lines = [[2 * i + c for i in range(count // 2)] for c in range(2)]
        partial = lax.psum_scatter(
            partial, "seq", scatter_dimension=0, axis_index_groups=lines, tiled=False
        )[None]
        gq, gk, gv = run_kernel(
            finish_kernel,
            "finish",
            [((rows, model), f32)] * 3,
            (self.ids, *every),
            scratch=[pltpu.VMEM((groups,) + part, bf16)],
            scalars=1,
        )
        (input_grad,) = run_kernel(
            sum_rows_kernel, "sum_rows", [(full, f32)], (grad_res, partial)
        )
        core = self.position % 2
        bias_q = lax.dynamic_slice_in_dim(sums[0], core * rows, rows)
        bias_v = lax.dynamic_slice_in_dim(sums[0], 2 * width + core * rows, rows)
        return input_grad, gq, bias_q, gk, gv, bias_v


def one_hot(index, count):
    return (index[..., None] == jnp.arange(count, dtype=jnp.int32)).astype(bf16)


def with_halo(block, axis, dim, width):
    count = lax.axis_size(axis)
    forward = [(i, i + 1) for i in range(count - 1)]
    backward = [(target, source) for source, target in forward]
    low = lax.ppermute(
        lax.slice_in_dim(block, block.shape[dim] - width, None, axis=dim), axis, forward
    )
    high = lax.ppermute(lax.slice_in_dim(block, 0, width, axis=dim), axis, backward)
    return jnp.concatenate([low, block, high], axis=dim)


def broadcast(block, axis, owner):
    block = jnp.where(lax.axis_index(axis) == owner, block, jnp.zeros_like(block))
    return lax.psum(block, axis)


class TokenAttention:
    def __init__(self, hidden, weights, biases, segments, random_blocks, output_weight, vec_local):
        self.splits = splits = lax.axis_size("seq")
        self.position = position = lax.axis_index("seq")
        self.ids = device_ids() * jnp.array([1, 0, 1], jnp.int32)
        self.hidden = hidden
        self.segments = segments
        self.random_blocks = random_blocks
        self.weights = [lax.all_gather(w, "seq", axis=0, tiled=True) for w in weights]
        self.output_weight = lax.all_gather(output_weight, "seq", axis=0, tiled=True)[None]
        vec = lax.all_gather(vec_local, "seq")
        self.vec = vec.transpose(1, 0, 2).reshape(vec_local.shape[0], -1).astype(f32)

    def forward(self):
        hidden, segments = self.hidden, self.segments
        splits, position = self.splits, self.position
        seq_count = segments.shape[0]
        row_count, model = hidden.shape
        piece_len = row_count // seq_count
        size = model // HEADS
        per = piece_len // BLOCK
        slots = self.random_blocks.shape[3]
        reqs = seq_count * per * HEADS * slots
        cap = max(2, 3 * reqs // (2 * splits) + 1)
        vec = self.vec
        wq, wk, wv = self.weights
        query = (matmul(hidden, wq) + vec[0:1]).astype(bf16)
        keys = matmul(hidden, wk).astype(bf16)
        values = (matmul(hidden, wv) + vec[1:2]).astype(bf16)
        joined = jnp.concatenate([keys, values], 1).reshape(seq_count, piece_len, 2 * model)
        extended = with_halo(joined, "seq", 1, BLOCK)
        first = broadcast(joined[:, :BLOCK], "seq", 0)
        last = broadcast(joined[:, piece_len - BLOCK :], "seq", splits - 1)
        tiles = seq_count * per * HEADS
        tile_size = BLOCK * 2 * size
        kv_tiles = (
            joined.reshape(seq_count, per, BLOCK, 2, HEADS, size)
            .transpose(0, 1, 4, 2, 3, 5)
            .reshape(tiles, tile_size)
        )
        req = jnp.arange(reqs, dtype=jnp.int32)
        req_seq = req // (per * HEADS * slots)
        req_head = req // slots % HEADS
        earlier = (req[:, None] > req[None, :]).astype(jnp.int32)
        everyone = (
            self.random_blocks.reshape(seq_count, splits, per, HEADS, slots)
            .transpose(1, 0, 2, 3, 4)
            .reshape(splits, reqs)
        )
        is_mine = (everyone // per == position).astype(jnp.int32)
        place = jnp.sum(is_mine[:, None, :] * earlier, 2)
        slot = jnp.where(is_mine == 1, place, cap)
        tile_of = (req_seq * per + everyone % per) * HEADS + req_head
        chosen = slot[:, :, None] == jnp.arange(cap, dtype=jnp.int32)
        send = jnp.sum(jnp.where(chosen, tile_of[:, :, None], 0), 1).reshape(splits * cap)
        self.send = one_hot(send, tiles)
        outgoing = matmul(self.send, kv_tiles).astype(bf16).reshape(splits, cap, tile_size)
        incoming = lax.all_to_all(outgoing, "seq", 0, 0, tiled=True)
        asked = lax.dynamic_slice_in_dim(self.random_blocks, position * per, per, 1)
        owner = asked.reshape(reqs) // per
        before = jnp.sum((owner[:, None] == owner[None, :]).astype(jnp.int32) * earlier, 1)
        self.arrival = one_hot(owner * cap + before, splits * cap)
        fetched = matmul(self.arrival, incoming.reshape(splits * cap, tile_size)).astype(bf16)
        moved = fetched.reshape(seq_count, per, HEADS, slots * BLOCK, 2, size)
        spans = [slice(i * BLOCK, (i + 3) * BLOCK) for i in range(per)]
        fixed = jnp.stack(
            [jnp.concatenate([extended[:, span], first, last], 1) for span in spans], 1
        )
        fixed = fixed.reshape(seq_count, per, 5 * BLOCK, 2, HEADS, size)
        paired = jnp.concatenate(
            [fixed.transpose(3, 0, 1, 4, 2, 5), moved.transpose(4, 0, 1, 2, 3, 5)], 4
        )
        self.keys, self.values = paired[0], paired[1]
        edge = jnp.full((seq_count, BLOCK), -1, jnp.int32)
        padded = jnp.concatenate([edge, segments, edge], 1)
        query_seg = lax.dynamic_slice_in_dim(segments, position * piece_len, piece_len, 1)
        ext_seg = lax.dynamic_slice_in_dim(padded, position * piece_len, piece_len + 2 * BLOCK, 1)
        always = jnp.full((seq_count, 2 * BLOCK), -2, jnp.int32)
        seg_fixed = jnp.stack(
            [jnp.concatenate([ext_seg[:, span], always], 1) for span in spans], 1
        )
        seg_fixed = jnp.broadcast_to(
            seg_fixed[:, :, None], (seq_count, per, HEADS, 5 * BLOCK)
        )
        seg_blocks = segments.reshape(seq_count, -1, BLOCK)
        asked_hot = one_hot(asked, seg_blocks.shape[1])
        seg_moved = jnp.einsum(
            "gjhrb,gbt->gjhrt", asked_hot, seg_blocks.astype(bf16), preferred_element_type=f32
        ).astype(jnp.int32)
        key_seg = jnp.concatenate(
            [seg_fixed, seg_moved.reshape(seq_count, per, HEADS, slots * BLOCK)], 3
        )[:, :, :, None, :]
        self.allowed = (
            query_seg.reshape(seq_count, per, 1, BLOCK, 1) == key_seg
        ) | (key_seg == -2)
        self.query = query.reshape(seq_count, per, BLOCK, HEADS, size)
        scores = self.scores()
        top = jnp.max(scores, -1, keepdims=True)
        powers = jnp.exp(scores - top)
        total = jnp.sum(powers, -1, keepdims=True)
        self.log_total = top + jnp.log(total)
        attended = jnp.einsum(
            "gjhqk,gjhke->gjqhe",
            (powers / total).astype(bf16),
            self.values,
            preferred_element_type=f32,
        )
        return attended.astype(bf16).reshape(row_count, model).T[None]

    def scores(self):
        raw = jnp.einsum("gjqhe,gjhke->gjhqk", self.query, self.keys, preferred_element_type=f32)
        return jnp.where(self.allowed, raw * self.query.shape[-1] ** -0.5, MASKED)

    def inner_weights(self, inner_weight, outer_weight):
        splits = self.splits
        groups, group = lax.axis_size("dp"), lax.axis_index("dp")
        rows = inner_weight.shape[0]
        units, model = outer_weight.shape[0] // groups, outer_weight.shape[1]
        inner = inner_weight.reshape(rows, splits, groups, units)
        outer = outer_weight.reshape(groups, units, model)
        inner = lax.dynamic_index_in_dim(inner, group, 2, keepdims=False).reshape(rows, model)
        outer = lax.dynamic_index_in_dim(outer, group, 0, keepdims=False)
        both = lax.all_gather(jnp.concatenate([inner, outer], 0), "seq")
        both = both.reshape(splits, 2, rows, model).transpose(1, 0, 2, 3)
        self.both = both.reshape(1, 2 * model, model)

    def backward(self, grads, grad_res, share):
        hidden = self.hidden
        grad = grads[0].T
        self.shares = exchange_all(share)
        splits, position = self.splits, self.position
        seq_count, per, _, _, size = self.query.shape
        row_count, model = hidden.shape
        piece_len = per * BLOCK
        slots = self.random_blocks.shape[3]
        scale = size**-0.5
        probs = jnp.exp(self.scores() - self.log_total)
        grad_split = grad.reshape(seq_count, per, BLOCK, HEADS, size)
        grad_probs = jnp.einsum(
            "gjqhe,gjhke->gjhqk", grad_split, self.values, preferred_element_type=f32
        )
        weighted = jnp.sum(probs * grad_probs, -1, keepdims=True)
        grad_scores = (probs * (grad_probs - weighted)).astype(bf16)
        grad_query = (
            jnp.einsum("gjhqk,gjhke->gjqhe", grad_scores, self.keys, preferred_element_type=f32)
            * scale
        )
        grad_key = (
            jnp.einsum("gjhqk,gjqhe->gjhke", grad_scores, self.query, preferred_element_type=f32)
            * scale
        )
        grad_value = jnp.einsum(
            "gjhqk,gjqhe->gjhke", probs.astype(bf16), grad_split, preferred_element_type=f32
        )
        paired = jnp.stack([grad_key, grad_value], 0)
        fixed_len = 5 * BLOCK
        fixed = (
            paired[:, :, :, :, :fixed_len]
            .transpose(1, 2, 4, 0, 3, 5)
            .reshape(seq_count, per, fixed_len, 2 * model)
        )
        moved = (
            paired[:, :, :, :, fixed_len:]
            .transpose(1, 2, 3, 4, 0, 5)
            .reshape(seq_count * per * HEADS * slots, BLOCK * 2 * size)
        )
        ext = jnp.zeros((seq_count, piece_len + 2 * BLOCK, 2 * model), f32)
        for i in range(per):
            ext = ext.at[:, i * BLOCK : (i + 3) * BLOCK].add(fixed[:, i, : 3 * BLOCK])
        first = jnp.sum(fixed[:, :, 3 * BLOCK : 4 * BLOCK], 1)
        last = jnp.sum(fixed[:, :, 4 * BLOCK :], 1)
        rims = jnp.concatenate([ext[:, :BLOCK], ext[:, piece_len + BLOCK :]], 1)
        beside = with_halo(rims.astype(bf16), "seq", 1, BLOCK).astype(f32)
        kv_grad = ext[:, BLOCK : BLOCK + piece_len]
        kv_grad = kv_grad.at[:, :BLOCK].add(beside[:, :BLOCK])
        kv_grad = kv_grad.at[:, piece_len - BLOCK :].add(beside[:, 3 * BLOCK :])
        first, last = lax.psum((first, last), "seq")
        kv_grad = kv_grad.at[:, :BLOCK].add(jnp.where(position == 0, first, 0.0))
        kv_grad = kv_grad.at[:, piece_len - BLOCK :].add(
            jnp.where(position == splits - 1, last, 0.0)
        )
        cap = self.send.shape[0] // splits
        outgoing = left_product(self.arrival, moved.astype(bf16)).astype(bf16)
        returned = lax.all_to_all(
            outgoing.reshape(splits, cap, -1), "seq", 0, 0, tiled=True
        ).reshape(splits * cap, -1)
        kv_grad = kv_grad + (
            left_product(self.send, returned)
            .reshape(seq_count, per, HEADS, BLOCK, 2, size)
            .transpose(0, 1, 3, 4, 2, 5)
            .reshape(seq_count, piece_len, 2 * model)
        )
        kv_grad = kv_grad.reshape(row_count, 2 * model).astype(bf16)
        grad_query = grad_query.reshape(row_count, model).astype(bf16)
        grads = (grad_query, kv_grad[:, :model], kv_grad[:, model:])
        input_grad = grad_res
        shares = []
        for part, weight in zip(grads, self.weights):
            input_grad = input_grad + right_product(part, weight)
            full = left_product(hidden, part)
            share = lax.psum_scatter(full, "seq", scatter_dimension=0, tiled=True)
            shares.append(lax.psum(share.astype(bf16), "dp").astype(f32))
        biases = jnp.stack([jnp.sum(grads[i].astype(f32), 0) for i in (0, 2)], 1)
        biases = lax.psum_scatter(biases, "seq", scatter_dimension=0, tiled=True)
        biases = lax.psum(biases.astype(bf16), "dp").astype(f32)
        return input_grad, shares[0], biases[:, 0], shares[1], shares[2], biases[:, 1]


def local(
    hidden_in,
    query_weight,
    query_bias,
    key_weight,
    value_weight,
    value_bias,
    output_weight,
    output_bias,
    first_gain,
    first_shift,
    inner_weight,
    inner_bias,
    outer_weight,
    outer_bias,
    second_gain,
    second_shift,
    segments,
    random_blocks,
    cotangent,
):
    seq_count, piece_len, model = hidden_in.shape
    splits = lax.axis_size("seq")
    groups = lax.axis_size("dp")
    row_count = seq_count * piece_len
    rows = model // splits
    units = outer_weight.shape[0] // groups
    hidden = hidden_in.reshape(row_count, model)
    by_heads = (
        seq_count == 1 and groups == 4 and 2 < splits and HEADS % max(1, splits // 2) == 0
    )
    vec_local = jnp.concatenate(
        [
            v.reshape(-1, rows)
            for v in (
                query_bias,
                value_bias,
                output_bias,
                first_gain,
                first_shift,
                outer_bias,
                second_gain,
                second_shift,
                inner_bias,
            )
        ]
    )
    attention = (HeadAttention if by_heads else TokenAttention)(
        hidden,
        (query_weight, key_weight, value_weight),
        (query_bias, value_bias),
        segments,
        random_blocks,
        output_weight,
        vec_local,
    )
    attention.inner_weights(inner_weight, outer_weight)
    attended = attention.forward()
    vec = attention.vec
    ids = attention.ids
    w_out = attention.output_weight
    full = (row_count, model)
    wide = (groups * row_count, splits * units)
    low, normed, inverse = run_kernel(
        project_kernel,
        "project",
        [(full, bf16), (full, f32), ((row_count, 128), f32)],
        (w_out, hidden, vec, attended),
        flops=2 * row_count * model * model,
    )
    lows = exchange_all(low)
    work = 2 * wide[0] * wide[1] * model
    both = attention.both
    parts = run_kernel(
        functools.partial(forward_kernel, parts=groups),
        "forward",
        [(full, f32)] + [(full, bf16)] * (groups - 1) + [(wide, f32), (wide, bf16)],
        (ids, vec, both, *lows),
        scratch=[
            pltpu.VMEM(both.shape, bf16),
            pltpu.VMEM((groups,) + full, bf16),
            pltpu.SemaphoreType.DMA((groups + 2,)),
        ],
        scalars=1,
        raw=range(2, 3 + groups),
        flops=2 * work,
        powers=wide[0] * wide[1],
        grant=10 << 20,
    )
    inner, act = parts[groups:]
    layer_out, grad_low, grad_mix, sums2 = run_kernel(
        middle_kernel,
        "middle",
        [(full, bf16), (full, bf16), (full, f32), ((8, model), f32)],
        (*exchange_parts(parts), normed, cotangent.reshape(row_count, model), vec),
    )
    grads = exchange_all(grad_low)
    parts = run_kernel(
        functools.partial(backward_kernel, parts=groups),
        "backward",
        [(full, f32)] + [(full, bf16)] * (groups - 1) + [(wide, bf16), ((1, wide[1]), f32)],
        (both, inner, *grads),
        flops=2 * work,
        powers=wide[0] * wide[1],
    )
    recv = exchange_parts(parts[:groups])
    (above,) = run_kernel(
        functools.partial(inner_outer_kernel, parts=groups),
        "inner_outer",
        [((splits, 2 * rows + 8, model), bf16)],
        (parts[groups], act, sums2, parts[groups + 1], *lows, *grads),
        flops=2 * work,
        grant=(1 if by_heads else 4) * VMEM_BYTES,
    )
    slots = attended.shape[0]
    below = rows + 8
    grad_res, stacked, *grad_att = run_kernel(
        functools.partial(residual_kernel, parts=groups),
        "residual",
        [(full, f32), ((splits, 3 * rows + 16, model), bf16)]
        + [(attended.shape[1:], bf16)] * slots,
        (ids, grad_mix, normed, inverse, vec, w_out, attended, above, *recv),
        scratch=[
            pltpu.VMEM(full, f32),
            pltpu.VMEM(attended.shape, bf16),
            pltpu.VMEM((splits, below, model), bf16),
            pltpu.SemaphoreType.DMA((slots + 3,)),
        ],
        scalars=1,
        raw_outs=range(2 + slots),
        flops=4 * row_count * model * model,
        grant=2 * VMEM_BYTES,
    )
    share = lax.psum_scatter(stacked, "seq", scatter_dimension=0, tiled=False)
    if by_heads:
        grad_att = line_parts(grad_att)
    input_grad, gq, bias_q, gk, gv, bias_v = attention.backward(grad_att, grad_res, share)
    d_inner, d_outer, d_output, vectors = finish_inner(ids, attention.shares, rows)
    first_sums = vectors[groups + 1]
    second_sums = vectors[groups]

    def cut(line, i):
        return line[i * rows : (i + 1) * rows]

    return (
        layer_out.reshape(seq_count, piece_len, model),
        input_grad.reshape(seq_count, piece_len, model),
        gq,
        bias_q,
        gk,
        gv,
        bias_v,
        d_output,
        cut(first_sums, 2),
        cut(first_sums, 0),
        cut(first_sums, 1),
        d_inner,
        vectors[:groups, 3 * rows : 3 * rows + units].reshape(-1),
        d_outer,
        cut(second_sums, 2),
        cut(second_sums, 0),
        cut(second_sums, 1),
    )


def solution(mesh):
    in_specs = (
        P("dp", "seq", None),
        P("seq", None),
        P("seq"),
        P("seq", None),
        P("seq", None),
        P("seq"),
        P("seq", None),
        P("seq"),
        P("seq"),
        P("seq"),
        P("seq", None),
        P("seq"),
        P("seq", None),
        P("seq"),
        P("seq"),
        P("seq"),
        P("dp", None),
        P("dp", None, None, None),
        P("dp", "seq", None),
    )
    out_specs = (
        P("dp", "seq", None),
        P("dp", "seq", None),
        P("seq", None),
        P("seq"),
        P("seq", None),
        P("seq", None),
        P("seq"),
        P("seq", None),
        P("seq"),
        P("seq"),
        P("seq"),
        P("seq", None),
        P("seq"),
        P("seq", None),
        P("seq"),
        P("seq"),
        P("seq"),
    )
    return jax.shard_map(local, mesh=mesh, in_specs=in_specs, out_specs=out_specs, check_vma=False)
```

```python
import functools

import jax
import jax.numpy as jnp
from jax import lax
from jax.experimental import pallas as pl
from jax.experimental.pallas import tpu as pltpu
from jax.sharding import PartitionSpec as P

HEADS = 12
BLOCK = 64
EPSILON = 1e-12
MASKED = -1000000000.0
GELU_A = 0.7978845608028654
GELU_B = 0.044715
VMEM_BYTES = 6 << 20
bf16 = jnp.bfloat16
f32 = jnp.float32


def matmul(left, right):
    return jnp.dot(left, right, preferred_element_type=f32)


def left_product(left, right):
    return lax.dot_general(left, right, (((0,), (0,)), ((), ())), preferred_element_type=f32)


def right_product(left, right):
    return lax.dot_general(left, right, (((1,), (1,)), ((), ())), preferred_element_type=f32)


def run_kernel(
    kernel, name, outs, args, scratch=(), scalars=0, raw=(), raw_outs=(), flops=0, powers=0, grant=VMEM_BYTES
):
    def spec(i, held):
        return pl.BlockSpec(memory_space=pltpu.MemorySpace.HBM if i in held else pltpu.VMEM)

    specs = [pl.BlockSpec(memory_space=pltpu.SMEM)] * scalars
    specs += [spec(i, raw) for i in range(scalars, len(args))]
    shapes = [jax.ShapeDtypeStruct(shape, dtype) for shape, dtype in outs]
    moved = sum(a.size * a.dtype.itemsize for a in (*args, *shapes))
    out_shape = tuple(pltpu.HBM(o.shape, o.dtype) if i in raw_outs else o for i, o in enumerate(shapes))
    args = [
        pltpu.with_memory_space_constraint(a, pltpu.HBM) if i in raw else a
        for i, a in enumerate(args)
    ]
    return pl.pallas_call(
        kernel,
        name=name,
        out_shape=out_shape,
        in_specs=specs,
        out_specs=tuple(spec(i, raw_outs) for i in range(len(outs))),
        scratch_shapes=list(scratch),
        compiler_params=pltpu.CompilerParams(vmem_limit_bytes=grant),
        cost_estimate=pl.CostEstimate(flops=flops, bytes_accessed=moved, transcendentals=powers),
    )(*args)


def normalize(values):
    center = values - jnp.mean(values, -1, keepdims=True)
    spread = jnp.mean(center * center, -1, keepdims=True)
    inverse = lax.rsqrt(spread + EPSILON)
    return center * inverse, inverse


def norm_back(grad, normed, inverse, gain):
    scaled = grad * gain
    return inverse * (
        scaled
        - jnp.mean(scaled, -1, keepdims=True)
        - normed * jnp.mean(scaled * normed, -1, keepdims=True)
    )


def bias_rows(be_ref, bn, same, head, block, blocks, block_len):
    width = same.shape[1]
    rows = [
        jnp.broadcast_to(be_ref[head * blocks + block + i : head * blocks + block + i + 1, :], (block_len, width))
        for i in range(same.shape[0] // block_len)
    ]
    return jnp.where(same, jnp.concatenate(rows, 0), bn)


def bias_rows(lines, bn, same):
    count, width = lines.shape
    length = same.shape[0] // count
    rows = [jnp.broadcast_to(lines[i : i + 1, :], (length, width)) for i in range(count)]
    return jnp.where(same, jnp.concatenate(rows, 0), bn)


def here():
    position = lax.axis_index("seq")
    return lax.rem(position, 2), lax.div(position, 2), lax.axis_index("dp")


def concat_kernel(*refs):
    out = refs[-1]
    at = 0
    for r in refs[:-1]:
        rows = r.shape[0]
        out[at : at + rows] = r[...]
        at += rows


def stack_kernel(*refs):
    for k, r in enumerate(refs[:-1]):
        refs[-1][k] = r[...]


def cut_kernel(wq, wk, wv, *refs):
    ids = here()
    outs = refs[:-3]
    raw, scratch, sems = refs[-3:]
    _, half, _ = raw.shape
    start = pl.multiple_of(lax.rem(ids[2], 2) * half, half)
    copies = [
        pltpu.make_async_copy(w.at[pl.ds(start, half), :], raw.at[i], sems.at[i])
        for i, w in enumerate((wq, wk, wv))
    ]
    for copy in copies:
        copy.start()
    for copy in copies:
        copy.wait()
    chips, _, wide = scratch.shape
    width = wide // 3
    for chip in range(chips):
        scratch[chip] = jnp.concatenate(
            [raw[i, :, chip * width : (chip + 1) * width] for i in range(3)], 1
        )
    for k, out in enumerate(outs):
        out[...] = scratch[ids[1] ^ k]


def assemble_kernel(mine, other, out):
    ids = here()
    core = ids[0]
    own = lax.rem(ids[2], 2)
    _, chips, _, _ = mine.shape
    for h in range(2):
        for k in range(chips):
            chip = ids[1] ^ k
            out[2 * chip + core, own ^ h] = mine[h, k]
            out[2 * chip + 1 - core, own ^ h] = other[h, k]


def cut_output_kernel(wo, vec, out):
    ids = here()
    half = wo.shape[0] // 2
    count, rows = vec.shape
    start = pl.multiple_of(lax.rem(lax.div(ids[2], 2), 2) * half, half)
    tall, model = out.shape
    each = model // rows
    out[:half, :] = wo[pl.ds(start, half), :]
    lines = []
    for first in range(0, count, each):
        parts = [vec[i : i + 1, :] for i in range(first, min(count, first + each))]
        parts += [jnp.zeros((1, rows), bf16)] * (each - len(parts))
        lines.append(jnp.concatenate(parts, 1))
    fill = jnp.zeros((tall - half - len(lines), model), bf16)
    out[half:, :] = jnp.concatenate(lines + [fill], 0)


def cut_inner_kernel(w1, w2, out, scratch):
    ids = here()
    groups, rows, model = scratch.shape
    units = w2.shape[0] // groups
    pieces = model // units
    for g in range(groups):
        scratch[g] = jnp.concatenate(
            [
                w1[:, (s * groups + g) * units : (s * groups + g + 1) * units]
                for s in range(pieces)
            ],
            1,
        )
    out[:rows, :] = scratch[ids[2]]
    out[rows:, :] = w2[pl.ds(pl.multiple_of(ids[2] * units, units), units), :]


def assemble_output_kernel(mine, other, out, vec, scratch):
    ids = here()
    core = ids[0]
    pieces, _, half, _ = out.shape
    chips = pieces // 2
    own = lax.rem(lax.div(ids[2], 2), 2)
    for k in range(chips):
        chip = ids[1] ^ k
        scratch[2 * chip + core] = mine[0, k, half:, :]
        scratch[2 * chip + 1 - core] = other[0, k, half:, :]
        for h in range(2):
            out[2 * chip + core, own ^ h] = mine[h, k, :half, :]
            out[2 * chip + 1 - core, own ^ h] = other[h, k, :half, :]
    rows = 2 * half
    each = vec.shape[1] // rows
    lines = [scratch[piece].astype(f32) for piece in range(pieces)]
    for i in range(vec.shape[0]):
        at, first = i // each, i % each * rows
        vec[i : i + 1, :] = jnp.concatenate(
            [line[at : at + 1, first : first + rows] for line in lines], 1
        )


def attend_kernel(w, be, bn, sk, sq, ours, theirs, hid_raw, *refs):
    ids = here()
    att = refs[0]
    kept = refs[1:5]
    hid, qo, ko, vo, lse, qs, s_all, p_all, sems = refs[5:]
    count = 2
    step = hid_raw.shape[0] // count
    loads = [
        pltpu.make_async_copy(
            hid_raw.at[pl.ds(i * step, step)], hid.at[pl.ds(i * step, step)], sems.at[4 + i]
        )
        for i in range(count)
    ]
    for load in loads:
        load.start()
    copies = [
        pltpu.make_async_copy(here, there, sems.at[i])
        for i, (here, there) in enumerate(zip((qo, ko, vo, lse), kept))
    ]
    pieces, piece_len, width = qs.shape
    chips = pieces // 2
    core = ids[0]
    size = 64
    heads = width // size
    model = hid.shape[2]
    ours, theirs = ours[...].astype(f32), theirs[...].astype(f32)
    first = jnp.where(core == 0, ours, theirs)
    second = jnp.where(core == 0, theirs, ours)
    biases = jnp.concatenate([first, second], 1)
    qb, vb = biases[0:1, :], biases[1:2, :]
    for i, load in enumerate(loads):
        load.wait()
        some = slice(i * step, (i + 1) * step)
        span = slice(i * step * piece_len, (i + 1) * step * piece_len)
        product = matmul(hid[some].reshape(step * piece_len, model), w[...])
        query = (product[:, :width] + qb).astype(bf16) * bf16(size**-0.5)
        qs[some] = query.reshape(step, piece_len, width)
        ko[span] = product[:, width : 2 * width].astype(bf16)
        vo[span] = (product[:, 2 * width :] + vb).astype(bf16)
    lane = lax.broadcasted_iota(jnp.int32, (piece_len, 128), 1)
    for k in range(chips):
        qo[k] = qs[2 * (ids[1] ^ k) + core]
    for copy in copies[:3]:
        copy.start()
    logs = [jnp.zeros((piece_len, 128), f32)] * chips
    parts = [[] for _ in range(chips)]
    for head in range(heads):
        cols = slice(head * size, (head + 1) * size)
        queries = qo[:, :, cols].reshape(chips * piece_len, size)
        s_all[...] = right_product(queries, ko[:, cols])
        shares = []
        for k in range(chips):
            chip = ids[1] ^ k
            rows = slice(k * piece_len, (k + 1) * piece_len)
            same = sq[chip] == sk[...]
            scores = s_all[rows, :] + bias_rows(be[head * chips + chip], bn[...], same)
            top = jnp.max(scores, -1, keepdims=True)
            powers = jnp.exp(scores - top)
            total = jnp.sum(powers, -1, keepdims=True)
            p_all[rows, :] = powers.astype(bf16)
            shares.append(1.0 / total)
            logs[k] = jnp.where(lane == head, top + jnp.log(total), logs[k])
        out = matmul(p_all[...], vo[:, cols])
        for k in range(chips):
            parts[k].append(out[k * piece_len : (k + 1) * piece_len] * shares[k])
    for k in range(chips):
        att[ids[1] ^ k] = jnp.concatenate(parts[k], 1).T.astype(bf16)
        lse[k] = logs[k]
    copies[3].start()
    for copy in copies:
        copy.wait()


def attend_back_kernel(hid_raw, q_raw, k_raw, v_raw, lse_raw, be, bn, sk, sq, *refs):
    ids = here()
    chips, piece_len, width = q_raw.shape
    ga_raw = refs[:chips]
    dq, mine, other, dw_mine, dw_other = refs[chips : chips + 5]
    hid, q, k, v, lse, ga, s_all, g_all, ds_all, p_all, dkv, dws, sems = refs[chips + 5 :]
    copies = [
        pltpu.make_async_copy(there, here, sems.at[i])
        for i, (there, here) in enumerate(
            zip((q_raw, k_raw, v_raw, lse_raw, hid_raw), (q, k, v, lse, hid))
        )
    ]
    copies[4:4] = [
        pltpu.make_async_copy(there, ga.at[i], sems.at[5 + i]) for i, there in enumerate(ga_raw)
    ]
    for copy in copies:
        copy.start()
    pieces = 2 * chips
    core = ids[0]
    size = 64
    heads = width // size
    dks = []
    dvs = []
    dqs = [[None] * heads for _ in range(chips)]
    for copy in copies[:-1]:
        copy.wait()
    gas = jnp.concatenate([ga[i].astype(f32).T.astype(bf16) for i in range(chips)], 0)
    for head in range(heads):
        cols = slice(head * size, (head + 1) * size)
        key = k[:, cols]
        value = v[:, cols]
        queries = q[:, :, cols].reshape(chips * piece_len, size)
        grads = gas[:, cols]
        s_all[...] = right_product(queries, key)
        g_all[...] = right_product(grads, value)
        for i in range(chips):
            chip = ids[1] ^ i
            rows = slice(i * piece_len, (i + 1) * piece_len)
            same = sq[chip] == sk[...]
            scores = s_all[rows, :] + bias_rows(be[head * chips + chip], bn[...], same)
            probs = jnp.exp(scores - lse[i, :, head : head + 1])
            grad = g_all[rows, :]
            weighted = jnp.sum(probs * grad, -1, keepdims=True)
            ds_all[rows, :] = (probs * (grad - weighted)).astype(bf16)
            p_all[rows, :] = probs.astype(bf16)
        grad_q = (matmul(ds_all[...], key) * (size**-0.5)).astype(bf16)
        for i in range(chips):
            dqs[i][head] = grad_q[i * piece_len : (i + 1) * piece_len]
        dks.append(left_product(ds_all[...], queries).astype(bf16))
        dvs.append(left_product(p_all[...], grads).astype(bf16))
    for i in range(chips):
        dq[i] = jnp.concatenate(dqs[i], 1)
    joined = jnp.concatenate(dks + dvs, 1)
    dkv[...] = joined.reshape(pieces, piece_len, 2 * width)
    for i in range(chips):
        chip = ids[1] ^ i
        mine[i] = dkv[2 * chip + core]
        other[i] = dkv[2 * chip + 1 - core]
    copies[-1].wait()
    _, _, model = hid.shape
    tokens = hid[...].reshape(pieces * piece_len, model)
    owned = jnp.concatenate([hid[2 * (ids[1] ^ i) + core] for i in range(chips)], 0)
    grad_q = dq[...].reshape(chips * piece_len, width)
    weights = jnp.concatenate([left_product(owned, grad_q), left_product(tokens, joined)], 1)
    groups = dw_mine.shape[0]
    rows = dws.shape[2]
    dws[...] = weights.reshape(dws.shape)
    for i in range(chips):
        chip = ids[1] ^ i
        for j in range(groups):
            span = slice(i * rows, (i + 1) * rows)
            dw_mine[j, span] = dws[2 * chip + core, ids[2] ^ j]
            dw_other[j, span] = dws[2 * chip + 1 - core, ids[2] ^ j].astype(bf16)
    total = jnp.concatenate(
        [
            jnp.sum(grad_q.astype(f32), 0, keepdims=True),
            jnp.sum(joined.astype(f32), 0, keepdims=True),
        ],
        1,
    )
    total = jnp.broadcast_to(total, (8, 3 * width))
    for j in range(groups):
        dw_mine[j, chips * rows :] = total
        dw_other[j, chips * rows :] = total.astype(bf16)


def input_grad_kernel(dq, mine, recv, w, out, scratch):
    ids = here()
    chips, piece_len, width = dq.shape
    dkv = (mine[...].astype(f32) + recv[...].astype(f32)).astype(bf16)
    grads = jnp.concatenate([dq[...], dkv], 2).reshape(chips * piece_len, 3 * width)
    total = right_product(grads, w[...])
    scratch[...] = total.astype(bf16).reshape(scratch.shape)
    for chip in range(chips):
        out[chip] = scratch[ids[1] ^ chip]


def add_kernel(left, right, out):
    out[...] = (left[...].astype(f32) + right[...].astype(f32)).astype(out.dtype)


def sum_rows_kernel(first, parts, out):
    total = first[...]
    for i in range(parts.shape[0]):
        total = total + parts[i].astype(f32)
    out[...] = total


def add_split_kernel(left, right, *outs):
    for k, out in enumerate(outs):
        out[...] = (left[k].astype(f32) + right[k].astype(f32)).astype(out.dtype)


def sum_split_kernel(*refs, parts, rows):
    total = refs[0][...].astype(f32)
    for r in refs[1:parts]:
        total = total + r[...].astype(f32)
    for k, out in enumerate(refs[parts:]):
        out[...] = total[k * rows : k * rows + out.shape[0]].astype(out.dtype)


def sum_lead_kernel(parts, *outs, rows):
    total = parts[0].astype(f32)
    for i in range(1, parts.shape[0]):
        total = total + parts[i].astype(f32)
    for k, out in enumerate(outs):
        out[...] = total[k * rows : k * rows + out.shape[0]].astype(out.dtype)


def project_kernel(wo, hid, vec, att, low, normed, inverse):
    branch = vec[2:3, :] + jnp.zeros(hid.shape, f32)
    for chip in range(att.shape[0]):
        branch = branch + left_product(att[chip], wo[chip])
    n1, r1 = normalize(hid[...].astype(f32) + branch)
    low[...] = (n1 * vec[3:4, :] + vec[4:5, :]).astype(bf16)
    normed[...] = n1
    inverse[...] = jnp.broadcast_to(r1, inverse.shape)


def gelu_parts(v):
    return jnp.tanh(GELU_A * (v + GELU_B * (v * v * v)))


def two_weights(both):
    pieces, rows, model = both.shape
    half = rows // 2
    first = both[:, :half, :].reshape(pieces * half, model)
    return first, both[:, half:, :].reshape(pieces * half, model)


def forward_kernel(vec, both_raw, *refs, parts):
    raw = refs[:parts]
    outs = refs[parts : 2 * parts]
    inner_ref, act_ref, both, x, sems = refs[2 * parts :]
    half = both.shape[1] // 2
    copies = [pltpu.make_async_copy(r, x.at[i], sems.at[i]) for i, r in enumerate(raw)]
    for i in range(2):
        span = (slice(None), pl.ds(i * half, half), slice(None))
        copies.append(pltpu.make_async_copy(both_raw.at[span], both.at[span], sems.at[parts + i]))
    for copy in copies:
        copy.start()
    for copy in copies[:-1]:
        copy.wait()
    _, rows, model = x.shape
    weight1 = both[:, :half, :].reshape(-1, model)
    inner = matmul(x[...].reshape(parts * rows, model), weight1) + vec[pl.ds(8 + lax.axis_index("dp"), 1), :]
    act = (0.5 * inner * (1.0 + gelu_parts(inner))).astype(bf16)
    inner_ref[...] = inner
    act_ref[...] = act
    copies[-1].wait()
    mixed = matmul(act, both[:, half:, :].reshape(-1, model))
    for i in range(parts):
        outs[i][...] = mixed[i * rows : (i + 1) * rows].astype(outs[i].dtype)


def middle_kernel(*refs):
    recv = refs[:-7]
    normed, cot, vec, out, low, mix, sums = refs[-7:]
    first = normed[...] * vec[3:4, :] + vec[4:5, :]
    mixed = vec[5:6, :]
    for r in recv:
        mixed = mixed + r[...].astype(f32)
    n2, r2 = normalize(first + mixed)
    gain = vec[6:7, :]
    out[...] = (n2 * gain + vec[7:8, :]).astype(bf16)
    g = cot[...].astype(f32)
    grad = norm_back(g, n2, r2, gain)
    rounded = grad.astype(bf16)
    mix[...] = grad
    low[...] = rounded
    sums[0:1, :] = jnp.sum(g * n2, 0, keepdims=True)
    sums[1:2, :] = jnp.sum(g, 0, keepdims=True)
    sums[2:3, :] = jnp.sum(rounded.astype(f32), 0, keepdims=True)
    sums[3:, :] = jnp.zeros((5, sums.shape[1]), f32)


def backward_kernel(both, inner_ref, *refs, parts):
    grads = refs[:parts]
    outs = refs[parts : 2 * parts]
    gi_ref, total = refs[2 * parts :]
    rows = grads[0].shape[0]
    weight1, weight2 = two_weights(both)
    gm = jnp.concatenate([r[...] for r in grads], 0)
    grad_act = right_product(gm, weight2)
    v = inner_ref[...]
    t = gelu_parts(v)
    slope = 0.5 * (1.0 + t) + 0.5 * v * (1.0 - t * t) * (GELU_A * (1.0 + 3.0 * GELU_B * (v * v)))
    gi = (grad_act * slope).astype(bf16)
    gi_ref[...] = gi
    first = right_product(gi, weight1)
    for i in range(parts):
        outs[i][...] = first[i * rows : (i + 1) * rows].astype(outs[i].dtype)
    total[...] = jnp.sum(gi.astype(f32), 0, keepdims=True)


def inner_outer_kernel(gi, act, sums, total, *refs, parts):
    x = refs[:parts]
    grads = refs[parts : 2 * parts]
    out = refs[2 * parts]
    pieces, tall, model = out.shape
    units = (tall - 8) // 2
    gm = jnp.concatenate([r[...] for r in grads], 0)
    tokens = jnp.concatenate([r[...] for r in x], 0)
    out[:, :units, :] = left_product(tokens, gi[...]).astype(bf16).reshape(pieces, units, model)
    out[:, units : 2 * units, :] = (
        left_product(act[...], gm).astype(bf16).reshape(pieces, units, model)
    )
    vectors = [sums[i : i + 1, :] for i in range(3)] + [total[...]]
    for piece in range(pieces):
        put_vectors(out, piece, piece, 2 * units, vectors, units)


def residual_kernel(mix, normed, inverse, vec, wo, att, above, *refs, parts, lined):
    ids = here() if lined else (0, 0, 0)
    recv = refs[:parts]
    res_raw, stacked = refs[parts : parts + 2]
    back_raw = refs[parts + 2 : -4]
    res, back, out, sems = refs[-4:]
    copies = []

    def send(here, there):
        copies.append(pltpu.make_async_copy(here, there, sems.at[len(copies)]))
        copies[-1].start()

    tall = above.shape[1] - 8
    send(above.at[:, pl.ds(0, tall), :], stacked.at[:, pl.ds(0, tall), :])
    first = mix[...]
    for r in recv:
        first = first + r[...].astype(f32)
    n1 = normed[...]
    grad = norm_back(first, n1, inverse[:, 0:1], vec[3:4, :])
    rounded = grad.astype(bf16)
    for k, raw in enumerate(back_raw):
        back[k] = right_product(wo[ids[1] ^ k], rounded).astype(bf16)
        send(back.at[k], raw)
    res[...] = grad
    send(res, res_raw)
    vectors = [jnp.zeros((1, wo.shape[2]), f32)] * 4 + [
        jnp.sum(first * n1, 0, keepdims=True),
        jnp.sum(first, 0, keepdims=True),
        jnp.sum(rounded.astype(f32), 0, keepdims=True),
    ]
    rows = out.shape[1] - 8
    each = out.shape[0] // att.shape[0]
    for chip in range(att.shape[0]):
        part = matmul(att[chip], rounded).astype(bf16)
        for i in range(each):
            piece = each * chip + i
            out[piece, 8:] = part[i * rows : (i + 1) * rows]
            put_vectors(out, piece, piece, 0, vectors, rows)
            out[piece, :8] = out[piece, :8] + above[piece, tall:]
    send(out, stacked.at[:, pl.ds(tall, rows + 8), :])
    for copy in copies:
        copy.wait()


def put_vectors(out, piece, at, row, vectors, rows):
    parts = [v[:, piece * rows : (piece + 1) * rows] for v in vectors]
    fill = out.shape[2] - rows * len(parts)
    line = jnp.concatenate(parts + [jnp.zeros((1, fill), f32)], 1)
    out[at, row : row + 8, :] = jnp.broadcast_to(line, (8, out.shape[2])).astype(bf16)


def ordered(ids, refs, scratch):
    for k, r in enumerate(refs):
        scratch[ids[2] ^ k] = r[...]


def finish_inner_kernel(*refs, parts):
    ids = here()
    inner, outer, output, vectors, scratch = refs[parts:]
    ordered(ids, refs[:parts], scratch)
    rows = inner.shape[0]
    units = outer.shape[0] // parts
    pieces = scratch.shape[2] // units
    for piece in range(pieces):
        inner[:, piece * parts * units : (piece + 1) * parts * units] = jnp.concatenate(
            [
                scratch[g, :rows, piece * units : (piece + 1) * units].astype(f32)
                for g in range(parts)
            ],
            1,
        )
    total = jnp.zeros((1, scratch.shape[2]), f32)
    at = rows + units
    for g in range(parts):
        outer[g * units : (g + 1) * units, :] = scratch[g, rows:at, :].astype(f32)
        line = scratch[g, at : at + 8, :].astype(f32)[0:1]
        vectors[g : g + 1, :] = line
        total = total + line
    vectors[parts : parts + 1, :] = total
    if scratch.shape[1] > at + 8:
        last = scratch[0, at + 8 :, :].astype(f32)
        for g in range(1, parts):
            last = last + scratch[g, at + 8 :, :].astype(f32)
        output[...] = last


def finish_kernel(*refs):
    ids = here()
    parts = len(refs) - 4
    gq, gk, gv, scratch = refs[parts:]
    quarters, chips, rows, wide = scratch.shape
    for j, r in enumerate(refs[:parts]):
        for k in range(chips):
            scratch[ids[2] ^ j, ids[1] ^ k] = r[k]
    width = wide // 3
    for part in range(quarters):
        block = [scratch[part, chip].astype(f32) for chip in range(chips)]
        for i, out in enumerate((gq, gk, gv)):
            out[part * rows : (part + 1) * rows, :] = jnp.concatenate(
                [b[:, i * width : (i + 1) * width] for b in block], 1
            )


def log_counts(count):
    return jnp.where(count > 0, jnp.log(jnp.maximum(count, 1).astype(f32)), MASKED)


def exchange(array, k):
    count = lax.axis_size("dp")
    return lax.ppermute(array, "dp", [(i, i ^ k) for i in range(count)])


def exchange_all(array):
    return [array] + [exchange(array, k) for k in range(1, lax.axis_size("dp"))]


def exchange_parts(parts):
    return [parts[0]] + [exchange(parts[k], k) for k in range(1, lax.axis_size("dp"))]


def swap_cores(array):
    count = lax.axis_size("seq")
    return lax.ppermute(array, "seq", [(i, i ^ 1) for i in range(count)])


def line_exchange(array, k):
    count = lax.axis_size("seq")
    return lax.ppermute(array, "seq", [(i, i ^ (2 * k)) for i in range(count)])


def line_parts(parts):
    return [parts[0]] + [line_exchange(parts[k], k) for k in range(1, len(parts))]


def tied(value, *others):
    return lax.optimization_barrier((value,) + others)[0]


def add_split(left, right, outs):
    return run_kernel(add_split_kernel, "add", outs, (left, right))


def sum_split(arrays, outs):
    return run_kernel(
        functools.partial(sum_split_kernel, parts=len(arrays), rows=outs[0][0][0]),
        "sum",
        outs,
        tuple(arrays),
    )


def line_all(array):
    return [array] + [line_exchange(array, k) for k in range(1, lax.axis_size("seq") // 2)]


def along_line(array):
    count = lax.axis_size("seq")
    lines = [[2 * i + c for i in range(count // 2)] for c in range(2)]
    return lax.all_to_all(array, "seq", 0, 0, tiled=True, axis_index_groups=lines)


def stack(*arrays):
    shape = (len(arrays),) + arrays[0].shape
    return run_kernel(stack_kernel, "stack", [(shape, bf16)], arrays)[0]


def concat(*arrays):
    shape = (sum(a.shape[0] for a in arrays),) + arrays[0].shape[1:]
    return run_kernel(concat_kernel, "concat", [(shape, bf16)], arrays)[0]


def finish_inner(shares, rows):
    groups = len(shares)
    share = shares[0]
    model = share.shape[1]
    return run_kernel(
        functools.partial(finish_inner_kernel, parts=groups),
        "finish_inner",
        [
            ((rows, groups * model), f32),
            ((groups * rows, model), f32),
            ((rows, model), f32),
            ((8, model), f32),
        ],
        tuple(shares),
        scratch=[pltpu.VMEM((groups,) + share.shape, bf16)],
    )


class HeadAttention:
    def __init__(self, hidden, weights, biases, segments, random_blocks, output_weight, vec_local):
        self.splits = splits = lax.axis_size("seq")
        self.chips = chips = splits // 2
        self.position = position = lax.axis_index("seq")
        core = position % 2
        chip = position // 2
        group = lax.axis_index("dp")
        self.packed = lax.all_gather(hidden, "seq")
        piece_len, model = hidden.shape
        rows = model // splits
        width = model // chips
        heads = HEADS // chips
        half = rows // 2
        cut = run_kernel(
            cut_kernel,
            "cut",
            [((half, 3 * width), bf16)] * chips,
            tuple(weights),
            scratch=[
                pltpu.VMEM((3, half, model), bf16),
                pltpu.VMEM((chips, half, 3 * width), bf16),
                pltpu.SemaphoreType.DMA((3,)),
            ],
            raw=range(3),
        )
        cut = stack(*line_parts(cut))
        cut_next = exchange(cut, 1)
        (out_half,) = run_kernel(
            cut_output_kernel,
            "cut_output",
            [((half + 8, model), bf16)],
            (output_weight, vec_local),
        )
        cut = stack(cut, cut_next)
        (weight,) = run_kernel(
            assemble_kernel,
            "assemble",
            [((splits, 2, half, 3 * width), bf16)],
            (cut, swap_cores(cut)),
        )
        self.out_half = stack(*line_all(tied(out_half, cut_next)))
        self.out_next = exchange(self.out_half, 2)
        self.weight = weight.reshape(model, 3 * width)
        self.biases = biases
        self.hidden = hidden
        block_count = segments.shape[1] // BLOCK
        per_piece = piece_len // BLOCK
        own = random_blocks[0].reshape(chips, 2, per_piece, HEADS, -1)
        own = lax.dynamic_index_in_dim(own, core, 1, keepdims=False)
        own = lax.dynamic_slice_in_dim(own, chip * heads, heads, 2)
        own = own.reshape(chips * per_piece, heads, -1).transpose(1, 0, 2)
        block = jnp.arange(block_count, dtype=jnp.int32)
        mine = (
            (jnp.arange(chips, dtype=jnp.int32)[:, None] * 2 + core) * per_piece
            + jnp.arange(per_piece, dtype=jnp.int32)[None, :]
        ).reshape(-1)
        ends = ((block == 0) | (block == block_count - 1)).astype(jnp.int32)
        near = (jnp.abs(block[None, :] - mine[:, None]) <= 1).astype(jnp.int32)
        listed = jnp.sum((own[..., None] == block).astype(jnp.int32), 2)
        count = listed + near[None] + ends
        self.same_bias = jnp.repeat(log_counts(count), BLOCK, axis=2).reshape(
            heads * chips, per_piece, -1
        )
        self.other_bias = jnp.repeat(
            jnp.where(ends > 0, 0.0, MASKED).astype(f32)[None], BLOCK, axis=1
        )
        self.key_seg = segments
        self.query_seg = lax.dynamic_index_in_dim(
            segments.reshape(chips, 2, piece_len), core, 1, keepdims=False
        ).reshape(chips, piece_len, 1)
        self.piece_len, self.width, self.model = piece_len, width, model

    def masks(self):
        return (self.same_bias, self.other_bias, self.key_seg, self.query_seg)

    def inner_weights(self, inner_weight, outer_weight):
        groups = lax.axis_size("dp")
        rows = inner_weight.shape[0]
        units = outer_weight.shape[0] // groups
        (both,) = run_kernel(
            cut_inner_kernel,
            "cut_inner",
            [((rows + units, self.model), bf16)],
            (inner_weight, outer_weight),
            scratch=[pltpu.VMEM((groups, rows, self.model), bf16)],
        )
        self.pair = jnp.stack(self.biases, 0)
        self.pair_other = swap_cores(self.pair)
        self.both = lax.all_gather(tied(both, self.packed, self.weight, self.out_half), "seq")

    def forward(self):
        chips, piece_len, width, model = self.chips, self.piece_len, self.width, self.model
        tokens = self.splits * piece_len
        one = (chips, piece_len, width)
        kept = [
            (one, bf16),
            ((tokens, width), bf16),
            ((tokens, width), bf16),
            ((chips, piece_len, 128), f32),
        ]
        att, self.q, self.k, self.v, self.lse = run_kernel(
            attend_kernel,
            "attend",
            [((chips, width, piece_len), bf16)] + kept,
            (self.weight, *self.masks(), self.pair, self.pair_other, self.packed),
            scratch=[pltpu.VMEM(self.packed.shape, bf16)]
            + [pltpu.VMEM(*spec) for spec in kept]
            + [
                pltpu.VMEM((self.splits, piece_len, width), bf16),
                pltpu.VMEM((chips * piece_len, tokens), f32),
                pltpu.VMEM((chips * piece_len, tokens), bf16),
                pltpu.SemaphoreType.DMA((len(kept) + 2,)),
            ],
            raw=(7,),
            raw_outs=range(1, 1 + len(kept)),
            flops=6 * tokens * model * width + 2 * tokens * tokens * width,
            powers=tokens * tokens * 3 // 2,
            grant=16 << 20,
        )
        out_half = stack(tied(self.out_half, att), self.out_next)
        half = model // self.splits // 2
        weight, self.vec = run_kernel(
            assemble_output_kernel,
            "assemble_output",
            [((self.splits, 2, half, model), bf16), ((16, model), f32)],
            (out_half, swap_cores(out_half)),
            scratch=[pltpu.VMEM((self.splits, 8, model), bf16)],
        )
        self.output_weight = weight.reshape(chips, width, model)
        att = along_line(att)
        return att

    def backward(self, grads, grad_res, share):
        chips, piece_len, width = self.chips, self.piece_len, self.width
        splits, model = self.splits, self.model
        groups = lax.axis_size("dp")
        tokens = splits * piece_len
        rows = model // splits
        one = (chips, piece_len, width)
        two = (chips, piece_len, 2 * width)
        quarter = (rows // groups, 3 * width)
        group = (chips * quarter[0] + 8, 3 * width)
        wide = ((groups,) + group, bf16)
        keep = (self.packed, self.q, self.k, self.v, self.lse)
        dq, mine, other, dw_mine, dw_other = run_kernel(
            attend_back_kernel,
            "attend_back",
            [(one, bf16), (two, bf16), (two, bf16), (wide[0], f32), wide],
            keep + self.masks() + tuple(grads),
            scratch=[pltpu.VMEM(a.shape, a.dtype) for a in keep]
            + [
                pltpu.VMEM((chips,) + grads[0].shape, bf16),
                pltpu.VMEM((chips * piece_len, tokens), f32),
                pltpu.VMEM((chips * piece_len, tokens), f32),
                pltpu.VMEM((chips * piece_len, tokens), bf16),
                pltpu.VMEM((chips * piece_len, tokens), bf16),
                pltpu.VMEM((splits, piece_len, 2 * width), bf16),
                pltpu.VMEM((splits, groups) + quarter, f32),
                pltpu.SemaphoreType.DMA((len(keep) + chips,)),
            ],
            raw=(*range(5), *range(9, 9 + chips)),
            flops=5 * tokens * tokens * width + 6 * tokens * model * width,
            powers=tokens * tokens * 3 // 2,
            grant=24 << 20,
        )
        recv = swap_cores(other)
        dws = add_split(dw_mine, swap_cores(dw_other), [(group, bf16)] * groups)
        dws = exchange_parts(dws)
        full = (piece_len, model)
        *dws, sums = sum_split(dws, [(quarter, bf16)] * chips + [((8, 3 * width), f32)])
        dq = tied(dq, dws[0])
        (partial,) = run_kernel(
            input_grad_kernel,
            "input_grad",
            [((chips,) + full, bf16)],
            (dq, mine, recv, self.weight),
            scratch=[pltpu.VMEM((chips,) + full, bf16)],
            flops=3 * tokens * model * width,
        )
        dws = line_parts(dws)
        part = (chips,) + quarter
        dw = stack(*dws)
        every = exchange_all(dw)
        self.shares = exchange_all(tied(share, *every[1:]))
        count = splits
        lines = [[2 * i + c for i in range(count // 2)] for c in range(2)]
        partial = lax.psum_scatter(
            partial, "seq", scatter_dimension=0, axis_index_groups=lines, tiled=False
        )[None]
        gq, gk, gv = run_kernel(
            finish_kernel,
            "finish",
            [((rows, model), f32)] * 3,
            tuple(every),
            scratch=[pltpu.VMEM((groups,) + part, bf16)],
        )
        (input_grad,) = run_kernel(
            sum_rows_kernel, "sum_rows", [(full, f32)], (grad_res, partial)
        )
        core = self.position % 2
        bias_q = lax.dynamic_slice_in_dim(sums[0], core * rows, rows)
        bias_v = lax.dynamic_slice_in_dim(sums[0], 2 * width + core * rows, rows)
        return input_grad, gq, bias_q, gk, gv, bias_v


def one_hot(index, count):
    return (index[..., None] == jnp.arange(count, dtype=jnp.int32)).astype(bf16)


def with_halo(block, axis, dim, width):
    count = lax.axis_size(axis)
    forward = [(i, i + 1) for i in range(count - 1)]
    backward = [(target, source) for source, target in forward]
    low = lax.ppermute(
        lax.slice_in_dim(block, block.shape[dim] - width, None, axis=dim), axis, forward
    )
    high = lax.ppermute(lax.slice_in_dim(block, 0, width, axis=dim), axis, backward)
    return jnp.concatenate([low, block, high], axis=dim)


def broadcast(block, axis, owner):
    block = jnp.where(lax.axis_index(axis) == owner, block, jnp.zeros_like(block))
    return lax.psum(block, axis)


class TokenAttention:
    def __init__(self, hidden, weights, biases, segments, random_blocks, output_weight, vec_local):
        self.splits = splits = lax.axis_size("seq")
        self.position = position = lax.axis_index("seq")
        self.hidden = hidden
        self.segments = segments
        self.random_blocks = random_blocks
        self.weights = [lax.all_gather(w, "seq", axis=0, tiled=True) for w in weights]
        self.output_weight = lax.all_gather(output_weight, "seq", axis=0, tiled=True)[None]
        vec = lax.all_gather(vec_local, "seq")
        self.vec = vec.transpose(1, 0, 2).reshape(vec_local.shape[0], -1).astype(f32)

    def forward(self):
        hidden, segments = self.hidden, self.segments
        splits, position = self.splits, self.position
        seq_count = segments.shape[0]
        row_count, model = hidden.shape
        piece_len = row_count // seq_count
        size = model // HEADS
        per = piece_len // BLOCK
        slots = self.random_blocks.shape[3]
        reqs = seq_count * per * HEADS * slots
        cap = max(2, 3 * reqs // (2 * splits) + 1)
        vec = self.vec
        wq, wk, wv = self.weights
        query = (matmul(hidden, wq) + vec[0:1]).astype(bf16)
        keys = matmul(hidden, wk).astype(bf16)
        values = (matmul(hidden, wv) + vec[1:2]).astype(bf16)
        joined = jnp.concatenate([keys, values], 1).reshape(seq_count, piece_len, 2 * model)
        extended = with_halo(joined, "seq", 1, BLOCK)
        first = broadcast(joined[:, :BLOCK], "seq", 0)
        last = broadcast(joined[:, piece_len - BLOCK :], "seq", splits - 1)
        tiles = seq_count * per * HEADS
        tile_size = BLOCK * 2 * size
        kv_tiles = (
            joined.reshape(seq_count, per, BLOCK, 2, HEADS, size)
            .transpose(0, 1, 4, 2, 3, 5)
            .reshape(tiles, tile_size)
        )
        req = jnp.arange(reqs, dtype=jnp.int32)
        req_seq = req // (per * HEADS * slots)
        req_head = req // slots % HEADS
        earlier = (req[:, None] > req[None, :]).astype(jnp.int32)
        everyone = (
            self.random_blocks.reshape(seq_count, splits, per, HEADS, slots)
            .transpose(1, 0, 2, 3, 4)
            .reshape(splits, reqs)
        )
        is_mine = (everyone // per == position).astype(jnp.int32)
        place = jnp.sum(is_mine[:, None, :] * earlier, 2)
        slot = jnp.where(is_mine == 1, place, cap)
        tile_of = (req_seq * per + everyone % per) * HEADS + req_head
        chosen = slot[:, :, None] == jnp.arange(cap, dtype=jnp.int32)
        send = jnp.sum(jnp.where(chosen, tile_of[:, :, None], 0), 1).reshape(splits * cap)
        self.send = one_hot(send, tiles)
        outgoing = matmul(self.send, kv_tiles).astype(bf16).reshape(splits, cap, tile_size)
        incoming = lax.all_to_all(outgoing, "seq", 0, 0, tiled=True)
        asked = lax.dynamic_slice_in_dim(self.random_blocks, position * per, per, 1)
        owner = asked.reshape(reqs) // per
        before = jnp.sum((owner[:, None] == owner[None, :]).astype(jnp.int32) * earlier, 1)
        self.arrival = one_hot(owner * cap + before, splits * cap)
        fetched = matmul(self.arrival, incoming.reshape(splits * cap, tile_size)).astype(bf16)
        moved = fetched.reshape(seq_count, per, HEADS, slots * BLOCK, 2, size)
        spans = [slice(i * BLOCK, (i + 3) * BLOCK) for i in range(per)]
        fixed = jnp.stack(
            [jnp.concatenate([extended[:, span], first, last], 1) for span in spans], 1
        )
        fixed = fixed.reshape(seq_count, per, 5 * BLOCK, 2, HEADS, size)
        paired = jnp.concatenate(
            [fixed.transpose(3, 0, 1, 4, 2, 5), moved.transpose(4, 0, 1, 2, 3, 5)], 4
        )
        self.keys, self.values = paired[0], paired[1]
        edge = jnp.full((seq_count, BLOCK), -1, jnp.int32)
        padded = jnp.concatenate([edge, segments, edge], 1)
        query_seg = lax.dynamic_slice_in_dim(segments, position * piece_len, piece_len, 1)
        ext_seg = lax.dynamic_slice_in_dim(padded, position * piece_len, piece_len + 2 * BLOCK, 1)
        always = jnp.full((seq_count, 2 * BLOCK), -2, jnp.int32)
        seg_fixed = jnp.stack(
            [jnp.concatenate([ext_seg[:, span], always], 1) for span in spans], 1
        )
        seg_fixed = jnp.broadcast_to(
            seg_fixed[:, :, None], (seq_count, per, HEADS, 5 * BLOCK)
        )
        seg_blocks = segments.reshape(seq_count, -1, BLOCK)
        asked_hot = one_hot(asked, seg_blocks.shape[1])
        seg_moved = jnp.einsum(
            "gjhrb,gbt->gjhrt", asked_hot, seg_blocks.astype(bf16), preferred_element_type=f32
        ).astype(jnp.int32)
        key_seg = jnp.concatenate(
            [seg_fixed, seg_moved.reshape(seq_count, per, HEADS, slots * BLOCK)], 3
        )[:, :, :, None, :]
        self.allowed = (
            query_seg.reshape(seq_count, per, 1, BLOCK, 1) == key_seg
        ) | (key_seg == -2)
        self.query = query.reshape(seq_count, per, BLOCK, HEADS, size)
        scores = self.scores()
        top = jnp.max(scores, -1, keepdims=True)
        powers = jnp.exp(scores - top)
        total = jnp.sum(powers, -1, keepdims=True)
        self.log_total = top + jnp.log(total)
        attended = jnp.einsum(
            "gjhqk,gjhke->gjqhe",
            (powers / total).astype(bf16),
            self.values,
            preferred_element_type=f32,
        )
        return attended.astype(bf16).reshape(row_count, model).T[None]

    def scores(self):
        raw = jnp.einsum("gjqhe,gjhke->gjhqk", self.query, self.keys, preferred_element_type=f32)
        return jnp.where(self.allowed, raw * self.query.shape[-1] ** -0.5, MASKED)

    def inner_weights(self, inner_weight, outer_weight):
        splits = self.splits
        groups, group = lax.axis_size("dp"), lax.axis_index("dp")
        rows = inner_weight.shape[0]
        units, model = outer_weight.shape[0] // groups, outer_weight.shape[1]
        inner = inner_weight.reshape(rows, splits, groups, units)
        outer = outer_weight.reshape(groups, units, model)
        inner = lax.dynamic_index_in_dim(inner, group, 2, keepdims=False).reshape(rows, model)
        outer = lax.dynamic_index_in_dim(outer, group, 0, keepdims=False)
        both = lax.all_gather(jnp.concatenate([inner, outer], 0), "seq")
        both = both.reshape(splits, 2, rows, model).transpose(1, 0, 2, 3)
        self.both = both.reshape(1, 2 * model, model)

    def backward(self, grads, grad_res, share):
        hidden = self.hidden
        grad = grads[0].T
        self.shares = exchange_all(share)
        splits, position = self.splits, self.position
        seq_count, per, _, _, size = self.query.shape
        row_count, model = hidden.shape
        piece_len = per * BLOCK
        slots = self.random_blocks.shape[3]
        scale = size**-0.5
        probs = jnp.exp(self.scores() - self.log_total)
        grad_split = grad.reshape(seq_count, per, BLOCK, HEADS, size)
        grad_probs = jnp.einsum(
            "gjqhe,gjhke->gjhqk", grad_split, self.values, preferred_element_type=f32
        )
        weighted = jnp.sum(probs * grad_probs, -1, keepdims=True)
        grad_scores = (probs * (grad_probs - weighted)).astype(bf16)
        grad_query = (
            jnp.einsum("gjhqk,gjhke->gjqhe", grad_scores, self.keys, preferred_element_type=f32)
            * scale
        )
        grad_key = (
            jnp.einsum("gjhqk,gjqhe->gjhke", grad_scores, self.query, preferred_element_type=f32)
            * scale
        )
        grad_value = jnp.einsum(
            "gjhqk,gjqhe->gjhke", probs.astype(bf16), grad_split, preferred_element_type=f32
        )
        paired = jnp.stack([grad_key, grad_value], 0)
        fixed_len = 5 * BLOCK
        fixed = (
            paired[:, :, :, :, :fixed_len]
            .transpose(1, 2, 4, 0, 3, 5)
            .reshape(seq_count, per, fixed_len, 2 * model)
        )
        moved = (
            paired[:, :, :, :, fixed_len:]
            .transpose(1, 2, 3, 4, 0, 5)
            .reshape(seq_count * per * HEADS * slots, BLOCK * 2 * size)
        )
        ext = jnp.zeros((seq_count, piece_len + 2 * BLOCK, 2 * model), f32)
        for i in range(per):
            ext = ext.at[:, i * BLOCK : (i + 3) * BLOCK].add(fixed[:, i, : 3 * BLOCK])
        first = jnp.sum(fixed[:, :, 3 * BLOCK : 4 * BLOCK], 1)
        last = jnp.sum(fixed[:, :, 4 * BLOCK :], 1)
        rims = jnp.concatenate([ext[:, :BLOCK], ext[:, piece_len + BLOCK :]], 1)
        beside = with_halo(rims.astype(bf16), "seq", 1, BLOCK).astype(f32)
        kv_grad = ext[:, BLOCK : BLOCK + piece_len]
        kv_grad = kv_grad.at[:, :BLOCK].add(beside[:, :BLOCK])
        kv_grad = kv_grad.at[:, piece_len - BLOCK :].add(beside[:, 3 * BLOCK :])
        first, last = lax.psum((first, last), "seq")
        kv_grad = kv_grad.at[:, :BLOCK].add(jnp.where(position == 0, first, 0.0))
        kv_grad = kv_grad.at[:, piece_len - BLOCK :].add(
            jnp.where(position == splits - 1, last, 0.0)
        )
        cap = self.send.shape[0] // splits
        outgoing = left_product(self.arrival, moved.astype(bf16)).astype(bf16)
        returned = lax.all_to_all(
            outgoing.reshape(splits, cap, -1), "seq", 0, 0, tiled=True
        ).reshape(splits * cap, -1)
        kv_grad = kv_grad + (
            left_product(self.send, returned)
            .reshape(seq_count, per, HEADS, BLOCK, 2, size)
            .transpose(0, 1, 3, 4, 2, 5)
            .reshape(seq_count, piece_len, 2 * model)
        )
        kv_grad = kv_grad.reshape(row_count, 2 * model).astype(bf16)
        grad_query = grad_query.reshape(row_count, model).astype(bf16)
        grads = (grad_query, kv_grad[:, :model], kv_grad[:, model:])
        input_grad = grad_res
        shares = []
        for part, weight in zip(grads, self.weights):
            input_grad = input_grad + right_product(part, weight)
            full = left_product(hidden, part)
            share = lax.psum_scatter(full, "seq", scatter_dimension=0, tiled=True)
            shares.append(lax.psum(share.astype(bf16), "dp").astype(f32))
        biases = jnp.stack([jnp.sum(grads[i].astype(f32), 0) for i in (0, 2)], 1)
        biases = lax.psum_scatter(biases, "seq", scatter_dimension=0, tiled=True)
        biases = lax.psum(biases.astype(bf16), "dp").astype(f32)
        return input_grad, shares[0], biases[:, 0], shares[1], shares[2], biases[:, 1]


def local(
    hidden_in,
    query_weight,
    query_bias,
    key_weight,
    value_weight,
    value_bias,
    output_weight,
    output_bias,
    first_gain,
    first_shift,
    inner_weight,
    inner_bias,
    outer_weight,
    outer_bias,
    second_gain,
    second_shift,
    segments,
    random_blocks,
    cotangent,
):
    seq_count, piece_len, model = hidden_in.shape
    splits = lax.axis_size("seq")
    groups = lax.axis_size("dp")
    row_count = seq_count * piece_len
    rows = model // splits
    units = outer_weight.shape[0] // groups
    hidden = hidden_in.reshape(row_count, model)
    by_heads = (
        seq_count == 1 and groups == 4 and 2 < splits and HEADS % max(1, splits // 2) == 0
    )
    vec_local = jnp.concatenate(
        [
            v.reshape(-1, rows)
            for v in (
                query_bias,
                value_bias,
                output_bias,
                first_gain,
                first_shift,
                outer_bias,
                second_gain,
                second_shift,
                inner_bias,
            )
        ]
    )
    attention = (HeadAttention if by_heads else TokenAttention)(
        hidden,
        (query_weight, key_weight, value_weight),
        (query_bias, value_bias),
        segments,
        random_blocks,
        output_weight,
        vec_local,
    )
    attention.inner_weights(inner_weight, outer_weight)
    attended = attention.forward()
    vec = attention.vec
    w_out = attention.output_weight
    full = (row_count, model)
    wide = (groups * row_count, splits * units)
    low, normed, inverse = run_kernel(
        project_kernel,
        "project",
        [(full, bf16), (full, f32), ((row_count, 128), f32)],
        (w_out, hidden, vec, attended),
        flops=2 * row_count * model * model,
    )
    lows = exchange_all(low)
    work = 2 * wide[0] * wide[1] * model
    both = attention.both
    parts = run_kernel(
        functools.partial(forward_kernel, parts=groups),
        "forward",
        [(full, f32)] + [(full, bf16)] * (groups - 1) + [(wide, f32), (wide, bf16)],
        (vec, both, *lows),
        scratch=[
            pltpu.VMEM(both.shape, bf16),
            pltpu.VMEM((groups,) + full, bf16),
            pltpu.SemaphoreType.DMA((groups + 2,)),
        ],
        raw=range(1, 2 + groups),
        flops=2 * work,
        powers=wide[0] * wide[1],
        grant=10 << 20,
    )
    inner, act = parts[groups:]
    layer_out, grad_low, grad_mix, sums2 = run_kernel(
        middle_kernel,
        "middle",
        [(full, bf16), (full, bf16), (full, f32), ((8, model), f32)],
        (*exchange_parts(parts), normed, cotangent.reshape(row_count, model), vec),
    )
    grads = exchange_all(grad_low)
    parts = run_kernel(
        functools.partial(backward_kernel, parts=groups),
        "backward",
        [(full, f32)] + [(full, bf16)] * (groups - 1) + [(wide, bf16), ((1, wide[1]), f32)],
        (both, inner, *grads),
        flops=2 * work,
        powers=wide[0] * wide[1],
    )
    recv = exchange_parts(parts[:groups])
    (above,) = run_kernel(
        functools.partial(inner_outer_kernel, parts=groups),
        "inner_outer",
        [((splits, 2 * rows + 8, model), bf16)],
        (parts[groups], act, sums2, parts[groups + 1], *lows, *grads),
        flops=2 * work,
        grant=(1 if by_heads else 4) * VMEM_BYTES,
    )
    slots = attended.shape[0]
    below = rows + 8
    grad_res, stacked, *grad_att = run_kernel(
        functools.partial(residual_kernel, parts=groups, lined=by_heads),
        "residual",
        [(full, f32), ((splits, 3 * rows + 8, model), bf16)]
        + [(attended.shape[1:], bf16)] * slots,
        (grad_mix, normed, inverse, vec, w_out, attended, above, *recv),
        scratch=[
            pltpu.VMEM(full, f32),
            pltpu.VMEM(attended.shape, bf16),
            pltpu.VMEM((splits, below, model), bf16),
            pltpu.SemaphoreType.DMA((slots + 3,)),
        ],
        raw_outs=range(2 + slots),
        flops=4 * row_count * model * model,
        grant=2 * VMEM_BYTES,
    )
    share = lax.psum_scatter(stacked, "seq", scatter_dimension=0, tiled=False)
    if by_heads:
        grad_att = line_parts(grad_att)
    input_grad, gq, bias_q, gk, gv, bias_v = attention.backward(grad_att, grad_res, share)
    d_inner, d_outer, d_output, vectors = finish_inner(attention.shares, rows)
    norm_sums = vectors[groups]

    def cut(line, i):
        return line[i * rows : (i + 1) * rows]

    return (
        layer_out.reshape(seq_count, piece_len, model),
        input_grad.reshape(seq_count, piece_len, model),
        gq,
        bias_q,
        gk,
        gv,
        bias_v,
        d_output,
        cut(norm_sums, 6),
        cut(norm_sums, 4),
        cut(norm_sums, 5),
        d_inner,
        vectors[:groups, 3 * rows : 3 * rows + units].reshape(-1),
        d_outer,
        cut(norm_sums, 2),
        cut(norm_sums, 0),
        cut(norm_sums, 1),
    )


def solution(mesh):
    in_specs = (
        P("dp", "seq", None),
        P("seq", None),
        P("seq"),
        P("seq", None),
        P("seq", None),
        P("seq"),
        P("seq", None),
        P("seq"),
        P("seq"),
        P("seq"),
        P("seq", None),
        P("seq"),
        P("seq", None),
        P("seq"),
        P("seq"),
        P("seq"),
        P("dp", None),
        P("dp", None, None, None),
        P("dp", "seq", None),
    )
    out_specs = (
        P("dp", "seq", None),
        P("dp", "seq", None),
        P("seq", None),
        P("seq"),
        P("seq", None),
        P("seq", None),
        P("seq"),
        P("seq", None),
        P("seq"),
        P("seq"),
        P("seq"),
        P("seq", None),
        P("seq"),
        P("seq", None),
        P("seq"),
        P("seq"),
        P("seq"),
    )
    return jax.shard_map(local, mesh=mesh, in_specs=in_specs, out_specs=out_specs, check_vma=False)
```

```python
import functools

import jax
import jax.numpy as jnp
from jax import lax
from jax.experimental import pallas as pl
from jax.experimental.pallas import tpu as pltpu
from jax.sharding import PartitionSpec as P

HEADS = 12
BLOCK = 64
EPSILON = 1e-12
MASKED = -1000000000.0
GELU_A = 0.7978845608028654
GELU_B = 0.044715
VMEM_BYTES = 6 << 20
bf16 = jnp.bfloat16
f32 = jnp.float32


def matmul(left, right):
    return jnp.dot(left, right, preferred_element_type=f32)


def left_product(left, right):
    return lax.dot_general(left, right, (((0,), (0,)), ((), ())), preferred_element_type=f32)


def right_product(left, right):
    return lax.dot_general(left, right, (((1,), (1,)), ((), ())), preferred_element_type=f32)


def run_kernel(
    kernel, name, outs, args, scratch=(), scalars=0, raw=(), raw_outs=(), flops=0, powers=0, grant=VMEM_BYTES
):
    def spec(i, held):
        return pl.BlockSpec(memory_space=pltpu.MemorySpace.HBM if i in held else pltpu.VMEM)

    specs = [pl.BlockSpec(memory_space=pltpu.SMEM)] * scalars
    specs += [spec(i, raw) for i in range(scalars, len(args))]
    shapes = [jax.ShapeDtypeStruct(shape, dtype) for shape, dtype in outs]
    moved = sum(a.size * a.dtype.itemsize for a in (*args, *shapes))
    out_shape = tuple(pltpu.HBM(o.shape, o.dtype) if i in raw_outs else o for i, o in enumerate(shapes))
    args = [
        pltpu.with_memory_space_constraint(a, pltpu.HBM) if i in raw else a
        for i, a in enumerate(args)
    ]
    return pl.pallas_call(
        kernel,
        name=name,
        out_shape=out_shape,
        in_specs=specs,
        out_specs=tuple(spec(i, raw_outs) for i in range(len(outs))),
        scratch_shapes=list(scratch),
        compiler_params=pltpu.CompilerParams(vmem_limit_bytes=grant),
        cost_estimate=pl.CostEstimate(flops=flops, bytes_accessed=moved, transcendentals=powers),
    )(*args)


def normalize(values):
    center = values - jnp.mean(values, -1, keepdims=True)
    spread = jnp.mean(center * center, -1, keepdims=True)
    inverse = lax.rsqrt(spread + EPSILON)
    return center * inverse, inverse


def norm_back(grad, normed, inverse, gain):
    scaled = grad * gain
    return inverse * (
        scaled
        - jnp.mean(scaled, -1, keepdims=True)
        - normed * jnp.mean(scaled * normed, -1, keepdims=True)
    )


def bias_rows(be_ref, bn, same, head, block, blocks, block_len):
    width = same.shape[1]
    rows = [
        jnp.broadcast_to(be_ref[head * blocks + block + i : head * blocks + block + i + 1, :], (block_len, width))
        for i in range(same.shape[0] // block_len)
    ]
    return jnp.where(same, jnp.concatenate(rows, 0), bn)


def bias_rows(lines, bn, same):
    count, width = lines.shape
    length = same.shape[0] // count
    rows = [jnp.broadcast_to(lines[i : i + 1, :], (length, width)) for i in range(count)]
    return jnp.where(same, jnp.concatenate(rows, 0), bn)


def here():
    position = lax.axis_index("seq")
    return lax.rem(position, 2), lax.div(position, 2), lax.axis_index("dp")


def concat_kernel(*refs):
    out = refs[-1]
    at = 0
    for r in refs[:-1]:
        rows = r.shape[0]
        out[at : at + rows] = r[...]
        at += rows


def stack_kernel(*refs):
    for k, r in enumerate(refs[:-1]):
        refs[-1][k] = r[...]


def cut_kernel(wq, wk, wv, *refs):
    ids = here()
    outs = refs[:-3]
    raw, scratch, sems = refs[-3:]
    _, half, _ = raw.shape
    start = pl.multiple_of(lax.rem(ids[2], 2) * half, half)
    copies = [
        pltpu.make_async_copy(w.at[pl.ds(start, half), :], raw.at[i], sems.at[i])
        for i, w in enumerate((wq, wk, wv))
    ]
    for copy in copies:
        copy.start()
    for copy in copies:
        copy.wait()
    chips, _, wide = scratch.shape
    width = wide // 3
    for chip in range(chips):
        scratch[chip] = jnp.concatenate(
            [raw[i, :, chip * width : (chip + 1) * width] for i in range(3)], 1
        )
    for k, out in enumerate(outs):
        out[...] = scratch[ids[1] ^ k]


def assemble_kernel(mine, other, out):
    ids = here()
    core = ids[0]
    own = lax.rem(ids[2], 2)
    _, chips, _, _ = mine.shape
    for h in range(2):
        for k in range(chips):
            chip = ids[1] ^ k
            out[2 * chip + core, own ^ h] = mine[h, k]
            out[2 * chip + 1 - core, own ^ h] = other[h, k]


def cut_output_kernel(wo, vec, out):
    ids = here()
    half = wo.shape[0] // 2
    count, rows = vec.shape
    start = pl.multiple_of(lax.rem(lax.div(ids[2], 2), 2) * half, half)
    tall, model = out.shape
    each = model // rows
    out[:half, :] = wo[pl.ds(start, half), :]
    lines = []
    for first in range(0, count, each):
        parts = [vec[i : i + 1, :] for i in range(first, min(count, first + each))]
        parts += [jnp.zeros((1, rows), bf16)] * (each - len(parts))
        lines.append(jnp.concatenate(parts, 1))
    fill = jnp.zeros((tall - half - len(lines), model), bf16)
    out[half:, :] = jnp.concatenate(lines + [fill], 0)


def cut_inner_kernel(w1, w2, out, scratch):
    ids = here()
    groups, rows, model = scratch.shape
    units = w2.shape[0] // groups
    pieces = model // units
    for g in range(groups):
        scratch[g] = jnp.concatenate(
            [
                w1[:, (s * groups + g) * units : (s * groups + g + 1) * units]
                for s in range(pieces)
            ],
            1,
        )
    out[:rows, :] = scratch[ids[2]]
    out[rows:, :] = w2[pl.ds(pl.multiple_of(ids[2] * units, units), units), :]


def assemble_output_kernel(mine, other, out, vec, scratch):
    ids = here()
    core = ids[0]
    pieces, _, half, _ = out.shape
    chips = pieces // 2
    own = lax.rem(lax.div(ids[2], 2), 2)
    for k in range(chips):
        chip = ids[1] ^ k
        scratch[2 * chip + core] = mine[0, k, half:, :]
        scratch[2 * chip + 1 - core] = other[0, k, half:, :]
        for h in range(2):
            out[2 * chip + core, own ^ h] = mine[h, k, :half, :]
            out[2 * chip + 1 - core, own ^ h] = other[h, k, :half, :]
    rows = 2 * half
    each = vec.shape[1] // rows
    lines = [scratch[piece].astype(f32) for piece in range(pieces)]
    for i in range(vec.shape[0]):
        at, first = i // each, i % each * rows
        vec[i : i + 1, :] = jnp.concatenate(
            [line[at : at + 1, first : first + rows] for line in lines], 1
        )


def attend_kernel(w, be, bn, sk, sq, ours, theirs, hid_raw, *refs):
    ids = here()
    att = refs[0]
    kept = refs[1:5]
    hid, qo, ko, vo, lse, qs, s_all, p_all, sems = refs[5:]
    count = 2
    step = hid_raw.shape[0] // count
    loads = [
        pltpu.make_async_copy(
            hid_raw.at[pl.ds(i * step, step)], hid.at[pl.ds(i * step, step)], sems.at[4 + i]
        )
        for i in range(count)
    ]
    for load in loads:
        load.start()
    copies = [
        pltpu.make_async_copy(here, there, sems.at[i])
        for i, (here, there) in enumerate(zip((qo, ko, vo, lse), kept))
    ]
    pieces, piece_len, width = qs.shape
    chips = pieces // 2
    core = ids[0]
    size = 64
    heads = width // size
    model = hid.shape[2]
    ours, theirs = ours[...].astype(f32), theirs[...].astype(f32)
    first = jnp.where(core == 0, ours, theirs)
    second = jnp.where(core == 0, theirs, ours)
    biases = jnp.concatenate([first, second], 1)
    qb, vb = biases[0:1, :], biases[1:2, :]
    for i, load in enumerate(loads):
        load.wait()
        some = slice(i * step, (i + 1) * step)
        span = slice(i * step * piece_len, (i + 1) * step * piece_len)
        product = matmul(hid[some].reshape(step * piece_len, model), w[...])
        query = (product[:, :width] + qb).astype(bf16) * bf16(size**-0.5)
        qs[some] = query.reshape(step, piece_len, width)
        ko[span] = product[:, width : 2 * width].astype(bf16)
        vo[span] = (product[:, 2 * width :] + vb).astype(bf16)
    lane = lax.broadcasted_iota(jnp.int32, (piece_len, 128), 1)
    for k in range(chips):
        qo[k] = qs[2 * (ids[1] ^ k) + core]
    for copy in copies[:3]:
        copy.start()
    logs = [jnp.zeros((piece_len, 128), f32)] * chips
    parts = [[] for _ in range(chips)]
    for head in range(heads):
        cols = slice(head * size, (head + 1) * size)
        queries = qo[:, :, cols].reshape(chips * piece_len, size)
        s_all[...] = right_product(queries, ko[:, cols])
        shares = []
        for k in range(chips):
            chip = ids[1] ^ k
            rows = slice(k * piece_len, (k + 1) * piece_len)
            same = sq[chip] == sk[...]
            scores = s_all[rows, :] + bias_rows(be[head * chips + chip], bn[...], same)
            top = jnp.max(scores, -1, keepdims=True)
            powers = jnp.exp(scores - top)
            total = jnp.sum(powers, -1, keepdims=True)
            p_all[rows, :] = powers.astype(bf16)
            shares.append(1.0 / total)
            logs[k] = jnp.where(lane == head, top + jnp.log(total), logs[k])
        out = matmul(p_all[...], vo[:, cols])
        for k in range(chips):
            parts[k].append(out[k * piece_len : (k + 1) * piece_len] * shares[k])
    for k in range(chips):
        att[ids[1] ^ k] = jnp.concatenate(parts[k], 1).T.astype(bf16)
        lse[k] = logs[k]
    copies[3].start()
    for copy in copies:
        copy.wait()


def attend_back_kernel(hid_raw, q_raw, k_raw, v_raw, lse_raw, be, bn, sk, sq, *refs):
    ids = here()
    chips, piece_len, width = q_raw.shape
    ga_raw = refs[:chips]
    dq, mine, other, dw_mine, dw_other = refs[chips : chips + 5]
    hid, q, k, v, lse, ga, s_all, g_all, ds_all, p_all, dkv, dws, sems = refs[chips + 5 :]
    copies = [
        pltpu.make_async_copy(there, here, sems.at[i])
        for i, (there, here) in enumerate(
            zip((q_raw, k_raw, v_raw, lse_raw, hid_raw), (q, k, v, lse, hid))
        )
    ]
    copies[4:4] = [
        pltpu.make_async_copy(there, ga.at[i], sems.at[5 + i]) for i, there in enumerate(ga_raw)
    ]
    for copy in copies:
        copy.start()
    pieces = 2 * chips
    core = ids[0]
    size = 64
    heads = width // size
    dks = []
    dvs = []
    dqs = [[None] * heads for _ in range(chips)]
    for copy in copies[:-1]:
        copy.wait()
    gas = jnp.concatenate([ga[i].astype(f32).T.astype(bf16) for i in range(chips)], 0)
    for head in range(heads):
        cols = slice(head * size, (head + 1) * size)
        key = k[:, cols]
        value = v[:, cols]
        queries = q[:, :, cols].reshape(chips * piece_len, size)
        grads = gas[:, cols]
        s_all[...] = right_product(queries, key)
        g_all[...] = right_product(grads, value)
        for i in range(chips):
            chip = ids[1] ^ i
            rows = slice(i * piece_len, (i + 1) * piece_len)
            same = sq[chip] == sk[...]
            scores = s_all[rows, :] + bias_rows(be[head * chips + chip], bn[...], same)
            probs = jnp.exp(scores - lse[i, :, head : head + 1])
            grad = g_all[rows, :]
            weighted = jnp.sum(probs * grad, -1, keepdims=True)
            ds_all[rows, :] = (probs * (grad - weighted)).astype(bf16)
            p_all[rows, :] = probs.astype(bf16)
        grad_q = (matmul(ds_all[...], key) * (size**-0.5)).astype(bf16)
        for i in range(chips):
            dqs[i][head] = grad_q[i * piece_len : (i + 1) * piece_len]
        dks.append(left_product(ds_all[...], queries).astype(bf16))
        dvs.append(left_product(p_all[...], grads).astype(bf16))
    for i in range(chips):
        dq[i] = jnp.concatenate(dqs[i], 1)
    joined = jnp.concatenate(dks + dvs, 1)
    dkv[...] = joined.reshape(pieces, piece_len, 2 * width)
    for i in range(chips):
        chip = ids[1] ^ i
        mine[i] = dkv[2 * chip + core]
        other[i] = dkv[2 * chip + 1 - core]
    copies[-1].wait()
    _, _, model = hid.shape
    tokens = hid[...].reshape(pieces * piece_len, model)
    owned = jnp.concatenate([hid[2 * (ids[1] ^ i) + core] for i in range(chips)], 0)
    grad_q = dq[...].reshape(chips * piece_len, width)
    weights = jnp.concatenate([left_product(owned, grad_q), left_product(tokens, joined)], 1)
    groups = dw_mine.shape[0]
    rows = dws.shape[2]
    dws[...] = weights.reshape(dws.shape)
    for i in range(chips):
        chip = ids[1] ^ i
        for j in range(groups):
            span = slice(i * rows, (i + 1) * rows)
            dw_mine[j, span] = dws[2 * chip + core, ids[2] ^ j]
            dw_other[j, span] = dws[2 * chip + 1 - core, ids[2] ^ j].astype(bf16)
    total = jnp.concatenate(
        [
            jnp.sum(grad_q.astype(f32), 0, keepdims=True),
            jnp.sum(joined.astype(f32), 0, keepdims=True),
        ],
        1,
    )
    total = jnp.broadcast_to(total, (8, 3 * width))
    for j in range(groups):
        dw_mine[j, chips * rows :] = total
        dw_other[j, chips * rows :] = total.astype(bf16)


def input_grad_kernel(dq, mine, recv, w, out, scratch):
    ids = here()
    chips, piece_len, width = dq.shape
    dkv = (mine[...].astype(f32) + recv[...].astype(f32)).astype(bf16)
    grads = jnp.concatenate([dq[...], dkv], 2).reshape(chips * piece_len, 3 * width)
    total = right_product(grads, w[...])
    scratch[...] = total.astype(bf16).reshape(scratch.shape)
    for chip in range(chips):
        out[chip] = scratch[ids[1] ^ chip]


def add_kernel(left, right, out):
    out[...] = (left[...].astype(f32) + right[...].astype(f32)).astype(out.dtype)


def add_split_kernel(left, right, *outs):
    for k, out in enumerate(outs):
        out[...] = (left[k].astype(f32) + right[k].astype(f32)).astype(out.dtype)


def sum_split_kernel(*refs, parts, rows):
    total = refs[0][...].astype(f32)
    for r in refs[1:parts]:
        total = total + r[...].astype(f32)
    for k, out in enumerate(refs[parts:]):
        out[...] = total[k * rows : k * rows + out.shape[0]].astype(out.dtype)


def sum_lead_kernel(parts, *outs, rows):
    total = parts[0].astype(f32)
    for i in range(1, parts.shape[0]):
        total = total + parts[i].astype(f32)
    for k, out in enumerate(outs):
        out[...] = total[k * rows : k * rows + out.shape[0]].astype(out.dtype)


def project_kernel(wo, hid, vec, att, low, normed, inverse):
    branch = vec[2:3, :] + jnp.zeros(hid.shape, f32)
    for chip in range(att.shape[0]):
        branch = branch + left_product(att[chip], wo[chip])
    n1, r1 = normalize(hid[...].astype(f32) + branch)
    low[...] = (n1 * vec[3:4, :] + vec[4:5, :]).astype(bf16)
    normed[...] = n1
    inverse[...] = jnp.broadcast_to(r1, inverse.shape)


def gelu_parts(v):
    return jnp.tanh(GELU_A * (v + GELU_B * (v * v * v)))


def two_weights(both):
    pieces, rows, model = both.shape
    half = rows // 2
    first = both[:, :half, :].reshape(pieces * half, model)
    return first, both[:, half:, :].reshape(pieces * half, model)


def forward_kernel(vec, both_raw, *refs, parts):
    raw = refs[:parts]
    outs = refs[parts : 2 * parts]
    inner_ref, act_ref, both, x, sems = refs[2 * parts :]
    half = both.shape[1] // 2
    copies = [pltpu.make_async_copy(r, x.at[i], sems.at[i]) for i, r in enumerate(raw)]
    for i in range(2):
        span = (slice(None), pl.ds(i * half, half), slice(None))
        copies.append(pltpu.make_async_copy(both_raw.at[span], both.at[span], sems.at[parts + i]))
    for copy in copies:
        copy.start()
    for copy in copies[:-1]:
        copy.wait()
    _, rows, model = x.shape
    weight1 = both[:, :half, :].reshape(-1, model)
    inner = matmul(x[...].reshape(parts * rows, model), weight1) + vec[pl.ds(8 + lax.axis_index("dp"), 1), :]
    act = (0.5 * inner * (1.0 + gelu_parts(inner))).astype(bf16)
    inner_ref[...] = inner
    act_ref[...] = act
    copies[-1].wait()
    mixed = matmul(act, both[:, half:, :].reshape(-1, model))
    for i in range(parts):
        outs[i][...] = mixed[i * rows : (i + 1) * rows].astype(outs[i].dtype)


def middle_kernel(*refs):
    recv = refs[:-7]
    normed, cot, vec, out, low, mix, sums = refs[-7:]
    first = normed[...] * vec[3:4, :] + vec[4:5, :]
    mixed = vec[5:6, :]
    for r in recv:
        mixed = mixed + r[...].astype(f32)
    n2, r2 = normalize(first + mixed)
    gain = vec[6:7, :]
    out[...] = (n2 * gain + vec[7:8, :]).astype(bf16)
    g = cot[...].astype(f32)
    grad = norm_back(g, n2, r2, gain)
    rounded = grad.astype(bf16)
    mix[...] = grad
    low[...] = rounded
    sums[0:1, :] = jnp.sum(g * n2, 0, keepdims=True)
    sums[1:2, :] = jnp.sum(g, 0, keepdims=True)
    sums[2:3, :] = jnp.sum(rounded.astype(f32), 0, keepdims=True)
    sums[3:, :] = jnp.zeros((5, sums.shape[1]), f32)


def backward_kernel(both, inner_ref, *refs, parts):
    grads = refs[:parts]
    outs = refs[parts : 2 * parts]
    gi_ref, total = refs[2 * parts :]
    rows = grads[0].shape[0]
    weight1, weight2 = two_weights(both)
    gm = jnp.concatenate([r[...] for r in grads], 0)
    grad_act = right_product(gm, weight2)
    v = inner_ref[...]
    t = gelu_parts(v)
    slope = 0.5 * (1.0 + t) + 0.5 * v * (1.0 - t * t) * (GELU_A * (1.0 + 3.0 * GELU_B * (v * v)))
    gi = (grad_act * slope).astype(bf16)
    gi_ref[...] = gi
    first = right_product(gi, weight1)
    for i in range(parts):
        outs[i][...] = first[i * rows : (i + 1) * rows].astype(outs[i].dtype)
    total[...] = jnp.sum(gi.astype(f32), 0, keepdims=True)


def inner_outer_kernel(gi, act, sums, total, *refs, parts):
    x = refs[:parts]
    grads = refs[parts : 2 * parts]
    out = refs[2 * parts]
    pieces, tall, model = out.shape
    units = (tall - 8) // 2
    gm = jnp.concatenate([r[...] for r in grads], 0)
    tokens = jnp.concatenate([r[...] for r in x], 0)
    out[:, :units, :] = left_product(tokens, gi[...]).astype(bf16).reshape(pieces, units, model)
    out[:, units : 2 * units, :] = (
        left_product(act[...], gm).astype(bf16).reshape(pieces, units, model)
    )
    vectors = [sums[i : i + 1, :] for i in range(3)] + [total[...]]
    for piece in range(pieces):
        put_vectors(out, piece, piece, 2 * units, vectors, units)


def residual_kernel(mix, normed, inverse, vec, wo, att, above, *refs, parts, lined):
    ids = here() if lined else (0, 0, 0)
    recv = refs[:parts]
    res_raw, stacked = refs[parts : parts + 2]
    back_raw = refs[parts + 2 : -4]
    res, back, out, sems = refs[-4:]
    copies = []

    def send(here, there):
        copies.append(pltpu.make_async_copy(here, there, sems.at[len(copies)]))
        copies[-1].start()

    tall = above.shape[1] - 8
    send(above.at[:, pl.ds(0, tall), :], stacked.at[:, pl.ds(0, tall), :])
    first = mix[...]
    for r in recv:
        first = first + r[...].astype(f32)
    n1 = normed[...]
    grad = norm_back(first, n1, inverse[:, 0:1], vec[3:4, :])
    rounded = grad.astype(bf16)
    for k, raw in enumerate(back_raw):
        back[k] = right_product(wo[ids[1] ^ k], rounded).astype(bf16)
        send(back.at[k], raw)
    res[...] = grad
    send(res, res_raw)
    vectors = [jnp.zeros((1, wo.shape[2]), f32)] * 4 + [
        jnp.sum(first * n1, 0, keepdims=True),
        jnp.sum(first, 0, keepdims=True),
        jnp.sum(rounded.astype(f32), 0, keepdims=True),
    ]
    rows = out.shape[1] - 8
    each = out.shape[0] // att.shape[0]
    for chip in range(att.shape[0]):
        part = matmul(att[chip], rounded).astype(bf16)
        for i in range(each):
            piece = each * chip + i
            out[piece, 8:] = part[i * rows : (i + 1) * rows]
            put_vectors(out, piece, piece, 0, vectors, rows)
            out[piece, :8] = out[piece, :8] + above[piece, tall:]
    send(out, stacked.at[:, pl.ds(tall, rows + 8), :])
    for copy in copies:
        copy.wait()


def put_vectors(out, piece, at, row, vectors, rows):
    parts = [v[:, piece * rows : (piece + 1) * rows] for v in vectors]
    fill = out.shape[2] - rows * len(parts)
    line = jnp.concatenate(parts + [jnp.zeros((1, fill), f32)], 1)
    out[at, row : row + 8, :] = jnp.broadcast_to(line, (8, out.shape[2])).astype(bf16)


def finish_inner_kernel(*refs, parts, summed):
    ids = here()
    if summed:
        raws = refs[parts : parts + 2]
        inner, outer, output, vectors, total_ref, scratch, res, part, sems = refs[parts + 2 :]
        copies = [
            pltpu.make_async_copy(raw, held, sems.at[1 + i])
            for i, (raw, held) in enumerate(zip(raws, (res, part)))
        ]
        for copy in copies:
            copy.start()
    else:
        inner, outer, output, vectors, scratch, sems = refs[parts:]
    own = pltpu.make_async_copy(refs[0], scratch.at[ids[2]], sems.at[0])
    own.start()
    for k in range(1, parts):
        scratch[ids[2] ^ k] = refs[k][...]
    own.wait()
    rows = inner.shape[0]
    units = outer.shape[0] // parts
    pieces = scratch.shape[2] // units
    for piece in range(pieces):
        inner[:, piece * parts * units : (piece + 1) * parts * units] = jnp.concatenate(
            [
                scratch[g, :rows, piece * units : (piece + 1) * units].astype(f32)
                for g in range(parts)
            ],
            1,
        )
    total = jnp.zeros((1, scratch.shape[2]), f32)
    at = rows + units
    for g in range(parts):
        outer[g * units : (g + 1) * units, :] = scratch[g, rows:at, :].astype(f32)
        line = scratch[g, at : at + 8, :].astype(f32)[0:1]
        vectors[g : g + 1, :] = line
        total = total + line
    vectors[parts : parts + 1, :] = total
    if scratch.shape[1] > at + 8:
        last = scratch[0, at + 8 :, :].astype(f32)
        for g in range(1, parts):
            last = last + scratch[g, at + 8 :, :].astype(f32)
        output[...] = last
    if summed:
        for copy in copies:
            copy.wait()
        total_ref[...] = res[...] + part[...].astype(f32)


def finish_kernel(*refs):
    ids = here()
    parts = len(refs) - 4
    gq, gk, gv, scratch = refs[parts:]
    quarters, chips, rows, wide = scratch.shape
    for j, r in enumerate(refs[:parts]):
        for k in range(chips):
            scratch[ids[2] ^ j, ids[1] ^ k] = r[k]
    width = wide // 3
    for part in range(quarters):
        block = [scratch[part, chip].astype(f32) for chip in range(chips)]
        for i, out in enumerate((gq, gk, gv)):
            out[part * rows : (part + 1) * rows, :] = jnp.concatenate(
                [b[:, i * width : (i + 1) * width] for b in block], 1
            )


def log_counts(count):
    return jnp.where(count > 0, jnp.log(jnp.maximum(count, 1).astype(f32)), MASKED)


def exchange(array, k):
    count = lax.axis_size("dp")
    return lax.ppermute(array, "dp", [(i, i ^ k) for i in range(count)])


def exchange_all(array):
    return [array] + [exchange(array, k) for k in range(1, lax.axis_size("dp"))]


def exchange_parts(parts):
    return [parts[0]] + [exchange(parts[k], k) for k in range(1, lax.axis_size("dp"))]


def swap_cores(array):
    count = lax.axis_size("seq")
    return lax.ppermute(array, "seq", [(i, i ^ 1) for i in range(count)])


def line_exchange(array, k):
    count = lax.axis_size("seq")
    return lax.ppermute(array, "seq", [(i, i ^ (2 * k)) for i in range(count)])


def line_parts(parts):
    return [parts[0]] + [line_exchange(parts[k], k) for k in range(1, len(parts))]


def tied(value, *others):
    return lax.optimization_barrier((value,) + others)[0]


def add_split(left, right, outs):
    return run_kernel(add_split_kernel, "add", outs, (left, right))


def sum_split(arrays, outs):
    return run_kernel(
        functools.partial(sum_split_kernel, parts=len(arrays), rows=outs[0][0][0]),
        "sum",
        outs,
        tuple(arrays),
    )


def line_all(array):
    return [array] + [line_exchange(array, k) for k in range(1, lax.axis_size("seq") // 2)]


def along_line(array):
    count = lax.axis_size("seq")
    lines = [[2 * i + c for i in range(count // 2)] for c in range(2)]
    return lax.all_to_all(array, "seq", 0, 0, tiled=True, axis_index_groups=lines)


def stack(*arrays):
    shape = (len(arrays),) + arrays[0].shape
    return run_kernel(stack_kernel, "stack", [(shape, bf16)], arrays)[0]


def concat(*arrays):
    shape = (sum(a.shape[0] for a in arrays),) + arrays[0].shape[1:]
    return run_kernel(concat_kernel, "concat", [(shape, bf16)], arrays)[0]


def finish_inner(shares, rows, terms=()):
    groups = len(shares)
    share = shares[0]
    model = share.shape[1]
    outs = [
        ((rows, groups * model), f32),
        ((groups * rows, model), f32),
        ((rows, model), f32),
        ((8, model), f32),
    ]
    scratch = [pltpu.VMEM((groups,) + share.shape, bf16)]
    if terms:
        outs.append((terms[0].shape, f32))
        scratch += [pltpu.VMEM(t.shape, t.dtype) for t in terms]
    return run_kernel(
        functools.partial(finish_inner_kernel, parts=groups, summed=bool(terms)),
        "finish_inner",
        outs,
        (*shares, *terms),
        scratch=scratch + [pltpu.SemaphoreType.DMA((1 + len(terms),))],
        raw=(0, *range(groups, groups + len(terms))),
        grant=2 * VMEM_BYTES,
    )


class HeadAttention:
    def __init__(self, hidden, weights, biases, segments, random_blocks, output_weight, vec_local):
        self.splits = splits = lax.axis_size("seq")
        self.chips = chips = splits // 2
        self.position = position = lax.axis_index("seq")
        core = position % 2
        chip = position // 2
        group = lax.axis_index("dp")
        self.packed = lax.all_gather(hidden, "seq")
        piece_len, model = hidden.shape
        rows = model // splits
        width = model // chips
        heads = HEADS // chips
        half = rows // 2
        cut = run_kernel(
            cut_kernel,
            "cut",
            [((half, 3 * width), bf16)] * chips,
            tuple(weights),
            scratch=[
                pltpu.VMEM((3, half, model), bf16),
                pltpu.VMEM((chips, half, 3 * width), bf16),
                pltpu.SemaphoreType.DMA((3,)),
            ],
            raw=range(3),
        )
        cut = stack(*line_parts(cut))
        cut_next = exchange(cut, 1)
        (out_half,) = run_kernel(
            cut_output_kernel,
            "cut_output",
            [((half + 8, model), bf16)],
            (output_weight, vec_local),
        )
        cut = stack(cut, cut_next)
        (weight,) = run_kernel(
            assemble_kernel,
            "assemble",
            [((splits, 2, half, 3 * width), bf16)],
            (cut, swap_cores(cut)),
        )
        self.out_half = stack(*line_all(tied(out_half, cut_next)))
        self.out_next = exchange(self.out_half, 2)
        self.weight = weight.reshape(model, 3 * width)
        self.biases = biases
        self.hidden = hidden
        block_count = segments.shape[1] // BLOCK
        per_piece = piece_len // BLOCK
        own = random_blocks[0].reshape(chips, 2, per_piece, HEADS, -1)
        own = lax.dynamic_index_in_dim(own, core, 1, keepdims=False)
        own = lax.dynamic_slice_in_dim(own, chip * heads, heads, 2)
        own = own.reshape(chips * per_piece, heads, -1).transpose(1, 0, 2)
        block = jnp.arange(block_count, dtype=jnp.int32)
        mine = (
            (jnp.arange(chips, dtype=jnp.int32)[:, None] * 2 + core) * per_piece
            + jnp.arange(per_piece, dtype=jnp.int32)[None, :]
        ).reshape(-1)
        ends = ((block == 0) | (block == block_count - 1)).astype(jnp.int32)
        near = (jnp.abs(block[None, :] - mine[:, None]) <= 1).astype(jnp.int32)
        listed = jnp.sum((own[..., None] == block).astype(jnp.int32), 2)
        count = listed + near[None] + ends
        self.same_bias = jnp.repeat(log_counts(count), BLOCK, axis=2).reshape(
            heads * chips, per_piece, -1
        )
        self.other_bias = jnp.repeat(
            jnp.where(ends > 0, 0.0, MASKED).astype(f32)[None], BLOCK, axis=1
        )
        self.key_seg = segments
        self.query_seg = lax.dynamic_index_in_dim(
            segments.reshape(chips, 2, piece_len), core, 1, keepdims=False
        ).reshape(chips, piece_len, 1)
        self.piece_len, self.width, self.model = piece_len, width, model

    def masks(self):
        return (self.same_bias, self.other_bias, self.key_seg, self.query_seg)

    def inner_weights(self, inner_weight, outer_weight):
        groups = lax.axis_size("dp")
        rows = inner_weight.shape[0]
        units = outer_weight.shape[0] // groups
        (both,) = run_kernel(
            cut_inner_kernel,
            "cut_inner",
            [((rows + units, self.model), bf16)],
            (inner_weight, outer_weight),
            scratch=[pltpu.VMEM((groups, rows, self.model), bf16)],
        )
        self.pair = jnp.stack(self.biases, 0)
        self.pair_other = swap_cores(self.pair)
        self.both = lax.all_gather(tied(both, self.packed, self.weight, self.out_half), "seq")

    def forward(self):
        chips, piece_len, width, model = self.chips, self.piece_len, self.width, self.model
        tokens = self.splits * piece_len
        one = (chips, piece_len, width)
        kept = [
            (one, bf16),
            ((tokens, width), bf16),
            ((tokens, width), bf16),
            ((chips, piece_len, 128), f32),
        ]
        att, self.q, self.k, self.v, self.lse = run_kernel(
            attend_kernel,
            "attend",
            [((chips, width, piece_len), bf16)] + kept,
            (self.weight, *self.masks(), self.pair, self.pair_other, self.packed),
            scratch=[pltpu.VMEM(self.packed.shape, bf16)]
            + [pltpu.VMEM(*spec) for spec in kept]
            + [
                pltpu.VMEM((self.splits, piece_len, width), bf16),
                pltpu.VMEM((chips * piece_len, tokens), f32),
                pltpu.VMEM((chips * piece_len, tokens), bf16),
                pltpu.SemaphoreType.DMA((len(kept) + 2,)),
            ],
            raw=(7,),
            raw_outs=range(1, 1 + len(kept)),
            flops=6 * tokens * model * width + 2 * tokens * tokens * width,
            powers=tokens * tokens * 3 // 2,
            grant=16 << 20,
        )
        out_half = stack(tied(self.out_half, att), self.out_next)
        half = model // self.splits // 2
        weight, self.vec = run_kernel(
            assemble_output_kernel,
            "assemble_output",
            [((self.splits, 2, half, model), bf16), ((16, model), f32)],
            (out_half, swap_cores(out_half)),
            scratch=[pltpu.VMEM((self.splits, 8, model), bf16)],
        )
        self.output_weight = weight.reshape(chips, width, model)
        att = along_line(att)
        return att

    def backward(self, grads, grad_res, share):
        chips, piece_len, width = self.chips, self.piece_len, self.width
        splits, model = self.splits, self.model
        groups = lax.axis_size("dp")
        tokens = splits * piece_len
        rows = model // splits
        one = (chips, piece_len, width)
        two = (chips, piece_len, 2 * width)
        quarter = (rows // groups, 3 * width)
        group = (chips * quarter[0] + 8, 3 * width)
        wide = ((groups,) + group, bf16)
        keep = (self.packed, self.q, self.k, self.v, self.lse)
        dq, mine, other, dw_mine, dw_other = run_kernel(
            attend_back_kernel,
            "attend_back",
            [(one, bf16), (two, bf16), (two, bf16), (wide[0], f32), wide],
            keep + self.masks() + tuple(grads),
            scratch=[pltpu.VMEM(a.shape, a.dtype) for a in keep]
            + [
                pltpu.VMEM((chips,) + grads[0].shape, bf16),
                pltpu.VMEM((chips * piece_len, tokens), f32),
                pltpu.VMEM((chips * piece_len, tokens), f32),
                pltpu.VMEM((chips * piece_len, tokens), bf16),
                pltpu.VMEM((chips * piece_len, tokens), bf16),
                pltpu.VMEM((splits, piece_len, 2 * width), bf16),
                pltpu.VMEM((splits, groups) + quarter, f32),
                pltpu.SemaphoreType.DMA((len(keep) + chips,)),
            ],
            raw=(*range(5), *range(9, 9 + chips)),
            flops=5 * tokens * tokens * width + 6 * tokens * model * width,
            powers=tokens * tokens * 3 // 2,
            grant=24 << 20,
        )
        recv = swap_cores(other)
        dws = add_split(dw_mine, swap_cores(dw_other), [(group, bf16)] * groups)
        dws = exchange_parts(dws)
        full = (piece_len, model)
        *dws, sums = sum_split(dws, [(quarter, bf16)] * chips + [((8, 3 * width), f32)])
        dq = tied(dq, dws[0])
        (partial,) = run_kernel(
            input_grad_kernel,
            "input_grad",
            [((chips,) + full, bf16)],
            (dq, mine, recv, self.weight),
            scratch=[pltpu.VMEM((chips,) + full, bf16)],
            flops=3 * tokens * model * width,
        )
        dws = line_parts(dws)
        part = (chips,) + quarter
        dw = stack(*dws)
        every = exchange_all(dw)
        self.shares = exchange_all(tied(share, *every[1:]))
        count = splits
        lines = [[2 * i + c for i in range(count // 2)] for c in range(2)]
        partial = lax.psum_scatter(
            partial, "seq", scatter_dimension=0, axis_index_groups=lines, tiled=False
        )
        gq, gk, gv = run_kernel(
            finish_kernel,
            "finish",
            [((rows, model), f32)] * 3,
            tuple(every),
            scratch=[pltpu.VMEM((groups,) + part, bf16)],
        )
        *self.finished, input_grad = finish_inner(self.shares, rows, (grad_res, partial))
        core = self.position % 2
        bias_q = lax.dynamic_slice_in_dim(sums[0], core * rows, rows)
        bias_v = lax.dynamic_slice_in_dim(sums[0], 2 * width + core * rows, rows)
        return input_grad, gq, bias_q, gk, gv, bias_v


def one_hot(index, count):
    return (index[..., None] == jnp.arange(count, dtype=jnp.int32)).astype(bf16)


def with_halo(block, axis, dim, width):
    count = lax.axis_size(axis)
    forward = [(i, i + 1) for i in range(count - 1)]
    backward = [(target, source) for source, target in forward]
    low = lax.ppermute(
        lax.slice_in_dim(block, block.shape[dim] - width, None, axis=dim), axis, forward
    )
    high = lax.ppermute(lax.slice_in_dim(block, 0, width, axis=dim), axis, backward)
    return jnp.concatenate([low, block, high], axis=dim)


def broadcast(block, axis, owner):
    block = jnp.where(lax.axis_index(axis) == owner, block, jnp.zeros_like(block))
    return lax.psum(block, axis)


class TokenAttention:
    def __init__(self, hidden, weights, biases, segments, random_blocks, output_weight, vec_local):
        self.splits = splits = lax.axis_size("seq")
        self.position = position = lax.axis_index("seq")
        self.hidden = hidden
        self.segments = segments
        self.random_blocks = random_blocks
        self.weights = [lax.all_gather(w, "seq", axis=0, tiled=True) for w in weights]
        self.output_weight = lax.all_gather(output_weight, "seq", axis=0, tiled=True)[None]
        vec = lax.all_gather(vec_local, "seq")
        self.vec = vec.transpose(1, 0, 2).reshape(vec_local.shape[0], -1).astype(f32)

    def forward(self):
        hidden, segments = self.hidden, self.segments
        splits, position = self.splits, self.position
        seq_count = segments.shape[0]
        row_count, model = hidden.shape
        piece_len = row_count // seq_count
        size = model // HEADS
        per = piece_len // BLOCK
        slots = self.random_blocks.shape[3]
        reqs = seq_count * per * HEADS * slots
        cap = max(2, 3 * reqs // (2 * splits) + 1)
        vec = self.vec
        wq, wk, wv = self.weights
        query = (matmul(hidden, wq) + vec[0:1]).astype(bf16)
        keys = matmul(hidden, wk).astype(bf16)
        values = (matmul(hidden, wv) + vec[1:2]).astype(bf16)
        joined = jnp.concatenate([keys, values], 1).reshape(seq_count, piece_len, 2 * model)
        extended = with_halo(joined, "seq", 1, BLOCK)
        first = broadcast(joined[:, :BLOCK], "seq", 0)
        last = broadcast(joined[:, piece_len - BLOCK :], "seq", splits - 1)
        tiles = seq_count * per * HEADS
        tile_size = BLOCK * 2 * size
        kv_tiles = (
            joined.reshape(seq_count, per, BLOCK, 2, HEADS, size)
            .transpose(0, 1, 4, 2, 3, 5)
            .reshape(tiles, tile_size)
        )
        req = jnp.arange(reqs, dtype=jnp.int32)
        req_seq = req // (per * HEADS * slots)
        req_head = req // slots % HEADS
        earlier = (req[:, None] > req[None, :]).astype(jnp.int32)
        everyone = (
            self.random_blocks.reshape(seq_count, splits, per, HEADS, slots)
            .transpose(1, 0, 2, 3, 4)
            .reshape(splits, reqs)
        )
        is_mine = (everyone // per == position).astype(jnp.int32)
        place = jnp.sum(is_mine[:, None, :] * earlier, 2)
        slot = jnp.where(is_mine == 1, place, cap)
        tile_of = (req_seq * per + everyone % per) * HEADS + req_head
        chosen = slot[:, :, None] == jnp.arange(cap, dtype=jnp.int32)
        send = jnp.sum(jnp.where(chosen, tile_of[:, :, None], 0), 1).reshape(splits * cap)
        self.send = one_hot(send, tiles)
        outgoing = matmul(self.send, kv_tiles).astype(bf16).reshape(splits, cap, tile_size)
        incoming = lax.all_to_all(outgoing, "seq", 0, 0, tiled=True)
        asked = lax.dynamic_slice_in_dim(self.random_blocks, position * per, per, 1)
        owner = asked.reshape(reqs) // per
        before = jnp.sum((owner[:, None] == owner[None, :]).astype(jnp.int32) * earlier, 1)
        self.arrival = one_hot(owner * cap + before, splits * cap)
        fetched = matmul(self.arrival, incoming.reshape(splits * cap, tile_size)).astype(bf16)
        moved = fetched.reshape(seq_count, per, HEADS, slots * BLOCK, 2, size)
        spans = [slice(i * BLOCK, (i + 3) * BLOCK) for i in range(per)]
        fixed = jnp.stack(
            [jnp.concatenate([extended[:, span], first, last], 1) for span in spans], 1
        )
        fixed = fixed.reshape(seq_count, per, 5 * BLOCK, 2, HEADS, size)
        paired = jnp.concatenate(
            [fixed.transpose(3, 0, 1, 4, 2, 5), moved.transpose(4, 0, 1, 2, 3, 5)], 4
        )
        self.keys, self.values = paired[0], paired[1]
        edge = jnp.full((seq_count, BLOCK), -1, jnp.int32)
        padded = jnp.concatenate([edge, segments, edge], 1)
        query_seg = lax.dynamic_slice_in_dim(segments, position * piece_len, piece_len, 1)
        ext_seg = lax.dynamic_slice_in_dim(padded, position * piece_len, piece_len + 2 * BLOCK, 1)
        always = jnp.full((seq_count, 2 * BLOCK), -2, jnp.int32)
        seg_fixed = jnp.stack(
            [jnp.concatenate([ext_seg[:, span], always], 1) for span in spans], 1
        )
        seg_fixed = jnp.broadcast_to(
            seg_fixed[:, :, None], (seq_count, per, HEADS, 5 * BLOCK)
        )
        seg_blocks = segments.reshape(seq_count, -1, BLOCK)
        asked_hot = one_hot(asked, seg_blocks.shape[1])
        seg_moved = jnp.einsum(
            "gjhrb,gbt->gjhrt", asked_hot, seg_blocks.astype(bf16), preferred_element_type=f32
        ).astype(jnp.int32)
        key_seg = jnp.concatenate(
            [seg_fixed, seg_moved.reshape(seq_count, per, HEADS, slots * BLOCK)], 3
        )[:, :, :, None, :]
        self.allowed = (
            query_seg.reshape(seq_count, per, 1, BLOCK, 1) == key_seg
        ) | (key_seg == -2)
        self.query = query.reshape(seq_count, per, BLOCK, HEADS, size)
        scores = self.scores()
        top = jnp.max(scores, -1, keepdims=True)
        powers = jnp.exp(scores - top)
        total = jnp.sum(powers, -1, keepdims=True)
        self.log_total = top + jnp.log(total)
        attended = jnp.einsum(
            "gjhqk,gjhke->gjqhe",
            (powers / total).astype(bf16),
            self.values,
            preferred_element_type=f32,
        )
        return attended.astype(bf16).reshape(row_count, model).T[None]

    def scores(self):
        raw = jnp.einsum("gjqhe,gjhke->gjhqk", self.query, self.keys, preferred_element_type=f32)
        return jnp.where(self.allowed, raw * self.query.shape[-1] ** -0.5, MASKED)

    def inner_weights(self, inner_weight, outer_weight):
        splits = self.splits
        groups, group = lax.axis_size("dp"), lax.axis_index("dp")
        rows = inner_weight.shape[0]
        units, model = outer_weight.shape[0] // groups, outer_weight.shape[1]
        inner = inner_weight.reshape(rows, splits, groups, units)
        outer = outer_weight.reshape(groups, units, model)
        inner = lax.dynamic_index_in_dim(inner, group, 2, keepdims=False).reshape(rows, model)
        outer = lax.dynamic_index_in_dim(outer, group, 0, keepdims=False)
        both = lax.all_gather(jnp.concatenate([inner, outer], 0), "seq")
        both = both.reshape(splits, 2, rows, model).transpose(1, 0, 2, 3)
        self.both = both.reshape(1, 2 * model, model)

    def backward(self, grads, grad_res, share):
        hidden = self.hidden
        grad = grads[0].T
        self.finished = finish_inner(exchange_all(share), hidden.shape[1] // self.splits)
        splits, position = self.splits, self.position
        seq_count, per, _, _, size = self.query.shape
        row_count, model = hidden.shape
        piece_len = per * BLOCK
        slots = self.random_blocks.shape[3]
        scale = size**-0.5
        probs = jnp.exp(self.scores() - self.log_total)
        grad_split = grad.reshape(seq_count, per, BLOCK, HEADS, size)
        grad_probs = jnp.einsum(
            "gjqhe,gjhke->gjhqk", grad_split, self.values, preferred_element_type=f32
        )
        weighted = jnp.sum(probs * grad_probs, -1, keepdims=True)
        grad_scores = (probs * (grad_probs - weighted)).astype(bf16)
        grad_query = (
            jnp.einsum("gjhqk,gjhke->gjqhe", grad_scores, self.keys, preferred_element_type=f32)
            * scale
        )
        grad_key = (
            jnp.einsum("gjhqk,gjqhe->gjhke", grad_scores, self.query, preferred_element_type=f32)
            * scale
        )
        grad_value = jnp.einsum(
            "gjhqk,gjqhe->gjhke", probs.astype(bf16), grad_split, preferred_element_type=f32
        )
        paired = jnp.stack([grad_key, grad_value], 0)
        fixed_len = 5 * BLOCK
        fixed = (
            paired[:, :, :, :, :fixed_len]
            .transpose(1, 2, 4, 0, 3, 5)
            .reshape(seq_count, per, fixed_len, 2 * model)
        )
        moved = (
            paired[:, :, :, :, fixed_len:]
            .transpose(1, 2, 3, 4, 0, 5)
            .reshape(seq_count * per * HEADS * slots, BLOCK * 2 * size)
        )
        ext = jnp.zeros((seq_count, piece_len + 2 * BLOCK, 2 * model), f32)
        for i in range(per):
            ext = ext.at[:, i * BLOCK : (i + 3) * BLOCK].add(fixed[:, i, : 3 * BLOCK])
        first = jnp.sum(fixed[:, :, 3 * BLOCK : 4 * BLOCK], 1)
        last = jnp.sum(fixed[:, :, 4 * BLOCK :], 1)
        rims = jnp.concatenate([ext[:, :BLOCK], ext[:, piece_len + BLOCK :]], 1)
        beside = with_halo(rims.astype(bf16), "seq", 1, BLOCK).astype(f32)
        kv_grad = ext[:, BLOCK : BLOCK + piece_len]
        kv_grad = kv_grad.at[:, :BLOCK].add(beside[:, :BLOCK])
        kv_grad = kv_grad.at[:, piece_len - BLOCK :].add(beside[:, 3 * BLOCK :])
        first, last = lax.psum((first, last), "seq")
        kv_grad = kv_grad.at[:, :BLOCK].add(jnp.where(position == 0, first, 0.0))
        kv_grad = kv_grad.at[:, piece_len - BLOCK :].add(
            jnp.where(position == splits - 1, last, 0.0)
        )
        cap = self.send.shape[0] // splits
        outgoing = left_product(self.arrival, moved.astype(bf16)).astype(bf16)
        returned = lax.all_to_all(
            outgoing.reshape(splits, cap, -1), "seq", 0, 0, tiled=True
        ).reshape(splits * cap, -1)
        kv_grad = kv_grad + (
            left_product(self.send, returned)
            .reshape(seq_count, per, HEADS, BLOCK, 2, size)
            .transpose(0, 1, 3, 4, 2, 5)
            .reshape(seq_count, piece_len, 2 * model)
        )
        kv_grad = kv_grad.reshape(row_count, 2 * model).astype(bf16)
        grad_query = grad_query.reshape(row_count, model).astype(bf16)
        grads = (grad_query, kv_grad[:, :model], kv_grad[:, model:])
        input_grad = grad_res
        shares = []
        for part, weight in zip(grads, self.weights):
            input_grad = input_grad + right_product(part, weight)
            full = left_product(hidden, part)
            share = lax.psum_scatter(full, "seq", scatter_dimension=0, tiled=True)
            shares.append(lax.psum(share.astype(bf16), "dp").astype(f32))
        biases = jnp.stack([jnp.sum(grads[i].astype(f32), 0) for i in (0, 2)], 1)
        biases = lax.psum_scatter(biases, "seq", scatter_dimension=0, tiled=True)
        biases = lax.psum(biases.astype(bf16), "dp").astype(f32)
        return input_grad, shares[0], biases[:, 0], shares[1], shares[2], biases[:, 1]


def local(
    hidden_in,
    query_weight,
    query_bias,
    key_weight,
    value_weight,
    value_bias,
    output_weight,
    output_bias,
    first_gain,
    first_shift,
    inner_weight,
    inner_bias,
    outer_weight,
    outer_bias,
    second_gain,
    second_shift,
    segments,
    random_blocks,
    cotangent,
):
    seq_count, piece_len, model = hidden_in.shape
    splits = lax.axis_size("seq")
    groups = lax.axis_size("dp")
    row_count = seq_count * piece_len
    rows = model // splits
    units = outer_weight.shape[0] // groups
    hidden = hidden_in.reshape(row_count, model)
    by_heads = (
        seq_count == 1 and groups == 4 and 2 < splits and HEADS % max(1, splits // 2) == 0
    )
    vec_local = jnp.concatenate(
        [
            v.reshape(-1, rows)
            for v in (
                query_bias,
                value_bias,
                output_bias,
                first_gain,
                first_shift,
                outer_bias,
                second_gain,
                second_shift,
                inner_bias,
            )
        ]
    )
    attention = (HeadAttention if by_heads else TokenAttention)(
        hidden,
        (query_weight, key_weight, value_weight),
        (query_bias, value_bias),
        segments,
        random_blocks,
        output_weight,
        vec_local,
    )
    attention.inner_weights(inner_weight, outer_weight)
    attended = attention.forward()
    vec = attention.vec
    w_out = attention.output_weight
    full = (row_count, model)
    wide = (groups * row_count, splits * units)
    low, normed, inverse = run_kernel(
        project_kernel,
        "project",
        [(full, bf16), (full, f32), ((row_count, 128), f32)],
        (w_out, hidden, vec, attended),
        flops=2 * row_count * model * model,
    )
    lows = exchange_all(low)
    work = 2 * wide[0] * wide[1] * model
    both = attention.both
    parts = run_kernel(
        functools.partial(forward_kernel, parts=groups),
        "forward",
        [(full, f32)] + [(full, bf16)] * (groups - 1) + [(wide, f32), (wide, bf16)],
        (vec, both, *lows),
        scratch=[
            pltpu.VMEM(both.shape, bf16),
            pltpu.VMEM((groups,) + full, bf16),
            pltpu.SemaphoreType.DMA((groups + 2,)),
        ],
        raw=range(1, 2 + groups),
        flops=2 * work,
        powers=wide[0] * wide[1],
        grant=10 << 20,
    )
    inner, act = parts[groups:]
    layer_out, grad_low, grad_mix, sums2 = run_kernel(
        middle_kernel,
        "middle",
        [(full, bf16), (full, bf16), (full, f32), ((8, model), f32)],
        (*exchange_parts(parts), normed, cotangent.reshape(row_count, model), vec),
    )
    grads = exchange_all(grad_low)
    parts = run_kernel(
        functools.partial(backward_kernel, parts=groups),
        "backward",
        [(full, f32)] + [(full, bf16)] * (groups - 1) + [(wide, bf16), ((1, wide[1]), f32)],
        (both, inner, *grads),
        flops=2 * work,
        powers=wide[0] * wide[1],
    )
    recv = exchange_parts(parts[:groups])
    (above,) = run_kernel(
        functools.partial(inner_outer_kernel, parts=groups),
        "inner_outer",
        [((splits, 2 * rows + 8, model), bf16)],
        (parts[groups], act, sums2, parts[groups + 1], *lows, *grads),
        flops=2 * work,
        grant=(1 if by_heads else 4) * VMEM_BYTES,
    )
    slots = attended.shape[0]
    below = rows + 8
    grad_res, stacked, *grad_att = run_kernel(
        functools.partial(residual_kernel, parts=groups, lined=by_heads),
        "residual",
        [(full, f32), ((splits, 3 * rows + 8, model), bf16)]
        + [(attended.shape[1:], bf16)] * slots,
        (grad_mix, normed, inverse, vec, w_out, attended, above, *recv),
        scratch=[
            pltpu.VMEM(full, f32),
            pltpu.VMEM(attended.shape, bf16),
            pltpu.VMEM((splits, below, model), bf16),
            pltpu.SemaphoreType.DMA((slots + 3,)),
        ],
        raw_outs=range(2 + slots),
        flops=4 * row_count * model * model,
        grant=2 * VMEM_BYTES,
    )
    share = lax.psum_scatter(stacked, "seq", scatter_dimension=0, tiled=False)
    if by_heads:
        grad_att = line_parts(grad_att)
    input_grad, gq, bias_q, gk, gv, bias_v = attention.backward(grad_att, grad_res, share)
    d_inner, d_outer, d_output, vectors = attention.finished
    norm_sums = vectors[groups]

    def cut(line, i):
        return line[i * rows : (i + 1) * rows]

    return (
        layer_out.reshape(seq_count, piece_len, model),
        input_grad.reshape(seq_count, piece_len, model),
        gq,
        bias_q,
        gk,
        gv,
        bias_v,
        d_output,
        cut(norm_sums, 6),
        cut(norm_sums, 4),
        cut(norm_sums, 5),
        d_inner,
        vectors[:groups, 3 * rows : 3 * rows + units].reshape(-1),
        d_outer,
        cut(norm_sums, 2),
        cut(norm_sums, 0),
        cut(norm_sums, 1),
    )


def solution(mesh):
    in_specs = (
        P("dp", "seq", None),
        P("seq", None),
        P("seq"),
        P("seq", None),
        P("seq", None),
        P("seq"),
        P("seq", None),
        P("seq"),
        P("seq"),
        P("seq"),
        P("seq", None),
        P("seq"),
        P("seq", None),
        P("seq"),
        P("seq"),
        P("seq"),
        P("dp", None),
        P("dp", None, None, None),
        P("dp", "seq", None),
    )
    out_specs = (
        P("dp", "seq", None),
        P("dp", "seq", None),
        P("seq", None),
        P("seq"),
        P("seq", None),
        P("seq", None),
        P("seq"),
        P("seq", None),
        P("seq"),
        P("seq"),
        P("seq"),
        P("seq", None),
        P("seq"),
        P("seq", None),
        P("seq"),
        P("seq"),
        P("seq"),
    )
    return jax.shard_map(local, mesh=mesh, in_specs=in_specs, out_specs=out_specs, check_vma=False)
```

```python
import functools

import jax
import jax.numpy as jnp
from jax import lax
from jax.experimental import pallas as pl
from jax.experimental.pallas import tpu as pltpu
from jax.sharding import PartitionSpec as P

HEADS = 12
BLOCK = 64
EPSILON = 1e-12
MASKED = -1000000000.0
GELU_A = 0.7978845608028654
GELU_B = 0.044715
VMEM_BYTES = 6 << 20
bf16 = jnp.bfloat16
f32 = jnp.float32


def matmul(left, right):
    return jnp.dot(left, right, preferred_element_type=f32)


def left_product(left, right):
    return lax.dot_general(left, right, (((0,), (0,)), ((), ())), preferred_element_type=f32)


def right_product(left, right):
    return lax.dot_general(left, right, (((1,), (1,)), ((), ())), preferred_element_type=f32)


def run_kernel(
    kernel, name, outs, args, scratch=(), scalars=0, raw=(), raw_outs=(), flops=0, powers=0, grant=VMEM_BYTES
):
    def spec(i, held):
        return pl.BlockSpec(memory_space=pltpu.MemorySpace.HBM if i in held else pltpu.VMEM)

    specs = [pl.BlockSpec(memory_space=pltpu.SMEM)] * scalars
    specs += [spec(i, raw) for i in range(scalars, len(args))]
    shapes = [jax.ShapeDtypeStruct(shape, dtype) for shape, dtype in outs]
    moved = sum(a.size * a.dtype.itemsize for a in (*args, *shapes))
    out_shape = tuple(pltpu.HBM(o.shape, o.dtype) if i in raw_outs else o for i, o in enumerate(shapes))
    args = [
        pltpu.with_memory_space_constraint(a, pltpu.HBM) if i in raw else a
        for i, a in enumerate(args)
    ]
    return pl.pallas_call(
        kernel,
        name=name,
        out_shape=out_shape,
        in_specs=specs,
        out_specs=tuple(spec(i, raw_outs) for i in range(len(outs))),
        scratch_shapes=list(scratch),
        compiler_params=pltpu.CompilerParams(vmem_limit_bytes=grant),
        cost_estimate=pl.CostEstimate(flops=flops, bytes_accessed=moved, transcendentals=powers),
    )(*args)


def normalize(values):
    center = values - jnp.mean(values, -1, keepdims=True)
    spread = jnp.mean(center * center, -1, keepdims=True)
    inverse = lax.rsqrt(spread + EPSILON)
    return center * inverse, inverse


def norm_back(grad, normed, inverse, gain):
    scaled = grad * gain
    return inverse * (
        scaled
        - jnp.mean(scaled, -1, keepdims=True)
        - normed * jnp.mean(scaled * normed, -1, keepdims=True)
    )


def bias_rows(be_ref, bn, same, head, block, blocks, block_len):
    width = same.shape[1]
    rows = [
        jnp.broadcast_to(be_ref[head * blocks + block + i : head * blocks + block + i + 1, :], (block_len, width))
        for i in range(same.shape[0] // block_len)
    ]
    return jnp.where(same, jnp.concatenate(rows, 0), bn)


def bias_rows(lines, bn, same):
    count, width = lines.shape
    length = same.shape[0] // count
    rows = [jnp.broadcast_to(lines[i : i + 1, :], (length, width)) for i in range(count)]
    return jnp.where(same, jnp.concatenate(rows, 0), bn)


def here():
    position = lax.axis_index("seq")
    return lax.rem(position, 2), lax.div(position, 2), lax.axis_index("dp")


def concat_kernel(*refs):
    out = refs[-1]
    at = 0
    for r in refs[:-1]:
        rows = r.shape[0]
        out[at : at + rows] = r[...]
        at += rows


def stack_kernel(*refs):
    for k, r in enumerate(refs[:-1]):
        refs[-1][k] = r[...]


def cut_kernel(wq, wk, wv, *refs):
    ids = here()
    outs = refs[:-3]
    raw, scratch, sems = refs[-3:]
    _, half, _ = raw.shape
    start = pl.multiple_of(lax.rem(ids[2], 2) * half, half)
    copies = [
        pltpu.make_async_copy(w.at[pl.ds(start, half), :], raw.at[i], sems.at[i])
        for i, w in enumerate((wq, wk, wv))
    ]
    for copy in copies:
        copy.start()
    for copy in copies:
        copy.wait()
    chips, _, wide = scratch.shape
    width = wide // 3
    for chip in range(chips):
        scratch[chip] = jnp.concatenate(
            [raw[i, :, chip * width : (chip + 1) * width] for i in range(3)], 1
        )
    for k, out in enumerate(outs):
        out[...] = scratch[ids[1] ^ k]


def assemble_kernel(mine, other, out):
    ids = here()
    core = ids[0]
    own = lax.rem(ids[2], 2)
    _, chips, _, _ = mine.shape
    for h in range(2):
        for k in range(chips):
            chip = ids[1] ^ k
            out[2 * chip + core, own ^ h] = mine[h, k]
            out[2 * chip + 1 - core, own ^ h] = other[h, k]


def cut_output_kernel(wo, vec, out):
    ids = here()
    half = wo.shape[0] // 2
    count, rows = vec.shape
    start = pl.multiple_of(lax.rem(lax.div(ids[2], 2), 2) * half, half)
    tall, model = out.shape
    each = model // rows
    out[:half, :] = wo[pl.ds(start, half), :]
    lines = []
    for first in range(0, count, each):
        parts = [vec[i : i + 1, :] for i in range(first, min(count, first + each))]
        parts += [jnp.zeros((1, rows), bf16)] * (each - len(parts))
        lines.append(jnp.concatenate(parts, 1))
    fill = jnp.zeros((tall - half - len(lines), model), bf16)
    out[half:, :] = jnp.concatenate(lines + [fill], 0)


def cut_inner_kernel(w1, w2, out, scratch):
    ids = here()
    groups, rows, model = scratch.shape
    units = w2.shape[0] // groups
    pieces = model // units
    for g in range(groups):
        scratch[g] = jnp.concatenate(
            [
                w1[:, (s * groups + g) * units : (s * groups + g + 1) * units]
                for s in range(pieces)
            ],
            1,
        )
    out[:rows, :] = scratch[ids[2]]
    out[rows:, :] = w2[pl.ds(pl.multiple_of(ids[2] * units, units), units), :]


def assemble_output_kernel(mine, other, out, vec, scratch):
    ids = here()
    core = ids[0]
    pieces, _, half, _ = out.shape
    chips = pieces // 2
    own = lax.rem(lax.div(ids[2], 2), 2)
    for k in range(chips):
        chip = ids[1] ^ k
        scratch[2 * chip + core] = mine[0, k, half:, :]
        scratch[2 * chip + 1 - core] = other[0, k, half:, :]
        for h in range(2):
            out[2 * chip + core, own ^ h] = mine[h, k, :half, :]
            out[2 * chip + 1 - core, own ^ h] = other[h, k, :half, :]
    rows = 2 * half
    each = vec.shape[1] // rows
    lines = [scratch[piece].astype(f32) for piece in range(pieces)]
    for i in range(vec.shape[0]):
        at, first = i // each, i % each * rows
        vec[i : i + 1, :] = jnp.concatenate(
            [line[at : at + 1, first : first + rows] for line in lines], 1
        )


def attend_kernel(w, be, bn, sk, sq, ours, theirs, hid_raw, *refs):
    ids = here()
    att = refs[0]
    kept = refs[1:5]
    hid, qo, ko, vo, lse, qs, s_all, p_all, sems = refs[5:]
    count = 2
    step = hid_raw.shape[0] // count
    loads = [
        pltpu.make_async_copy(
            hid_raw.at[pl.ds(i * step, step)], hid.at[pl.ds(i * step, step)], sems.at[4 + i]
        )
        for i in range(count)
    ]
    for load in loads:
        load.start()
    copies = [
        pltpu.make_async_copy(here, there, sems.at[i])
        for i, (here, there) in enumerate(zip((qo, ko, vo, lse), kept))
    ]
    pieces, piece_len, width = qs.shape
    chips = pieces // 2
    core = ids[0]
    size = 64
    heads = width // size
    model = hid.shape[2]
    ours, theirs = ours[...].astype(f32), theirs[...].astype(f32)
    first = jnp.where(core == 0, ours, theirs)
    second = jnp.where(core == 0, theirs, ours)
    biases = jnp.concatenate([first, second], 1)
    qb, vb = biases[0:1, :], biases[1:2, :]
    for i, load in enumerate(loads):
        load.wait()
        some = slice(i * step, (i + 1) * step)
        span = slice(i * step * piece_len, (i + 1) * step * piece_len)
        product = matmul(hid[some].reshape(step * piece_len, model), w[...])
        query = (product[:, :width] + qb).astype(bf16) * bf16(size**-0.5)
        qs[some] = query.reshape(step, piece_len, width)
        ko[span] = product[:, width : 2 * width].astype(bf16)
        vo[span] = (product[:, 2 * width :] + vb).astype(bf16)
    lane = lax.broadcasted_iota(jnp.int32, (piece_len, 128), 1)
    for k in range(chips):
        qo[k] = qs[2 * (ids[1] ^ k) + core]
    for copy in copies[:3]:
        copy.start()
    logs = [jnp.zeros((piece_len, 128), f32)] * chips
    parts = [[] for _ in range(chips)]
    for head in range(heads):
        cols = slice(head * size, (head + 1) * size)
        queries = qo[:, :, cols].reshape(chips * piece_len, size)
        s_all[...] = right_product(queries, ko[:, cols])
        shares = []
        for k in range(chips):
            chip = ids[1] ^ k
            rows = slice(k * piece_len, (k + 1) * piece_len)
            same = sq[chip] == sk[...]
            scores = s_all[rows, :] + bias_rows(be[head * chips + chip], bn[...], same)
            top = jnp.max(scores, -1, keepdims=True)
            powers = jnp.exp(scores - top)
            total = jnp.sum(powers, -1, keepdims=True)
            p_all[rows, :] = powers.astype(bf16)
            shares.append(1.0 / total)
            logs[k] = jnp.where(lane == head, top + jnp.log(total), logs[k])
        out = matmul(p_all[...], vo[:, cols])
        for k in range(chips):
            parts[k].append(out[k * piece_len : (k + 1) * piece_len] * shares[k])
    for k in range(chips):
        att[ids[1] ^ k] = jnp.concatenate(parts[k], 1).T.astype(bf16)
        lse[k] = logs[k]
    copies[3].start()
    for copy in copies:
        copy.wait()


def attend_back_kernel(hid_raw, q_raw, k_raw, v_raw, lse_raw, be, bn, sk, sq, *refs):
    ids = here()
    chips, piece_len, width = q_raw.shape
    ga_raw = refs[:chips]
    dq, mine, other, dw_mine, dw_other = refs[chips : chips + 5]
    hid, q, k, v, lse, ga, s_all, g_all, ds_all, p_all, dkv, dws, sems = refs[chips + 5 :]
    copies = [
        pltpu.make_async_copy(there, here, sems.at[i])
        for i, (there, here) in enumerate(
            zip((q_raw, k_raw, v_raw, lse_raw, hid_raw), (q, k, v, lse, hid))
        )
    ]
    copies[4:4] = [
        pltpu.make_async_copy(there, ga.at[i], sems.at[5 + i]) for i, there in enumerate(ga_raw)
    ]
    for copy in copies:
        copy.start()
    pieces = 2 * chips
    core = ids[0]
    size = 64
    heads = width // size
    dks = []
    dvs = []
    dqs = [[None] * heads for _ in range(chips)]
    for copy in copies[:-1]:
        copy.wait()
    gas = jnp.concatenate([ga[i].astype(f32).T.astype(bf16) for i in range(chips)], 0)
    for head in range(heads):
        cols = slice(head * size, (head + 1) * size)
        key = k[:, cols]
        value = v[:, cols]
        queries = q[:, :, cols].reshape(chips * piece_len, size)
        grads = gas[:, cols]
        s_all[...] = right_product(queries, key)
        g_all[...] = right_product(grads, value)
        for i in range(chips):
            chip = ids[1] ^ i
            rows = slice(i * piece_len, (i + 1) * piece_len)
            same = sq[chip] == sk[...]
            scores = s_all[rows, :] + bias_rows(be[head * chips + chip], bn[...], same)
            probs = jnp.exp(scores - lse[i, :, head : head + 1])
            grad = g_all[rows, :]
            weighted = jnp.sum(probs * grad, -1, keepdims=True)
            ds_all[rows, :] = (probs * (grad - weighted)).astype(bf16)
            p_all[rows, :] = probs.astype(bf16)
        grad_q = (matmul(ds_all[...], key) * (size**-0.5)).astype(bf16)
        for i in range(chips):
            dqs[i][head] = grad_q[i * piece_len : (i + 1) * piece_len]
        dks.append(left_product(ds_all[...], queries).astype(bf16))
        dvs.append(left_product(p_all[...], grads).astype(bf16))
    for i in range(chips):
        dq[i] = jnp.concatenate(dqs[i], 1)
    joined = jnp.concatenate(dks + dvs, 1)
    dkv[...] = joined.reshape(pieces, piece_len, 2 * width)
    for i in range(chips):
        chip = ids[1] ^ i
        mine[i] = dkv[2 * chip + core]
        other[i] = dkv[2 * chip + 1 - core]
    copies[-1].wait()
    _, _, model = hid.shape
    tokens = hid[...].reshape(pieces * piece_len, model)
    owned = jnp.concatenate([hid[2 * (ids[1] ^ i) + core] for i in range(chips)], 0)
    grad_q = dq[...].reshape(chips * piece_len, width)
    weights = jnp.concatenate([left_product(owned, grad_q), left_product(tokens, joined)], 1)
    groups = dw_mine.shape[0]
    rows = dws.shape[2]
    dws[...] = weights.reshape(dws.shape)
    for i in range(chips):
        chip = ids[1] ^ i
        for j in range(groups):
            span = slice(i * rows, (i + 1) * rows)
            dw_mine[j, span] = dws[2 * chip + core, ids[2] ^ j]
            dw_other[j, span] = dws[2 * chip + 1 - core, ids[2] ^ j].astype(bf16)
    total = jnp.concatenate(
        [
            jnp.sum(grad_q.astype(f32), 0, keepdims=True),
            jnp.sum(joined.astype(f32), 0, keepdims=True),
        ],
        1,
    )
    total = jnp.broadcast_to(total, (8, 3 * width))
    for j in range(groups):
        dw_mine[j, chips * rows :] = total
        dw_other[j, chips * rows :] = total.astype(bf16)


def input_grad_kernel(dq, mine, recv, w, out, scratch):
    ids = here()
    chips, piece_len, width = dq.shape
    dkv = (mine[...].astype(f32) + recv[...].astype(f32)).astype(bf16)
    grads = jnp.concatenate([dq[...], dkv], 2).reshape(chips * piece_len, 3 * width)
    total = right_product(grads, w[...])
    scratch[...] = total.astype(bf16).reshape(scratch.shape)
    for chip in range(chips):
        out[chip] = scratch[ids[1] ^ chip]


def add_kernel(left, right, out):
    out[...] = (left[...].astype(f32) + right[...].astype(f32)).astype(out.dtype)


def sum_rows_kernel(first, parts, out):
    total = first[...]
    for i in range(parts.shape[0]):
        total = total + parts[i].astype(f32)
    out[...] = total


def add_split_kernel(left, right, *outs):
    for k, out in enumerate(outs):
        out[...] = (left[k].astype(f32) + right[k].astype(f32)).astype(out.dtype)


def sum_split_kernel(*refs, parts, rows):
    total = refs[0][...].astype(f32)
    for r in refs[1:parts]:
        total = total + r[...].astype(f32)
    for k, out in enumerate(refs[parts:]):
        out[...] = total[k * rows : k * rows + out.shape[0]].astype(out.dtype)


def sum_lead_kernel(parts, *outs, rows):
    total = parts[0].astype(f32)
    for i in range(1, parts.shape[0]):
        total = total + parts[i].astype(f32)
    for k, out in enumerate(outs):
        out[...] = total[k * rows : k * rows + out.shape[0]].astype(out.dtype)


def project_kernel(wo, hid, vec, att, low, normed, inverse):
    branch = vec[2:3, :] + jnp.zeros(hid.shape, f32)
    for chip in range(att.shape[0]):
        branch = branch + left_product(att[chip], wo[chip])
    n1, r1 = normalize(hid[...].astype(f32) + branch)
    low[...] = (n1 * vec[3:4, :] + vec[4:5, :]).astype(bf16)
    normed[...] = n1
    inverse[...] = jnp.broadcast_to(r1, inverse.shape)


def gelu_parts(v):
    return jnp.tanh(GELU_A * (v + GELU_B * (v * v * v)))


def two_weights(both):
    pieces, rows, model = both.shape
    half = rows // 2
    first = both[:, :half, :].reshape(pieces * half, model)
    return first, both[:, half:, :].reshape(pieces * half, model)


def forward_kernel(vec, both_raw, *refs, parts):
    raw = refs[:parts]
    outs = refs[parts : 2 * parts]
    inner_ref, act_ref, both, x, sems = refs[2 * parts :]
    half = both.shape[1] // 2
    copies = [pltpu.make_async_copy(r, x.at[i], sems.at[i]) for i, r in enumerate(raw)]
    for i in range(2):
        span = (slice(None), pl.ds(i * half, half), slice(None))
        copies.append(pltpu.make_async_copy(both_raw.at[span], both.at[span], sems.at[parts + i]))
    for copy in copies:
        copy.start()
    for copy in copies[:-1]:
        copy.wait()
    _, rows, model = x.shape
    weight1 = both[:, :half, :].reshape(-1, model)
    inner = matmul(x[...].reshape(parts * rows, model), weight1) + vec[pl.ds(8 + lax.axis_index("dp"), 1), :]
    act = (0.5 * inner * (1.0 + gelu_parts(inner))).astype(bf16)
    inner_ref[...] = inner
    act_ref[...] = act
    copies[-1].wait()
    mixed = matmul(act, both[:, half:, :].reshape(-1, model))
    for i in range(parts):
        outs[i][...] = mixed[i * rows : (i + 1) * rows].astype(outs[i].dtype)


def middle_kernel(*refs):
    recv = refs[:-7]
    normed, cot, vec, out, low, mix, sums = refs[-7:]
    first = normed[...] * vec[3:4, :] + vec[4:5, :]
    mixed = vec[5:6, :]
    for r in recv:
        mixed = mixed + r[...].astype(f32)
    n2, r2 = normalize(first + mixed)
    gain = vec[6:7, :]
    out[...] = (n2 * gain + vec[7:8, :]).astype(bf16)
    g = cot[...].astype(f32)
    grad = norm_back(g, n2, r2, gain)
    rounded = grad.astype(bf16)
    mix[...] = grad
    low[...] = rounded
    sums[0:1, :] = jnp.sum(g * n2, 0, keepdims=True)
    sums[1:2, :] = jnp.sum(g, 0, keepdims=True)
    sums[2:3, :] = jnp.sum(rounded.astype(f32), 0, keepdims=True)
    sums[3:, :] = jnp.zeros((5, sums.shape[1]), f32)


def backward_kernel(both, inner_ref, *refs, parts):
    grads = refs[:parts]
    outs = refs[parts : 2 * parts]
    gi_ref, total = refs[2 * parts :]
    rows = grads[0].shape[0]
    weight1, weight2 = two_weights(both)
    gm = jnp.concatenate([r[...] for r in grads], 0)
    grad_act = right_product(gm, weight2)
    v = inner_ref[...]
    t = gelu_parts(v)
    slope = 0.5 * (1.0 + t) + 0.5 * v * (1.0 - t * t) * (GELU_A * (1.0 + 3.0 * GELU_B * (v * v)))
    gi = (grad_act * slope).astype(bf16)
    gi_ref[...] = gi
    first = right_product(gi, weight1)
    for i in range(parts):
        outs[i][...] = first[i * rows : (i + 1) * rows].astype(outs[i].dtype)
    total[...] = jnp.sum(gi.astype(f32), 0, keepdims=True)


def inner_outer_kernel(gi, act, sums, total, *refs, parts):
    x = refs[:parts]
    grads = refs[parts : 2 * parts]
    out = refs[2 * parts]
    pieces, tall, model = out.shape
    units = (tall - 8) // 2
    gm = jnp.concatenate([r[...] for r in grads], 0)
    tokens = jnp.concatenate([r[...] for r in x], 0)
    out[:, :units, :] = left_product(tokens, gi[...]).astype(bf16).reshape(pieces, units, model)
    out[:, units : 2 * units, :] = (
        left_product(act[...], gm).astype(bf16).reshape(pieces, units, model)
    )
    vectors = [sums[i : i + 1, :] for i in range(3)] + [total[...]]
    for piece in range(pieces):
        put_vectors(out, piece, piece, 2 * units, vectors, units)


def residual_kernel(mix, normed, inverse, vec, wo, att, above, *refs, parts, lined):
    ids = here() if lined else (0, 0, 0)
    recv = refs[:parts]
    res_raw, stacked = refs[parts : parts + 2]
    back_raw = refs[parts + 2 : -4]
    res, back, out, sems = refs[-4:]
    copies = []

    def send(here, there):
        copies.append(pltpu.make_async_copy(here, there, sems.at[len(copies)]))
        copies[-1].start()

    tall = above.shape[1] - 8
    send(above.at[:, pl.ds(0, tall), :], stacked.at[:, pl.ds(0, tall), :])
    first = mix[...]
    for r in recv:
        first = first + r[...].astype(f32)
    n1 = normed[...]
    grad = norm_back(first, n1, inverse[:, 0:1], vec[3:4, :])
    rounded = grad.astype(bf16)
    for k, raw in enumerate(back_raw):
        back[k] = right_product(wo[ids[1] ^ k], rounded).astype(bf16)
        send(back.at[k], raw)
    res[...] = grad
    send(res, res_raw)
    vectors = [jnp.zeros((1, wo.shape[2]), f32)] * 4 + [
        jnp.sum(first * n1, 0, keepdims=True),
        jnp.sum(first, 0, keepdims=True),
        jnp.sum(rounded.astype(f32), 0, keepdims=True),
    ]
    rows = out.shape[1] - 8
    each = out.shape[0] // att.shape[0]
    for chip in range(att.shape[0]):
        part = matmul(att[chip], rounded).astype(bf16)
        for i in range(each):
            piece = each * chip + i
            out[piece, 8:] = part[i * rows : (i + 1) * rows]
            put_vectors(out, piece, piece, 0, vectors, rows)
            out[piece, :8] = out[piece, :8] + above[piece, tall:]
    send(out, stacked.at[:, pl.ds(tall, rows + 8), :])
    for copy in copies:
        copy.wait()


def put_vectors(out, piece, at, row, vectors, rows):
    parts = [v[:, piece * rows : (piece + 1) * rows] for v in vectors]
    fill = out.shape[2] - rows * len(parts)
    line = jnp.concatenate(parts + [jnp.zeros((1, fill), f32)], 1)
    out[at, row : row + 8, :] = jnp.broadcast_to(line, (8, out.shape[2])).astype(bf16)


def ordered(ids, refs, scratch):
    for k, r in enumerate(refs):
        scratch[ids[2] ^ k] = r[...]


def finish_inner_kernel(*refs, parts):
    ids = here()
    inner, outer, output, vectors, scratch = refs[parts:]
    ordered(ids, refs[:parts], scratch)
    rows = inner.shape[0]
    units = outer.shape[0] // parts
    pieces = scratch.shape[2] // units
    for piece in range(pieces):
        inner[:, piece * parts * units : (piece + 1) * parts * units] = jnp.concatenate(
            [
                scratch[g, :rows, piece * units : (piece + 1) * units].astype(f32)
                for g in range(parts)
            ],
            1,
        )
    total = jnp.zeros((1, scratch.shape[2]), f32)
    at = rows + units
    for g in range(parts):
        outer[g * units : (g + 1) * units, :] = scratch[g, rows:at, :].astype(f32)
        line = scratch[g, at : at + 8, :].astype(f32)[0:1]
        vectors[g : g + 1, :] = line
        total = total + line
    vectors[parts : parts + 1, :] = total
    bias = [vectors[g : g + 1, 3 * rows : 4 * rows] for g in range(parts)]
    fill = jnp.zeros((1, scratch.shape[2] - parts * rows), f32)
    vectors[parts + 1 : parts + 2, :] = jnp.concatenate(bias + [fill], 1)
    if scratch.shape[1] > at + 8:
        last = scratch[0, at + 8 :, :].astype(f32)
        for g in range(1, parts):
            last = last + scratch[g, at + 8 :, :].astype(f32)
        output[...] = last


def finish_kernel(*refs):
    ids = here()
    parts = len(refs) - 4
    gq, gk, gv, scratch = refs[parts:]
    quarters, chips, rows, wide = scratch.shape
    for j, r in enumerate(refs[:parts]):
        for k in range(chips):
            scratch[ids[2] ^ j, ids[1] ^ k] = r[k]
    width = wide // 3
    for part in range(quarters):
        block = [scratch[part, chip].astype(f32) for chip in range(chips)]
        for i, out in enumerate((gq, gk, gv)):
            out[part * rows : (part + 1) * rows, :] = jnp.concatenate(
                [b[:, i * width : (i + 1) * width] for b in block], 1
            )


def log_counts(count):
    return jnp.where(count > 0, jnp.log(jnp.maximum(count, 1).astype(f32)), MASKED)


def exchange(array, k):
    count = lax.axis_size("dp")
    return lax.ppermute(array, "dp", [(i, i ^ k) for i in range(count)])


def exchange_all(array):
    return [array] + [exchange(array, k) for k in range(1, lax.axis_size("dp"))]


def exchange_parts(parts):
    return [parts[0]] + [exchange(parts[k], k) for k in range(1, lax.axis_size("dp"))]


def swap_cores(array):
    count = lax.axis_size("seq")
    return lax.ppermute(array, "seq", [(i, i ^ 1) for i in range(count)])


def line_exchange(array, k):
    count = lax.axis_size("seq")
    return lax.ppermute(array, "seq", [(i, i ^ (2 * k)) for i in range(count)])


def line_parts(parts):
    return [parts[0]] + [line_exchange(parts[k], k) for k in range(1, len(parts))]


def tied(value, *others):
    return lax.optimization_barrier((value,) + others)[0]


def add_split(left, right, outs):
    return run_kernel(add_split_kernel, "add", outs, (left, right))


def sum_split(arrays, outs):
    return run_kernel(
        functools.partial(sum_split_kernel, parts=len(arrays), rows=outs[0][0][0]),
        "sum",
        outs,
        tuple(arrays),
    )


def line_all(array):
    return [array] + [line_exchange(array, k) for k in range(1, lax.axis_size("seq") // 2)]


def along_line(array):
    count = lax.axis_size("seq")
    lines = [[2 * i + c for i in range(count // 2)] for c in range(2)]
    return lax.all_to_all(array, "seq", 0, 0, tiled=True, axis_index_groups=lines)


def stack(*arrays):
    shape = (len(arrays),) + arrays[0].shape
    return run_kernel(stack_kernel, "stack", [(shape, bf16)], arrays)[0]


def concat(*arrays):
    shape = (sum(a.shape[0] for a in arrays),) + arrays[0].shape[1:]
    return run_kernel(concat_kernel, "concat", [(shape, bf16)], arrays)[0]


def finish_inner(shares, rows):
    groups = len(shares)
    share = shares[0]
    model = share.shape[1]
    return run_kernel(
        functools.partial(finish_inner_kernel, parts=groups),
        "finish_inner",
        [
            ((rows, groups * model), f32),
            ((groups * rows, model), f32),
            ((rows, model), f32),
            ((8, model), f32),
        ],
        tuple(shares),
        scratch=[pltpu.VMEM((groups,) + share.shape, bf16)],
    )


class HeadAttention:
    def __init__(self, hidden, weights, biases, segments, random_blocks, output_weight, vec_local):
        self.splits = splits = lax.axis_size("seq")
        self.chips = chips = splits // 2
        self.position = position = lax.axis_index("seq")
        core = position % 2
        chip = position // 2
        group = lax.axis_index("dp")
        self.packed = lax.all_gather(hidden, "seq")
        piece_len, model = hidden.shape
        rows = model // splits
        width = model // chips
        heads = HEADS // chips
        half = rows // 2
        cut = run_kernel(
            cut_kernel,
            "cut",
            [((half, 3 * width), bf16)] * chips,
            tuple(weights),
            scratch=[
                pltpu.VMEM((3, half, model), bf16),
                pltpu.VMEM((chips, half, 3 * width), bf16),
                pltpu.SemaphoreType.DMA((3,)),
            ],
            raw=range(3),
        )
        cut = stack(*line_parts(cut))
        cut_next = exchange(cut, 1)
        (out_half,) = run_kernel(
            cut_output_kernel,
            "cut_output",
            [((half + 8, model), bf16)],
            (output_weight, vec_local),
        )
        cut = stack(cut, cut_next)
        (weight,) = run_kernel(
            assemble_kernel,
            "assemble",
            [((splits, 2, half, 3 * width), bf16)],
            (cut, swap_cores(cut)),
        )
        self.out_half = stack(*line_all(tied(out_half, cut_next)))
        self.out_next = exchange(self.out_half, 2)
        self.weight = weight.reshape(model, 3 * width)
        self.biases = biases
        self.hidden = hidden
        block_count = segments.shape[1] // BLOCK
        per_piece = piece_len // BLOCK
        own = random_blocks[0].reshape(chips, 2, per_piece, HEADS, -1)
        own = lax.dynamic_index_in_dim(own, core, 1, keepdims=False)
        own = lax.dynamic_slice_in_dim(own, chip * heads, heads, 2)
        own = own.reshape(chips * per_piece, heads, -1).transpose(1, 0, 2)
        block = jnp.arange(block_count, dtype=jnp.int32)
        mine = (
            (jnp.arange(chips, dtype=jnp.int32)[:, None] * 2 + core) * per_piece
            + jnp.arange(per_piece, dtype=jnp.int32)[None, :]
        ).reshape(-1)
        ends = ((block == 0) | (block == block_count - 1)).astype(jnp.int32)
        near = (jnp.abs(block[None, :] - mine[:, None]) <= 1).astype(jnp.int32)
        listed = jnp.sum((own[..., None] == block).astype(jnp.int32), 2)
        count = listed + near[None] + ends
        self.same_bias = jnp.repeat(log_counts(count), BLOCK, axis=2).reshape(
            heads * chips, per_piece, -1
        )
        self.other_bias = jnp.repeat(
            jnp.where(ends > 0, 0.0, MASKED).astype(f32)[None], BLOCK, axis=1
        )
        self.key_seg = segments
        self.query_seg = lax.dynamic_index_in_dim(
            segments.reshape(chips, 2, piece_len), core, 1, keepdims=False
        ).reshape(chips, piece_len, 1)
        self.piece_len, self.width, self.model = piece_len, width, model

    def masks(self):
        return (self.same_bias, self.other_bias, self.key_seg, self.query_seg)

    def inner_weights(self, inner_weight, outer_weight):
        groups = lax.axis_size("dp")
        rows = inner_weight.shape[0]
        units = outer_weight.shape[0] // groups
        (both,) = run_kernel(
            cut_inner_kernel,
            "cut_inner",
            [((rows + units, self.model), bf16)],
            (inner_weight, outer_weight),
            scratch=[pltpu.VMEM((groups, rows, self.model), bf16)],
        )
        self.pair = jnp.stack(self.biases, 0)
        self.pair_other = swap_cores(self.pair)
        self.both = lax.all_gather(tied(both, self.packed, self.weight, self.out_half), "seq")

    def forward(self):
        chips, piece_len, width, model = self.chips, self.piece_len, self.width, self.model
        tokens = self.splits * piece_len
        one = (chips, piece_len, width)
        kept = [
            (one, bf16),
            ((tokens, width), bf16),
            ((tokens, width), bf16),
            ((chips, piece_len, 128), f32),
        ]
        att, self.q, self.k, self.v, self.lse = run_kernel(
            attend_kernel,
            "attend",
            [((chips, width, piece_len), bf16)] + kept,
            (self.weight, *self.masks(), self.pair, self.pair_other, self.packed),
            scratch=[pltpu.VMEM(self.packed.shape, bf16)]
            + [pltpu.VMEM(*spec) for spec in kept]
            + [
                pltpu.VMEM((self.splits, piece_len, width), bf16),
                pltpu.VMEM((chips * piece_len, tokens), f32),
                pltpu.VMEM((chips * piece_len, tokens), bf16),
                pltpu.SemaphoreType.DMA((len(kept) + 2,)),
            ],
            raw=(7,),
            raw_outs=range(1, 1 + len(kept)),
            flops=6 * tokens * model * width + 2 * tokens * tokens * width,
            powers=tokens * tokens * 3 // 2,
            grant=16 << 20,
        )
        out_half = stack(tied(self.out_half, att), self.out_next)
        half = model // self.splits // 2
        weight, self.vec = run_kernel(
            assemble_output_kernel,
            "assemble_output",
            [((self.splits, 2, half, model), bf16), ((16, model), f32)],
            (out_half, swap_cores(out_half)),
            scratch=[pltpu.VMEM((self.splits, 8, model), bf16)],
        )
        self.output_weight = weight.reshape(chips, width, model)
        att = along_line(att)
        return att

    def backward(self, grads, grad_res, share):
        chips, piece_len, width = self.chips, self.piece_len, self.width
        splits, model = self.splits, self.model
        groups = lax.axis_size("dp")
        tokens = splits * piece_len
        rows = model // splits
        one = (chips, piece_len, width)
        two = (chips, piece_len, 2 * width)
        quarter = (rows // groups, 3 * width)
        group = (chips * quarter[0] + 8, 3 * width)
        wide = ((groups,) + group, bf16)
        keep = (self.packed, self.q, self.k, self.v, self.lse)
        dq, mine, other, dw_mine, dw_other = run_kernel(
            attend_back_kernel,
            "attend_back",
            [(one, bf16), (two, bf16), (two, bf16), (wide[0], f32), wide],
            keep + self.masks() + tuple(grads),
            scratch=[pltpu.VMEM(a.shape, a.dtype) for a in keep]
            + [
                pltpu.VMEM((chips,) + grads[0].shape, bf16),
                pltpu.VMEM((chips * piece_len, tokens), f32),
                pltpu.VMEM((chips * piece_len, tokens), f32),
                pltpu.VMEM((chips * piece_len, tokens), bf16),
                pltpu.VMEM((chips * piece_len, tokens), bf16),
                pltpu.VMEM((splits, piece_len, 2 * width), bf16),
                pltpu.VMEM((splits, groups) + quarter, f32),
                pltpu.SemaphoreType.DMA((len(keep) + chips,)),
            ],
            raw=(*range(5), *range(9, 9 + chips)),
            flops=5 * tokens * tokens * width + 6 * tokens * model * width,
            powers=tokens * tokens * 3 // 2,
            grant=24 << 20,
        )
        recv = swap_cores(other)
        dws = add_split(dw_mine, swap_cores(dw_other), [(group, bf16)] * groups)
        dws = exchange_parts(dws)
        full = (piece_len, model)
        *dws, sums = sum_split(dws, [(quarter, bf16)] * chips + [((8, 3 * width), f32)])
        dq = tied(dq, dws[0])
        (partial,) = run_kernel(
            input_grad_kernel,
            "input_grad",
            [((chips,) + full, bf16)],
            (dq, mine, recv, self.weight),
            scratch=[pltpu.VMEM((chips,) + full, bf16)],
            flops=3 * tokens * model * width,
        )
        dws = line_parts(dws)
        part = (chips,) + quarter
        dw = stack(*dws)
        every = exchange_all(dw)
        self.shares = exchange_all(tied(share, *every[1:]))
        count = splits
        lines = [[2 * i + c for i in range(count // 2)] for c in range(2)]
        partial = lax.psum_scatter(
            partial, "seq", scatter_dimension=0, axis_index_groups=lines, tiled=False
        )[None]
        gq, gk, gv = run_kernel(
            finish_kernel,
            "finish",
            [((rows, model), f32)] * 3,
            tuple(every),
            scratch=[pltpu.VMEM((groups,) + part, bf16)],
        )
        (input_grad,) = run_kernel(
            sum_rows_kernel, "sum_rows", [(full, f32)], (grad_res, partial)
        )
        core = self.position % 2
        bias_q = lax.dynamic_slice_in_dim(sums[0], core * rows, rows)
        bias_v = lax.dynamic_slice_in_dim(sums[0], 2 * width + core * rows, rows)
        return input_grad, gq, bias_q, gk, gv, bias_v


def one_hot(index, count):
    return (index[..., None] == jnp.arange(count, dtype=jnp.int32)).astype(bf16)


def with_halo(block, axis, dim, width):
    count = lax.axis_size(axis)
    forward = [(i, i + 1) for i in range(count - 1)]
    backward = [(target, source) for source, target in forward]
    low = lax.ppermute(
        lax.slice_in_dim(block, block.shape[dim] - width, None, axis=dim), axis, forward
    )
    high = lax.ppermute(lax.slice_in_dim(block, 0, width, axis=dim), axis, backward)
    return jnp.concatenate([low, block, high], axis=dim)


def broadcast(block, axis, owner):
    block = jnp.where(lax.axis_index(axis) == owner, block, jnp.zeros_like(block))
    return lax.psum(block, axis)


class TokenAttention:
    def __init__(self, hidden, weights, biases, segments, random_blocks, output_weight, vec_local):
        self.splits = splits = lax.axis_size("seq")
        self.position = position = lax.axis_index("seq")
        self.hidden = hidden
        self.segments = segments
        self.random_blocks = random_blocks
        self.weights = [lax.all_gather(w, "seq", axis=0, tiled=True) for w in weights]
        self.output_weight = lax.all_gather(output_weight, "seq", axis=0, tiled=True)[None]
        vec = lax.all_gather(vec_local, "seq")
        self.vec = vec.transpose(1, 0, 2).reshape(vec_local.shape[0], -1).astype(f32)

    def forward(self):
        hidden, segments = self.hidden, self.segments
        splits, position = self.splits, self.position
        seq_count = segments.shape[0]
        row_count, model = hidden.shape
        piece_len = row_count // seq_count
        size = model // HEADS
        per = piece_len // BLOCK
        slots = self.random_blocks.shape[3]
        reqs = seq_count * per * HEADS * slots
        cap = max(2, 3 * reqs // (2 * splits) + 1)
        vec = self.vec
        wq, wk, wv = self.weights
        query = (matmul(hidden, wq) + vec[0:1]).astype(bf16)
        keys = matmul(hidden, wk).astype(bf16)
        values = (matmul(hidden, wv) + vec[1:2]).astype(bf16)
        joined = jnp.concatenate([keys, values], 1).reshape(seq_count, piece_len, 2 * model)
        extended = with_halo(joined, "seq", 1, BLOCK)
        first = broadcast(joined[:, :BLOCK], "seq", 0)
        last = broadcast(joined[:, piece_len - BLOCK :], "seq", splits - 1)
        tiles = seq_count * per * HEADS
        tile_size = BLOCK * 2 * size
        kv_tiles = (
            joined.reshape(seq_count, per, BLOCK, 2, HEADS, size)
            .transpose(0, 1, 4, 2, 3, 5)
            .reshape(tiles, tile_size)
        )
        req = jnp.arange(reqs, dtype=jnp.int32)
        req_seq = req // (per * HEADS * slots)
        req_head = req // slots % HEADS
        earlier = (req[:, None] > req[None, :]).astype(jnp.int32)
        everyone = (
            self.random_blocks.reshape(seq_count, splits, per, HEADS, slots)
            .transpose(1, 0, 2, 3, 4)
            .reshape(splits, reqs)
        )
        is_mine = (everyone // per == position).astype(jnp.int32)
        place = jnp.sum(is_mine[:, None, :] * earlier, 2)
        slot = jnp.where(is_mine == 1, place, cap)
        tile_of = (req_seq * per + everyone % per) * HEADS + req_head
        chosen = slot[:, :, None] == jnp.arange(cap, dtype=jnp.int32)
        send = jnp.sum(jnp.where(chosen, tile_of[:, :, None], 0), 1).reshape(splits * cap)
        self.send = one_hot(send, tiles)
        outgoing = matmul(self.send, kv_tiles).astype(bf16).reshape(splits, cap, tile_size)
        incoming = lax.all_to_all(outgoing, "seq", 0, 0, tiled=True)
        asked = lax.dynamic_slice_in_dim(self.random_blocks, position * per, per, 1)
        owner = asked.reshape(reqs) // per
        before = jnp.sum((owner[:, None] == owner[None, :]).astype(jnp.int32) * earlier, 1)
        self.arrival = one_hot(owner * cap + before, splits * cap)
        fetched = matmul(self.arrival, incoming.reshape(splits * cap, tile_size)).astype(bf16)
        moved = fetched.reshape(seq_count, per, HEADS, slots * BLOCK, 2, size)
        spans = [slice(i * BLOCK, (i + 3) * BLOCK) for i in range(per)]
        fixed = jnp.stack(
            [jnp.concatenate([extended[:, span], first, last], 1) for span in spans], 1
        )
        fixed = fixed.reshape(seq_count, per, 5 * BLOCK, 2, HEADS, size)
        paired = jnp.concatenate(
            [fixed.transpose(3, 0, 1, 4, 2, 5), moved.transpose(4, 0, 1, 2, 3, 5)], 4
        )
        self.keys, self.values = paired[0], paired[1]
        edge = jnp.full((seq_count, BLOCK), -1, jnp.int32)
        padded = jnp.concatenate([edge, segments, edge], 1)
        query_seg = lax.dynamic_slice_in_dim(segments, position * piece_len, piece_len, 1)
        ext_seg = lax.dynamic_slice_in_dim(padded, position * piece_len, piece_len + 2 * BLOCK, 1)
        always = jnp.full((seq_count, 2 * BLOCK), -2, jnp.int32)
        seg_fixed = jnp.stack(
            [jnp.concatenate([ext_seg[:, span], always], 1) for span in spans], 1
        )
        seg_fixed = jnp.broadcast_to(
            seg_fixed[:, :, None], (seq_count, per, HEADS, 5 * BLOCK)
        )
        seg_blocks = segments.reshape(seq_count, -1, BLOCK)
        asked_hot = one_hot(asked, seg_blocks.shape[1])
        seg_moved = jnp.einsum(
            "gjhrb,gbt->gjhrt", asked_hot, seg_blocks.astype(bf16), preferred_element_type=f32
        ).astype(jnp.int32)
        key_seg = jnp.concatenate(
            [seg_fixed, seg_moved.reshape(seq_count, per, HEADS, slots * BLOCK)], 3
        )[:, :, :, None, :]
        self.allowed = (
            query_seg.reshape(seq_count, per, 1, BLOCK, 1) == key_seg
        ) | (key_seg == -2)
        self.query = query.reshape(seq_count, per, BLOCK, HEADS, size)
        scores = self.scores()
        top = jnp.max(scores, -1, keepdims=True)
        powers = jnp.exp(scores - top)
        total = jnp.sum(powers, -1, keepdims=True)
        self.log_total = top + jnp.log(total)
        attended = jnp.einsum(
            "gjhqk,gjhke->gjqhe",
            (powers / total).astype(bf16),
            self.values,
            preferred_element_type=f32,
        )
        return attended.astype(bf16).reshape(row_count, model).T[None]

    def scores(self):
        raw = jnp.einsum("gjqhe,gjhke->gjhqk", self.query, self.keys, preferred_element_type=f32)
        return jnp.where(self.allowed, raw * self.query.shape[-1] ** -0.5, MASKED)

    def inner_weights(self, inner_weight, outer_weight):
        splits = self.splits
        groups, group = lax.axis_size("dp"), lax.axis_index("dp")
        rows = inner_weight.shape[0]
        units, model = outer_weight.shape[0] // groups, outer_weight.shape[1]
        inner = inner_weight.reshape(rows, splits, groups, units)
        outer = outer_weight.reshape(groups, units, model)
        inner = lax.dynamic_index_in_dim(inner, group, 2, keepdims=False).reshape(rows, model)
        outer = lax.dynamic_index_in_dim(outer, group, 0, keepdims=False)
        both = lax.all_gather(jnp.concatenate([inner, outer], 0), "seq")
        both = both.reshape(splits, 2, rows, model).transpose(1, 0, 2, 3)
        self.both = both.reshape(1, 2 * model, model)

    def backward(self, grads, grad_res, share):
        hidden = self.hidden
        grad = grads[0].T
        self.shares = exchange_all(share)
        splits, position = self.splits, self.position
        seq_count, per, _, _, size = self.query.shape
        row_count, model = hidden.shape
        piece_len = per * BLOCK
        slots = self.random_blocks.shape[3]
        scale = size**-0.5
        probs = jnp.exp(self.scores() - self.log_total)
        grad_split = grad.reshape(seq_count, per, BLOCK, HEADS, size)
        grad_probs = jnp.einsum(
            "gjqhe,gjhke->gjhqk", grad_split, self.values, preferred_element_type=f32
        )
        weighted = jnp.sum(probs * grad_probs, -1, keepdims=True)
        grad_scores = (probs * (grad_probs - weighted)).astype(bf16)
        grad_query = (
            jnp.einsum("gjhqk,gjhke->gjqhe", grad_scores, self.keys, preferred_element_type=f32)
            * scale
        )
        grad_key = (
            jnp.einsum("gjhqk,gjqhe->gjhke", grad_scores, self.query, preferred_element_type=f32)
            * scale
        )
        grad_value = jnp.einsum(
            "gjhqk,gjqhe->gjhke", probs.astype(bf16), grad_split, preferred_element_type=f32
        )
        paired = jnp.stack([grad_key, grad_value], 0)
        fixed_len = 5 * BLOCK
        fixed = (
            paired[:, :, :, :, :fixed_len]
            .transpose(1, 2, 4, 0, 3, 5)
            .reshape(seq_count, per, fixed_len, 2 * model)
        )
        moved = (
            paired[:, :, :, :, fixed_len:]
            .transpose(1, 2, 3, 4, 0, 5)
            .reshape(seq_count * per * HEADS * slots, BLOCK * 2 * size)
        )
        ext = jnp.zeros((seq_count, piece_len + 2 * BLOCK, 2 * model), f32)
        for i in range(per):
            ext = ext.at[:, i * BLOCK : (i + 3) * BLOCK].add(fixed[:, i, : 3 * BLOCK])
        first = jnp.sum(fixed[:, :, 3 * BLOCK : 4 * BLOCK], 1)
        last = jnp.sum(fixed[:, :, 4 * BLOCK :], 1)
        rims = jnp.concatenate([ext[:, :BLOCK], ext[:, piece_len + BLOCK :]], 1)
        beside = with_halo(rims.astype(bf16), "seq", 1, BLOCK).astype(f32)
        kv_grad = ext[:, BLOCK : BLOCK + piece_len]
        kv_grad = kv_grad.at[:, :BLOCK].add(beside[:, :BLOCK])
        kv_grad = kv_grad.at[:, piece_len - BLOCK :].add(beside[:, 3 * BLOCK :])
        first, last = lax.psum((first, last), "seq")
        kv_grad = kv_grad.at[:, :BLOCK].add(jnp.where(position == 0, first, 0.0))
        kv_grad = kv_grad.at[:, piece_len - BLOCK :].add(
            jnp.where(position == splits - 1, last, 0.0)
        )
        cap = self.send.shape[0] // splits
        outgoing = left_product(self.arrival, moved.astype(bf16)).astype(bf16)
        returned = lax.all_to_all(
            outgoing.reshape(splits, cap, -1), "seq", 0, 0, tiled=True
        ).reshape(splits * cap, -1)
        kv_grad = kv_grad + (
            left_product(self.send, returned)
            .reshape(seq_count, per, HEADS, BLOCK, 2, size)
            .transpose(0, 1, 3, 4, 2, 5)
            .reshape(seq_count, piece_len, 2 * model)
        )
        kv_grad = kv_grad.reshape(row_count, 2 * model).astype(bf16)
        grad_query = grad_query.reshape(row_count, model).astype(bf16)
        grads = (grad_query, kv_grad[:, :model], kv_grad[:, model:])
        input_grad = grad_res
        shares = []
        for part, weight in zip(grads, self.weights):
            input_grad = input_grad + right_product(part, weight)
            full = left_product(hidden, part)
            share = lax.psum_scatter(full, "seq", scatter_dimension=0, tiled=True)
            shares.append(lax.psum(share.astype(bf16), "dp").astype(f32))
        biases = jnp.stack([jnp.sum(grads[i].astype(f32), 0) for i in (0, 2)], 1)
        biases = lax.psum_scatter(biases, "seq", scatter_dimension=0, tiled=True)
        biases = lax.psum(biases.astype(bf16), "dp").astype(f32)
        return input_grad, shares[0], biases[:, 0], shares[1], shares[2], biases[:, 1]


def local(
    hidden_in,
    query_weight,
    query_bias,
    key_weight,
    value_weight,
    value_bias,
    output_weight,
    output_bias,
    first_gain,
    first_shift,
    inner_weight,
    inner_bias,
    outer_weight,
    outer_bias,
    second_gain,
    second_shift,
    segments,
    random_blocks,
    cotangent,
):
    seq_count, piece_len, model = hidden_in.shape
    splits = lax.axis_size("seq")
    groups = lax.axis_size("dp")
    row_count = seq_count * piece_len
    rows = model // splits
    units = outer_weight.shape[0] // groups
    hidden = hidden_in.reshape(row_count, model)
    by_heads = (
        seq_count == 1 and groups == 4 and 2 < splits and HEADS % max(1, splits // 2) == 0
    )
    vec_local = jnp.concatenate(
        [
            v.reshape(-1, rows)
            for v in (
                query_bias,
                value_bias,
                output_bias,
                first_gain,
                first_shift,
                outer_bias,
                second_gain,
                second_shift,
                inner_bias,
            )
        ]
    )
    attention = (HeadAttention if by_heads else TokenAttention)(
        hidden,
        (query_weight, key_weight, value_weight),
        (query_bias, value_bias),
        segments,
        random_blocks,
        output_weight,
        vec_local,
    )
    attention.inner_weights(inner_weight, outer_weight)
    attended = attention.forward()
    vec = attention.vec
    w_out = attention.output_weight
    full = (row_count, model)
    wide = (groups * row_count, splits * units)
    low, normed, inverse = run_kernel(
        project_kernel,
        "project",
        [(full, bf16), (full, f32), ((row_count, 128), f32)],
        (w_out, hidden, vec, attended),
        flops=2 * row_count * model * model,
    )
    lows = exchange_all(low)
    work = 2 * wide[0] * wide[1] * model
    both = attention.both
    parts = run_kernel(
        functools.partial(forward_kernel, parts=groups),
        "forward",
        [(full, f32)] + [(full, bf16)] * (groups - 1) + [(wide, f32), (wide, bf16)],
        (vec, both, *lows),
        scratch=[
            pltpu.VMEM(both.shape, bf16),
            pltpu.VMEM((groups,) + full, bf16),
            pltpu.SemaphoreType.DMA((groups + 2,)),
        ],
        raw=range(1, 2 + groups),
        flops=2 * work,
        powers=wide[0] * wide[1],
        grant=10 << 20,
    )
    inner, act = parts[groups:]
    layer_out, grad_low, grad_mix, sums2 = run_kernel(
        middle_kernel,
        "middle",
        [(full, bf16), (full, bf16), (full, f32), ((8, model), f32)],
        (*exchange_parts(parts), normed, cotangent.reshape(row_count, model), vec),
    )
    grads = exchange_all(grad_low)
    parts = run_kernel(
        functools.partial(backward_kernel, parts=groups),
        "backward",
        [(full, f32)] + [(full, bf16)] * (groups - 1) + [(wide, bf16), ((1, wide[1]), f32)],
        (both, inner, *grads),
        flops=2 * work,
        powers=wide[0] * wide[1],
    )
    recv = exchange_parts(parts[:groups])
    (above,) = run_kernel(
        functools.partial(inner_outer_kernel, parts=groups),
        "inner_outer",
        [((splits, 2 * rows + 8, model), bf16)],
        (parts[groups], act, sums2, parts[groups + 1], *lows, *grads),
        flops=2 * work,
        grant=(1 if by_heads else 4) * VMEM_BYTES,
    )
    slots = attended.shape[0]
    below = rows + 8
    grad_res, stacked, *grad_att = run_kernel(
        functools.partial(residual_kernel, parts=groups, lined=by_heads),
        "residual",
        [(full, f32), ((splits, 3 * rows + 8, model), bf16)]
        + [(attended.shape[1:], bf16)] * slots,
        (grad_mix, normed, inverse, vec, w_out, attended, above, *recv),
        scratch=[
            pltpu.VMEM(full, f32),
            pltpu.VMEM(attended.shape, bf16),
            pltpu.VMEM((splits, below, model), bf16),
            pltpu.SemaphoreType.DMA((slots + 3,)),
        ],
        raw_outs=range(2 + slots),
        flops=4 * row_count * model * model,
        grant=2 * VMEM_BYTES,
    )
    share = lax.psum_scatter(stacked, "seq", scatter_dimension=0, tiled=False)
    if by_heads:
        grad_att = line_parts(grad_att)
    input_grad, gq, bias_q, gk, gv, bias_v = attention.backward(grad_att, grad_res, share)
    d_inner, d_outer, d_output, vectors = finish_inner(attention.shares, rows)
    norm_sums = vectors[groups]

    def cut(line, i):
        return line[i * rows : (i + 1) * rows]

    return (
        layer_out.reshape(seq_count, piece_len, model),
        input_grad.reshape(seq_count, piece_len, model),
        gq,
        bias_q,
        gk,
        gv,
        bias_v,
        d_output,
        cut(norm_sums, 6),
        cut(norm_sums, 4),
        cut(norm_sums, 5),
        d_inner,
        vectors[groups + 1, : groups * units],
        d_outer,
        cut(norm_sums, 2),
        cut(norm_sums, 0),
        cut(norm_sums, 1),
    )


def solution(mesh):
    in_specs = (
        P("dp", "seq", None),
        P("seq", None),
        P("seq"),
        P("seq", None),
        P("seq", None),
        P("seq"),
        P("seq", None),
        P("seq"),
        P("seq"),
        P("seq"),
        P("seq", None),
        P("seq"),
        P("seq", None),
        P("seq"),
        P("seq"),
        P("seq"),
        P("dp", None),
        P("dp", None, None, None),
        P("dp", "seq", None),
    )
    out_specs = (
        P("dp", "seq", None),
        P("dp", "seq", None),
        P("seq", None),
        P("seq"),
        P("seq", None),
        P("seq", None),
        P("seq"),
        P("seq", None),
        P("seq"),
        P("seq"),
        P("seq"),
        P("seq", None),
        P("seq"),
        P("seq", None),
        P("seq"),
        P("seq"),
        P("seq"),
    )
    return jax.shard_map(local, mesh=mesh, in_specs=in_specs, out_specs=out_specs, check_vma=False)
```
